32 devices in a mesh: dp: 16 (over z, y, x), mp: 2 (over core).
Axes of the slice: x: 2, y: 2, z: 4, core: 2. Of those that a mesh axis runs over, the one named last changes fastest.
Arguments:
- query_in: bfloat16 [32, 64, 768], P('dp'), may hold values from -6 to 6
- passage_in: bfloat16 [32, 512, 768], P('dp'), may hold values from -6 to 6
- query_len: int32 [32], P('dp'), may hold values from 8 to 64, as said below
- passage_len: int32 [32], P('dp'), may hold values from 64 to 512, as said below
- positive: int32 [32], P('dp'), may hold values from 0 to 31, each once
- step: int32 [1], replicated, may hold values from 2 to 7
- rates: float32 [5], replicated, may hold values from 0.02 to 0.6, as said below
- attn_master: float32 [4, 768, 768], P(None, 'dp', 'mp')
- attn_first: float32 [4, 768, 768], P(None, 'dp', 'mp')
- attn_second: float32 [4, 768, 768], P(None, 'dp', 'mp'), as said below
- attn_average: float32 [4, 768, 768], P(None, 'dp', 'mp')
- ffn_master: float32 [2, 768, 3072], P(None, 'dp', 'mp')
- ffn_first: float32 [2, 768, 3072], P(None, 'dp', 'mp')
- ffn_second: float32 [2, 768, 3072], P(None, 'dp', 'mp'), as said below
- ffn_average: float32 [2, 768, 3072], P(None, 'dp', 'mp')
- norm_params: float32 [6, 768], replicated, as said below
- norm_first: float32 [6, 768], replicated
- norm_second: float32 [6, 768], replicated, as said below
- norm_average: float32 [6, 768], replicated, as said below
- col_bias: float32 [4608], P('mp'), may hold values from -1 to 1
- col_first: float32 [4608], P('mp')
- col_second: float32 [4608], P('mp'), as said below
- col_average: float32 [4608], P('mp'), may hold values from -1 to 1
Outputs:
- loss: float32 [1], replicated
- query_grad: float32 [32, 64, 768], P('dp')
- passage_grad: float32 [32, 512, 768], P('dp')
- attn_master_new: float32 [4, 768, 768], P(None, 'dp', 'mp')
- attn_first_new: float32 [4, 768, 768], P(None, 'dp', 'mp')
- attn_second_new: float32 [4, 768, 768], P(None, 'dp', 'mp')
- attn_average_new: float32 [4, 768, 768], P(None, 'dp', 'mp')
- ffn_master_new: float32 [2, 768, 3072], P(None, 'dp', 'mp')
- ffn_first_new: float32 [2, 768, 3072], P(None, 'dp', 'mp')
- ffn_second_new: float32 [2, 768, 3072], P(None, 'dp', 'mp')
- ffn_average_new: float32 [2, 768, 3072], P(None, 'dp', 'mp')
- norm_params_new: float32 [6, 768], replicated
- norm_first_new: float32 [6, 768], replicated
- norm_second_new: float32 [6, 768], replicated
- norm_average_new: float32 [6, 768], replicated
- col_bias_new: float32 [4608], P('mp')
- col_first_new: float32 [4608], P('mp')
- col_second_new: float32 [4608], P('mp')
- col_average_new: float32 [4608], P('mp')
- attn_copy_new: bfloat16 [4, 768, 768], P(None, 'dp', 'mp')
- ffn_copy_new: bfloat16 [2, 768, 3072], P(None, 'dp', 'mp')
The draws below stay inside these ranges and needn't reach their ends.
Inputs may be any that keep to these rules, and one draw needn't show every extreme that they name: A query's valid tokens are its first query_len tokens; the first 2 queries are full. A passage's valid tokens are its first passage_len tokens; the first 2 passages are full. The three rates of averaging lie in 0.4 to 0.6; both learning rates are positive. `attn_second`: positive. `ffn_second`: positive. `norm_params`: gains positive. `norm_second`: positive. `norm_average`: gains positive. `col_second`: positive.
All inputs are finite; a program needn't handle non-finite values.
Results may differ from the reference program's by a relative error of at most 0.0085.
The reference program's roundings to bfloat16 on the way count: a program that leaves them out, or rounds other values in their place, can miss the bound.
Values may be sent and summed in bfloat16 or wider, within the bound.
A program may use at most 192 MiB of HBM per device.

```python
import math
import jax
import jax.numpy as jnp
from jax import lax

D = 768
HEADS = 12
HD = 64
FF = 3072
QLEN = 64
PLEN = 512
PAIRS_DEV = 2
PAIRS = 32
N_MP = 2


def signed_draw(key, shape):
    return jnp.clip(jax.random.normal(key, shape, jnp.float32), -4.0, 4.0)


def square_factor(key, shape):
    return 2.0 * jnp.exp(jax.random.uniform(key, shape, jnp.float32, math.log(0.5), math.log(2.0)))


def attn_spread():
    return jnp.array([1.4, 1.4, 1.0, 5.0], jnp.float32)[:, None, None] / math.sqrt(D)


def attn_grad_size():
    return jnp.array([0.005, 0.005, 0.02, 0.03], jnp.float32)[:, None, None] / math.sqrt(PAIRS)


def ffn_spread():
    return jnp.array([1.0 / math.sqrt(D), 1.0 / math.sqrt(FF)], jnp.float32)[:, None, None]


def ffn_grad_size():
    return 0.04 / math.sqrt(PAIRS)


def norm_grad_size():
    return jnp.array([0.075, 0.015, 0.075, 0.075, 0.015, 0.075], jnp.float32)[:, None] / math.sqrt(PAIRS)


def col_grad_size():
    return 0.1 / math.sqrt(PAIRS)


def norm_like(key):
    center = jnp.array([0.0, 1.0, 0.0, 0.0, 1.0, 0.0], jnp.float32)[:, None]
    spread = jnp.array([0.2, 0.15, 0.2, 0.2, 0.15, 0.02], jnp.float32)[:, None]
    return center + spread * signed_draw(key, (6, D))


def span_draw(key, most):
    least = max(1, most // 8)
    drawn = jax.random.randint(key, (PAIRS,), least, most + 1)
    return jnp.where(jnp.arange(PAIRS) < PAIRS_DEV, most, drawn).astype(jnp.int32)


def draw_query_len(key, part):
    return span_draw(jax.random.fold_in(key, 101), QLEN)


def draw_passage_len(key, part):
    return span_draw(jax.random.fold_in(key, 102), PLEN)


def draw_rates(key, part):
    uniform_part = jax.random.uniform(jax.random.fold_in(key, 103), (5,), jnp.float32)
    matrix_low = 1.0 / math.sqrt(D)
    lower = jnp.array([0.4, 0.4, 0.4, matrix_low, 0.2], jnp.float32)
    upper = jnp.array([0.6, 0.6, 0.6, 1.5 * matrix_low, 0.4], jnp.float32)
    return lower + (upper - lower) * uniform_part


def draw_attn_master(key, part):
    return signed_draw(jax.random.fold_in(key, 111), (4, D, D)) * attn_spread()


def draw_attn_first(key, part):
    return signed_draw(jax.random.fold_in(key, 112), (4, D, D)) * attn_grad_size()


def draw_attn_second(key, part):
    return square_factor(jax.random.fold_in(key, 113), (4, D, D)) * attn_grad_size() ** 2


def draw_attn_average(key, part):
    return signed_draw(jax.random.fold_in(key, 114), (4, D, D)) * attn_spread()


def draw_ffn_master(key, part):
    return signed_draw(jax.random.fold_in(key, 121), (2, D, FF)) * ffn_spread()


def draw_ffn_first(key, part):
    return signed_draw(jax.random.fold_in(key, 122), (2, D, FF)) * ffn_grad_size()


def draw_ffn_second(key, part):
    return square_factor(jax.random.fold_in(key, 123), (2, D, FF)) * ffn_grad_size() ** 2


def draw_ffn_average(key, part):
    return signed_draw(jax.random.fold_in(key, 124), (2, D, FF)) * ffn_spread()


def draw_norm_params(key, part):
    return norm_like(jax.random.fold_in(key, 131))


def draw_norm_first(key, part):
    return signed_draw(jax.random.fold_in(key, 132), (6, D)) * norm_grad_size()


def draw_norm_second(key, part):
    return square_factor(jax.random.fold_in(key, 133), (6, D)) * norm_grad_size() ** 2


def draw_norm_average(key, part):
    return norm_like(jax.random.fold_in(key, 134))


def draw_col_first(key, part):
    return signed_draw(jax.random.fold_in(key, 142), (2 * D + FF,)) * col_grad_size()


def draw_col_second(key, part):
    return square_factor(jax.random.fold_in(key, 143), (2 * D + FF,)) * col_grad_size() ** 2


def level_of(key, dims, cuts, low, largest):
    level = 1.0
    for dim, shards_of in cuts:
        steps = jax.random.uniform(jax.random.fold_in(jax.random.fold_in(key, 6), dim), (shards_of,), jnp.float32, low / len(cuts), largest / len(cuts))
        level = level * jnp.repeat(jnp.exp(steps), dims[dim] // shards_of).reshape((-1,) + (1,) * (len(dims) - 1 - dim))
    return level


def bell_draw(key, dims, scale, bound, cuts=(), kind=jnp.bfloat16):
    result = scale * jax.random.normal(key, dims, jnp.float32)
    if cuts:
        result = result * level_of(key, dims, cuts, -0.22, 0.18)
    return jnp.clip(result, -bound, bound).astype(kind)


def setup_inputs(seed: int = 0) -> dict:
    seeds = jax.random.split(jax.random.key(seed), 24)
    return {
        "query_in": bell_draw(seeds[0], (PAIRS, QLEN, D), 1.0, 6.0, ((0, 16),)),
        "passage_in": bell_draw(seeds[1], (PAIRS, PLEN, D), 1.0, 6.0, ((0, 16),)),
        "query_len": draw_query_len(jax.random.fold_in(seeds[23], 71), 0),
        "passage_len": draw_passage_len(jax.random.fold_in(seeds[23], 71), 0),
        "positive": jax.random.permutation(seeds[4], PAIRS).astype(jnp.int32),
        "step": jax.random.randint(seeds[5], (1,), 2, 8).astype(jnp.int32),
        "rates": draw_rates(jax.random.fold_in(seeds[23], 71), 0),
        "attn_master": draw_attn_master(jax.random.fold_in(seeds[23], 71), 0),
        "attn_first": draw_attn_first(jax.random.fold_in(seeds[23], 71), 0),
        "attn_second": draw_attn_second(jax.random.fold_in(seeds[23], 71), 0),
        "attn_average": draw_attn_average(jax.random.fold_in(seeds[23], 71), 0),
        "ffn_master": draw_ffn_master(jax.random.fold_in(seeds[23], 71), 0),
        "ffn_first": draw_ffn_first(jax.random.fold_in(seeds[23], 71), 0),
        "ffn_second": draw_ffn_second(jax.random.fold_in(seeds[23], 71), 0),
        "ffn_average": draw_ffn_average(jax.random.fold_in(seeds[23], 71), 0),
        "norm_params": draw_norm_params(jax.random.fold_in(seeds[23], 71), 0),
        "norm_first": draw_norm_first(jax.random.fold_in(seeds[23], 71), 0),
        "norm_second": draw_norm_second(jax.random.fold_in(seeds[23], 71), 0),
        "norm_average": draw_norm_average(jax.random.fold_in(seeds[23], 71), 0),
        "col_bias": bell_draw(seeds[19], (2 * D + FF,), 0.2, 1.0, ((0, 2),), jnp.float32),
        "col_first": draw_col_first(jax.random.fold_in(seeds[23], 71), 0),
        "col_second": draw_col_second(jax.random.fold_in(seeds[23], 71), 0),
        "col_average": bell_draw(seeds[22], (2 * D + FF,), 0.2, 1.0, ((0, 2),), jnp.float32),
    }


@jax.custom_vjp
def low(v):
    return lax.optimization_barrier(v.astype(jnp.bfloat16)).astype(jnp.float32)

@jax.custom_vjp
def low_back(v):
    return v

def low_keep(v):
    return (low(v), None)

def low_pass(kept, grad):
    return (grad,)

def back_keep(v):
    return (v, None)

def back_low(kept, grad):
    return (low(grad),)
low.defvjp(low_keep, low_pass)
low_back.defvjp(back_keep, back_low)
PRECISE = lax.Precision.HIGHEST
NEG_FILL = -1e+30
SOFTMAX_TEMPER = 0.02
NORM_EPS = 1e-12
DECAY_WEIGHT = 0.01
ADAM_EPS = 1e-08

def both_ways(value):
    return low_back(low(value))

def matrix_product(left, right):
    return jnp.dot(left, right, precision=PRECISE, preferred_element_type=jnp.float32)

def norm_rows(values, gain, shift):
    center = values - lax.optimization_barrier(jnp.mean(values, axis=-1, keepdims=True))
    spread = lax.optimization_barrier(jnp.mean(center * center, axis=-1, keepdims=True))
    return center * lax.rsqrt(spread + NORM_EPS) * gain + shift

def attend(heads_q, heads_k, heads_v, length):
    similarity_scores = jnp.einsum('qhd,khd->hqk', heads_q, heads_k, precision=PRECISE)
    similarity_scores = low_back(similarity_scores) * HD ** (-0.5)
    key_valid = jnp.arange(heads_k.shape[0]) < length
    similarity_scores = jnp.where(key_valid[None, None, :], similarity_scores, NEG_FILL)
    row_top = lax.optimization_barrier(jnp.max(similarity_scores, axis=-1, keepdims=True))
    exp_scores = jnp.exp(similarity_scores - row_top)
    attn_probs = exp_scores / lax.optimization_barrier(jnp.sum(exp_scores, axis=-1, keepdims=True))
    return jnp.einsum('hqk,khd->qhd', low(attn_probs), heads_v, precision=PRECISE)

def unpack_columns(col_bias):
    blocks = col_bias.reshape(N_MP, -1)
    part_width = D // N_MP
    query_bias = blocks[:, :part_width].reshape(D)
    value_bias = blocks[:, part_width:2 * part_width].reshape(D)
    hidden_bias = blocks[:, 2 * part_width:].reshape(FF)
    return (query_bias, value_bias, hidden_bias)

def pool_unit(values, length, slots):
    token_mask = (jnp.arange(slots) < length).astype(jnp.float32)
    pooled = lax.optimization_barrier(jnp.sum(values * token_mask[:, None], axis=0)) / length.astype(jnp.float32)
    return pooled * lax.rsqrt(jnp.sum(pooled * pooled) + 1e-06)

def to_heads(values):
    return values.reshape(values.shape[0], HEADS, HD)

def embed_pair(params, query_x, passage_x, query_length, passage_length):
    attn_w, ffn_w, norm_p, col_b = params
    query_bias, value_bias, hidden_bias = unpack_columns(col_b)
    tokens = jnp.concatenate([query_x, passage_x], axis=0)
    proj_q = to_heads(both_ways(matrix_product(tokens, attn_w[0]) + query_bias))
    proj_k = to_heads(both_ways(matrix_product(tokens, attn_w[1])))
    proj_v = to_heads(both_ways(matrix_product(tokens, attn_w[2]) + value_bias))
    out_query = attend(proj_q[:QLEN], proj_k[:QLEN], proj_v[:QLEN], query_length)
    out_passage = attend(proj_q[QLEN:], proj_k[QLEN:], proj_v[QLEN:], passage_length)
    mixed_heads = both_ways(jnp.concatenate([out_query, out_passage], axis=0).reshape(-1, D))
    branch = low_back(matrix_product(mixed_heads, attn_w[3].T))
    first_norm = norm_rows(tokens + branch + norm_p[0], norm_p[1], norm_p[2])
    hidden = low_back(matrix_product(low(first_norm), ffn_w[0]) + hidden_bias)
    active = low(jax.nn.gelu(hidden, approximate=False))
    branch_two = low_back(matrix_product(active, ffn_w[1].T))
    second_norm = norm_rows(first_norm + branch_two + norm_p[3], norm_p[4], norm_p[5])
    unit_q = pool_unit(second_norm[:QLEN], query_length, QLEN)
    unit_p = pool_unit(second_norm[QLEN:], passage_length, PLEN)
    return (unit_q, unit_p)

def info_nce(query_vectors, passage_vectors, positive):
    similarity_scores = matrix_product(query_vectors, passage_vectors.T) / SOFTMAX_TEMPER
    row_top = lax.optimization_barrier(jnp.max(similarity_scores, axis=1, keepdims=True))
    log_total = row_top[:, 0] + jnp.log(lax.optimization_barrier(jnp.sum(jnp.exp(similarity_scores - row_top), axis=1)))
    picked = jnp.take_along_axis(similarity_scores, positive[:, None].astype(jnp.int32), axis=1)[:, 0]
    return jnp.mean(log_total - picked)

def adam_update(master, first, second, average, grad, rate, decay_w, rates, step_count):
    first_new = rates[0] * first + (1.0 - rates[0]) * grad
    second_new = rates[1] * second + (1.0 - rates[1]) * grad * grad
    fixed_one = first_new / (1.0 - rates[0] ** step_count)
    fixed_two = second_new / (1.0 - rates[1] ** step_count)
    master_new = master - rate * (fixed_one / (jnp.sqrt(fixed_two) + ADAM_EPS) + decay_w * master)
    average_new = rates[2] * average + (1.0 - rates[2]) * master_new
    return (master_new, first_new, second_new, average_new)

def reference(query_in, passage_in, query_len, passage_len, positive, step, rates, attn_master, attn_first, attn_second, attn_average, ffn_master, ffn_first, ffn_second, ffn_average, norm_params, norm_first, norm_second, norm_average, col_bias, col_first, col_second, col_average):
    params = (low(attn_master), low(ffn_master), norm_params, col_bias)
    query_x = query_in.astype(jnp.float32)
    passage_x = passage_in.astype(jnp.float32)

    def forward_step(carry, item):
        return (carry, embed_pair(params, item[0], item[1], item[2], item[3]))
    _, (query_vectors, passage_vectors) = lax.scan(forward_step, None, (query_x, passage_x, query_len, passage_len))

    def loss_of(left, right):
        return info_nce(left, right, positive)
    loss_value, loss_pull = jax.vjp(loss_of, query_vectors, passage_vectors)
    grad_uq, grad_up = loss_pull(jnp.ones_like(loss_value))
    zero_grads = jax.tree.map(jnp.zeros_like, params)

    def backward_step(running, item):
        query_row, passage_row, query_length, passage_length, cot_q, cot_p = item

        def pair_fn(prm, left, right):
            return embed_pair(prm, left, right, query_length, passage_length)
        _, pull = jax.vjp(pair_fn, params, query_row, passage_row)
        grad_params, grad_query, grad_passage = pull((cot_q, cot_p))
        return (jax.tree.map(jnp.add, running, grad_params), (grad_query, grad_passage))
    grads, (query_grad, passage_grad) = lax.scan(backward_step, zero_grads, (query_x, passage_x, query_len, passage_len, grad_uq, grad_up))
    step_count = step[0].astype(jnp.float32)
    attn_out = adam_update(attn_master, attn_first, attn_second, attn_average, grads[0], rates[3], DECAY_WEIGHT, rates, step_count)
    ffn_out = adam_update(ffn_master, ffn_first, ffn_second, ffn_average, grads[1], rates[3], DECAY_WEIGHT, rates, step_count)
    norm_out = adam_update(norm_params, norm_first, norm_second, norm_average, grads[2], rates[4], 0.0, rates, step_count)
    col_out = adam_update(col_bias, col_first, col_second, col_average, grads[3], rates[4], 0.0, rates, step_count)
    return (loss_value.reshape(1), query_grad, passage_grad, attn_out[0], attn_out[1], attn_out[2], attn_out[3], ffn_out[0], ffn_out[1], ffn_out[2], ffn_out[3], norm_out[0], norm_out[1], norm_out[2], norm_out[3], col_out[0], col_out[1], col_out[2], col_out[3], attn_out[0].astype(jnp.bfloat16), ffn_out[0].astype(jnp.bfloat16))
```

```python
import functools

import jax
import jax.numpy as jnp
from jax import lax
from jax.experimental import pallas as pl
from jax.experimental.pallas import tpu as pltpu
from jax.sharding import PartitionSpec as P

HD = 64
LANES = 128
NEG_FILL = -1e30
SOFTMAX_TEMPER = 0.02
NORM_EPS = 1e-12
POOL_EPS = 1e-06
DECAY_WEIGHT = 0.01
ADAM_EPS = 1e-08
PRECISE = lax.Precision.HIGHEST
MESH = pl.DeviceIdType.MESH
MIB = 2**20
F32 = jnp.float32
BF16 = jnp.bfloat16

ERFC_STEP = 0.46
ERFC_HALF = (
    0.5 * 0.26113873056821263,
    0.5 * 0.23637801512084577,
    0.5 * 0.3601812301921897,
    -0.5 * 0.18740624158431016,
    0.5 * 0.6751549397754679,
    -0.5 * 0.4305350150859377,
    0.5 * 0.0850883282904581,
)
ROOT_HALF = 0.7071067811865476
DENSITY = 0.3989422804014327


def gelu_and_slope(hidden):
    bell = jnp.exp(hidden * hidden * (-0.5))
    step = 1.0 / (1.0 + (ERFC_STEP * ROOT_HALF) * jnp.abs(hidden))
    tail = ERFC_HALF[6]
    for coefficient in ERFC_HALF[5::-1]:
        tail = tail * step + coefficient
    tail = tail * step * bell
    below = jnp.where(hidden >= 0.0, 1.0 - tail, tail)
    return hidden * below, below + hidden * bell * DENSITY


def mm(left, right):
    return jnp.dot(left, right, preferred_element_type=F32)


def mm_nt(left, right):
    return lax.dot_general(left, right, (((1,), (1,)), ((), ())), preferred_element_type=F32)


def mm_tn(left, right):
    return lax.dot_general(left, right, (((0,), (0,)), ((), ())), preferred_element_type=F32)


def gather_kernel(
    attn_ref, ffn_ref, col_ref, attn_own, ffn_own, attn_oth, ffn_oth, col_oth,
    z_send, z_recv, x_send, x_recv, y_send, y_recv, d_send, d_recv, c_send, c_recv, b_send, b_recv, here_sem,
):
    me = lax.axis_index("dp")
    core = lax.axis_index("mp")
    x, y, z = lax.rem(me, 2), lax.rem(me // 2, 2), me // 4
    rows = attn_ref.shape[1]
    half = ffn_ref.shape[2] // 2

    def index_of(zz, yy, xx):
        return (zz * 2 + yy) * 2 + xx

    column = [lax.rem(z - k + 4, 4) for k in range(4)]
    z_peer = [None] + [(index_of(lax.rem(z + k, 4), y, x), core) for k in range(1, 4)]
    x_peer = (index_of(z, y, 1 - x), core)
    y_peer = (index_of(z, 1 - y, x), core)
    c_peer = (me, 1 - core)

    barrier = pltpu.get_barrier_semaphore()
    for peer in [*z_peer[1:], x_peer, y_peer, c_peer]:
        pl.semaphore_signal(barrier, inc=1, device_id=peer, device_id_type=MESH)
    pl.semaphore_wait(barrier, 6)

    def span(index, count=1):
        return pl.ds(pl.multiple_of(index * rows, rows), count * rows)

    def whole(chunk, index, count=1, other=False):
        if chunk == 0:
            return (attn_oth if other else attn_own).at[:, span(index, count), :]
        return (ffn_oth if other else ffn_own).at[chunk - 1, span(index, count), :]

    def part(chunk, index, which):
        if chunk == 0:
            return attn_own.at[pl.ds(2 * which, 2), span(index), :]
        return ffn_own.at[chunk - 1, span(index), pl.ds(which * half, half)]

    def mine(chunk):
        return attn_ref if chunk == 0 else ffn_ref.at[chunk - 1]

    sends = []

    def push(source, target, send, recv, peer):
        copy = pltpu.make_async_remote_copy(
            src_ref=source, dst_ref=target, send_sem=send, recv_sem=recv, device_id=peer, device_id_type=MESH
        )
        copy.start()
        sends.append(copy)

    def landed(target, send, recv, peer):
        pltpu.make_async_remote_copy(
            src_ref=target, dst_ref=target, send_sem=send, recv_sem=recv, device_id=peer, device_id_type=MESH
        ).wait_recv()

    local = []
    for q in range(3):
        copy = pltpu.make_async_copy(mine(q), whole(q, me), here_sem.at[q])
        copy.start()
        local.append(copy)
        for k in range(1, 4):
            push(mine(q), whole(q, me), z_send.at[q, k], z_recv.at[q, k], z_peer[k])
        push(mine(q), whole(q, me), x_send.at[q, 0], x_recv.at[q, 0], x_peer)
        push(mine(q), whole(q, me), y_send.at[q, 0], y_recv.at[q, 0], y_peer)
    push(col_ref, col_oth, b_send, b_recv, c_peer)

    def along_column(q):
        for k in range(1, 4):
            block = index_of(column[k], y, x)
            landed(whole(q, block), z_send.at[q, k], z_recv.at[q, k], z_peer[k])
            push(whole(q, block), whole(q, block), x_send.at[q, k], x_recv.at[q, k], x_peer)
            push(whole(q, block), whole(q, block), y_send.at[q, k], y_recv.at[q, k], y_peer)

    def round_corner(q):
        for k in range(4):
            beside = index_of(column[k], y, 1 - x)
            landed(whole(q, beside), x_send.at[q, k], x_recv.at[q, k], x_peer)
            push(part(q, beside, 0), part(q, beside, 0), d_send.at[q, k, 0], d_recv.at[q, k, 0], y_peer)
            beside = index_of(column[k], 1 - y, x)
            landed(whole(q, beside), y_send.at[q, k], y_recv.at[q, k], y_peer)
            push(part(q, beside, 1), part(q, beside, 1), d_send.at[q, k, 1], d_recv.at[q, k, 1], x_peer)

    def to_other_core(q):
        local[q].wait()
        for k in range(4):
            across = index_of(column[k], 1 - y, 1 - x)
            landed(part(q, across, 0), d_send.at[q, k, 0], d_recv.at[q, k, 0], y_peer)
            landed(part(q, across, 1), d_send.at[q, k, 1], d_recv.at[q, k, 1], x_peer)
            layer = index_of(column[k], 0, 0)
            push(whole(q, layer, 4), whole(q, layer, 4, True), c_send.at[q, k], c_recv.at[q, k], c_peer)

    along_column(0)
    round_corner(0)
    along_column(1)
    round_corner(1)
    to_other_core(0)
    along_column(2)
    round_corner(2)
    to_other_core(1)
    to_other_core(2)
    for q in range(3):
        for k in range(4):
            layer = index_of(column[k], 0, 0)
            landed(whole(q, layer, 4, True), c_send.at[q, k], c_recv.at[q, k], c_peer)
    landed(col_oth, b_send, b_recv, c_peer)
    for copy in sends:
        copy.wait_send()


def gather_weights(attn_low, ffn_low, col_bias):
    count, rows, width = attn_low.shape
    hidden = ffn_low.shape[2]
    full = rows * 16
    attn_shape = jax.ShapeDtypeStruct((count, full, width), BF16)
    ffn_shape = jax.ShapeDtypeStruct((2, full, hidden), BF16)
    dma = pltpu.SemaphoreType.DMA
    col = col_bias.reshape(-1, LANES)
    anywhere = pl.BlockSpec(memory_space=pltpu.HBM)
    outs = pl.pallas_call(
        gather_kernel,
        out_shape=(attn_shape, ffn_shape, attn_shape, ffn_shape, jax.ShapeDtypeStruct(col.shape, F32)),
        in_specs=[anywhere] * 3,
        out_specs=(anywhere,) * 5,
        scratch_shapes=[
            dma((3, 4)), dma((3, 4)), dma((3, 4)), dma((3, 4)), dma((3, 4)), dma((3, 4)),
            dma((3, 4, 2)), dma((3, 4, 2)), dma((3, 4)), dma((3, 4)), dma(()), dma(()), dma((3,)),
        ],
        compiler_params=pltpu.CompilerParams(collective_id=0, has_side_effects=True),
        name="gather_weights",
    )(attn_low, ffn_low, col)
    attn_own, ffn_own, attn_oth, ffn_oth, col_oth = outs
    return (attn_own, attn_oth), (ffn_own, ffn_oth), (col_bias, col_oth.reshape(-1))


def exchange_kernel(total, mine_ref, all_ref, here_sem, send_sem, recv_sem):
    me = lax.axis_index("dp") * 2 + lax.axis_index("mp")

    def device(step):
        rank = lax.rem(me + step, total)
        return (rank // 2, lax.rem(rank, 2))

    barrier = pltpu.get_barrier_semaphore()
    for step in range(1, total):
        pl.semaphore_signal(barrier, inc=1, device_id=device(step), device_id_type=MESH)
    pl.semaphore_wait(barrier, total - 1)
    local = pltpu.make_async_copy(mine_ref, all_ref.at[me], here_sem)
    local.start()
    copies = []
    for step in range(1, total):
        copy = pltpu.make_async_remote_copy(
            src_ref=mine_ref,
            dst_ref=all_ref.at[me],
            send_sem=send_sem.at[step],
            recv_sem=recv_sem.at[step],
            device_id=device(step),
            device_id_type=MESH,
        )
        copy.start()
        copies.append(copy)
    local.wait()
    for copy in copies:
        copy.wait()


def gather_rows(mine, total):
    slabs = mine.reshape(-1, LANES)
    every = pl.pallas_call(
        functools.partial(exchange_kernel, total),
        out_shape=jax.ShapeDtypeStruct((total,) + slabs.shape, F32),
        in_specs=[pl.BlockSpec(memory_space=pltpu.VMEM)],
        out_specs=pl.BlockSpec(memory_space=pltpu.VMEM),
        scratch_shapes=[
            pltpu.SemaphoreType.DMA(()),
            pltpu.SemaphoreType.DMA((total,)),
            pltpu.SemaphoreType.DMA((total,)),
        ],
        compiler_params=pltpu.CompilerParams(collective_id=1, has_side_effects=True),
        name="gather_rows",
    )(slabs)
    return every.reshape(total, -1)


def first_head(shape):
    return lax.broadcasted_iota(jnp.int32, shape, 1) < HD


def attend_kernel(spans, lens_ref, q_ref, k_ref, v_ref, o_ref):
    for index, (start, slots) in enumerate(spans):
        length = lens_ref[index]
        keys = k_ref[0, pl.ds(start, slots), :]
        values = v_ref[0, pl.ds(start, slots), :]
        lane = first_head(keys.shape)
        scaled = keys * jnp.asarray(HD**-0.5, BF16)
        zero = jnp.zeros_like(scaled)
        head_keys = (jnp.where(lane, scaled, zero), jnp.where(lane, zero, scaled))
        block = min(slots, 256)
        for at in range(0, slots, block):
            queries = q_ref[0, pl.ds(start + at, block), :]
            outs = []
            for head in range(2):
                scores = mm_nt(queries, head_keys[head])
                valid = lax.broadcasted_iota(jnp.int32, scores.shape, 1) < length
                scores = jnp.where(valid, scores, NEG_FILL)
                top = jnp.max(scores, axis=1, keepdims=True)
                weight = jnp.exp(scores - top)
                total = jnp.sum(weight, axis=1, keepdims=True)
                probs = (weight * (1.0 / total)).astype(BF16)
                outs.append(mm(probs, values))
            o_ref[pl.ds(start + at, block), :] = jnp.where(
                first_head(outs[0].shape), outs[0], outs[1]
            ).astype(BF16)


def attend_back_kernel(spans, lens_ref, q_ref, k_ref, v_ref, g_ref, d_ref):
    scale = HD**-0.5
    for index, (start, slots) in enumerate(spans):
        length = lens_ref[index]
        keys = k_ref[0, pl.ds(start, slots), :]
        values = v_ref[0, pl.ds(start, slots), :]
        lane = first_head(keys.shape)
        scaled = keys * jnp.asarray(scale, BF16)
        zero = jnp.zeros_like(scaled)
        head_keys = (jnp.where(lane, scaled, zero), jnp.where(lane, zero, scaled))
        head_values = (jnp.where(lane, values, zero), jnp.where(lane, zero, values))
        block = min(slots, 256)
        grad_k = [None, None]
        grad_v = [None, None]
        for at in range(0, slots, block):
            queries = q_ref[0, pl.ds(start + at, block), :]
            grads = g_ref[pl.ds(start + at, block), :]
            grad_q = []
            for head in range(2):
                scores = mm_nt(head_keys[head], queries)
                valid = lax.broadcasted_iota(jnp.int32, scores.shape, 0) < length
                scores = jnp.where(valid, scores, NEG_FILL)
                top = jnp.max(scores, axis=0, keepdims=True)
                weight = jnp.exp(scores - top)
                total = jnp.sum(weight, axis=0, keepdims=True)
                probs = weight * (1.0 / total)
                grad_probs = mm_nt(head_values[head], grads)
                inner = jnp.sum(probs * grad_probs, axis=0, keepdims=True)
                grad_scores = (probs * (grad_probs - inner)).astype(BF16)
                part_v = mm(probs.astype(BF16), grads)
                part_k = mm(grad_scores, queries)
                grad_v[head] = part_v if at == 0 else grad_v[head] + part_v
                grad_k[head] = part_k if at == 0 else grad_k[head] + part_k
                grad_q.append(mm_tn(grad_scores, keys))
            d_ref[0, pl.ds(start + at, block), :] = (
                jnp.where(first_head(grad_q[0].shape), grad_q[0], grad_q[1]) * scale
            ).astype(BF16)
        d_ref[1, pl.ds(start, slots), :] = (jnp.where(lane, grad_k[0], grad_k[1]) * scale).astype(BF16)
        d_ref[2, pl.ds(start, slots), :] = jnp.where(lane, grad_v[0], grad_v[1]).astype(BF16)


def head_specs(tokens):
    return [pl.BlockSpec((1, tokens, LANES), functools.partial(lambda s, i, lens: (s, 0, i), s)) for s in range(3)]


def attend(proj, lens, spans):
    _, tokens, width = proj.shape
    flops = sum(4 * slots * slots * width for _, slots in spans)
    return pl.pallas_call(
        functools.partial(attend_kernel, spans),
        out_shape=jax.ShapeDtypeStruct((tokens, width), BF16),
        grid_spec=pltpu.PrefetchScalarGridSpec(
            num_scalar_prefetch=1,
            grid=(width // LANES,),
            in_specs=head_specs(tokens),
            out_specs=pl.BlockSpec((tokens, LANES), lambda i, lens: (0, i)),
        ),
        compiler_params=pltpu.CompilerParams(vmem_limit_bytes=40 * MIB),
        cost_estimate=pl.CostEstimate(flops=8 * flops, bytes_accessed=8 * tokens * width, transcendentals=0),
        name="attend",
    )(lens, proj, proj, proj)


def attend_back(proj, grad_out, lens, spans):
    _, tokens, width = proj.shape
    flops = sum(10 * slots * slots * width for _, slots in spans)
    return pl.pallas_call(
        functools.partial(attend_back_kernel, spans),
        out_shape=jax.ShapeDtypeStruct((3, tokens, width), BF16),
        grid_spec=pltpu.PrefetchScalarGridSpec(
            num_scalar_prefetch=1,
            grid=(width // LANES,),
            in_specs=head_specs(tokens) + [pl.BlockSpec((tokens, LANES), lambda i, lens: (0, i))],
            out_specs=pl.BlockSpec((3, tokens, LANES), lambda i, lens: (0, 0, i)),
        ),
        compiler_params=pltpu.CompilerParams(vmem_limit_bytes=40 * MIB),
        cost_estimate=pl.CostEstimate(flops=8 * flops, bytes_accessed=14 * tokens * width, transcendentals=0),
        name="attend_back",
    )(lens, proj, proj, proj, grad_out)


def up_kernel(x_ref, w_ref, b_ref, g_ref, s_ref):
    hidden = mm(x_ref[...], w_ref[0]) + b_ref[...]
    active, slope = gelu_and_slope(hidden)
    g_ref[...] = active.astype(BF16)
    s_ref[...] = slope


def feed_up(low, ffn_half, bias):
    tokens, width = low.shape
    units = ffn_half.shape[2]
    tile = 256
    return pl.pallas_call(
        up_kernel,
        out_shape=(jax.ShapeDtypeStruct((tokens, units), BF16), jax.ShapeDtypeStruct((tokens, units), F32)),
        grid=(units // tile,),
        in_specs=[
            pl.BlockSpec((tokens, width), lambda i: (0, 0)),
            pl.BlockSpec((1, width, tile), lambda i: (0, 0, i)),
            pl.BlockSpec((1, tile), lambda i: (0, i)),
        ],
        out_specs=(pl.BlockSpec((tokens, tile), lambda i: (0, i)), pl.BlockSpec((tokens, tile), lambda i: (0, i))),
        compiler_params=pltpu.CompilerParams(vmem_limit_bytes=40 * MIB),
        cost_estimate=pl.CostEstimate(
            flops=2 * tokens * width * units, bytes_accessed=8 * tokens * units, transcendentals=tokens * units
        ),
        name="feed_up",
    )(low, ffn_half, bias.reshape(1, -1))


def swap_cores(values):
    return lax.ppermute(values, "mp", [(0, 1), (1, 0)])


def scatter_sum(own_parts, other_parts):
    me = lax.axis_index("dp")
    size = lax.axis_size("dp")
    summed = [own + swap_cores(other).astype(F32) for own, other in zip(own_parts, other_parts)]
    if size != 16:
        return [lax.psum_scatter(value, "dp", scatter_dimension=1, tiled=True) for value in summed]
    bits = (lax.rem(me, 2), lax.rem(me // 2, 2))
    level = me // 4
    neighbour = ([(i, i ^ 1) for i in range(16)], [(i, i ^ 2) for i in range(16)])
    columns = []
    for part, value in enumerate(summed):
        count, full, width = value.shape
        value = value.reshape(count, 4, 2, 2, full // 16, width)
        for axis in (0, 1) if part == 0 else (1, 0):
            at = value.ndim - 3 if axis == 0 else 2
            keep = lax.dynamic_index_in_dim(value, bits[axis], at, keepdims=False)
            send = lax.dynamic_index_in_dim(value, 1 - bits[axis], at, keepdims=False).astype(BF16)
            value = keep + lax.ppermute(send, "dp", neighbour[axis]).astype(F32)
        columns.append(value)
    results = []
    for value in columns:
        total = lax.dynamic_index_in_dim(value, level, 1, keepdims=False)
        for step in range(1, 4):
            send = lax.dynamic_index_in_dim(value, lax.rem(level + step, 4), 1, keepdims=False).astype(BF16)
            got = lax.ppermute(send, "dp", [(i, (i + 4 * step) % 16) for i in range(16)])
            total = total + got.astype(F32)
        results.append(total)
    return results


def sum_all(values):
    size = lax.axis_size("dp")
    if size != 16:
        return lax.psum(values, "dp")
    for bit in (1, 2, 4, 8):
        values = values + lax.ppermute(values, "dp", [(i, i ^ bit) for i in range(16)])
    return values


def adam_update(master, first, second, average, grad, rate, decay_w, rates, step_count):
    first_new = rates[0] * first + (1.0 - rates[0]) * grad
    second_new = rates[1] * second + (1.0 - rates[1]) * grad * grad
    fixed_one = first_new / (1.0 - rates[0] ** step_count)
    fixed_two = second_new / (1.0 - rates[1] ** step_count)
    master_new = master - rate * (fixed_one / (jnp.sqrt(fixed_two) + ADAM_EPS) + decay_w * master)
    average_new = rates[2] * average + (1.0 - rates[2]) * master_new
    return (master_new, first_new, second_new, average_new)


def normalize(values):
    center = values - jnp.mean(values, axis=-1, keepdims=True)
    spread = jnp.mean(center * center, axis=-1, keepdims=True)
    inverse = lax.rsqrt(spread + NORM_EPS)
    return center * inverse, inverse


def normalize_back(unit, inverse, grad_unit):
    return inverse * (
        grad_unit
        - jnp.mean(grad_unit, axis=-1, keepdims=True)
        - unit * jnp.mean(grad_unit * unit, axis=-1, keepdims=True)
    )


def per_device(
    query_in,
    passage_in,
    query_len,
    passage_len,
    positive,
    step,
    rates,
    attn_master,
    attn_first,
    attn_second,
    attn_average,
    ffn_master,
    ffn_first,
    ffn_second,
    ffn_average,
    norm_params,
    norm_first,
    norm_second,
    norm_average,
    col_bias,
    col_first,
    col_second,
    col_average,
):
    core = lax.axis_index("mp")
    size = lax.axis_size("dp")
    query_slots, model_width = query_in.shape[1:]
    passage_slots = passage_in.shape[1]
    pairs = query_in.shape[0] * size
    spans = ((0, query_slots), (query_slots, passage_slots))

    def pick(values, index):
        return lax.dynamic_index_in_dim(values, index, 0, keepdims=False)

    tokens = jnp.concatenate([pick(query_in, core), pick(passage_in, core)], axis=0)
    lens = jnp.stack([pick(query_len, core), pick(passage_len, core)])

    attn_low, ffn_low = attn_master.astype(BF16), ffn_master.astype(BF16)
    if size == 16:
        attn_w, ffn_w, col = gather_weights(attn_low, ffn_low, col_bias)
    else:
        attn_full = lax.all_gather(attn_low, "dp", axis=1, tiled=True)
        ffn_full = lax.all_gather(ffn_low, "dp", axis=1, tiled=True)
        attn_w = (attn_full, swap_cores(attn_full))
        ffn_w = (ffn_full, swap_cores(ffn_full))
        col = (col_bias, swap_cores(col_bias))
    width = attn_w[0].shape[2]

    projected, mixed = [], []
    branch = None
    for half in range(2):
        bias = jnp.stack([col[half][:width], jnp.zeros((width,), F32), col[half][width : 2 * width]])
        proj = (
            jnp.einsum("td,sde->ste", tokens, attn_w[half][:3], preferred_element_type=F32) + bias[:, None, :]
        ).astype(BF16)
        out = attend(proj, lens, spans)
        part = mm_nt(out, attn_w[half][3])
        branch = part if branch is None else branch + part
        projected.append(proj)
        mixed.append(out)
    z_one = tokens.astype(F32) + branch + norm_params[0]
    unit_one, inverse_one = normalize(z_one)
    first_norm = unit_one * norm_params[1] + norm_params[2]
    first_low = first_norm.astype(BF16)
    active, slope = [], []
    branch_two = None
    for half in range(2):
        act, slo = feed_up(first_low, ffn_w[half], col[half][2 * width :])
        part = mm_nt(act, ffn_w[half][1])
        branch_two = part if branch_two is None else branch_two + part
        active.append(act)
        slope.append(slo)
    z_two = first_norm + branch_two + norm_params[3]
    unit_two, inverse_two = normalize(z_two)
    places = jnp.arange(query_slots + passage_slots)
    in_query = (places < query_slots) & (places < lens[0])
    in_passage = (places >= query_slots) & (places - query_slots < lens[1])
    share = (
        jnp.stack([in_query, in_passage]).astype(F32) / lens.astype(F32)[:, None]
    )
    mean_unit = jnp.dot(share, unit_two, precision=PRECISE, preferred_element_type=F32)
    pooled = mean_unit * norm_params[4] + norm_params[5]
    shrink = lax.rsqrt(jnp.sum(pooled * pooled, axis=1, keepdims=True) + POOL_EPS)
    embed = pooled * shrink

    target_mine = jnp.broadcast_to(pick(positive, core).astype(F32), (LANES,))
    payload = jnp.concatenate([embed.reshape(-1), target_mine])
    if size == 16:
        every = gather_rows(payload, pairs)
    else:
        every = lax.all_gather(payload, ("dp", "mp"), axis=0)
    every_q = every[:, :model_width]
    every_p = every[:, model_width : 2 * model_width]
    target = (jnp.arange(pairs)[None, :].astype(F32) == every[:, 2 * model_width :][:, :1]).astype(F32)
    logits = lax.dot_general(every_q, every_p, (((1,), (1,)), ((), ())), precision=PRECISE) / SOFTMAX_TEMPER
    row_top = jnp.max(logits, axis=1, keepdims=True)
    exp_logits = jnp.exp(logits - row_top)
    row_total = jnp.sum(exp_logits, axis=1, keepdims=True)
    log_total = row_top[:, 0] + jnp.log(row_total[:, 0])
    loss_value = (jnp.sum(log_total - jnp.sum(logits * target, axis=1)) / pairs).reshape(1)
    grad_logits = (exp_logits / row_total - target) / (pairs * SOFTMAX_TEMPER)
    rank = lax.axis_index("dp") * lax.axis_size("mp") + core
    grad_uq = jnp.dot(pick(grad_logits, rank)[None], every_p, precision=PRECISE)
    grad_up = jnp.dot(
        lax.dynamic_index_in_dim(grad_logits, rank, 1, keepdims=False)[None], every_q, precision=PRECISE
    )
    grad_embed = jnp.concatenate([grad_uq, grad_up], axis=0)

    grad_pooled = shrink * (grad_embed - embed * jnp.sum(grad_embed * embed, axis=1, keepdims=True))
    grad_gain_two = jnp.sum(grad_pooled * mean_unit, axis=0)
    grad_shift_two = jnp.sum(grad_pooled, axis=0)
    grad_unit_two = lax.dot_general(
        share, grad_pooled * norm_params[4], (((0,), (0,)), ((), ())), precision=PRECISE
    )
    grad_ztwo = normalize_back(unit_two, inverse_two, grad_unit_two)
    grad_bias_two = jnp.sum(grad_ztwo, axis=0)
    grad_two_low = grad_ztwo.astype(BF16)

    hidden = ffn_w[0].shape[2]
    cut = hidden // 2

    def two_parts(values):
        return values[:, :cut], values[:, cut:]

    def parted_product(left, halves):
        own = [mm_tn(left, part)[None] for part in two_parts(halves[0])]
        other = [mm_tn(left, part).astype(BF16)[None] for part in two_parts(halves[1])]
        return own, other

    down_grad = scatter_sum(*parted_product(grad_two_low, active))
    grad_hidden, grad_first = [], grad_ztwo
    for half in (1, 0):
        grad_hid = (mm(grad_two_low, ffn_w[half][1]) * slope[half]).astype(BF16)
        grad_hidden.insert(0, grad_hid)
        grad_first = grad_first + mm_nt(grad_hid, ffn_w[half][0])
    grad_hidden_bias = [jnp.sum(value.astype(F32), axis=0) for value in grad_hidden]
    up_grad = scatter_sum(*parted_product(first_low, grad_hidden))

    grad_gain_one = jnp.sum(grad_first * unit_one, axis=0)
    grad_shift_one = jnp.sum(grad_first, axis=0)
    grad_zone = normalize_back(unit_one, inverse_one, grad_first * norm_params[1])
    grad_bias_out = jnp.sum(grad_zone, axis=0)
    grad_one_low = grad_zone.astype(BF16)
    grad_tokens = grad_zone
    grad_query_bias, grad_value_bias, attn_parts = [None, None], [None, None], [None, None]
    for half in (1, 0):
        grad_out = mm(grad_one_low, attn_w[half][3]).astype(BF16)
        grad_proj = attend_back(projected[half], grad_out, lens, spans)
        grad_query_bias[half] = jnp.sum(grad_proj[0].astype(F32), axis=0)
        grad_value_bias[half] = jnp.sum(grad_proj[2].astype(F32), axis=0)
        in_grads = jnp.einsum("td,ste->sde", tokens, grad_proj, preferred_element_type=F32)
        out_grad = mm_tn(grad_one_low, mixed[half])
        parts = [in_grads[:2], jnp.stack([in_grads[2], out_grad])]
        attn_parts[half] = parts if half == 0 else [part.astype(BF16) for part in parts]
        for index in range(3):
            grad_tokens = grad_tokens + mm_nt(grad_proj[index], attn_w[half][index])
    attn_grads = scatter_sum(*attn_parts)

    col_parts = [
        jnp.concatenate([grad_query_bias[half], grad_value_bias[half], grad_hidden_bias[half]]) for half in range(2)
    ]
    norm_part = jnp.stack(
        [grad_bias_out, grad_gain_one, grad_shift_one, grad_bias_two, grad_gain_two, grad_shift_two]
    )
    norm_part = norm_part + swap_cores(norm_part)
    col_part = col_parts[0] + swap_cores(col_parts[1])
    small = sum_all(jnp.concatenate([norm_part.reshape(-1), col_part]))
    norm_grad = small[: norm_part.size].reshape(norm_part.shape)
    col_grad = small[norm_part.size :]

    step_count = step[0].astype(F32)
    attn_grad = jnp.concatenate(attn_grads, axis=0)
    ffn_grad = jnp.stack([jnp.concatenate(parts, axis=-1)[0] for parts in (up_grad, down_grad)])
    attn_out = adam_update(
        attn_master, attn_first, attn_second, attn_average, attn_grad, rates[3], DECAY_WEIGHT, rates, step_count
    )
    ffn_out = adam_update(
        ffn_master, ffn_first, ffn_second, ffn_average, ffn_grad, rates[3], DECAY_WEIGHT, rates, step_count
    )
    norm_out = adam_update(
        norm_params, norm_first, norm_second, norm_average, norm_grad, rates[4], 0.0, rates, step_count
    )
    col_out = adam_update(col_bias, col_first, col_second, col_average, col_grad, rates[4], 0.0, rates, step_count)

    grad_twin = swap_cores(grad_tokens)
    first_pair = jnp.where(core == 0, grad_tokens, grad_twin)
    second_pair = jnp.where(core == 0, grad_twin, grad_tokens)
    query_grad = jnp.stack([first_pair[:query_slots], second_pair[:query_slots]])
    passage_grad = jnp.stack([first_pair[query_slots:], second_pair[query_slots:]])
    return (
        loss_value,
        query_grad,
        passage_grad,
        *attn_out,
        *ffn_out,
        *norm_out,
        *col_out,
        attn_out[0].astype(BF16),
        ffn_out[0].astype(BF16),
    )


def solution(mesh):
    matrix = P(None, "dp", "mp")
    rows = P("dp", None, None)
    placed = (rows, rows, P("dp"), P("dp"), P("dp"), P(), P(), *[matrix] * 8, *[P()] * 4, *[P("mp")] * 4)
    return jax.shard_map(
        per_device,
        mesh=mesh,
        in_specs=placed,
        out_specs=(P(), rows, rows, *[matrix] * 8, *[P()] * 4, *[P("mp")] * 4, matrix, matrix),
        check_vma=False,
    )
```

```python
import functools

import jax
import jax.numpy as jnp
from jax import lax
from jax.experimental import pallas as pl
from jax.experimental.pallas import tpu as pltpu
from jax.sharding import PartitionSpec as P

HD = 64
LANES = 128
NEG_FILL = -1e30
SOFTMAX_TEMPER = 0.02
NORM_EPS = 1e-12
POOL_EPS = 1e-06
DECAY_WEIGHT = 0.01
ADAM_EPS = 1e-08
PRECISE = lax.Precision.HIGHEST
MESH = pl.DeviceIdType.MESH
MIB = 2**20
F32 = jnp.float32
BF16 = jnp.bfloat16

ERFC_STEP = 0.46
ERFC_HALF = (
    0.5 * 0.26113873056821263,
    0.5 * 0.23637801512084577,
    0.5 * 0.3601812301921897,
    -0.5 * 0.18740624158431016,
    0.5 * 0.6751549397754679,
    -0.5 * 0.4305350150859377,
    0.5 * 0.0850883282904581,
)
ROOT_HALF = 0.7071067811865476
DENSITY = 0.3989422804014327


def gelu_and_slope(hidden):
    bell = jnp.exp(hidden * hidden * (-0.5))
    step = 1.0 / (1.0 + (ERFC_STEP * ROOT_HALF) * jnp.abs(hidden))
    tail = ERFC_HALF[6]
    for coefficient in ERFC_HALF[5::-1]:
        tail = tail * step + coefficient
    tail = tail * step * bell
    below = jnp.where(hidden >= 0.0, 1.0 - tail, tail)
    return hidden * below, below + hidden * bell * DENSITY


def mm(left, right):
    return jnp.dot(left, right, preferred_element_type=F32)


def mm_nt(left, right):
    return lax.dot_general(left, right, (((1,), (1,)), ((), ())), preferred_element_type=F32)


def mm_tn(left, right):
    return lax.dot_general(left, right, (((0,), (0,)), ((), ())), preferred_element_type=F32)


def normalize(values):
    center = values - jnp.mean(values, axis=-1, keepdims=True)
    spread = jnp.mean(center * center, axis=-1, keepdims=True)
    inverse = lax.rsqrt(spread + NORM_EPS)
    return center * inverse, inverse


def first_head(shape):
    return lax.broadcasted_iota(jnp.int32, shape, 1) < HD


ROW_BLOCK = 144


def forward_kernel(
    spans,
    lens_ref, x_ref, attn_ref, ffn_ref, col_ref, norm_ref,
    attn_out, ffn_out, proj_out, mixed_out, unit_out, inverse_out, low_out, active_out, slope_out, z_out,
    attn_w, ffn_w, col_far, proj, mixed, unit, inverse, low, active, slope, z_two,
    z_send, z_recv, x_send, x_recv, y_send, y_recv, d_send, d_recv, c_send, c_recv, b_send, b_recv, here_sem, out_sem,
):
    me = lax.axis_index("dp")
    core = lax.axis_index("mp")
    x, y, z = lax.rem(me, 2), lax.rem(me // 2, 2), me // 4
    rows = attn_ref.shape[1]
    half_units = ffn_ref.shape[2] // 2
    width = attn_ref.shape[2]
    units = ffn_ref.shape[2]
    tokens = x_ref.shape[0]

    def index_of(zz, yy, xx):
        return (zz * 2 + yy) * 2 + xx

    column = [lax.rem(z - k + 4, 4) for k in range(4)]
    z_peer = [None] + [(index_of(lax.rem(z + k, 4), y, x), core) for k in range(1, 4)]
    x_peer = (index_of(z, y, 1 - x), core)
    y_peer = (index_of(z, 1 - y, x), core)
    c_peer = (me, 1 - core)

    barrier = pltpu.get_barrier_semaphore()
    for peer in [*z_peer[1:], x_peer, y_peer, c_peer]:
        pl.semaphore_signal(barrier, inc=1, device_id=peer, device_id_type=MESH)
    pl.semaphore_wait(barrier, 6)

    def span(index, count=1):
        return pl.ds(pl.multiple_of(index * rows, rows), count * rows)

    def whole(chunk, index, count=1, far=0):
        if chunk == 0:
            return attn_w.at[far, :, span(index, count), :]
        return ffn_w.at[far, chunk - 1, span(index, count), :]

    def part(chunk, index, which):
        if chunk == 0:
            return attn_w.at[0, pl.ds(2 * which, 2), span(index), :]
        return ffn_w.at[0, chunk - 1, span(index), pl.ds(which * half_units, half_units)]

    def mine(chunk):
        return attn_ref if chunk == 0 else ffn_ref.at[chunk - 1]

    sends = []
    stores = []

    def push(source, target, send, recv, peer):
        copy = pltpu.make_async_remote_copy(
            src_ref=source, dst_ref=target, send_sem=send, recv_sem=recv, device_id=peer, device_id_type=MESH
        )
        copy.start()
        sends.append(copy)

    def landed(target, send, recv, peer):
        pltpu.make_async_remote_copy(
            src_ref=target, dst_ref=target, send_sem=send, recv_sem=recv, device_id=peer, device_id_type=MESH
        ).wait_recv()

    def store(source, target):
        copy = pltpu.make_async_copy(source, target, out_sem.at[len(stores)])
        copy.start()
        stores.append(copy)

    local = []
    for q in range(3):
        copy = pltpu.make_async_copy(mine(q), whole(q, me), here_sem.at[q])
        copy.start()
        local.append(copy)
        for k in range(1, 4):
            push(mine(q), whole(q, me), z_send.at[q, k], z_recv.at[q, k], z_peer[k])
        push(mine(q), whole(q, me), x_send.at[q, 0], x_recv.at[q, 0], x_peer)
        push(mine(q), whole(q, me), y_send.at[q, 0], y_recv.at[q, 0], y_peer)
    push(col_ref, col_far, b_send, b_recv, c_peer)

    def along_column(q):
        for k in range(1, 4):
            block = index_of(column[k], y, x)
            landed(whole(q, block), z_send.at[q, k], z_recv.at[q, k], z_peer[k])
            push(whole(q, block), whole(q, block), x_send.at[q, k], x_recv.at[q, k], x_peer)
            push(whole(q, block), whole(q, block), y_send.at[q, k], y_recv.at[q, k], y_peer)

    def round_corner(q, ks=range(4)):
        for k in ks:
            beside = index_of(column[k], y, 1 - x)
            landed(whole(q, beside), x_send.at[q, k], x_recv.at[q, k], x_peer)
            push(part(q, beside, 0), part(q, beside, 0), d_send.at[q, k, 0], d_recv.at[q, k, 0], y_peer)
            beside = index_of(column[k], 1 - y, x)
            landed(whole(q, beside), y_send.at[q, k], y_recv.at[q, k], y_peer)
            push(part(q, beside, 1), part(q, beside, 1), d_send.at[q, k, 1], d_recv.at[q, k, 1], x_peer)

    def to_other_core(q, ks=range(4)):
        for k in ks:
            if k == 0:
                local[q].wait()
            across = index_of(column[k], 1 - y, 1 - x)
            landed(part(q, across, 0), d_send.at[q, k, 0], d_recv.at[q, k, 0], y_peer)
            landed(part(q, across, 1), d_send.at[q, k, 1], d_recv.at[q, k, 1], x_peer)
            layer = index_of(column[k], 0, 0)
            push(whole(q, layer, 4), whole(q, layer, 4, 1), c_send.at[q, k], c_recv.at[q, k], c_peer)

    def from_other_core(q):
        for k in range(4):
            layer = index_of(column[k], 0, 0)
            landed(whole(q, layer, 4, 1), c_send.at[q, k], c_recv.at[q, k], c_peer)

    def bias(half, start, count):
        source = col_ref if half == 0 else col_far
        return source[pl.ds(0, 1), pl.ds(start, count)]

    def project(half):
        for index in range(3):
            value = mm(x_ref[...], attn_w[half, index])
            if index != 1:
                value = value + bias(half, (index // 2) * width, width)
            proj[half, index] = value.astype(BF16)

    def heads(half, pair):
        lanes = pl.ds(pair * LANES, LANES)
        for index, (start, slots) in enumerate(spans):
            length = lens_ref[index]
            keys = proj[half, 1, pl.ds(start, slots), lanes]
            values = proj[half, 2, pl.ds(start, slots), lanes]
            lane = first_head(keys.shape)
            scaled = keys * jnp.asarray(HD**-0.5, BF16)
            zero = jnp.zeros_like(scaled)
            head_keys = (jnp.where(lane, scaled, zero), jnp.where(lane, zero, scaled))
            block = min(slots, 256)
            for at in range(0, slots, block):
                queries = proj[half, 0, pl.ds(start + at, block), lanes]
                outs = []
                for head in range(2):
                    scores = mm_nt(queries, head_keys[head])
                    valid = lax.broadcasted_iota(jnp.int32, scores.shape, 1) < length
                    scores = jnp.where(valid, scores, NEG_FILL)
                    top = jnp.max(scores, axis=1, keepdims=True)
                    weight = jnp.exp(scores - top)
                    total = jnp.sum(weight, axis=1, keepdims=True)
                    probs = (weight * (1.0 / total)).astype(BF16)
                    outs.append(mm(probs, values))
                mixed[half, pl.ds(start + at, block), lanes] = jnp.where(
                    first_head(outs[0].shape), outs[0], outs[1]
                ).astype(BF16)

    def first_norm():
        for at in range(0, tokens, ROW_BLOCK):
            block = pl.ds(at, ROW_BLOCK)
            value = mm_nt(mixed[0, block, :], attn_w[0, 3]) + mm_nt(mixed[1, block, :], attn_w[1, 3])
            value = x_ref[block, :].astype(F32) + value + norm_ref[pl.ds(0, 1), :]
            normed, scale = normalize(value)
            unit[block, :] = normed
            inverse[block, :] = jnp.broadcast_to(scale, (ROW_BLOCK, LANES))
            value = normed * norm_ref[pl.ds(1, 1), :] + norm_ref[pl.ds(2, 1), :]
            z_two[block, :] = value
            low[block, :] = value.astype(BF16)

    tile = 256

    def up(half):
        @pl.loop(0, units // tile)
        def _(index):
            lanes = pl.ds(pl.multiple_of(index * tile, tile), tile)
            source = col_ref if half == 0 else col_far
            shift = source[pl.ds(0, 1), pl.ds(pl.multiple_of(2 * width + index * tile, tile), tile)]
            hidden = mm(low[...], ffn_w[half, 0, :, lanes]) + shift
            value, grad = gelu_and_slope(hidden)
            active[half, :, lanes] = value.astype(BF16)
            slope[half, :, lanes] = grad

    def down(half):
        @pl.loop(0, tokens // ROW_BLOCK)
        def _(index):
            block = pl.ds(pl.multiple_of(index * ROW_BLOCK, ROW_BLOCK), ROW_BLOCK)
            value = z_two[block, :] + mm_nt(active[half, block, :], ffn_w[half, 1])
            if half == 1:
                value = value + norm_ref[pl.ds(3, 1), :]
            z_two[block, :] = value

    along_column(0)
    round_corner(0)
    along_column(1)
    to_other_core(0)
    landed(col_far, b_send, b_recv, c_peer)
    store(attn_w.at[0], attn_out.at[0])
    project(0)
    heads(0, 0)
    heads(0, 1)
    round_corner(1, (0, 1))
    heads(0, 2)
    from_other_core(0)
    store(attn_w.at[1], attn_out.at[1])
    project(1)
    round_corner(1, (2, 3))
    store(proj, proj_out)
    heads(1, 0)
    along_column(2)
    heads(1, 1)
    round_corner(2, (0,))
    heads(1, 2)
    to_other_core(1)
    store(mixed, mixed_out)
    first_norm()
    store(unit, unit_out)
    store(inverse, inverse_out)
    store(low, low_out)
    round_corner(2, (1, 2))
    store(ffn_w.at[0, 0], ffn_out.at[0, 0])
    up(0)
    store(slope.at[0], slope_out.at[0])
    from_other_core(1)
    store(ffn_w.at[1, 0], ffn_out.at[1, 0])
    round_corner(2, (3,))
    to_other_core(2, (0, 1))
    up(1)
    store(active, active_out)
    store(slope.at[1], slope_out.at[1])
    to_other_core(2, (2, 3))
    store(ffn_w.at[0, 1], ffn_out.at[0, 1])
    down(0)
    from_other_core(2)
    store(ffn_w.at[1, 1], ffn_out.at[1, 1])
    down(1)
    store(z_two, z_out)
    for copy in stores:
        copy.wait()
    for copy in sends:
        copy.wait_send()


def forward(tokens, lens, attn_low, ffn_low, col_bias, norm_params, spans):
    count, rows, width = attn_low.shape
    units = ffn_low.shape[2]
    full = rows * 16
    slots, model = tokens.shape
    dma = pltpu.SemaphoreType.DMA
    col = jnp.broadcast_to(col_bias[None], (8, col_bias.shape[0]))
    norms = jnp.concatenate([norm_params, jnp.zeros((2, model), F32)], axis=0)
    anywhere = pl.BlockSpec(memory_space=pltpu.HBM)
    vmem = pl.BlockSpec(memory_space=pltpu.VMEM)
    results = (
        ((2, count, full, width), BF16),
        ((2, 2, full, units), BF16),
        ((2, 3, slots, width), BF16),
        ((2, slots, width), BF16),
        ((slots, model), F32),
        ((slots, LANES), F32),
        ((slots, model), BF16),
        ((2, slots, units), BF16),
        ((2, slots, units), F32),
        ((slots, model), F32),
    )
    held = [pltpu.VMEM(*results[0]), pltpu.VMEM(*results[1]), pltpu.VMEM(col.shape, F32)]
    held += [pltpu.VMEM(*result) for result in results[2:]]
    return pl.pallas_call(
        functools.partial(forward_kernel, spans),
        out_shape=tuple(jax.ShapeDtypeStruct(*result) for result in results),
        in_specs=[pl.BlockSpec(memory_space=pltpu.SMEM), vmem, anywhere, anywhere, vmem, vmem],
        out_specs=(anywhere,) * len(results),
        scratch_shapes=held
        + [dma((3, 4))] * 6
        + [dma((3, 4, 2))] * 2
        + [dma((3, 4))] * 2
        + [dma(()), dma(()), dma((3,)), dma((16,))],
        compiler_params=pltpu.CompilerParams(collective_id=0, has_side_effects=True, vmem_limit_bytes=56 * MIB),
        name="forward",
    )(lens, tokens, attn_low, ffn_low, col, norms)


SLAB = 16


def loss_kernel(
    spans, total,
    lens_ref, z_ref, norm_ref, target_ref,
    grad_ref, low_ref, small_ref,
    unit, slab, every, here_sem, send_sem, recv_sem,
):
    me = lax.axis_index("dp") * 2 + lax.axis_index("mp")
    model = z_ref.shape[1]
    pieces = model // LANES

    def device(step):
        rank = lax.rem(me + step, total)
        return (rank // 2, lax.rem(rank, 2))

    barrier = pltpu.get_barrier_semaphore()
    for step in range(1, total):
        pl.semaphore_signal(barrier, inc=1, device_id=device(step), device_id_type=MESH)

    gain, shift = norm_ref[pl.ds(4, 1), :], norm_ref[pl.ds(5, 1), :]
    embeds, shrinks, means, inverses = [], [], [], []
    for index, (start, slots) in enumerate(spans):
        length = lens_ref[index]
        step = min(slots, 128)
        mean = None
        scales = []
        for at in range(0, slots, step):
            block = pl.ds(start + at, step)
            normed, scale = normalize(z_ref[block, :])
            unit[block, :] = normed
            scales.append(scale)
            valid = (lax.broadcasted_iota(jnp.int32, (step, 1), 0) + at) < length
            piece = jnp.sum(jnp.where(valid, normed, 0.0), axis=0, keepdims=True)
            mean = piece if mean is None else mean + piece
        mean = mean / length.astype(F32)
        pooled = mean * gain + shift
        shrink = lax.rsqrt(jnp.sum(pooled * pooled, axis=1, keepdims=True) + POOL_EPS)
        embed = pooled * shrink
        for piece in range(pieces):
            slab[pl.ds(index * pieces + piece, 1), :] = embed[:, piece * LANES : (piece + 1) * LANES]
        embeds.append(embed)
        shrinks.append(shrink)
        means.append(mean)
        inverses.append(scales)
    slab[pl.ds(2 * pieces, 1), :] = target_ref[pl.ds(0, 1), :]

    pl.semaphore_wait(barrier, total - 1)
    local = pltpu.make_async_copy(slab, every.at[me], here_sem)
    local.start()
    copies = []
    for step in range(1, total):
        copy = pltpu.make_async_remote_copy(
            src_ref=slab,
            dst_ref=every.at[me],
            send_sem=send_sem.at[step],
            recv_sem=recv_sem.at[step],
            device_id=device(step),
            device_id_type=MESH,
        )
        copy.start()
        copies.append(copy)
    local.wait()
    for copy in copies:
        copy.wait_recv()

    queries = [every[:, piece, :] for piece in range(pieces)]
    passages = [every[:, pieces + piece, :] for piece in range(pieces)]
    positive = every[:, 2 * pieces, :][:, :1]
    logits = None
    for left, right in zip(queries, passages):
        value = lax.dot_general(
            left, right, (((1,), (1,)), ((), ())), precision=PRECISE, preferred_element_type=F32
        )
        logits = value if logits is None else logits + value
    logits = logits / SOFTMAX_TEMPER
    place = lax.broadcasted_iota(jnp.int32, logits.shape, 1)
    target = (place.astype(F32) == positive).astype(F32)
    top = jnp.max(logits, axis=1, keepdims=True)
    weight = jnp.exp(logits - top)
    row_total = jnp.sum(weight, axis=1, keepdims=True)
    log_total = top + jnp.log(row_total)
    loss = jnp.sum(log_total - jnp.sum(logits * target, axis=1, keepdims=True), axis=0, keepdims=True) / total
    grad_logits = (weight / row_total - target) / (total * SOFTMAX_TEMPER)
    line = lax.broadcasted_iota(jnp.int32, logits.shape, 0)
    grad_column = jnp.sum(jnp.where(place == me, grad_logits, 0.0), axis=1, keepdims=True)
    mine_row = lax.broadcasted_iota(jnp.int32, (total, LANES), 0) == me
    grad_q, grad_p = [], []
    for left, right in zip(queries, passages):
        value = jnp.dot(grad_logits, right, precision=PRECISE, preferred_element_type=F32)
        grad_q.append(jnp.sum(jnp.where(mine_row, value, 0.0), axis=0, keepdims=True))
        grad_p.append(jnp.sum(grad_column * left, axis=0, keepdims=True))
    grad_gain, grad_shift, grad_bias = None, None, None
    for index, (start, slots) in enumerate(spans):
        length = lens_ref[index]
        grad_embed = jnp.concatenate(grad_q if index == 0 else grad_p, axis=1)
        embed = embeds[index]
        grad_pooled = shrinks[index] * (grad_embed - embed * jnp.sum(grad_embed * embed, axis=1, keepdims=True))
        grad_gain = grad_pooled * means[index] + (0.0 if index == 0 else grad_gain)
        grad_shift = grad_pooled + (0.0 if index == 0 else grad_shift)
        spread = grad_pooled * gain / length.astype(F32)
        centered = spread - jnp.mean(spread, axis=1, keepdims=True)
        step = min(slots, 128)
        for at in range(0, slots, step):
            block = pl.ds(start + at, step)
            normed = unit[block, :]
            valid = (lax.broadcasted_iota(jnp.int32, (step, 1), 0) + at) < length
            scale = jnp.where(valid, inverses[index][at // step], 0.0)
            value = scale * (centered - normed * jnp.mean(spread * normed, axis=1, keepdims=True))
            grad_ref[block, :] = value
            low_ref[block, :] = value.astype(BF16)
            piece = jnp.sum(value, axis=0, keepdims=True)
            grad_bias = piece if grad_bias is None else grad_bias + piece
    small_ref[pl.ds(0, 1), :] = grad_bias
    small_ref[pl.ds(1, 1), :] = grad_gain
    small_ref[pl.ds(2, 1), :] = grad_shift
    small_ref[pl.ds(3, 1), :] = jnp.broadcast_to(loss, (1, model))
    small_ref[pl.ds(4, 4), :] = jnp.zeros((4, model), F32)
    for copy in copies:
        copy.wait_send()


def loss_and_gradient(z_two, lens, target, norm_params, spans, total):
    slots, model = z_two.shape
    norms = jnp.concatenate([norm_params, jnp.zeros((2, model), F32)], axis=0)
    vmem = pl.BlockSpec(memory_space=pltpu.VMEM)
    dma = pltpu.SemaphoreType.DMA
    return pl.pallas_call(
        functools.partial(loss_kernel, spans, total),
        out_shape=(
            jax.ShapeDtypeStruct((slots, model), F32),
            jax.ShapeDtypeStruct((slots, model), BF16),
            jax.ShapeDtypeStruct((8, model), F32),
        ),
        in_specs=[pl.BlockSpec(memory_space=pltpu.SMEM), vmem, vmem, vmem],
        out_specs=(vmem,) * 3,
        scratch_shapes=[
            pltpu.VMEM((slots, model), F32),
            pltpu.VMEM((SLAB, LANES), F32),
            pltpu.VMEM((total, SLAB, LANES), F32),
            dma(()), dma((total,)), dma((total,)),
        ],
        compiler_params=pltpu.CompilerParams(collective_id=1, has_side_effects=True, vmem_limit_bytes=40 * MIB),
        name="loss",
    )(lens, z_two, norms, target)


def attend_kernel(spans, lens_ref, q_ref, k_ref, v_ref, o_ref):
    for index, (start, slots) in enumerate(spans):
        length = lens_ref[index]
        keys = k_ref[0, pl.ds(start, slots), :]
        values = v_ref[0, pl.ds(start, slots), :]
        lane = first_head(keys.shape)
        scaled = keys * jnp.asarray(HD**-0.5, BF16)
        zero = jnp.zeros_like(scaled)
        head_keys = (jnp.where(lane, scaled, zero), jnp.where(lane, zero, scaled))
        block = min(slots, 256)
        for at in range(0, slots, block):
            queries = q_ref[0, pl.ds(start + at, block), :]
            outs = []
            for head in range(2):
                scores = mm_nt(queries, head_keys[head])
                valid = lax.broadcasted_iota(jnp.int32, scores.shape, 1) < length
                scores = jnp.where(valid, scores, NEG_FILL)
                top = jnp.max(scores, axis=1, keepdims=True)
                weight = jnp.exp(scores - top)
                total = jnp.sum(weight, axis=1, keepdims=True)
                probs = (weight * (1.0 / total)).astype(BF16)
                outs.append(mm(probs, values))
            o_ref[pl.ds(start + at, block), :] = jnp.where(
                first_head(outs[0].shape), outs[0], outs[1]
            ).astype(BF16)


def attend_back_kernel(spans, lens_ref, q_ref, k_ref, v_ref, g_ref, d_ref):
    scale = HD**-0.5
    for index, (start, slots) in enumerate(spans):
        length = lens_ref[index]
        keys = k_ref[0, pl.ds(start, slots), :]
        values = v_ref[0, pl.ds(start, slots), :]
        lane = first_head(keys.shape)
        scaled = keys * jnp.asarray(scale, BF16)
        zero = jnp.zeros_like(scaled)
        head_keys = (jnp.where(lane, scaled, zero), jnp.where(lane, zero, scaled))
        head_values = (jnp.where(lane, values, zero), jnp.where(lane, zero, values))
        block = min(slots, 256)
        grad_k = [None, None]
        grad_v = [None, None]
        for at in range(0, slots, block):
            queries = q_ref[0, pl.ds(start + at, block), :]
            grads = g_ref[pl.ds(start + at, block), :]
            grad_q = []
            for head in range(2):
                scores = mm_nt(head_keys[head], queries)
                valid = lax.broadcasted_iota(jnp.int32, scores.shape, 0) < length
                scores = jnp.where(valid, scores, NEG_FILL)
                top = jnp.max(scores, axis=0, keepdims=True)
                weight = jnp.exp(scores - top)
                total = jnp.sum(weight, axis=0, keepdims=True)
                probs = weight * (1.0 / total)
                grad_probs = mm_nt(head_values[head], grads)
                inner = jnp.sum(probs * grad_probs, axis=0, keepdims=True)
                grad_scores = (probs * (grad_probs - inner)).astype(BF16)
                part_v = mm(probs.astype(BF16), grads)
                part_k = mm(grad_scores, queries)
                grad_v[head] = part_v if at == 0 else grad_v[head] + part_v
                grad_k[head] = part_k if at == 0 else grad_k[head] + part_k
                grad_q.append(mm_tn(grad_scores, keys))
            d_ref[0, pl.ds(start + at, block), :] = (
                jnp.where(first_head(grad_q[0].shape), grad_q[0], grad_q[1]) * scale
            ).astype(BF16)
        d_ref[1, pl.ds(start, slots), :] = (jnp.where(lane, grad_k[0], grad_k[1]) * scale).astype(BF16)
        d_ref[2, pl.ds(start, slots), :] = jnp.where(lane, grad_v[0], grad_v[1]).astype(BF16)


def head_specs(tokens):
    return [pl.BlockSpec((1, tokens, LANES), functools.partial(lambda s, i, lens: (s, 0, i), s)) for s in range(3)]


def attend(proj, lens, spans):
    _, tokens, width = proj.shape
    flops = sum(4 * slots * slots * width for _, slots in spans)
    return pl.pallas_call(
        functools.partial(attend_kernel, spans),
        out_shape=jax.ShapeDtypeStruct((tokens, width), BF16),
        grid_spec=pltpu.PrefetchScalarGridSpec(
            num_scalar_prefetch=1,
            grid=(width // LANES,),
            in_specs=head_specs(tokens),
            out_specs=pl.BlockSpec((tokens, LANES), lambda i, lens: (0, i)),
        ),
        compiler_params=pltpu.CompilerParams(vmem_limit_bytes=40 * MIB),
        cost_estimate=pl.CostEstimate(flops=8 * flops, bytes_accessed=8 * tokens * width, transcendentals=0),
        name="attend",
    )(lens, proj, proj, proj)


def attend_back(proj, grad_out, lens, spans):
    _, tokens, width = proj.shape
    flops = sum(10 * slots * slots * width for _, slots in spans)
    return pl.pallas_call(
        functools.partial(attend_back_kernel, spans),
        out_shape=jax.ShapeDtypeStruct((3, tokens, width), BF16),
        grid_spec=pltpu.PrefetchScalarGridSpec(
            num_scalar_prefetch=1,
            grid=(width // LANES,),
            in_specs=head_specs(tokens) + [pl.BlockSpec((tokens, LANES), lambda i, lens: (0, i))],
            out_specs=pl.BlockSpec((3, tokens, LANES), lambda i, lens: (0, 0, i)),
        ),
        compiler_params=pltpu.CompilerParams(vmem_limit_bytes=40 * MIB),
        cost_estimate=pl.CostEstimate(flops=8 * flops, bytes_accessed=14 * tokens * width, transcendentals=0),
        name="attend_back",
    )(lens, proj, proj, proj, grad_out)


def up_kernel(x_ref, w_ref, b_ref, g_ref, s_ref):
    hidden = mm(x_ref[...], w_ref[0]) + b_ref[...]
    active, slope = gelu_and_slope(hidden)
    g_ref[...] = active.astype(BF16)
    s_ref[...] = slope


def feed_up(low, ffn_half, bias):
    tokens, width = low.shape
    units = ffn_half.shape[2]
    tile = 256
    return pl.pallas_call(
        up_kernel,
        out_shape=(jax.ShapeDtypeStruct((tokens, units), BF16), jax.ShapeDtypeStruct((tokens, units), F32)),
        grid=(units // tile,),
        in_specs=[
            pl.BlockSpec((tokens, width), lambda i: (0, 0)),
            pl.BlockSpec((1, width, tile), lambda i: (0, 0, i)),
            pl.BlockSpec((1, tile), lambda i: (0, i)),
        ],
        out_specs=(pl.BlockSpec((tokens, tile), lambda i: (0, i)), pl.BlockSpec((tokens, tile), lambda i: (0, i))),
        compiler_params=pltpu.CompilerParams(vmem_limit_bytes=40 * MIB),
        cost_estimate=pl.CostEstimate(
            flops=2 * tokens * width * units, bytes_accessed=8 * tokens * units, transcendentals=tokens * units
        ),
        name="feed_up",
    )(low, ffn_half, bias.reshape(1, -1))


def swap_cores(values):
    return lax.ppermute(values, "mp", [(0, 1), (1, 0)])


def scatter_sum(own_parts, other_parts):
    me = lax.axis_index("dp")
    size = lax.axis_size("dp")
    summed = [own + swap_cores(other).astype(F32) for own, other in zip(own_parts, other_parts)]
    if size != 16:
        return [lax.psum_scatter(value, "dp", scatter_dimension=1, tiled=True) for value in summed]
    bits = (lax.rem(me, 2), lax.rem(me // 2, 2))
    level = me // 4
    neighbour = ([(i, i ^ 1) for i in range(16)], [(i, i ^ 2) for i in range(16)])
    columns = []
    for part, value in enumerate(summed):
        count, full, width = value.shape
        value = value.reshape(count, 4, 2, 2, full // 16, width)
        for axis in (0, 1) if part == 0 else (1, 0):
            at = value.ndim - 3 if axis == 0 else 2
            keep = lax.dynamic_index_in_dim(value, bits[axis], at, keepdims=False)
            send = lax.dynamic_index_in_dim(value, 1 - bits[axis], at, keepdims=False).astype(BF16)
            value = keep + lax.ppermute(send, "dp", neighbour[axis]).astype(F32)
        columns.append(value)
    results = []
    for value in columns:
        total = lax.dynamic_index_in_dim(value, level, 1, keepdims=False)
        for step in range(1, 4):
            send = lax.dynamic_index_in_dim(value, lax.rem(level + step, 4), 1, keepdims=False).astype(BF16)
            got = lax.ppermute(send, "dp", [(i, (i + 4 * step) % 16) for i in range(16)])
            total = total + got.astype(F32)
        results.append(total)
    return results


def sum_all(values):
    size = lax.axis_size("dp")
    if size != 16:
        return lax.psum(values, "dp")
    for bit in (1, 2, 4, 8):
        values = values + lax.ppermute(values, "dp", [(i, i ^ bit) for i in range(16)])
    return values


def adam_update(master, first, second, average, grad, rate, decay_w, rates, step_count):
    first_new = rates[0] * first + (1.0 - rates[0]) * grad
    second_new = rates[1] * second + (1.0 - rates[1]) * grad * grad
    fixed_one = first_new / (1.0 - rates[0] ** step_count)
    fixed_two = second_new / (1.0 - rates[1] ** step_count)
    master_new = master - rate * (fixed_one / (jnp.sqrt(fixed_two) + ADAM_EPS) + decay_w * master)
    average_new = rates[2] * average + (1.0 - rates[2]) * master_new
    return (master_new, first_new, second_new, average_new)


def normalize_back(unit, inverse, grad_unit):
    return inverse * (
        grad_unit
        - jnp.mean(grad_unit, axis=-1, keepdims=True)
        - unit * jnp.mean(grad_unit * unit, axis=-1, keepdims=True)
    )


def forward_plain(tokens, lens, attn_low, ffn_low, col_bias, norm_params, spans):
    attn_full = lax.all_gather(attn_low, "dp", axis=1, tiled=True)
    ffn_full = lax.all_gather(ffn_low, "dp", axis=1, tiled=True)
    attn_w = (attn_full, swap_cores(attn_full))
    ffn_w = (ffn_full, swap_cores(ffn_full))
    col = (col_bias, swap_cores(col_bias))
    width = attn_w[0].shape[2]

    projected, mixed = [], []
    branch = None
    for half in range(2):
        bias = jnp.stack([col[half][:width], jnp.zeros((width,), F32), col[half][width : 2 * width]])
        proj = (
            jnp.einsum("td,sde->ste", tokens, attn_w[half][:3], preferred_element_type=F32) + bias[:, None, :]
        ).astype(BF16)
        out = attend(proj, lens, spans)
        part = mm_nt(out, attn_w[half][3])
        branch = part if branch is None else branch + part
        projected.append(proj)
        mixed.append(out)
    z_one = tokens.astype(F32) + branch + norm_params[0]
    unit_one, inverse_one = normalize(z_one)
    first_norm = unit_one * norm_params[1] + norm_params[2]
    first_low = first_norm.astype(BF16)
    active, slope = [], []
    branch_two = None
    for half in range(2):
        act, slo = feed_up(first_low, ffn_w[half], col[half][2 * width :])
        part = mm_nt(act, ffn_w[half][1])
        branch_two = part if branch_two is None else branch_two + part
        active.append(act)
        slope.append(slo)
    z_two = first_norm + branch_two + norm_params[3]
    return attn_w, ffn_w, projected, mixed, unit_one, inverse_one, first_low, active, slope, z_two


def loss_plain(z_two, lens, target_mine, norm_params, spans, pairs):
    query_slots, passage_slots = spans[0][1], spans[1][1]
    model_width = z_two.shape[1]
    core = lax.axis_index("mp")
    unit_two, inverse_two = normalize(z_two)
    places = jnp.arange(query_slots + passage_slots)
    in_query = (places < query_slots) & (places < lens[0])
    in_passage = (places >= query_slots) & (places - query_slots < lens[1])
    share = (
        jnp.stack([in_query, in_passage]).astype(F32) / lens.astype(F32)[:, None]
    )
    mean_unit = jnp.dot(share, unit_two, precision=PRECISE, preferred_element_type=F32)
    pooled = mean_unit * norm_params[4] + norm_params[5]
    shrink = lax.rsqrt(jnp.sum(pooled * pooled, axis=1, keepdims=True) + POOL_EPS)
    embed = pooled * shrink

    payload = jnp.concatenate([embed.reshape(-1), target_mine])
    every = lax.all_gather(payload, ("dp", "mp"), axis=0)
    every_q = every[:, :model_width]
    every_p = every[:, model_width : 2 * model_width]
    target = (jnp.arange(pairs)[None, :].astype(F32) == every[:, 2 * model_width :][:, :1]).astype(F32)
    logits = lax.dot_general(every_q, every_p, (((1,), (1,)), ((), ())), precision=PRECISE) / SOFTMAX_TEMPER
    row_top = jnp.max(logits, axis=1, keepdims=True)
    exp_logits = jnp.exp(logits - row_top)
    row_total = jnp.sum(exp_logits, axis=1, keepdims=True)
    log_total = row_top[:, 0] + jnp.log(row_total[:, 0])
    loss_value = (jnp.sum(log_total - jnp.sum(logits * target, axis=1)) / pairs).reshape(1)
    grad_logits = (exp_logits / row_total - target) / (pairs * SOFTMAX_TEMPER)
    rank = lax.axis_index("dp") * lax.axis_size("mp") + core
    grad_uq = jnp.dot(lax.dynamic_index_in_dim(grad_logits, rank, 0, keepdims=True), every_p, precision=PRECISE)
    grad_up = jnp.dot(
        lax.dynamic_index_in_dim(grad_logits, rank, 1, keepdims=False)[None], every_q, precision=PRECISE
    )
    grad_embed = jnp.concatenate([grad_uq, grad_up], axis=0)

    grad_pooled = shrink * (grad_embed - embed * jnp.sum(grad_embed * embed, axis=1, keepdims=True))
    grad_gain_two = jnp.sum(grad_pooled * mean_unit, axis=0)
    grad_shift_two = jnp.sum(grad_pooled, axis=0)
    grad_unit_two = lax.dot_general(
        share, grad_pooled * norm_params[4], (((0,), (0,)), ((), ())), precision=PRECISE
    )
    grad_ztwo = normalize_back(unit_two, inverse_two, grad_unit_two)
    grad_bias_two = jnp.sum(grad_ztwo, axis=0)
    grad_two_low = grad_ztwo.astype(BF16)
    return grad_ztwo, grad_two_low, loss_value, grad_bias_two, grad_gain_two, grad_shift_two


def per_device(
    query_in,
    passage_in,
    query_len,
    passage_len,
    positive,
    step,
    rates,
    attn_master,
    attn_first,
    attn_second,
    attn_average,
    ffn_master,
    ffn_first,
    ffn_second,
    ffn_average,
    norm_params,
    norm_first,
    norm_second,
    norm_average,
    col_bias,
    col_first,
    col_second,
    col_average,
):
    core = lax.axis_index("mp")
    size = lax.axis_size("dp")
    query_slots, model_width = query_in.shape[1:]
    passage_slots = passage_in.shape[1]
    pairs = query_in.shape[0] * size
    spans = ((0, query_slots), (query_slots, passage_slots))

    def pick(values, index):
        return lax.dynamic_index_in_dim(values, index, 0, keepdims=False)

    tokens = jnp.concatenate([pick(query_in, core), pick(passage_in, core)], axis=0)
    lens = jnp.stack([pick(query_len, core), pick(passage_len, core)])

    attn_low, ffn_low = attn_master.astype(BF16), ffn_master.astype(BF16)
    target = jnp.broadcast_to(pick(positive, core).astype(F32), (8, LANES))
    if size == 16:
        outs = forward(tokens, lens, attn_low, ffn_low, col_bias, norm_params, spans)
        attn_w, ffn_w, projected, mixed, unit_one, inverse_one, first_low, active, slope, z_two = outs
        inverse_one = inverse_one[:, :1]
        grad_ztwo, grad_two_low, small = loss_and_gradient(z_two, lens, target, norm_params, spans, pairs)
        loss_value = small[3, :1]
        grad_bias_two, grad_gain_two, grad_shift_two = small[0], small[1], small[2]
    else:
        outs = forward_plain(tokens, lens, attn_low, ffn_low, col_bias, norm_params, spans)
        attn_w, ffn_w, projected, mixed, unit_one, inverse_one, first_low, active, slope, z_two = outs
        outs = loss_plain(z_two, lens, target[0], norm_params, spans, pairs)
        grad_ztwo, grad_two_low, loss_value, grad_bias_two, grad_gain_two, grad_shift_two = outs

    cut = ffn_w[0].shape[2] // 2
    width = attn_w[0].shape[2]

    def two_parts(values):
        return values[:, :cut], values[:, cut:]

    def parted_product(left, halves):
        own = [mm_tn(left, part)[None] for part in two_parts(halves[0])]
        other = [mm_tn(left, part).astype(BF16)[None] for part in two_parts(halves[1])]
        return own, other

    down_grad = scatter_sum(*parted_product(grad_two_low, active))
    grad_hidden, grad_first = [], grad_ztwo
    for half in (1, 0):
        grad_hid = (mm(grad_two_low, ffn_w[half][1]) * slope[half]).astype(BF16)
        grad_hidden.insert(0, grad_hid)
        grad_first = grad_first + mm_nt(grad_hid, ffn_w[half][0])
    grad_hidden_bias = [jnp.sum(value.astype(F32), axis=0) for value in grad_hidden]
    up_grad = scatter_sum(*parted_product(first_low, grad_hidden))

    grad_gain_one = jnp.sum(grad_first * unit_one, axis=0)
    grad_shift_one = jnp.sum(grad_first, axis=0)
    grad_zone = normalize_back(unit_one, inverse_one, grad_first * norm_params[1])
    grad_bias_out = jnp.sum(grad_zone, axis=0)
    grad_one_low = grad_zone.astype(BF16)
    grad_tokens = grad_zone
    grad_query_bias, grad_value_bias, attn_parts = [None, None], [None, None], [None, None]
    for half in (1, 0):
        grad_out = mm(grad_one_low, attn_w[half][3]).astype(BF16)
        grad_proj = attend_back(projected[half], grad_out, lens, spans)
        grad_query_bias[half] = jnp.sum(grad_proj[0].astype(F32), axis=0)
        grad_value_bias[half] = jnp.sum(grad_proj[2].astype(F32), axis=0)
        in_grads = jnp.einsum("td,ste->sde", tokens, grad_proj, preferred_element_type=F32)
        out_grad = mm_tn(grad_one_low, mixed[half])
        parts = [in_grads[:2], jnp.stack([in_grads[2], out_grad])]
        attn_parts[half] = parts if half == 0 else [part.astype(BF16) for part in parts]
        for index in range(3):
            grad_tokens = grad_tokens + mm_nt(grad_proj[index], attn_w[half][index])
    attn_grads = scatter_sum(*attn_parts)

    col_parts = [
        jnp.concatenate([grad_query_bias[half], grad_value_bias[half], grad_hidden_bias[half]]) for half in range(2)
    ]
    norm_part = jnp.stack(
        [grad_bias_out, grad_gain_one, grad_shift_one, grad_bias_two, grad_gain_two, grad_shift_two]
    )
    norm_part = norm_part + swap_cores(norm_part)
    col_part = col_parts[0] + swap_cores(col_parts[1])
    small = sum_all(jnp.concatenate([norm_part.reshape(-1), col_part]))
    norm_grad = small[: norm_part.size].reshape(norm_part.shape)
    col_grad = small[norm_part.size :]

    step_count = step[0].astype(F32)
    attn_grad = jnp.concatenate(attn_grads, axis=0)
    ffn_grad = jnp.stack([jnp.concatenate(parts, axis=-1)[0] for parts in (up_grad, down_grad)])
    attn_out = adam_update(
        attn_master, attn_first, attn_second, attn_average, attn_grad, rates[3], DECAY_WEIGHT, rates, step_count
    )
    ffn_out = adam_update(
        ffn_master, ffn_first, ffn_second, ffn_average, ffn_grad, rates[3], DECAY_WEIGHT, rates, step_count
    )
    norm_out = adam_update(
        norm_params, norm_first, norm_second, norm_average, norm_grad, rates[4], 0.0, rates, step_count
    )
    col_out = adam_update(col_bias, col_first, col_second, col_average, col_grad, rates[4], 0.0, rates, step_count)

    grad_twin = swap_cores(grad_tokens)
    first_pair = jnp.where(core == 0, grad_tokens, grad_twin)
    second_pair = jnp.where(core == 0, grad_twin, grad_tokens)
    query_grad = jnp.stack([first_pair[:query_slots], second_pair[:query_slots]])
    passage_grad = jnp.stack([first_pair[query_slots:], second_pair[query_slots:]])
    return (
        loss_value,
        query_grad,
        passage_grad,
        *attn_out,
        *ffn_out,
        *norm_out,
        *col_out,
        attn_out[0].astype(BF16),
        ffn_out[0].astype(BF16),
    )


def solution(mesh):
    matrix = P(None, "dp", "mp")
    rows = P("dp", None, None)
    placed = (rows, rows, P("dp"), P("dp"), P("dp"), P(), P(), *[matrix] * 8, *[P()] * 4, *[P("mp")] * 4)
    return jax.shard_map(
        per_device,
        mesh=mesh,
        in_specs=placed,
        out_specs=(P(), rows, rows, *[matrix] * 8, *[P()] * 4, *[P("mp")] * 4, matrix, matrix),
        check_vma=False,
    )
```

```python
import functools

import jax
import jax.numpy as jnp
from jax import lax
from jax.experimental import pallas as pl
from jax.experimental.pallas import tpu as pltpu
from jax.sharding import PartitionSpec as P

HD = 64
LANES = 128
NEG_FILL = -1e30
SOFTMAX_TEMPER = 0.02
NORM_EPS = 1e-12
POOL_EPS = 1e-06
DECAY_WEIGHT = 0.01
ADAM_EPS = 1e-08
PRECISE = lax.Precision.HIGHEST
MESH = pl.DeviceIdType.MESH
MIB = 2**20
F32 = jnp.float32
BF16 = jnp.bfloat16

ERFC_STEP = 0.46
ERFC_HALF = (
    0.5 * 0.26113873056821263,
    0.5 * 0.23637801512084577,
    0.5 * 0.3601812301921897,
    -0.5 * 0.18740624158431016,
    0.5 * 0.6751549397754679,
    -0.5 * 0.4305350150859377,
    0.5 * 0.0850883282904581,
)
ROOT_HALF = 0.7071067811865476
DENSITY = 0.3989422804014327


def gelu_and_slope(hidden):
    bell = jnp.exp(hidden * hidden * (-0.5))
    step = 1.0 / (1.0 + (ERFC_STEP * ROOT_HALF) * jnp.abs(hidden))
    tail = ERFC_HALF[6]
    for coefficient in ERFC_HALF[5::-1]:
        tail = tail * step + coefficient
    tail = tail * step * bell
    below = jnp.where(hidden >= 0.0, 1.0 - tail, tail)
    return hidden * below, below + hidden * bell * DENSITY


def mm(left, right):
    return jnp.dot(left, right, preferred_element_type=F32)


def mm_nt(left, right):
    return lax.dot_general(left, right, (((1,), (1,)), ((), ())), preferred_element_type=F32)


def mm_tn(left, right):
    return lax.dot_general(left, right, (((0,), (0,)), ((), ())), preferred_element_type=F32)


def normalize(values):
    center = values - jnp.mean(values, axis=-1, keepdims=True)
    spread = jnp.mean(center * center, axis=-1, keepdims=True)
    inverse = lax.rsqrt(spread + NORM_EPS)
    return center * inverse, inverse


def first_head(shape):
    return lax.broadcasted_iota(jnp.int32, shape, 1) < HD


ROW_BLOCK = 144


def forward_kernel(
    spans,
    lens_ref, x_ref, attn_ref, ffn_ref, col_ref, norm_ref,
    attn_out, ffn_out, proj_out, mixed_out, unit_out, inverse_out, low_out, active_out, slope_out, z_out,
    attn_w, ffn_w, col_far, proj, mixed, unit, inverse, low, active, slope, z_two,
    z_send, z_recv, x_send, x_recv, y_send, y_recv, d_send, d_recv, c_send, c_recv, b_send, b_recv, here_sem, out_sem,
):
    me = lax.axis_index("dp")
    core = lax.axis_index("mp")
    x, y, z = lax.rem(me, 2), lax.rem(me // 2, 2), me // 4
    rows = attn_ref.shape[1]
    half_units = ffn_ref.shape[2] // 2
    width = attn_ref.shape[2]
    units = ffn_ref.shape[2]
    tokens = x_ref.shape[0]

    def index_of(zz, yy, xx):
        return (zz * 2 + yy) * 2 + xx

    column = [lax.rem(z - k + 4, 4) for k in range(4)]
    z_peer = [None] + [(index_of(lax.rem(z + k, 4), y, x), core) for k in range(1, 4)]
    x_peer = (index_of(z, y, 1 - x), core)
    y_peer = (index_of(z, 1 - y, x), core)
    c_peer = (me, 1 - core)

    barrier = pltpu.get_barrier_semaphore()
    for peer in [*z_peer[1:], x_peer, y_peer, c_peer]:
        pl.semaphore_signal(barrier, inc=1, device_id=peer, device_id_type=MESH)
    pl.semaphore_wait(barrier, 6)

    def span(index, count=1):
        return pl.ds(pl.multiple_of(index * rows, rows), count * rows)

    def whole(chunk, index, count=1, far=0):
        if chunk == 0:
            return attn_w.at[far, :, span(index, count), :]
        return ffn_w.at[far, chunk - 1, span(index, count), :]

    def part(chunk, index, which):
        if chunk == 0:
            return attn_w.at[0, pl.ds(2 * which, 2), span(index), :]
        return ffn_w.at[0, chunk - 1, span(index), pl.ds(which * half_units, half_units)]

    def mine(chunk):
        return attn_ref if chunk == 0 else ffn_ref.at[chunk - 1]

    sends = []
    stores = []

    def push(source, target, send, recv, peer):
        copy = pltpu.make_async_remote_copy(
            src_ref=source, dst_ref=target, send_sem=send, recv_sem=recv, device_id=peer, device_id_type=MESH
        )
        copy.start()
        sends.append(copy)

    def landed(target, send, recv, peer):
        pltpu.make_async_remote_copy(
            src_ref=target, dst_ref=target, send_sem=send, recv_sem=recv, device_id=peer, device_id_type=MESH
        ).wait_recv()

    def store(source, target):
        copy = pltpu.make_async_copy(source, target, out_sem.at[len(stores)])
        copy.start()
        stores.append(copy)

    local = []
    for q in range(3):
        copy = pltpu.make_async_copy(mine(q), whole(q, me), here_sem.at[q])
        copy.start()
        local.append(copy)
        for k in range(1, 4):
            push(mine(q), whole(q, me), z_send.at[q, k], z_recv.at[q, k], z_peer[k])
        push(mine(q), whole(q, me), x_send.at[q, 0], x_recv.at[q, 0], x_peer)
        push(mine(q), whole(q, me), y_send.at[q, 0], y_recv.at[q, 0], y_peer)
    push(col_ref, col_far, b_send, b_recv, c_peer)

    def along_column(q):
        for k in range(1, 4):
            block = index_of(column[k], y, x)
            landed(whole(q, block), z_send.at[q, k], z_recv.at[q, k], z_peer[k])
            push(whole(q, block), whole(q, block), x_send.at[q, k], x_recv.at[q, k], x_peer)
            push(whole(q, block), whole(q, block), y_send.at[q, k], y_recv.at[q, k], y_peer)

    def round_corner(q, ks=range(4)):
        for k in ks:
            beside = index_of(column[k], y, 1 - x)
            landed(whole(q, beside), x_send.at[q, k], x_recv.at[q, k], x_peer)
            push(part(q, beside, 0), part(q, beside, 0), d_send.at[q, k, 0], d_recv.at[q, k, 0], y_peer)
            beside = index_of(column[k], 1 - y, x)
            landed(whole(q, beside), y_send.at[q, k], y_recv.at[q, k], y_peer)
            push(part(q, beside, 1), part(q, beside, 1), d_send.at[q, k, 1], d_recv.at[q, k, 1], x_peer)

    def to_other_core(q, ks=range(4)):
        for k in ks:
            if k == 0:
                local[q].wait()
            across = index_of(column[k], 1 - y, 1 - x)
            landed(part(q, across, 0), d_send.at[q, k, 0], d_recv.at[q, k, 0], y_peer)
            landed(part(q, across, 1), d_send.at[q, k, 1], d_recv.at[q, k, 1], x_peer)
            layer = index_of(column[k], 0, 0)
            push(whole(q, layer, 4), whole(q, layer, 4, 1), c_send.at[q, k], c_recv.at[q, k], c_peer)

    def from_other_core(q):
        for k in range(4):
            layer = index_of(column[k], 0, 0)
            landed(whole(q, layer, 4, 1), c_send.at[q, k], c_recv.at[q, k], c_peer)

    def bias(half, start, count):
        source = col_ref if half == 0 else col_far
        return source[pl.ds(0, 1), pl.ds(start, count)]

    def project(half):
        for index in range(3):
            value = mm(x_ref[...], attn_w[half, index])
            if index != 1:
                value = value + bias(half, (index // 2) * width, width)
            proj[half, index] = value.astype(BF16)

    def heads(half, pair):
        lanes = pl.ds(pair * LANES, LANES)
        for index, (start, slots) in enumerate(spans):
            length = lens_ref[index]
            keys = proj[half, 1, pl.ds(start, slots), lanes]
            values = proj[half, 2, pl.ds(start, slots), lanes]
            lane = first_head(keys.shape)
            scaled = keys * jnp.asarray(HD**-0.5, BF16)
            zero = jnp.zeros_like(scaled)
            head_keys = (jnp.where(lane, scaled, zero), jnp.where(lane, zero, scaled))
            block = min(slots, 256)
            for at in range(0, slots, block):
                queries = proj[half, 0, pl.ds(start + at, block), lanes]
                outs = []
                for head in range(2):
                    scores = mm_nt(queries, head_keys[head])
                    valid = lax.broadcasted_iota(jnp.int32, scores.shape, 1) < length
                    scores = jnp.where(valid, scores, NEG_FILL)
                    top = jnp.max(scores, axis=1, keepdims=True)
                    weight = jnp.exp(scores - top)
                    total = jnp.sum(weight, axis=1, keepdims=True)
                    probs = (weight * (1.0 / total)).astype(BF16)
                    outs.append(mm(probs, values))
                mixed[half, pl.ds(start + at, block), lanes] = jnp.where(
                    first_head(outs[0].shape), outs[0], outs[1]
                ).astype(BF16)

    def first_norm():
        for at in range(0, tokens, ROW_BLOCK):
            block = pl.ds(at, ROW_BLOCK)
            value = mm_nt(mixed[0, block, :], attn_w[0, 3]) + mm_nt(mixed[1, block, :], attn_w[1, 3])
            value = x_ref[block, :].astype(F32) + value + norm_ref[pl.ds(0, 1), :]
            normed, scale = normalize(value)
            unit[block, :] = normed
            inverse[block, :] = jnp.broadcast_to(scale, (ROW_BLOCK, LANES))
            value = normed * norm_ref[pl.ds(1, 1), :] + norm_ref[pl.ds(2, 1), :]
            z_two[block, :] = value
            low[block, :] = value.astype(BF16)

    tile = 256

    def up(half):
        @pl.loop(0, units // tile)
        def _(index):
            lanes = pl.ds(pl.multiple_of(index * tile, tile), tile)
            source = col_ref if half == 0 else col_far
            shift = source[pl.ds(0, 1), pl.ds(pl.multiple_of(2 * width + index * tile, tile), tile)]
            hidden = mm(low[...], ffn_w[half, 0, :, lanes]) + shift
            value, grad = gelu_and_slope(hidden)
            active[half, :, lanes] = value.astype(BF16)
            slope[half, :, lanes] = grad

    def down(half):
        @pl.loop(0, tokens // ROW_BLOCK)
        def _(index):
            block = pl.ds(pl.multiple_of(index * ROW_BLOCK, ROW_BLOCK), ROW_BLOCK)
            value = z_two[block, :] + mm_nt(active[half, block, :], ffn_w[half, 1])
            if half == 1:
                value = value + norm_ref[pl.ds(3, 1), :]
            z_two[block, :] = value

    along_column(0)
    round_corner(0)
    along_column(1)
    to_other_core(0)
    landed(col_far, b_send, b_recv, c_peer)
    store(attn_w.at[0], attn_out.at[0])
    project(0)
    heads(0, 0)
    heads(0, 1)
    round_corner(1, (0, 1))
    heads(0, 2)
    from_other_core(0)
    store(attn_w.at[1], attn_out.at[1])
    project(1)
    round_corner(1, (2, 3))
    store(proj, proj_out)
    heads(1, 0)
    along_column(2)
    heads(1, 1)
    round_corner(2, (0,))
    heads(1, 2)
    to_other_core(1)
    store(mixed, mixed_out)
    first_norm()
    store(unit, unit_out)
    store(inverse, inverse_out)
    store(low, low_out)
    round_corner(2, (1, 2))
    store(ffn_w.at[0, 0], ffn_out.at[0, 0])
    up(0)
    store(slope.at[0], slope_out.at[0])
    from_other_core(1)
    store(ffn_w.at[1, 0], ffn_out.at[1, 0])
    round_corner(2, (3,))
    to_other_core(2, (0, 1))
    up(1)
    store(active, active_out)
    store(slope.at[1], slope_out.at[1])
    to_other_core(2, (2, 3))
    store(ffn_w.at[0, 1], ffn_out.at[0, 1])
    down(0)
    from_other_core(2)
    store(ffn_w.at[1, 1], ffn_out.at[1, 1])
    down(1)
    store(z_two, z_out)
    for copy in stores:
        copy.wait()
    for copy in sends:
        copy.wait_send()


def forward(tokens, lens, attn_low, ffn_low, col_bias, norm_params, spans):
    count, rows, width = attn_low.shape
    units = ffn_low.shape[2]
    full = rows * 16
    slots, model = tokens.shape
    dma = pltpu.SemaphoreType.DMA
    col = jnp.broadcast_to(col_bias[None], (8, col_bias.shape[0]))
    norms = jnp.concatenate([norm_params, jnp.zeros((2, model), F32)], axis=0)
    anywhere = pl.BlockSpec(memory_space=pltpu.HBM)
    vmem = pl.BlockSpec(memory_space=pltpu.VMEM)
    results = (
        ((2, count, full, width), BF16),
        ((2, 2, full, units), BF16),
        ((2, 3, slots, width), BF16),
        ((2, slots, width), BF16),
        ((slots, model), F32),
        ((slots, LANES), F32),
        ((slots, model), BF16),
        ((2, slots, units), BF16),
        ((2, slots, units), F32),
        ((slots, model), F32),
    )
    held = [pltpu.VMEM(*results[0]), pltpu.VMEM(*results[1]), pltpu.VMEM(col.shape, F32)]
    held += [pltpu.VMEM(*result) for result in results[2:]]
    return pl.pallas_call(
        functools.partial(forward_kernel, spans),
        out_shape=tuple(jax.ShapeDtypeStruct(*result) for result in results),
        in_specs=[pl.BlockSpec(memory_space=pltpu.SMEM), vmem, anywhere, anywhere, vmem, vmem],
        out_specs=(anywhere,) * len(results),
        scratch_shapes=held
        + [dma((3, 4))] * 6
        + [dma((3, 4, 2))] * 2
        + [dma((3, 4))] * 2
        + [dma(()), dma(()), dma((3,)), dma((16,))],
        compiler_params=pltpu.CompilerParams(collective_id=0, has_side_effects=True, vmem_limit_bytes=56 * MIB),
        name="forward",
    )(lens, tokens, attn_low, ffn_low, col, norms)


SLAB = 16


def loss_kernel(
    spans, total,
    lens_ref, z_ref, norm_ref, target_ref,
    grad_ref, low_ref, small_ref,
    unit, slab, every, here_sem, send_sem, recv_sem,
):
    me = lax.axis_index("dp") * 2 + lax.axis_index("mp")
    model = z_ref.shape[1]
    pieces = model // LANES

    def device(step):
        rank = lax.rem(me + step, total)
        return (rank // 2, lax.rem(rank, 2))

    barrier = pltpu.get_barrier_semaphore()
    for step in range(1, total):
        pl.semaphore_signal(barrier, inc=1, device_id=device(step), device_id_type=MESH)

    gain, shift = norm_ref[pl.ds(4, 1), :], norm_ref[pl.ds(5, 1), :]
    embeds, shrinks, means, inverses = [], [], [], []
    for index, (start, slots) in enumerate(spans):
        length = lens_ref[index]
        step = min(slots, 128)
        mean = None
        scales = []
        for at in range(0, slots, step):
            block = pl.ds(start + at, step)
            normed, scale = normalize(z_ref[block, :])
            unit[block, :] = normed
            scales.append(scale)
            valid = (lax.broadcasted_iota(jnp.int32, (step, 1), 0) + at) < length
            piece = jnp.sum(jnp.where(valid, normed, 0.0), axis=0, keepdims=True)
            mean = piece if mean is None else mean + piece
        mean = mean / length.astype(F32)
        pooled = mean * gain + shift
        shrink = lax.rsqrt(jnp.sum(pooled * pooled, axis=1, keepdims=True) + POOL_EPS)
        embed = pooled * shrink
        for piece in range(pieces):
            slab[pl.ds(index * pieces + piece, 1), :] = embed[:, piece * LANES : (piece + 1) * LANES]
        embeds.append(embed)
        shrinks.append(shrink)
        means.append(mean)
        inverses.append(scales)
    slab[pl.ds(2 * pieces, 1), :] = target_ref[pl.ds(0, 1), :]

    pl.semaphore_wait(barrier, total - 1)
    local = pltpu.make_async_copy(slab, every.at[me], here_sem)
    local.start()
    copies = []
    for step in range(1, total):
        copy = pltpu.make_async_remote_copy(
            src_ref=slab,
            dst_ref=every.at[me],
            send_sem=send_sem.at[step],
            recv_sem=recv_sem.at[step],
            device_id=device(step),
            device_id_type=MESH,
        )
        copy.start()
        copies.append(copy)
    local.wait()
    for copy in copies:
        copy.wait_recv()

    queries = [every[:, piece, :] for piece in range(pieces)]
    passages = [every[:, pieces + piece, :] for piece in range(pieces)]
    positive = every[:, 2 * pieces, :][:, :1]
    logits = None
    for left, right in zip(queries, passages):
        value = lax.dot_general(
            left, right, (((1,), (1,)), ((), ())), precision=PRECISE, preferred_element_type=F32
        )
        logits = value if logits is None else logits + value
    logits = logits / SOFTMAX_TEMPER
    place = lax.broadcasted_iota(jnp.int32, logits.shape, 1)
    target = (place.astype(F32) == positive).astype(F32)
    top = jnp.max(logits, axis=1, keepdims=True)
    weight = jnp.exp(logits - top)
    row_total = jnp.sum(weight, axis=1, keepdims=True)
    log_total = top + jnp.log(row_total)
    loss = jnp.sum(log_total - jnp.sum(logits * target, axis=1, keepdims=True), axis=0, keepdims=True) / total
    grad_logits = (weight / row_total - target) / (total * SOFTMAX_TEMPER)
    line = lax.broadcasted_iota(jnp.int32, logits.shape, 0)
    grad_column = jnp.sum(jnp.where(place == me, grad_logits, 0.0), axis=1, keepdims=True)
    mine_row = lax.broadcasted_iota(jnp.int32, (total, LANES), 0) == me
    grad_q, grad_p = [], []
    for left, right in zip(queries, passages):
        value = jnp.dot(grad_logits, right, precision=PRECISE, preferred_element_type=F32)
        grad_q.append(jnp.sum(jnp.where(mine_row, value, 0.0), axis=0, keepdims=True))
        grad_p.append(jnp.sum(grad_column * left, axis=0, keepdims=True))
    grad_gain, grad_shift, grad_bias = None, None, None
    for index, (start, slots) in enumerate(spans):
        length = lens_ref[index]
        grad_embed = jnp.concatenate(grad_q if index == 0 else grad_p, axis=1)
        embed = embeds[index]
        grad_pooled = shrinks[index] * (grad_embed - embed * jnp.sum(grad_embed * embed, axis=1, keepdims=True))
        grad_gain = grad_pooled * means[index] + (0.0 if index == 0 else grad_gain)
        grad_shift = grad_pooled + (0.0 if index == 0 else grad_shift)
        spread = grad_pooled * gain / length.astype(F32)
        centered = spread - jnp.mean(spread, axis=1, keepdims=True)
        step = min(slots, 128)
        for at in range(0, slots, step):
            block = pl.ds(start + at, step)
            normed = unit[block, :]
            valid = (lax.broadcasted_iota(jnp.int32, (step, 1), 0) + at) < length
            scale = jnp.where(valid, inverses[index][at // step], 0.0)
            value = scale * (centered - normed * jnp.mean(spread * normed, axis=1, keepdims=True))
            grad_ref[block, :] = value
            low_ref[block, :] = value.astype(BF16)
            piece = jnp.sum(value, axis=0, keepdims=True)
            grad_bias = piece if grad_bias is None else grad_bias + piece
    small_ref[pl.ds(0, 1), :] = grad_bias
    small_ref[pl.ds(1, 1), :] = grad_gain
    small_ref[pl.ds(2, 1), :] = grad_shift
    small_ref[pl.ds(3, 1), :] = jnp.broadcast_to(loss, (1, model))
    small_ref[pl.ds(4, 4), :] = jnp.zeros((4, model), F32)
    for copy in copies:
        copy.wait_send()


def loss_and_gradient(z_two, lens, target, norm_params, spans, total):
    slots, model = z_two.shape
    norms = jnp.concatenate([norm_params, jnp.zeros((2, model), F32)], axis=0)
    vmem = pl.BlockSpec(memory_space=pltpu.VMEM)
    dma = pltpu.SemaphoreType.DMA
    return pl.pallas_call(
        functools.partial(loss_kernel, spans, total),
        out_shape=(
            jax.ShapeDtypeStruct((slots, model), F32),
            jax.ShapeDtypeStruct((slots, model), BF16),
            jax.ShapeDtypeStruct((8, model), F32),
        ),
        in_specs=[pl.BlockSpec(memory_space=pltpu.SMEM), vmem, vmem, vmem],
        out_specs=(vmem,) * 3,
        scratch_shapes=[
            pltpu.VMEM((slots, model), F32),
            pltpu.VMEM((SLAB, LANES), F32),
            pltpu.VMEM((total, SLAB, LANES), F32),
            dma(()), dma((total,)), dma((total,)),
        ],
        compiler_params=pltpu.CompilerParams(collective_id=1, has_side_effects=True, vmem_limit_bytes=40 * MIB),
        name="loss",
    )(lens, z_two, norms, target)


def normalize_back(unit, inverse, grad_unit):
    return inverse * (
        grad_unit
        - jnp.mean(grad_unit, axis=-1, keepdims=True)
        - unit * jnp.mean(grad_unit * unit, axis=-1, keepdims=True)
    )


def backward_kernel(
    spans,
    lens_ref, attn_ref, ffn_ref, proj_ref, mixed_ref, unit_ref, inverse_ref, low_ref, active_ref, slope_ref,
    tokens_ref, grad_ref, grad_low_ref, norm_ref, small_ref,
    attn_out, ffn_out, small_out, query_out, passage_out,
    weight, proj, mixed, inverse, low, active, slope, tokens, total, down, grad_out, grad_proj,
    temp, far_send, far_recv, kept, one_send, one_recv, two_send, two_recv, z_send, z_recv, result, vector, vec_send, vec_recv,
    load_sem, slope_sem, c_send, c_recv, s1_send, s1_recv, s2_send, s2_recv, s3_send, s3_recv,
    v_send, v_recv, t_send, t_recv, credit, out_sem,
):
    me = lax.axis_index("dp")
    core = lax.axis_index("mp")
    x, y, z = lax.rem(me, 2), lax.rem(me // 2, 2), me // 4
    width = attn_ref.shape[3]
    model = attn_ref.shape[2]
    rows = model // 16
    slots = tokens.shape[0]

    def index_of(zz, yy, xx):
        return (zz * 2 + yy) * 2 + xx

    z_peer = [None] + [(index_of(lax.rem(z + k, 4), y, x), core) for k in range(1, 4)]
    x_peer = (index_of(z, y, 1 - x), core)
    y_peer = (index_of(z, 1 - y, x), core)
    c_peer = (me, 1 - core)
    near_peer = (index_of(z + 1 - 2 * lax.rem(z, 2), y, x), core)
    over_peer = (index_of(lax.rem(z + 2, 4), y, x), core)

    barrier = pltpu.get_barrier_semaphore()
    for peer in [*z_peer[1:], x_peer, y_peer, c_peer]:
        pl.semaphore_signal(barrier, inc=1, device_id=peer, device_id_type=MESH)

    sends = {}
    stores = []
    loads = {}

    def load(name, pairs):
        copies = []
        for source, target in pairs:
            copy = pltpu.make_async_copy(source, target, load_sem.at[sum(len(v) for v in loads.values()) + len(copies)])
            copy.start()
            copies.append(copy)
        loads[name] = copies

    def ready(name):
        for copy in loads[name]:
            copy.wait()

    def store(source, target):
        copy = pltpu.make_async_copy(source, target, out_sem.at[len(stores)])
        copy.start()
        stores.append(copy)

    def push(name, source, target, send, recv, peer):
        copy = pltpu.make_async_remote_copy(
            src_ref=source, dst_ref=target, send_sem=send, recv_sem=recv, device_id=peer, device_id_type=MESH
        )
        copy.start()
        sends[name] = copy

    def landed(target, send, recv, peer):
        pltpu.make_async_remote_copy(
            src_ref=target, dst_ref=target, send_sem=send, recv_sem=recv, device_id=peer, device_id_type=MESH
        ).wait_recv()

    def ffn_tiles(half, which):
        return [(ffn_ref.at[half, which, :, pl.ds(t * width, width)], None) for t in range(4)]

    def load_ffn(name, half, which, slot):
        load(name, [(src, weight.at[slot, t]) for t, (src, _) in enumerate(ffn_tiles(half, which))])

    def slope_tile(index):
        half, t = 1 - index // 4, index % 4
        return pltpu.make_async_copy(
            slope_ref.at[half, :, pl.ds(t * width, width)], slope.at[index % 2], slope_sem.at[index]
        )

    load("down", [(grad_low_ref, down)])
    load("active1", [(active_ref.at[1], active.at[1])])
    load_ffn("down1", 1, 1, 0)
    slope_tile(0).start()
    slope_tile(1).start()
    load("active0", [(active_ref.at[0], active.at[0])])
    load_ffn("down0", 0, 1, 1)
    load("low", [(low_ref, low)])
    load_ffn("up1", 1, 0, 2)
    load("total", [(grad_ref, total)])
    load("inverse", [(inverse_ref, inverse)])
    load("proj", [(proj_ref, proj), (mixed_ref, mixed), (tokens_ref, tokens)])
    pl.semaphore_wait(barrier, 6)

    def far_slot(q):
        return q % 2

    def send_far(q, t, value):
        if q == 2:
            sends[("c", 0, t)].wait_send()
        far_send[far_slot(q), t] = value.astype(BF16)
        push(
            ("c", q, t), far_send.at[far_slot(q), t], far_recv.at[far_slot(q), t], c_send.at[q, t], c_recv.at[q, t], c_peer
        )

    def side(t):
        steps = ((x, x_peer), (y, y_peer))
        return steps if t < 2 else steps[::-1]

    def block(index, count=1):
        return pl.ds(pl.multiple_of(index * rows, rows), count * rows)

    def first_step(q, t, lanes):
        landed(far_recv.at[far_slot(q), t], c_send.at[q, t], c_recv.at[q, t], c_peer)
        (bit, peer), _ = side(t)
        for layer in range(4):
            for other in range(2):
                if t < 2:
                    mine, theirs = index_of(layer, other, bit), index_of(layer, other, 1 - bit)
                else:
                    mine, theirs = index_of(layer, bit, other), index_of(layer, 1 - bit, other)
                at = layer * 2 + other
                far = far_recv[far_slot(q), t, block(theirs), :].astype(F32)
                one_send[q, t, pl.ds(at * rows, rows), :] = (temp[block(theirs), lanes] + far).astype(BF16)
                far = far_recv[far_slot(q), t, block(mine), :].astype(F32)
                kept[q, t, pl.ds(at * rows, rows), :] = temp[block(mine), lanes] + far
        push(("1", q, t), one_send.at[q, t], one_recv.at[q, t], s1_send.at[q, t], s1_recv.at[q, t], peer)

    def second_step(q, t):
        (_, before), (bit, peer) = side(t)
        landed(one_recv.at[q, t], s1_send.at[q, t], s1_recv.at[q, t], before)
        for layer in range(4):
            theirs = block(layer * 2 + 1 - bit)
            value = kept[q, t, theirs, :] + one_recv[q, t, theirs, :].astype(F32)
            two_send[q, t, pl.ds(layer * rows, rows), :] = value.astype(BF16)
            mine = block(layer * 2 + bit)
            kept[q, t, mine, :] = kept[q, t, mine, :] + one_recv[q, t, mine, :].astype(F32)
        push(("2", q, t), two_send.at[q, t], two_recv.at[q, t], s2_send.at[q, t], s2_recv.at[q, t], peer)

    def third_step(q, t):
        _, (bit, before) = side(t)
        landed(two_recv.at[q, t], s2_send.at[q, t], s2_recv.at[q, t], before)
        for k in range(1, 4):
            layer = lax.rem(z + k, 4)
            value = kept[q, t, block(layer * 2 + bit), :] + two_recv[q, t, block(layer), :].astype(F32)
            z_send[q, t, k - 1] = value.astype(BF16)
            push(
                ("3", q, t, k), z_send.at[q, t, k - 1], z_recv.at[q, t, k - 1], s3_send.at[q, t, k], s3_recv.at[q, t, k],
                z_peer[k],
            )
        result[q, t] = kept[q, t, block(z * 2 + bit), :] + two_recv[q, t, block(z), :].astype(F32)

    def last_step(q, t):
        for k in range(1, 4):
            landed(z_recv.at[q, t, k - 1], s3_send.at[q, t, k], s3_recv.at[q, t, k], z_peer[k])
        value = result[q, t]
        for k in range(3):
            value = value + z_recv[q, t, k].astype(F32)
        result[q, t] = value
        if q == 2:
            store(result.at[q, t], attn_out.at[t])
        else:
            store(result.at[q, t], ffn_out.at[1 - q, :, pl.ds(t * width, width)])

    tile_lanes = (pl.ds(0, width), pl.ds(width, width))
    pair_lanes = (pl.ds(0, 2 * width), pl.ds(2 * width, 2 * width))

    def far_product(q, left, right):
        for pair in range(2):
            value = mm_tn(left[...], right[:, pair_lanes[pair]])
            send_far(q, 2 * pair, value[:, :width])
            send_far(q, 2 * pair + 1, value[:, width:])

    def own_product(q, left, right):
        for pair in range(2):
            temp[...] = mm_tn(left[...], right[:, pair_lanes[pair]])
            first_step(q, 2 * pair, tile_lanes[0])
            first_step(q, 2 * pair + 1, tile_lanes[1])

    def hidden_grad(half, slot):
        for t in range(4):
            index = (1 - half) * 4 + t
            slope_tile(index).wait()
            lanes = pl.ds(t * width, width)
            value = (mm(down[...], weight[slot, t]) * slope[index % 2]).astype(BF16)
            active[half, :, lanes] = value
            vec = vector if half == 0 else vec_send.at[0]
            vec[pl.ds(9 + t // 2, 1), pl.ds((t % 2) * width, width)] = jnp.sum(
                value.astype(F32), axis=0, keepdims=True
            )
            if index + 2 < 8:
                slope_tile(index + 2).start()

    def add_back(source, slot, count):
        @pl.loop(0, slots // ROW_BLOCK)
        def _(index):
            at = pl.ds(pl.multiple_of(index * ROW_BLOCK, ROW_BLOCK), ROW_BLOCK)
            value = total[at, :]
            for t in range(count):
                value = value + mm_nt(source[at, pl.ds(t * width, width)], weight[slot, t])
            total[at, :] = value

    def first_norm_back():
        sums = [None, None, None]
        for start in range(0, slots, ROW_BLOCK):
            at = pl.ds(start, ROW_BLOCK)
            grad = total[at, :]
            normed = jnp.concatenate([slope[0, at, :], slope[1, at, :]], axis=1)
            back = normalize_back(normed, inverse[at, pl.ds(0, 1)], grad * norm_ref[pl.ds(1, 1), :])
            for index, value in enumerate((back, grad * normed, grad)):
                value = jnp.sum(value, axis=0, keepdims=True)
                sums[index] = value if sums[index] is None else sums[index] + value
            total[at, :] = back
            down[at, :] = back.astype(BF16)
        for index in range(3):
            vector[pl.ds(index, 1), :] = sums[index]
            vec_send[0, pl.ds(index, 1), :] = sums[index]

    def out_grad(slot):
        grad_out[...] = mm(down[...], weight[slot, 3]).astype(BF16)

    def heads_back(half, pair):
        lanes = pl.ds(pair * LANES, LANES)
        scale = HD**-0.5
        for index, (start, count) in enumerate(spans):
            length = lens_ref[index]
            keys = proj[half, 1, pl.ds(start, count), lanes]
            values = proj[half, 2, pl.ds(start, count), lanes]
            lane = first_head(keys.shape)
            scaled = keys * jnp.asarray(scale, BF16)
            zero = jnp.zeros_like(scaled)
            head_keys = (jnp.where(lane, scaled, zero), jnp.where(lane, zero, scaled))
            head_values = (jnp.where(lane, values, zero), jnp.where(lane, zero, values))
            piece = min(count, 256)
            grad_k = [None, None]
            grad_v = [None, None]
            for at in range(0, count, piece):
                queries = proj[half, 0, pl.ds(start + at, piece), lanes]
                grads = grad_out[pl.ds(start + at, piece), lanes]
                grad_q = []
                for head in range(2):
                    scores = mm_nt(head_keys[head], queries)
                    valid = lax.broadcasted_iota(jnp.int32, scores.shape, 0) < length
                    scores = jnp.where(valid, scores, NEG_FILL)
                    top = jnp.max(scores, axis=0, keepdims=True)
                    weights = jnp.exp(scores - top)
                    row_total = jnp.sum(weights, axis=0, keepdims=True)
                    probs = weights * (1.0 / row_total)
                    grad_probs = mm_nt(head_values[head], grads)
                    inner = jnp.sum(probs * grad_probs, axis=0, keepdims=True)
                    grad_scores = (probs * (grad_probs - inner)).astype(BF16)
                    part_v = mm(probs.astype(BF16), grads)
                    part_k = mm(grad_scores, queries)
                    grad_v[head] = part_v if at == 0 else grad_v[head] + part_v
                    grad_k[head] = part_k if at == 0 else grad_k[head] + part_k
                    grad_q.append(mm_tn(grad_scores, keys))
                grad_proj[half, pl.ds(start + at, piece), pl.ds(pair * LANES, LANES)] = (
                    jnp.where(first_head(grad_q[0].shape), grad_q[0], grad_q[1]) * scale
                ).astype(BF16)
            place = pl.ds(start, count)
            grad_proj[half, place, pl.ds(width + pair * LANES, LANES)] = (
                jnp.where(lane, grad_k[0], grad_k[1]) * scale
            ).astype(BF16)
            grad_proj[half, place, pl.ds(2 * width + pair * LANES, LANES)] = jnp.where(
                lane, grad_v[0], grad_v[1]
            ).astype(BF16)

    def attn_biases(half):
        vec = vector if half == 0 else vec_send.at[0]
        for at in (0, 1):
            value = grad_proj[half, :, pl.ds(2 * at * width, width)].astype(F32)
            vec[pl.ds(8, 1), pl.ds(at * width, width)] = jnp.sum(value, axis=0, keepdims=True)

    def vector_step(step, peer):
        if step:
            vec_send[step] = vector[...]
        push(("v", step), vec_send.at[step], vec_recv.at[step], v_send.at[step], v_recv.at[step], peer)

    def vector_sum(step, peer):
        landed(vec_recv.at[step], v_send.at[step], v_recv.at[step], peer)
        vector[...] = vector[...] + vec_recv[step]

    for target in (vector, vec_send.at[0]):
        target[pl.ds(3, 3), :] = small_ref[pl.ds(0, 3), :]
        target[pl.ds(6, 2), :] = jnp.zeros((2, model), F32)
        target[pl.ds(11, 5), :] = jnp.zeros((5, model), F32)

    ready("down")
    ready("active1")
    far_product(0, down, active.at[1])
    ready("down1")
    hidden_grad(1, 0)
    load_ffn("up0", 0, 0, 0)
    ready("active0")
    own_product(0, down, active.at[0])
    pl.semaphore_signal(credit, inc=1, device_id=c_peer, device_id_type=MESH)
    ready("low")
    far_product(1, low, active.at[1])
    ready("down0")
    hidden_grad(0, 1)
    load("unit", [(unit_ref.at[:, pl.ds(t * width, width)], slope.at[t]) for t in range(2)])
    load("attn1", [(attn_ref.at[1], weight.at[1])])
    ready("total")
    ready("up1")
    add_back(active.at[1], 2, 4)
    load("attn0", [(attn_ref.at[0], weight.at[2])])
    own_product(1, low, active.at[0])
    ready("up0")
    add_back(active.at[0], 0, 4)
    second_step(0, 0)
    second_step(0, 1)
    ready("inverse")
    ready("unit")
    first_norm_back()
    second_step(0, 2)
    second_step(0, 3)
    ready("attn1")
    ready("proj")
    out_grad(1)
    heads_back(1, 0)
    third_step(0, 0)
    third_step(0, 1)
    heads_back(1, 1)
    third_step(0, 2)
    third_step(0, 3)
    second_step(1, 0)
    second_step(1, 1)
    heads_back(1, 2)
    attn_biases(1)
    vector_step(0, c_peer)
    second_step(1, 2)
    second_step(1, 3)
    pl.semaphore_wait(credit, 1)
    value = mm_tn(tokens[...], grad_proj[1, :, pair_lanes[0]])
    send_far(2, 0, value[:, :width])
    send_far(2, 1, value[:, width:])
    send_far(2, 2, mm_tn(tokens[...], grad_proj[1, :, pl.ds(2 * width, width)]))
    send_far(2, 3, mm_tn(down[...], mixed[1]))
    ready("attn0")
    out_grad(2)
    heads_back(0, 0)
    for t in range(4):
        last_step(0, t)
    third_step(1, 0)
    third_step(1, 1)
    heads_back(0, 1)
    third_step(1, 2)
    third_step(1, 3)
    heads_back(0, 2)
    attn_biases(0)
    vector_sum(0, c_peer)
    vector_step(1, x_peer)
    temp[...] = mm_tn(tokens[...], grad_proj[0, :, pair_lanes[0]])
    first_step(2, 0, tile_lanes[0])
    first_step(2, 1, tile_lanes[1])
    temp[:, tile_lanes[0]] = mm_tn(tokens[...], grad_proj[0, :, pl.ds(2 * width, width)])
    first_step(2, 2, tile_lanes[0])
    temp[:, tile_lanes[1]] = mm_tn(down[...], mixed[0])
    first_step(2, 3, tile_lanes[1])
    vector_sum(1, x_peer)
    vector_step(2, y_peer)
    add_back(grad_proj.at[1], 1, 3)
    add_back(grad_proj.at[0], 2, 3)
    for source, target, at in ((0, query_out, 0), (spans[1][0], passage_out, 1)):
        part = total.at[pl.ds(source, spans[at][1]), :]
        store(part, target.at[core])
        push(("t", at), part, target.at[core], t_send.at[at], t_recv.at[at], c_peer)
    vector_sum(2, y_peer)
    vector_step(3, near_peer)
    for t in range(4):
        last_step(1, t)
    vector_sum(3, near_peer)
    vector_step(4, over_peer)
    for t in (0, 2, 1, 3):
        second_step(2, t)
    vector_sum(4, over_peer)
    store(vector, small_out)
    for t in (0, 2, 1, 3):
        third_step(2, t)
    for t in (0, 2, 1, 3):
        last_step(2, t)
    for source, target, at in ((0, query_out, 0), (spans[1][0], passage_out, 1)):
        landed(target.at[1 - core], t_send.at[at], t_recv.at[at], c_peer)
    for copy in stores:
        copy.wait()
    for name, copy in sends.items():
        if name[:2] != ("c", 0):
            copy.wait_send()


def backward(tokens, lens, kept, grad_ztwo, grad_low, norm_params, small, spans):
    attn_w, ffn_w, proj, mixed, unit, inverse, low, active, slope = kept
    slots, model = tokens.shape
    width = attn_w.shape[3]
    rows = model // 16
    norms = jnp.concatenate([norm_params, jnp.zeros((2, model), F32)], axis=0)
    anywhere = pl.BlockSpec(memory_space=pltpu.HBM)
    vmem = pl.BlockSpec(memory_space=pltpu.VMEM)
    dma = pltpu.SemaphoreType.DMA
    tile = (model, width)
    scratch = [
        pltpu.VMEM((3, 4) + tile, BF16),
        pltpu.VMEM(proj.shape, BF16),
        pltpu.VMEM(mixed.shape, BF16),
        pltpu.VMEM(inverse.shape, F32),
        pltpu.VMEM(low.shape, BF16),
        pltpu.VMEM(active.shape, BF16),
        pltpu.VMEM((2, slots, width), F32),
        pltpu.VMEM(tokens.shape, BF16),
        pltpu.VMEM((slots, model), F32),
        pltpu.VMEM((slots, model), BF16),
        pltpu.VMEM((slots, width), BF16),
        pltpu.VMEM((2, slots, 3 * width), BF16),
        pltpu.VMEM((model, 2 * width), F32),
        pltpu.VMEM((2, 4) + tile, BF16),
        pltpu.VMEM((2, 4) + tile, BF16),
        pltpu.VMEM((3, 4, 8 * rows, width), F32),
        pltpu.VMEM((3, 4, 8 * rows, width), BF16),
        pltpu.VMEM((3, 4, 8 * rows, width), BF16),
        pltpu.VMEM((3, 4, 4 * rows, width), BF16),
        pltpu.VMEM((3, 4, 4 * rows, width), BF16),
        pltpu.VMEM((3, 4, 3, rows, width), BF16),
        pltpu.VMEM((3, 4, 3, rows, width), BF16),
        pltpu.VMEM((3, 4, rows, width), F32),
        pltpu.VMEM((16, model), F32),
        pltpu.VMEM((5, 16, model), F32),
        pltpu.VMEM((5, 16, model), F32),
        dma((32,)), dma((8,)),
        dma((3, 4)), dma((3, 4)), dma((3, 4)), dma((3, 4)), dma((3, 4)), dma((3, 4)),
        dma((3, 4, 4)), dma((3, 4, 4)),
        dma((5,)), dma((5,)), dma((2,)), dma((2,)),
        pltpu.SemaphoreType.REGULAR,
        dma((20,)),
    ]
    return pl.pallas_call(
        functools.partial(backward_kernel, spans),
        out_shape=(
            jax.ShapeDtypeStruct((4, rows, width), F32),
            jax.ShapeDtypeStruct((2, rows, 4 * width), F32),
            jax.ShapeDtypeStruct((16, model), F32),
            jax.ShapeDtypeStruct((2, spans[0][1], model), F32),
            jax.ShapeDtypeStruct((2, spans[1][1], model), F32),
        ),
        in_specs=[pl.BlockSpec(memory_space=pltpu.SMEM)] + [anywhere] * 12 + [vmem, vmem],
        out_specs=(anywhere,) * 5,
        scratch_shapes=scratch,
        compiler_params=pltpu.CompilerParams(collective_id=2, has_side_effects=True, vmem_limit_bytes=60 * MIB),
        name="backward",
    )(lens, attn_w, ffn_w, proj, mixed, unit, inverse, low, active, slope, tokens, grad_ztwo, grad_low, norms, small)


def attend_kernel(spans, lens_ref, q_ref, k_ref, v_ref, o_ref):
    for index, (start, slots) in enumerate(spans):
        length = lens_ref[index]
        keys = k_ref[0, pl.ds(start, slots), :]
        values = v_ref[0, pl.ds(start, slots), :]
        lane = first_head(keys.shape)
        scaled = keys * jnp.asarray(HD**-0.5, BF16)
        zero = jnp.zeros_like(scaled)
        head_keys = (jnp.where(lane, scaled, zero), jnp.where(lane, zero, scaled))
        block = min(slots, 256)
        for at in range(0, slots, block):
            queries = q_ref[0, pl.ds(start + at, block), :]
            outs = []
            for head in range(2):
                scores = mm_nt(queries, head_keys[head])
                valid = lax.broadcasted_iota(jnp.int32, scores.shape, 1) < length
                scores = jnp.where(valid, scores, NEG_FILL)
                top = jnp.max(scores, axis=1, keepdims=True)
                weight = jnp.exp(scores - top)
                total = jnp.sum(weight, axis=1, keepdims=True)
                probs = (weight * (1.0 / total)).astype(BF16)
                outs.append(mm(probs, values))
            o_ref[pl.ds(start + at, block), :] = jnp.where(
                first_head(outs[0].shape), outs[0], outs[1]
            ).astype(BF16)


def attend_back_kernel(spans, lens_ref, q_ref, k_ref, v_ref, g_ref, d_ref):
    scale = HD**-0.5
    for index, (start, slots) in enumerate(spans):
        length = lens_ref[index]
        keys = k_ref[0, pl.ds(start, slots), :]
        values = v_ref[0, pl.ds(start, slots), :]
        lane = first_head(keys.shape)
        scaled = keys * jnp.asarray(scale, BF16)
        zero = jnp.zeros_like(scaled)
        head_keys = (jnp.where(lane, scaled, zero), jnp.where(lane, zero, scaled))
        head_values = (jnp.where(lane, values, zero), jnp.where(lane, zero, values))
        block = min(slots, 256)
        grad_k = [None, None]
        grad_v = [None, None]
        for at in range(0, slots, block):
            queries = q_ref[0, pl.ds(start + at, block), :]
            grads = g_ref[pl.ds(start + at, block), :]
            grad_q = []
            for head in range(2):
                scores = mm_nt(head_keys[head], queries)
                valid = lax.broadcasted_iota(jnp.int32, scores.shape, 0) < length
                scores = jnp.where(valid, scores, NEG_FILL)
                top = jnp.max(scores, axis=0, keepdims=True)
                weight = jnp.exp(scores - top)
                total = jnp.sum(weight, axis=0, keepdims=True)
                probs = weight * (1.0 / total)
                grad_probs = mm_nt(head_values[head], grads)
                inner = jnp.sum(probs * grad_probs, axis=0, keepdims=True)
                grad_scores = (probs * (grad_probs - inner)).astype(BF16)
                part_v = mm(probs.astype(BF16), grads)
                part_k = mm(grad_scores, queries)
                grad_v[head] = part_v if at == 0 else grad_v[head] + part_v
                grad_k[head] = part_k if at == 0 else grad_k[head] + part_k
                grad_q.append(mm_tn(grad_scores, keys))
            d_ref[0, pl.ds(start + at, block), :] = (
                jnp.where(first_head(grad_q[0].shape), grad_q[0], grad_q[1]) * scale
            ).astype(BF16)
        d_ref[1, pl.ds(start, slots), :] = (jnp.where(lane, grad_k[0], grad_k[1]) * scale).astype(BF16)
        d_ref[2, pl.ds(start, slots), :] = jnp.where(lane, grad_v[0], grad_v[1]).astype(BF16)


def head_specs(tokens):
    return [pl.BlockSpec((1, tokens, LANES), functools.partial(lambda s, i, lens: (s, 0, i), s)) for s in range(3)]


def attend(proj, lens, spans):
    _, tokens, width = proj.shape
    flops = sum(4 * slots * slots * width for _, slots in spans)
    return pl.pallas_call(
        functools.partial(attend_kernel, spans),
        out_shape=jax.ShapeDtypeStruct((tokens, width), BF16),
        grid_spec=pltpu.PrefetchScalarGridSpec(
            num_scalar_prefetch=1,
            grid=(width // LANES,),
            in_specs=head_specs(tokens),
            out_specs=pl.BlockSpec((tokens, LANES), lambda i, lens: (0, i)),
        ),
        compiler_params=pltpu.CompilerParams(vmem_limit_bytes=40 * MIB),
        cost_estimate=pl.CostEstimate(flops=8 * flops, bytes_accessed=8 * tokens * width, transcendentals=0),
        name="attend",
    )(lens, proj, proj, proj)


def attend_back(proj, grad_out, lens, spans):
    _, tokens, width = proj.shape
    flops = sum(10 * slots * slots * width for _, slots in spans)
    return pl.pallas_call(
        functools.partial(attend_back_kernel, spans),
        out_shape=jax.ShapeDtypeStruct((3, tokens, width), BF16),
        grid_spec=pltpu.PrefetchScalarGridSpec(
            num_scalar_prefetch=1,
            grid=(width // LANES,),
            in_specs=head_specs(tokens) + [pl.BlockSpec((tokens, LANES), lambda i, lens: (0, i))],
            out_specs=pl.BlockSpec((3, tokens, LANES), lambda i, lens: (0, 0, i)),
        ),
        compiler_params=pltpu.CompilerParams(vmem_limit_bytes=40 * MIB),
        cost_estimate=pl.CostEstimate(flops=8 * flops, bytes_accessed=14 * tokens * width, transcendentals=0),
        name="attend_back",
    )(lens, proj, proj, proj, grad_out)


def up_kernel(x_ref, w_ref, b_ref, g_ref, s_ref):
    hidden = mm(x_ref[...], w_ref[0]) + b_ref[...]
    active, slope = gelu_and_slope(hidden)
    g_ref[...] = active.astype(BF16)
    s_ref[...] = slope


def feed_up(low, ffn_half, bias):
    tokens, width = low.shape
    units = ffn_half.shape[2]
    tile = 256
    return pl.pallas_call(
        up_kernel,
        out_shape=(jax.ShapeDtypeStruct((tokens, units), BF16), jax.ShapeDtypeStruct((tokens, units), F32)),
        grid=(units // tile,),
        in_specs=[
            pl.BlockSpec((tokens, width), lambda i: (0, 0)),
            pl.BlockSpec((1, width, tile), lambda i: (0, 0, i)),
            pl.BlockSpec((1, tile), lambda i: (0, i)),
        ],
        out_specs=(pl.BlockSpec((tokens, tile), lambda i: (0, i)), pl.BlockSpec((tokens, tile), lambda i: (0, i))),
        compiler_params=pltpu.CompilerParams(vmem_limit_bytes=40 * MIB),
        cost_estimate=pl.CostEstimate(
            flops=2 * tokens * width * units, bytes_accessed=8 * tokens * units, transcendentals=tokens * units
        ),
        name="feed_up",
    )(low, ffn_half, bias.reshape(1, -1))


def swap_cores(values):
    return lax.ppermute(values, "mp", [(0, 1), (1, 0)])


def scatter_sum(own_parts, other_parts):
    summed = [own + swap_cores(other).astype(F32) for own, other in zip(own_parts, other_parts)]
    return [lax.psum_scatter(value, "dp", scatter_dimension=1, tiled=True) for value in summed]


def adam_update(master, first, second, average, grad, rate, decay_w, rates, step_count):
    first_new = rates[0] * first + (1.0 - rates[0]) * grad
    second_new = rates[1] * second + (1.0 - rates[1]) * grad * grad
    fixed_one = first_new / (1.0 - rates[0] ** step_count)
    fixed_two = second_new / (1.0 - rates[1] ** step_count)
    master_new = master - rate * (fixed_one / (jnp.sqrt(fixed_two) + ADAM_EPS) + decay_w * master)
    average_new = rates[2] * average + (1.0 - rates[2]) * master_new
    return (master_new, first_new, second_new, average_new)


def forward_plain(tokens, lens, attn_low, ffn_low, col_bias, norm_params, spans):
    attn_full = lax.all_gather(attn_low, "dp", axis=1, tiled=True)
    ffn_full = lax.all_gather(ffn_low, "dp", axis=1, tiled=True)
    attn_w = (attn_full, swap_cores(attn_full))
    ffn_w = (ffn_full, swap_cores(ffn_full))
    col = (col_bias, swap_cores(col_bias))
    width = attn_w[0].shape[2]

    projected, mixed = [], []
    branch = None
    for half in range(2):
        bias = jnp.stack([col[half][:width], jnp.zeros((width,), F32), col[half][width : 2 * width]])
        proj = (
            jnp.einsum("td,sde->ste", tokens, attn_w[half][:3], preferred_element_type=F32) + bias[:, None, :]
        ).astype(BF16)
        out = attend(proj, lens, spans)
        part = mm_nt(out, attn_w[half][3])
        branch = part if branch is None else branch + part
        projected.append(proj)
        mixed.append(out)
    z_one = tokens.astype(F32) + branch + norm_params[0]
    unit_one, inverse_one = normalize(z_one)
    first_norm = unit_one * norm_params[1] + norm_params[2]
    first_low = first_norm.astype(BF16)
    active, slope = [], []
    branch_two = None
    for half in range(2):
        act, slo = feed_up(first_low, ffn_w[half], col[half][2 * width :])
        part = mm_nt(act, ffn_w[half][1])
        branch_two = part if branch_two is None else branch_two + part
        active.append(act)
        slope.append(slo)
    z_two = first_norm + branch_two + norm_params[3]
    return attn_w, ffn_w, projected, mixed, unit_one, inverse_one, first_low, active, slope, z_two


def loss_plain(z_two, lens, target_mine, norm_params, spans, pairs):
    query_slots, passage_slots = spans[0][1], spans[1][1]
    model_width = z_two.shape[1]
    core = lax.axis_index("mp")
    unit_two, inverse_two = normalize(z_two)
    places = jnp.arange(query_slots + passage_slots)
    in_query = (places < query_slots) & (places < lens[0])
    in_passage = (places >= query_slots) & (places - query_slots < lens[1])
    share = (
        jnp.stack([in_query, in_passage]).astype(F32) / lens.astype(F32)[:, None]
    )
    mean_unit = jnp.dot(share, unit_two, precision=PRECISE, preferred_element_type=F32)
    pooled = mean_unit * norm_params[4] + norm_params[5]
    shrink = lax.rsqrt(jnp.sum(pooled * pooled, axis=1, keepdims=True) + POOL_EPS)
    embed = pooled * shrink

    payload = jnp.concatenate([embed.reshape(-1), target_mine])
    every = lax.all_gather(payload, ("dp", "mp"), axis=0)
    every_q = every[:, :model_width]
    every_p = every[:, model_width : 2 * model_width]
    target = (jnp.arange(pairs)[None, :].astype(F32) == every[:, 2 * model_width :][:, :1]).astype(F32)
    logits = lax.dot_general(every_q, every_p, (((1,), (1,)), ((), ())), precision=PRECISE) / SOFTMAX_TEMPER
    row_top = jnp.max(logits, axis=1, keepdims=True)
    exp_logits = jnp.exp(logits - row_top)
    row_total = jnp.sum(exp_logits, axis=1, keepdims=True)
    log_total = row_top[:, 0] + jnp.log(row_total[:, 0])
    loss_value = (jnp.sum(log_total - jnp.sum(logits * target, axis=1)) / pairs).reshape(1)
    grad_logits = (exp_logits / row_total - target) / (pairs * SOFTMAX_TEMPER)
    rank = lax.axis_index("dp") * lax.axis_size("mp") + core
    grad_uq = jnp.dot(lax.dynamic_index_in_dim(grad_logits, rank, 0, keepdims=True), every_p, precision=PRECISE)
    grad_up = jnp.dot(
        lax.dynamic_index_in_dim(grad_logits, rank, 1, keepdims=False)[None], every_q, precision=PRECISE
    )
    grad_embed = jnp.concatenate([grad_uq, grad_up], axis=0)

    grad_pooled = shrink * (grad_embed - embed * jnp.sum(grad_embed * embed, axis=1, keepdims=True))
    grad_gain_two = jnp.sum(grad_pooled * mean_unit, axis=0)
    grad_shift_two = jnp.sum(grad_pooled, axis=0)
    grad_unit_two = lax.dot_general(
        share, grad_pooled * norm_params[4], (((0,), (0,)), ((), ())), precision=PRECISE
    )
    grad_ztwo = normalize_back(unit_two, inverse_two, grad_unit_two)
    grad_bias_two = jnp.sum(grad_ztwo, axis=0)
    grad_two_low = grad_ztwo.astype(BF16)
    return grad_ztwo, grad_two_low, loss_value, grad_bias_two, grad_gain_two, grad_shift_two


def backward_plain(tokens, lens, kept, grad_ztwo, grad_two_low, norm_params, second_grads, spans):
    attn_w, ffn_w, projected, mixed, unit_one, inverse_one, first_low, active, slope = kept
    grad_bias_two, grad_gain_two, grad_shift_two = second_grads
    query_slots = spans[0][1]
    core = lax.axis_index("mp")
    cut = ffn_w[0].shape[2] // 2
    width = attn_w[0].shape[2]

    def two_parts(values):
        return values[:, :cut], values[:, cut:]

    def parted_product(left, halves):
        own = [mm_tn(left, part)[None] for part in two_parts(halves[0])]
        other = [mm_tn(left, part).astype(BF16)[None] for part in two_parts(halves[1])]
        return own, other

    down_grad = scatter_sum(*parted_product(grad_two_low, active))
    grad_hidden, grad_first = [], grad_ztwo
    for half in (1, 0):
        grad_hid = (mm(grad_two_low, ffn_w[half][1]) * slope[half]).astype(BF16)
        grad_hidden.insert(0, grad_hid)
        grad_first = grad_first + mm_nt(grad_hid, ffn_w[half][0])
    grad_hidden_bias = [jnp.sum(value.astype(F32), axis=0) for value in grad_hidden]
    up_grad = scatter_sum(*parted_product(first_low, grad_hidden))

    grad_gain_one = jnp.sum(grad_first * unit_one, axis=0)
    grad_shift_one = jnp.sum(grad_first, axis=0)
    grad_zone = normalize_back(unit_one, inverse_one, grad_first * norm_params[1])
    grad_bias_out = jnp.sum(grad_zone, axis=0)
    grad_one_low = grad_zone.astype(BF16)
    grad_tokens = grad_zone
    grad_query_bias, grad_value_bias, attn_parts = [None, None], [None, None], [None, None]
    for half in (1, 0):
        grad_out = mm(grad_one_low, attn_w[half][3]).astype(BF16)
        grad_proj = attend_back(projected[half], grad_out, lens, spans)
        grad_query_bias[half] = jnp.sum(grad_proj[0].astype(F32), axis=0)
        grad_value_bias[half] = jnp.sum(grad_proj[2].astype(F32), axis=0)
        in_grads = jnp.einsum("td,ste->sde", tokens, grad_proj, preferred_element_type=F32)
        out_grad = mm_tn(grad_one_low, mixed[half])
        parts = [in_grads[:2], jnp.stack([in_grads[2], out_grad])]
        attn_parts[half] = parts if half == 0 else [part.astype(BF16) for part in parts]
        for index in range(3):
            grad_tokens = grad_tokens + mm_nt(grad_proj[index], attn_w[half][index])
    attn_grads = scatter_sum(*attn_parts)

    col_parts = [
        jnp.concatenate([grad_query_bias[half], grad_value_bias[half], grad_hidden_bias[half]]) for half in range(2)
    ]
    norm_part = jnp.stack(
        [grad_bias_out, grad_gain_one, grad_shift_one, grad_bias_two, grad_gain_two, grad_shift_two]
    )
    norm_part = norm_part + swap_cores(norm_part)
    col_part = col_parts[0] + swap_cores(col_parts[1])
    small = lax.psum(jnp.concatenate([norm_part.reshape(-1), col_part]), "dp")
    norm_grad = small[: norm_part.size].reshape(norm_part.shape)
    col_grad = small[norm_part.size :]

    attn_grad = jnp.concatenate(attn_grads, axis=0)
    ffn_grad = jnp.stack([jnp.concatenate(parts, axis=-1)[0] for parts in (up_grad, down_grad)])
    grad_twin = swap_cores(grad_tokens)
    first_pair = jnp.where(core == 0, grad_tokens, grad_twin)
    second_pair = jnp.where(core == 0, grad_twin, grad_tokens)
    query_grad = jnp.stack([first_pair[:query_slots], second_pair[:query_slots]])
    passage_grad = jnp.stack([first_pair[query_slots:], second_pair[query_slots:]])
    return attn_grad, ffn_grad, norm_grad, col_grad, query_grad, passage_grad


def per_device(
    query_in,
    passage_in,
    query_len,
    passage_len,
    positive,
    step,
    rates,
    attn_master,
    attn_first,
    attn_second,
    attn_average,
    ffn_master,
    ffn_first,
    ffn_second,
    ffn_average,
    norm_params,
    norm_first,
    norm_second,
    norm_average,
    col_bias,
    col_first,
    col_second,
    col_average,
):
    core = lax.axis_index("mp")
    size = lax.axis_size("dp")
    query_slots, model_width = query_in.shape[1:]
    passage_slots = passage_in.shape[1]
    pairs = query_in.shape[0] * size
    spans = ((0, query_slots), (query_slots, passage_slots))

    def pick(values, index):
        return lax.dynamic_index_in_dim(values, index, 0, keepdims=False)

    tokens = jnp.concatenate([pick(query_in, core), pick(passage_in, core)], axis=0)
    lens = jnp.stack([pick(query_len, core), pick(passage_len, core)])

    attn_low, ffn_low = attn_master.astype(BF16), ffn_master.astype(BF16)
    target = jnp.broadcast_to(pick(positive, core).astype(F32), (8, LANES))
    if size == 16:
        outs = forward(tokens, lens, attn_low, ffn_low, col_bias, norm_params, spans)
        grad_ztwo, grad_two_low, small = loss_and_gradient(outs[9], lens, target, norm_params, spans, pairs)
        loss_value = small[3, :1]
    else:
        outs = forward_plain(tokens, lens, attn_low, ffn_low, col_bias, norm_params, spans)
        kept, z_two = outs[:9], outs[9]
        outs = loss_plain(z_two, lens, target[0], norm_params, spans, pairs)
        grad_ztwo, grad_two_low, loss_value, grad_bias_two, grad_gain_two, grad_shift_two = outs

    if size == 16:
        attn_grad, ffn_grad, vector, query_grad, passage_grad = backward(
            tokens, lens, outs[:9], grad_ztwo, grad_two_low, norm_params, small, spans
        )
        norm_grad, col_grad = vector[:6], vector[8:11].reshape(-1)
    else:
        attn_grad, ffn_grad, norm_grad, col_grad, query_grad, passage_grad = backward_plain(
            tokens, lens, kept, grad_ztwo, grad_two_low, norm_params,
            (grad_bias_two, grad_gain_two, grad_shift_two), spans,
        )

    step_count = step[0].astype(F32)
    attn_out = adam_update(
        attn_master, attn_first, attn_second, attn_average, attn_grad, rates[3], DECAY_WEIGHT, rates, step_count
    )
    ffn_out = adam_update(
        ffn_master, ffn_first, ffn_second, ffn_average, ffn_grad, rates[3], DECAY_WEIGHT, rates, step_count
    )
    norm_out = adam_update(
        norm_params, norm_first, norm_second, norm_average, norm_grad, rates[4], 0.0, rates, step_count
    )
    col_out = adam_update(col_bias, col_first, col_second, col_average, col_grad, rates[4], 0.0, rates, step_count)

    return (
        loss_value,
        query_grad,
        passage_grad,
        *attn_out,
        *ffn_out,
        *norm_out,
        *col_out,
        attn_out[0].astype(BF16),
        ffn_out[0].astype(BF16),
    )


def solution(mesh):
    matrix = P(None, "dp", "mp")
    rows = P("dp", None, None)
    placed = (rows, rows, P("dp"), P("dp"), P("dp"), P(), P(), *[matrix] * 8, *[P()] * 4, *[P("mp")] * 4)
    return jax.shard_map(
        per_device,
        mesh=mesh,
        in_specs=placed,
        out_specs=(P(), rows, rows, *[matrix] * 8, *[P()] * 4, *[P("mp")] * 4, matrix, matrix),
        check_vma=False,
    )
```

```python
import functools

import jax
import jax.numpy as jnp
from jax import lax
from jax.experimental import pallas as pl
from jax.experimental.pallas import tpu as pltpu
from jax.sharding import PartitionSpec as P

HD = 64
LANES = 128
NEG_FILL = -1e30
SOFTMAX_TEMPER = 0.02
NORM_EPS = 1e-12
POOL_EPS = 1e-06
DECAY_WEIGHT = 0.01
ADAM_EPS = 1e-08
PRECISE = lax.Precision.HIGHEST
MESH = pl.DeviceIdType.MESH
MIB = 2**20
F32 = jnp.float32
BF16 = jnp.bfloat16

ERFC_STEP = 0.46
ERFC_HALF = (
    0.5 * 0.26113873056821263,
    0.5 * 0.23637801512084577,
    0.5 * 0.3601812301921897,
    -0.5 * 0.18740624158431016,
    0.5 * 0.6751549397754679,
    -0.5 * 0.4305350150859377,
    0.5 * 0.0850883282904581,
)
ROOT_HALF = 0.7071067811865476
DENSITY = 0.3989422804014327


def gelu_and_slope(hidden):
    bell = jnp.exp(hidden * hidden * (-0.5))
    step = 1.0 / (1.0 + (ERFC_STEP * ROOT_HALF) * jnp.abs(hidden))
    tail = ERFC_HALF[6]
    for coefficient in ERFC_HALF[5::-1]:
        tail = tail * step + coefficient
    tail = tail * step * bell
    below = jnp.where(hidden >= 0.0, 1.0 - tail, tail)
    return hidden * below, below + hidden * bell * DENSITY


def mm(left, right):
    return jnp.dot(left, right, preferred_element_type=F32)


def mm_nt(left, right):
    return lax.dot_general(left, right, (((1,), (1,)), ((), ())), preferred_element_type=F32)


def mm_tn(left, right):
    return lax.dot_general(left, right, (((0,), (0,)), ((), ())), preferred_element_type=F32)


def first_head(shape):
    return lax.broadcasted_iota(jnp.int32, shape, 1) < HD


def stack_heads(values):
    place = lax.broadcasted_iota(jnp.int32, values.shape, 1) // HD
    zero = jnp.zeros_like(values)
    return jnp.concatenate(
        [jnp.where(place == head, values, zero) for head in range(values.shape[1] // HD)], axis=0
    )


def unstack_heads(values, count):
    place = lax.broadcasted_iota(jnp.int32, (count, values.shape[1]), 1) // HD
    total = None
    for head in range(values.shape[1] // HD):
        piece = jnp.where(place == head, values[head * count : (head + 1) * count], 0.0)
        total = piece if total is None else total + piece
    return total


def split_pair(values):
    lane = first_head(values.shape)
    zero = jnp.zeros_like(values)
    return jnp.where(lane, values, zero), jnp.where(lane, zero, values)


def probabilities(scores, length):
    valid = lax.broadcasted_iota(jnp.int32, scores.shape, 1) < length
    scores = jnp.where(valid, scores, NEG_FILL)
    weight = jnp.exp(scores - jnp.max(scores, axis=1, keepdims=True))
    return weight * (1.0 / jnp.sum(weight, axis=1, keepdims=True))


def normalize(values):
    center = values - jnp.mean(values, axis=-1, keepdims=True)
    spread = jnp.mean(center * center, axis=-1, keepdims=True)
    inverse = lax.rsqrt(spread + NORM_EPS)
    return center * inverse, inverse


def normalize_back(unit, inverse, grad_unit):
    return inverse * (
        grad_unit
        - jnp.mean(grad_unit, axis=-1, keepdims=True)
        - unit * jnp.mean(grad_unit * unit, axis=-1, keepdims=True)
    )


SCALE = HD**-0.5
SLAB = 16


class Mesh:
    def __init__(self):
        self.me = lax.axis_index("dp")
        self.core = lax.axis_index("mp")
        self.x, self.y, self.z = lax.rem(self.me, 2), lax.rem(self.me // 2, 2), self.me // 4
        self.x_peer = (self.index(self.z, self.y, 1 - self.x), self.core)
        self.y_peer = (self.index(self.z, 1 - self.y, self.x), self.core)
        self.c_peer = (self.me, 1 - self.core)
        self.z_peer = [None] + [(self.index(lax.rem(self.z + k, 4), self.y, self.x), self.core) for k in range(1, 4)]
        self.column = [lax.rem(self.z - k + 4, 4) for k in range(4)]

    def index(self, z, y, x):
        return (z * 2 + y) * 2 + x


def remote(source, target, send, recv, peer):
    return pltpu.make_async_remote_copy(
        src_ref=source, dst_ref=target, send_sem=send, recv_sem=recv, device_id=peer, device_id_type=MESH
    )


def forward_kernel(
    spans, total,
    query_len, passage_len, positive, query_ref, passage_ref, attn_ref, ffn_ref, col_ref, norm_ref,
    weight_out, proj_out, mixed_out, unit_out, inverse_out, low_out, active_out, slope_out, tokens_out,
    grad_out, grad_low_out, small_out,
    weight, proj, mixed, unit, inverse, low, active, slope, tokens, z_two, grad_low, small,
    col, attn_in, ffn_in, unit_two, slab, every,
    z_send, z_recv, x_send, x_recv, y_send, y_recv, d_send, d_recv, c_send, c_recv, b_send, b_recv, here_sem, out_sem,
    e_send, e_recv,
):
    at = Mesh()
    me, core = at.me, at.core
    my_rank = me * 2 + core
    rows, width = attn_ref.shape[1:]
    units = ffn_ref.shape[2]
    slots, model = tokens.shape

    def device(step):
        rank = lax.rem(my_rank + step, total)
        return (rank // 2, lax.rem(rank, 2))

    incoming = [
        pltpu.make_async_copy(attn_ref, attn_in, here_sem.at[0]),
        pltpu.make_async_copy(ffn_ref.at[0], ffn_in.at[0], here_sem.at[1]),
        pltpu.make_async_copy(ffn_ref.at[1], ffn_in.at[1], here_sem.at[2]),
        pltpu.make_async_copy(query_ref.at[core], tokens.at[pl.ds(*spans[0]), :], here_sem.at[3]),
        pltpu.make_async_copy(passage_ref.at[core], tokens.at[pl.ds(*spans[1]), :], here_sem.at[4]),
    ]
    for copy in incoming:
        copy.start()
    lens = (query_len[core], passage_len[core])
    barrier = pltpu.get_barrier_semaphore()
    for step in range(1, total):
        pl.semaphore_signal(barrier, inc=1, device_id=device(step), device_id_type=MESH)
    for line in range(col_ref.shape[0]):
        col[0, :, pl.ds(line * LANES, LANES)] = col_ref[pl.ds(line, 1), :]
    pl.semaphore_wait(barrier, total - 1)

    every_lane = pl.ds(0, units)
    half_lanes = (pl.ds(0, units // 2), pl.ds(units // 2, units // 2))

    def block(q, index, lanes=every_lane, count=1, far=0):
        return weight.at[far, q, pl.ds(pl.multiple_of(index * rows, rows), count * rows), lanes]

    sends = []
    stores = []

    def push(ref, send, recv, peer, target=None):
        copy = remote(ref, ref if target is None else target, send, recv, peer)
        copy.start()
        sends.append(copy)

    def landed(ref, send, recv, peer):
        remote(ref, ref, send, recv, peer).wait_recv()

    def store(source, target):
        copy = pltpu.make_async_copy(source, target, out_sem.at[len(stores)])
        copy.start()
        stores.append(copy)

    def cast_own(q):
        incoming[q].wait()
        here = pl.ds(pl.multiple_of(me * rows, rows), rows)
        if q == 0:
            for index in range(4):
                weight[0, 0, here, pl.ds(index * width, width)] = attn_in[index].astype(BF16)
        else:
            weight[0, q, here, :] = ffn_in[q - 1].astype(BF16)

    def own_along_column(q):
        for k in range(1, 4):
            push(block(q, me), z_send.at[q, k], z_recv.at[q, k], at.z_peer[k])

    def own_to_sides(q):
        push(block(q, me), x_send.at[q, 0], x_recv.at[q, 0], at.x_peer)
        push(block(q, me), y_send.at[q, 0], y_recv.at[q, 0], at.y_peer)

    def column_to_sides(q):
        for k in range(1, 4):
            ref = block(q, at.index(at.column[k], at.y, at.x))
            landed(ref, z_send.at[q, k], z_recv.at[q, k], at.z_peer[k])
            push(ref, x_send.at[q, k], x_recv.at[q, k], at.x_peer)
            push(ref, y_send.at[q, k], y_recv.at[q, k], at.y_peer)

    def round_corner(q, ks=range(4)):
        for k in ks:
            beside = at.index(at.column[k], at.y, 1 - at.x)
            landed(block(q, beside), x_send.at[q, k], x_recv.at[q, k], at.x_peer)
            push(block(q, beside, half_lanes[0]), d_send.at[q, k, 0], d_recv.at[q, k, 0], at.y_peer)
            beside = at.index(at.column[k], 1 - at.y, at.x)
            landed(block(q, beside), y_send.at[q, k], y_recv.at[q, k], at.y_peer)
            push(block(q, beside, half_lanes[1]), d_send.at[q, k, 1], d_recv.at[q, k, 1], at.x_peer)

    def to_other_core(q, ks=range(4)):
        for k in ks:
            across = at.index(at.column[k], 1 - at.y, 1 - at.x)
            landed(block(q, across, half_lanes[0]), d_send.at[q, k, 0], d_recv.at[q, k, 0], at.y_peer)
            landed(block(q, across, half_lanes[1]), d_send.at[q, k, 1], d_recv.at[q, k, 1], at.x_peer)
            layer = at.index(at.column[k], 0, 0)
            push(
                block(q, layer, every_lane, 4), c_send.at[q, k], c_recv.at[q, k], at.c_peer,
                block(q, layer, every_lane, 4, 1),
            )

    def from_other_core(q):
        for k in range(4):
            layer = at.index(at.column[k], 0, 0)
            landed(block(q, layer, every_lane, 4, 1), c_send.at[q, k], c_recv.at[q, k], at.c_peer)

    def project(half):
        bias = jnp.concatenate(
            [
                col[half, :, pl.ds(0, width)],
                jnp.zeros((1, width), F32),
                col[half, :, pl.ds(width, width)],
            ],
            axis=1,
        )
        proj[half] = (mm(tokens[...], weight[half, 0, :, pl.ds(0, 3 * width)]) + bias).astype(BF16)

    def query_heads(half):
        place = pl.ds(*spans[0])
        queries = stack_heads(proj[half, place, pl.ds(0, width)] * jnp.asarray(SCALE, BF16))
        probs = probabilities(mm_nt(queries, proj[half, place, pl.ds(width, width)]), lens[0])
        value = mm(probs.astype(BF16), proj[half, place, pl.ds(2 * width, width)])
        mixed[half, place, :] = unstack_heads(value, spans[0][1]).astype(BF16)

    def passage_heads(half, pair):
        place = pl.ds(*spans[1])
        queries = proj[half, place, pl.ds(pair * LANES, LANES)]
        keys = split_pair(proj[half, place, pl.ds(width + pair * LANES, LANES)] * jnp.asarray(SCALE, BF16))
        values = proj[half, place, pl.ds(2 * width + pair * LANES, LANES)]
        scores = [mm_nt(queries, key) for key in keys]
        outs = [mm(probabilities(score, lens[1]).astype(BF16), values) for score in scores]
        mixed[half, place, pl.ds(pair * LANES, LANES)] = jnp.where(first_head(outs[0].shape), *outs).astype(BF16)

    def first_norm():
        step = 192
        for start in range(0, slots, step):
            place = pl.ds(start, step)
            value = tokens[place, :].astype(F32) + norm_ref[pl.ds(0, 1), :]
            for half in range(2):
                value = value + mm_nt(mixed[half, place, :], weight[half, 0, :, pl.ds(3 * width, width)])
            normed, scale = normalize(value)
            unit[place, :] = normed
            inverse[place, :] = jnp.broadcast_to(scale, (step, LANES))
            value = normed * norm_ref[pl.ds(1, 1), :] + norm_ref[pl.ds(2, 1), :]
            z_two[place, :] = value + norm_ref[pl.ds(3, 1), :]
            low[place, :] = value.astype(BF16)

    tile = 256

    def up(half):
        for start in range(0, units, tile):
            lanes = pl.ds(start, tile)
            hidden = mm(low[...], weight[half, 1, :, lanes]) + col[half, :, pl.ds(2 * width + start, tile)]
            value, grad = gelu_and_slope(hidden)
            active[half, :, lanes] = value.astype(BF16)
            slope[half, :, lanes] = grad

    def down(half):
        z_two[...] = z_two[...] + mm_nt(active[half], weight[half, 2])

    cast_own(0)
    own_along_column(0)
    own_to_sides(0)
    push(col.at[0], b_send, b_recv, at.c_peer, col.at[1])
    cast_own(1)
    own_to_sides(1)
    cast_own(2)
    own_to_sides(2)
    incoming[3].wait()
    incoming[4].wait()
    store(tokens, tokens_out)
    column_to_sides(0)
    own_along_column(1)
    round_corner(0)
    to_other_core(0)
    project(0)
    column_to_sides(1)
    own_along_column(2)
    query_heads(0)
    passage_heads(0, 0)
    passage_heads(0, 1)
    passage_heads(0, 2)
    landed(col.at[1], b_send, b_recv, at.c_peer)
    from_other_core(0)
    project(1)
    for half in range(2):
        store(weight.at[half, 0], weight_out.at[half, 0])
    store(proj, proj_out)
    round_corner(1, (0, 1))
    query_heads(1)
    passage_heads(1, 0)
    passage_heads(1, 1)
    round_corner(1, (2, 3))
    passage_heads(1, 2)
    store(mixed, mixed_out)
    column_to_sides(2)
    first_norm()
    store(unit, unit_out)
    store(inverse, inverse_out)
    store(low, low_out)
    to_other_core(1)
    up(0)
    store(slope.at[0], slope_out.at[0])
    store(weight.at[0, 1], weight_out.at[0, 1])
    round_corner(2, (0, 1))
    from_other_core(1)
    up(1)
    store(slope.at[1], slope_out.at[1])
    store(weight.at[1, 1], weight_out.at[1, 1])
    store(active, active_out)
    round_corner(2, (2, 3))
    to_other_core(2)
    store(weight.at[0, 2], weight_out.at[0, 2])
    down(0)
    from_other_core(2)
    store(weight.at[1, 2], weight_out.at[1, 2])
    down(1)

    pieces = model // LANES
    gain, shift = norm_ref[pl.ds(4, 1), :], norm_ref[pl.ds(5, 1), :]
    embeds, shrinks, means, inverses, valids = [], [], [], [], []
    for index, (start, count) in enumerate(spans):
        normed, scale = normalize(z_two[pl.ds(start, count), :])
        unit_two[pl.ds(start, count), :] = normed
        valid = lax.broadcasted_iota(jnp.int32, (count, 1), 0) < lens[index]
        mean = jnp.sum(jnp.where(valid, normed, 0.0), axis=0, keepdims=True) / lens[index].astype(F32)
        pooled = mean * gain + shift
        shrink = lax.rsqrt(jnp.sum(pooled * pooled, axis=1, keepdims=True) + POOL_EPS)
        embed = pooled * shrink
        for piece in range(pieces):
            slab[pl.ds(index * pieces + piece, 1), :] = embed[:, piece * LANES : (piece + 1) * LANES]
        embeds.append(embed)
        shrinks.append(shrink)
        means.append(mean)
        inverses.append(jnp.where(valid, scale, 0.0))
    slab[pl.ds(2 * pieces, 1), :] = jnp.full((1, LANES), positive[core], jnp.int32).astype(F32)
    copies = []
    for step in range(1, total):
        copy = remote(slab, every.at[my_rank], e_send.at[step], e_recv.at[step], device(step))
        copy.start()
        copies.append(copy)
    sends.extend(copies)
    every[my_rank] = slab[...]
    for copy in copies:
        copy.wait_recv()

    queries = jnp.concatenate([every[:, piece, :] for piece in range(pieces)], axis=1)
    passages = jnp.concatenate([every[:, pieces + piece, :] for piece in range(pieces)], axis=1)
    wanted = every[:, 2 * pieces, :][:, :1]
    logits = lax.dot_general(
        queries, passages, (((1,), (1,)), ((), ())), precision=PRECISE, preferred_element_type=F32
    ) / SOFTMAX_TEMPER
    place = lax.broadcasted_iota(jnp.int32, logits.shape, 1)
    target = (place.astype(F32) == wanted).astype(F32)
    top = jnp.max(logits, axis=1, keepdims=True)
    weights = jnp.exp(logits - top)
    row_total = jnp.sum(weights, axis=1, keepdims=True)
    log_total = top + jnp.log(row_total)
    loss = jnp.sum(log_total - jnp.sum(logits * target, axis=1, keepdims=True), axis=0, keepdims=True) / total
    grad_logits = (weights / row_total - target) / (total * SOFTMAX_TEMPER)
    grad_column = jnp.sum(jnp.where(place == my_rank, grad_logits, 0.0), axis=1, keepdims=True)
    value = jnp.dot(grad_logits, passages, precision=PRECISE, preferred_element_type=F32)
    line = lax.broadcasted_iota(jnp.int32, value.shape, 0)
    grad_embeds = (
        jnp.sum(jnp.where(line == my_rank, value, 0.0), axis=0, keepdims=True),
        jnp.sum(grad_column * queries, axis=0, keepdims=True),
    )

    grad_gain, grad_shift, grad_bias = 0.0, 0.0, 0.0
    for index, (start, count) in enumerate(spans):
        embed, grad_embed = embeds[index], grad_embeds[index]
        grad_pooled = shrinks[index] * (grad_embed - embed * jnp.sum(grad_embed * embed, axis=1, keepdims=True))
        grad_gain = grad_gain + grad_pooled * means[index]
        grad_shift = grad_shift + grad_pooled
        spread = grad_pooled * gain / lens[index].astype(F32)
        centered = spread - jnp.mean(spread, axis=1, keepdims=True)
        normed = unit_two[pl.ds(start, count), :]
        value = inverses[index] * (centered - normed * jnp.mean(spread * normed, axis=1, keepdims=True))
        z_two[pl.ds(start, count), :] = value
        grad_low[pl.ds(start, count), :] = value.astype(BF16)
        grad_bias = grad_bias + jnp.sum(value, axis=0, keepdims=True)
    store(grad_low, grad_low_out)
    store(z_two, grad_out)
    small[pl.ds(0, 1), :] = grad_bias
    small[pl.ds(1, 1), :] = grad_gain
    small[pl.ds(2, 1), :] = grad_shift
    small[pl.ds(3, 1), :] = jnp.broadcast_to(loss, (1, model))
    small[pl.ds(4, 4), :] = jnp.zeros((4, model), F32)
    store(small, small_out)
    for copy in sends:
        copy.wait_send()
    for copy in stores:
        copy.wait()


def forward(query_in, passage_in, query_len, passage_len, positive, attn_master, ffn_master, col_bias, norm_params, spans, total):
    rows, width = attn_master.shape[1:]
    units = ffn_master.shape[2]
    slots, model = spans[1][0] + spans[1][1], query_in.shape[2]
    dma = pltpu.SemaphoreType.DMA
    col = col_bias.reshape(-1, LANES)
    anywhere = pl.BlockSpec(memory_space=pltpu.HBM)
    vmem = pl.BlockSpec(memory_space=pltpu.VMEM)
    smem = pl.BlockSpec(memory_space=pltpu.SMEM)
    results = (
        ((2, 3, model, units), BF16),
        ((2, slots, 3 * width), BF16),
        ((2, slots, width), BF16),
        ((slots, model), F32),
        ((slots, LANES), F32),
        ((slots, model), BF16),
        ((2, slots, units), BF16),
        ((2, slots, units), F32),
        ((slots, model), BF16),
        ((slots, model), F32),
        ((slots, model), BF16),
        ((8, model), F32),
    )
    return pl.pallas_call(
        functools.partial(forward_kernel, spans, total),
        out_shape=tuple(jax.ShapeDtypeStruct(*result) for result in results),
        in_specs=[smem] * 3 + [anywhere] * 4 + [vmem] * 2,
        out_specs=(anywhere,) * len(results),
        scratch_shapes=[pltpu.VMEM(*result) for result in results]
        + [
            pltpu.VMEM((2, 1, col_bias.shape[0]), F32),
            pltpu.VMEM(attn_master.shape, F32),
            pltpu.VMEM(ffn_master.shape, F32),
            pltpu.VMEM((slots, model), F32),
            pltpu.VMEM((SLAB, LANES), F32),
            pltpu.VMEM((total, SLAB, LANES), F32),
        ]
        + [dma((3, 4))] * 6
        + [dma((3, 4, 2))] * 2
        + [dma((3, 4))] * 2
        + [dma(()), dma(()), dma((5,)), dma((20,)), dma((total,)), dma((total,))],
        compiler_params=pltpu.CompilerParams(collective_id=0, has_side_effects=True, vmem_limit_bytes=58 * MIB),
        name="forward",
    )(query_len, passage_len, positive, query_in, passage_in, attn_master, ffn_master, col, norm_params)


def backward_kernel(
    spans,
    query_len, passage_len, weight_ref, proj_ref, mixed_ref, unit_ref, inverse_ref, low_ref, active_ref, slope_ref,
    tokens_ref, grad_ref, grad_low_ref, norm_ref, small_ref,
    attn_out, ffn_out, small_out, col_out, query_out, passage_out,
    weight, proj, mixed, inverse, low, active, slope, tokens, total, down, grad_out, grad_proj,
    temp, far_send, far_recv, kept, one_send, one_recv, two_send, two_recv, z_send, z_recv, result, vector, vec_send,
    vec_recv, col,
    load_sem, slope_sem, c_send, c_recv, s1_send, s1_recv, s2_send, s2_recv, s3_send, s3_recv,
    v_send, v_recv, t_send, t_recv, credit, out_sem,
):
    at = Mesh()
    me, core = at.me, at.core
    slots, model = tokens.shape
    width = grad_out.shape[1]
    rows = model // 16
    lens = (query_len[core], passage_len[core])
    near_peer = (at.index(at.z + 1 - 2 * lax.rem(at.z, 2), at.y, at.x), core)
    over_peer = at.z_peer[2]

    sends = {}
    stores = []
    loads = {}

    def load(name, *pairs):
        copies = []
        for source, target in pairs:
            copy = pltpu.make_async_copy(source, target, load_sem.at[sum(len(v) for v in loads.values()) + len(copies)])
            copy.start()
            copies.append(copy)
        loads[name] = copies

    def ready(name):
        for copy in loads[name]:
            copy.wait()

    def store(source, target):
        copy = pltpu.make_async_copy(source, target, out_sem.at[len(stores)])
        copy.start()
        stores.append(copy)

    def push(name, source, target, send, recv, peer):
        copy = remote(source, target, send, recv, peer)
        copy.start()
        sends[name] = copy

    def landed(target, send, recv, peer):
        remote(target, target, send, recv, peer).wait_recv()

    lanes_of = [pl.ds(t * width, width) for t in range(4)]
    pair_lanes = (pl.ds(0, 2 * width), pl.ds(2 * width, 2 * width))

    def slope_tile(half, t):
        index = half * 4 + t
        return pltpu.make_async_copy(slope_ref.at[half, :, lanes_of[t]], slope.at[t % 2], slope_sem.at[index])

    load("down", (grad_low_ref, down))
    load("active1", (active_ref.at[1], active.at[1]))
    barrier = pltpu.get_barrier_semaphore()
    for peer in [*at.z_peer[1:], at.x_peer, at.y_peer, at.c_peer]:
        pl.semaphore_signal(barrier, inc=1, device_id=peer, device_id_type=MESH)
    load("down1", (weight_ref.at[1, 2], weight.at[0]))
    slope_tile(1, 0).start()
    slope_tile(1, 1).start()
    load("active0", (active_ref.at[0], active.at[0]))

    def far_slot(q):
        return q % 2

    def send_far(q, t, value):
        if q == 2:
            sends[("c", 0, t)].wait_send()
        far_send[far_slot(q), t] = value.astype(BF16)
        push(
            ("c", q, t), far_send.at[far_slot(q), t], far_recv.at[far_slot(q), t], c_send.at[q, t], c_recv.at[q, t],
            at.c_peer,
        )

    def side(t):
        steps = ((at.x, at.x_peer), (at.y, at.y_peer))
        return steps if t % 2 == 0 else steps[::-1]

    def block(index, count=1):
        return pl.ds(pl.multiple_of(index * rows, rows), count * rows)

    def first_step(q, t, lanes):
        landed(far_recv.at[far_slot(q), t], c_send.at[q, t], c_recv.at[q, t], at.c_peer)
        (bit, peer), _ = side(t)
        for layer in range(4):
            for other in range(2):
                if t % 2 == 0:
                    mine, theirs = at.index(layer, other, bit), at.index(layer, other, 1 - bit)
                else:
                    mine, theirs = at.index(layer, bit, other), at.index(layer, 1 - bit, other)
                place = pl.ds((layer * 2 + other) * rows, rows)
                far = far_recv[far_slot(q), t, block(theirs), :].astype(F32)
                one_send[q, t, place, :] = (temp[block(theirs), lanes] + far).astype(BF16)
                far = far_recv[far_slot(q), t, block(mine), :].astype(F32)
                kept[q, t, place, :] = temp[block(mine), lanes] + far
        push(("1", q, t), one_send.at[q, t], one_recv.at[q, t], s1_send.at[q, t], s1_recv.at[q, t], peer)

    def second_step(q, t):
        (_, before), (bit, peer) = side(t)
        landed(one_recv.at[q, t], s1_send.at[q, t], s1_recv.at[q, t], before)
        for layer in range(4):
            theirs = block(layer * 2 + 1 - bit)
            value = kept[q, t, theirs, :] + one_recv[q, t, theirs, :].astype(F32)
            two_send[q, t, pl.ds(layer * rows, rows), :] = value.astype(BF16)
            mine = block(layer * 2 + bit)
            kept[q, t, mine, :] = kept[q, t, mine, :] + one_recv[q, t, mine, :].astype(F32)
        push(("2", q, t), two_send.at[q, t], two_recv.at[q, t], s2_send.at[q, t], s2_recv.at[q, t], peer)

    def third_step(q, t):
        _, (bit, before) = side(t)
        landed(two_recv.at[q, t], s2_send.at[q, t], s2_recv.at[q, t], before)
        for k in range(1, 4):
            layer = lax.rem(at.z + k, 4)
            value = kept[q, t, block(layer * 2 + bit), :] + two_recv[q, t, block(layer), :].astype(F32)
            z_send[q, t, k - 1] = value.astype(BF16)
            push(
                ("3", q, t, k), z_send.at[q, t, k - 1], z_recv.at[q, t, k - 1], s3_send.at[q, t, k], s3_recv.at[q, t, k],
                at.z_peer[k],
            )
        result[q, t] = kept[q, t, block(at.z * 2 + bit), :] + two_recv[q, t, block(at.z), :].astype(F32)

    def last_step(q, t):
        for k in range(1, 4):
            landed(z_recv.at[q, t, k - 1], s3_send.at[q, t, k], s3_recv.at[q, t, k], at.z_peer[k])
        value = result[q, t]
        for k in range(3):
            value = value + z_recv[q, t, k].astype(F32)
        result[q, t] = value
        if q < 2:
            store(result.at[q, t], ffn_out.at[1 - q, :, lanes_of[t]])
        elif t == 3:
            store(result.at[q, t], attn_out.at[3])
        else:
            for index in range(3):
                store(result.at[q, t, :, pl.ds(index * LANES, LANES)], attn_out.at[index, :, pl.ds(t * LANES, LANES)])

    def far_product(q, left, right):
        for pair in range(2):
            value = mm_tn(left[...], right[:, pair_lanes[pair]])
            send_far(q, 2 * pair, value[:, :width])
            send_far(q, 2 * pair + 1, value[:, width:])

    def own_product(q, left, right, pair):
        temp[...] = mm_tn(left[...], right[:, pair_lanes[pair]])
        first_step(q, 2 * pair, lanes_of[0])
        first_step(q, 2 * pair + 1, lanes_of[1])

    def hidden_grad(half, slot, pair, following):
        for t in (2 * pair, 2 * pair + 1):
            slope_tile(half, t).wait()
        value = mm(down[...], weight[slot, :, pair_lanes[pair]])
        for side_of, t in enumerate((2 * pair, 2 * pair + 1)):
            piece = (value[:, side_of * width : (side_of + 1) * width] * slope[side_of]).astype(BF16)
            active[half, :, lanes_of[t]] = piece
            vec = vector if half == 0 else vec_send.at[0]
            vec[pl.ds(9 + pair, 1), lanes_of[side_of]] = jnp.sum(piece.astype(F32), axis=0, keepdims=True)
        if following is not None:
            for t in (0, 1):
                slope_tile(following[0], 2 * following[1] + t).start()

    def add_back(source, slot, lanes):
        total[...] = total[...] + mm_nt(source, weight[slot, :, lanes])

    def first_norm_back():
        sums = [None, None, None]
        step = 192
        for start in range(0, slots, step):
            place = pl.ds(start, step)
            grad = total[place, :]
            normed = jnp.concatenate([slope[0, place, :], slope[1, place, :]], axis=1)
            back = normalize_back(normed, inverse[place, pl.ds(0, 1)], grad * norm_ref[pl.ds(1, 1), :])
            for index, value in enumerate((back, grad * normed, grad)):
                value = jnp.sum(value, axis=0, keepdims=True)
                sums[index] = value if sums[index] is None else sums[index] + value
            total[place, :] = back
            down[place, :] = back.astype(BF16)
        for index in range(3):
            vector[pl.ds(index, 1), :] = sums[index]
            vec_send[0, pl.ds(index, 1), :] = sums[index]

    def out_grad(slot):
        grad_out[...] = mm(down[...], weight[slot, :, lanes_of[3]]).astype(BF16)

    def query_back(half):
        place = pl.ds(*spans[0])
        queries = stack_heads(proj[half, place, lanes_of[0]])
        grads = stack_heads(grad_out[place, :])
        keys = proj[half, place, lanes_of[1]]
        probs = probabilities(mm_nt(queries * jnp.asarray(SCALE, BF16), keys), lens[0])
        grad_probs = mm_nt(grads, proj[half, place, lanes_of[2]])
        inner = jnp.sum(probs * grad_probs, axis=1, keepdims=True)
        grad_scores = (probs * (grad_probs - inner)).astype(BF16)
        value = unstack_heads(mm(grad_scores, keys), spans[0][1]) * SCALE
        grad_proj[half, place, lanes_of[0]] = value.astype(BF16)
        grad_proj[half, place, lanes_of[1]] = (mm_tn(grad_scores, queries) * SCALE).astype(BF16)
        grad_proj[half, place, lanes_of[2]] = mm_tn(probs.astype(BF16), grads).astype(BF16)

    def passage_back(half, pair):
        place = pl.ds(*spans[1])
        spot = [pl.ds(index * width + pair * LANES, LANES) for index in range(3)]
        queries, keys = proj[half, place, spot[0]], proj[half, place, spot[1]]
        grads = grad_out[place, pl.ds(pair * LANES, LANES)]
        scores = [mm_nt(queries, key) for key in split_pair(keys * jnp.asarray(SCALE, BF16))]
        grad_probs = [mm_nt(grads, value) for value in split_pair(proj[half, place, spot[2]])]
        outs = []
        for head in range(2):
            probs = probabilities(scores[head], lens[1])
            inner = jnp.sum(probs * grad_probs[head], axis=1, keepdims=True)
            grad_scores = (probs * (grad_probs[head] - inner)).astype(BF16)
            outs.append(
                (mm(grad_scores, keys) * SCALE, mm_tn(grad_scores, queries) * SCALE, mm_tn(probs.astype(BF16), grads))
            )
        lane = first_head(queries.shape)
        for index in range(3):
            grad_proj[half, place, spot[index]] = jnp.where(lane, outs[0][index], outs[1][index]).astype(BF16)

    def pair_product(half, pair):
        spot = [pl.ds(index * width + pair * LANES, LANES) for index in range(3)]
        return mm_tn(tokens[...], jnp.concatenate([grad_proj[half, :, lanes] for lanes in spot], axis=1))

    def attn_biases(half):
        vec = vector if half == 0 else vec_send.at[0]
        for index in (0, 1):
            value = grad_proj[half, :, lanes_of[2 * index]].astype(F32)
            vec[pl.ds(8, 1), lanes_of[index]] = jnp.sum(value, axis=0, keepdims=True)

    def vector_step(step, peer):
        if step:
            vec_send[step] = vector[...]
        push(("v", step), vec_send.at[step], vec_recv.at[step], v_send.at[step], v_recv.at[step], peer)

    def vector_sum(step, peer):
        landed(vec_recv.at[step], v_send.at[step], v_recv.at[step], peer)
        vector[...] = vector[...] + vec_recv[step]

    for target in (vector, vec_send.at[0]):
        target[pl.ds(3, 3), :] = small_ref[pl.ds(0, 3), :]
        target[pl.ds(6, 2), :] = jnp.zeros((2, model), F32)
        target[pl.ds(11, 5), :] = jnp.zeros((5, model), F32)

    ready("down")
    ready("active1")
    pl.semaphore_wait(barrier, 6)
    far_product(0, down, active.at[1])
    load("down0", (weight_ref.at[0, 2], weight.at[1]))
    load("low", (low_ref, low))
    ready("down1")
    hidden_grad(1, 0, 0, (1, 1))
    load("up1", (weight_ref.at[1, 1], weight.at[2]))
    ready("active0")
    own_product(0, down, active.at[0], 0)
    hidden_grad(1, 0, 1, (0, 0))
    load("up0", (weight_ref.at[0, 1], weight.at[0]))
    own_product(0, down, active.at[0], 1)
    pl.semaphore_signal(credit, inc=1, device_id=at.c_peer, device_id_type=MESH)
    load("total", (grad_ref, total))
    load("inverse", (inverse_ref, inverse))
    ready("down0")
    hidden_grad(0, 1, 0, (0, 1))
    ready("low")
    far_product(1, low, active.at[1])
    hidden_grad(0, 1, 1, None)
    load("unit", *[(unit_ref.at[:, lanes_of[t]], slope.at[t]) for t in range(2)])
    load("attn1", (weight_ref.at[1, 0], weight.at[1]))
    load("proj", (proj_ref, proj), (mixed_ref, mixed), (tokens_ref, tokens))
    ready("total")
    ready("up1")
    add_back(active[1], 2, pl.ds(0, 4 * width))
    load("attn0", (weight_ref.at[0, 0], weight.at[2]))
    own_product(1, low, active.at[0], 0)
    own_product(1, low, active.at[0], 1)
    ready("up0")
    add_back(active[0], 0, pl.ds(0, 4 * width))
    ready("inverse")
    ready("unit")
    first_norm_back()
    second_step(0, 0)
    second_step(0, 1)
    ready("proj")
    pl.semaphore_wait(credit, 1)
    send_far(2, 3, mm_tn(down[...], mixed[1]))
    ready("attn1")
    out_grad(1)
    query_back(1)
    passage_back(1, 0)
    send_far(2, 0, pair_product(1, 0))
    second_step(0, 2)
    second_step(0, 3)
    temp[:, lanes_of[0]] = mm_tn(down[...], mixed[0])
    first_step(2, 3, lanes_of[0])
    passage_back(1, 1)
    send_far(2, 1, pair_product(1, 1))
    third_step(0, 0)
    third_step(0, 1)
    passage_back(1, 2)
    send_far(2, 2, pair_product(1, 2))
    attn_biases(1)
    vector_step(0, at.c_peer)
    third_step(0, 2)
    third_step(0, 3)
    second_step(1, 0)
    second_step(1, 1)
    ready("attn0")
    out_grad(2)
    query_back(0)
    passage_back(0, 0)
    temp[:, lanes_of[1]] = pair_product(0, 0)
    first_step(2, 0, lanes_of[1])
    second_step(1, 2)
    second_step(1, 3)
    passage_back(0, 1)
    temp[:, lanes_of[0]] = pair_product(0, 1)
    first_step(2, 1, lanes_of[0])
    for t in range(4):
        last_step(0, t)
    passage_back(0, 2)
    temp[:, lanes_of[1]] = pair_product(0, 2)
    first_step(2, 2, lanes_of[1])
    third_step(1, 0)
    third_step(1, 1)
    attn_biases(0)
    vector_sum(0, at.c_peer)
    vector_step(1, at.x_peer)
    add_back(grad_proj[1], 1, pl.ds(0, 3 * width))
    third_step(1, 2)
    third_step(1, 3)
    second_step(2, 3)
    add_back(grad_proj[0], 2, pl.ds(0, 3 * width))
    for index, target in ((0, query_out), (1, passage_out)):
        part = total.at[pl.ds(*spans[index]), :]
        store(part, target.at[core])
        push(("t", index), part, target.at[core], t_send.at[index], t_recv.at[index], at.c_peer)
    vector_sum(1, at.x_peer)
    vector_step(2, at.y_peer)
    second_step(2, 0)
    for t in range(4):
        last_step(1, t)
    vector_sum(2, at.y_peer)
    vector_step(3, near_peer)
    second_step(2, 1)
    third_step(2, 3)
    vector_sum(3, near_peer)
    vector_step(4, over_peer)
    second_step(2, 2)
    third_step(2, 0)
    third_step(2, 1)
    vector_sum(4, over_peer)
    store(vector.at[pl.ds(0, 8), :], small_out)
    for line in range(3):
        for piece in range(model // LANES):
            col[pl.ds(line * (model // LANES) + piece, 1), :] = vector[pl.ds(8 + line, 1), pl.ds(piece * LANES, LANES)]
    store(col, col_out)
    third_step(2, 2)
    for t in (3, 0, 1, 2):
        last_step(2, t)
    for index, target in ((0, query_out), (1, passage_out)):
        landed(target.at[1 - core], t_send.at[index], t_recv.at[index], at.c_peer)
    for copy in stores:
        copy.wait()
    for name, copy in sends.items():
        if name[:2] != ("c", 0):
            copy.wait_send()


def backward(query_len, passage_len, kept, norm_params, spans):
    weight, proj, mixed, unit, inverse, low, active, slope, tokens, grad_ztwo, grad_low, small = kept
    slots, model = tokens.shape
    width = mixed.shape[2]
    rows = model // 16
    anywhere = pl.BlockSpec(memory_space=pltpu.HBM)
    vmem = pl.BlockSpec(memory_space=pltpu.VMEM)
    smem = pl.BlockSpec(memory_space=pltpu.SMEM)
    dma = pltpu.SemaphoreType.DMA
    lines = 3 * model // LANES
    scratch = [
        pltpu.VMEM((3, model, 4 * width), BF16),
        pltpu.VMEM(proj.shape, BF16),
        pltpu.VMEM(mixed.shape, BF16),
        pltpu.VMEM(inverse.shape, F32),
        pltpu.VMEM(low.shape, BF16),
        pltpu.VMEM(active.shape, BF16),
        pltpu.VMEM((2, slots, width), F32),
        pltpu.VMEM(tokens.shape, BF16),
        pltpu.VMEM((slots, model), F32),
        pltpu.VMEM((slots, model), BF16),
        pltpu.VMEM((slots, width), BF16),
        pltpu.VMEM((2, slots, 3 * width), BF16),
        pltpu.VMEM((model, 2 * width), F32),
        pltpu.VMEM((2, 4, model, width), BF16),
        pltpu.VMEM((2, 4, model, width), BF16),
        pltpu.VMEM((3, 4, 8 * rows, width), F32),
        pltpu.VMEM((3, 4, 8 * rows, width), BF16),
        pltpu.VMEM((3, 4, 8 * rows, width), BF16),
        pltpu.VMEM((3, 4, 4 * rows, width), BF16),
        pltpu.VMEM((3, 4, 4 * rows, width), BF16),
        pltpu.VMEM((3, 4, 3, rows, width), BF16),
        pltpu.VMEM((3, 4, 3, rows, width), BF16),
        pltpu.VMEM((3, 4, rows, width), F32),
        pltpu.VMEM((16, model), F32),
        pltpu.VMEM((5, 16, model), F32),
        pltpu.VMEM((5, 16, model), F32),
        pltpu.VMEM((lines, LANES), F32),
        dma((20,)), dma((8,)),
        dma((3, 4)), dma((3, 4)), dma((3, 4)), dma((3, 4)), dma((3, 4)), dma((3, 4)),
        dma((3, 4, 4)), dma((3, 4, 4)),
        dma((5,)), dma((5,)), dma((2,)), dma((2,)),
        pltpu.SemaphoreType.REGULAR,
        dma((24,)),
    ]
    return pl.pallas_call(
        functools.partial(backward_kernel, spans),
        out_shape=(
            jax.ShapeDtypeStruct((4, rows, width), F32),
            jax.ShapeDtypeStruct((2, rows, 4 * width), F32),
            jax.ShapeDtypeStruct((8, model), F32),
            jax.ShapeDtypeStruct((lines, LANES), F32),
            jax.ShapeDtypeStruct((2, spans[0][1], model), F32),
            jax.ShapeDtypeStruct((2, spans[1][1], model), F32),
        ),
        in_specs=[smem] * 2 + [anywhere] * 11 + [vmem, vmem],
        out_specs=(anywhere,) * 6,
        scratch_shapes=scratch,
        compiler_params=pltpu.CompilerParams(collective_id=2, has_side_effects=True, vmem_limit_bytes=60 * MIB),
        name="backward",
    )(query_len, passage_len, weight, proj, mixed, unit, inverse, low, active, slope, tokens, grad_ztwo, grad_low,
      norm_params, small)


def finish_kernel(
    step_ref, rates_ref, query_ref, passage_ref,
    attn_grad, ffn_grad, norm_grad, col_grad, loss_ref,
    attn_m, attn_f, attn_s, attn_a, ffn_m, ffn_f, ffn_s, ffn_a,
    norm_m, norm_f, norm_s, norm_a, col_m, col_f, col_s, col_a,
    loss_out, query_out, passage_out,
    attn_mo, attn_fo, attn_so, attn_ao, ffn_mo, ffn_fo, ffn_so, ffn_ao,
    norm_mo, norm_fo, norm_so, norm_ao, col_mo, col_fo, col_so, col_ao, attn_co, ffn_co,
    attn_in, attn_res, attn_low, ffn_in, ffn_res, ffn_low, norm_in, norm_res, col_in, col_res, small, in_sem, out_sem,
):
    loads, stores = [], []

    def load(source, target):
        copy = pltpu.make_async_copy(source, target, in_sem.at[len(loads)])
        copy.start()
        loads.append(copy)
        return copy

    def store(source, target):
        copy = pltpu.make_async_copy(source, target, out_sem.at[len(stores)])
        copy.start()
        stores.append(copy)

    groups = [
        [
            load(source.at[which], ffn_in.at[index, which])
            for index, source in enumerate((ffn_m, ffn_f, ffn_s, ffn_a, ffn_grad))
        ]
        for which in range(2)
    ]
    groups.append(
        [load(source, attn_in.at[index]) for index, source in enumerate((attn_m, attn_f, attn_s, attn_a, attn_grad))]
    )
    lines = norm_in.shape[1]
    groups.append(
        [load(source, norm_in.at[index]) for index, source in enumerate((norm_m, norm_f, norm_s, norm_a))]
        + [load(norm_grad, small.at[0]), load(loss_ref, small.at[1])]
        + [load(source, col_in.at[index]) for index, source in enumerate((col_m, col_f, col_s, col_a, col_grad))]
    )
    store(query_ref, query_out)
    store(passage_ref, passage_out)

    count = jnp.full((1, 1), step_ref[0], jnp.int32).astype(F32)
    rate = [jnp.full((1, 1), rates_ref[index], F32) for index in range(5)]
    to_first, to_second = [1.0 / (1.0 - jnp.exp(count * jnp.log(rate[index]))) for index in range(2)]

    def update(master, first, second, average, grad, learn, decay):
        first_new = rate[0] * first + (1.0 - rate[0]) * grad
        second_new = rate[1] * second + (1.0 - rate[1]) * grad * grad
        move = (first_new * to_first) / (jnp.sqrt(second_new * to_second) + ADAM_EPS)
        if decay:
            move = move + decay * master
        master_new = master - learn * move
        average_new = rate[2] * average + (1.0 - rate[2]) * master_new
        return master_new, first_new, second_new, average_new

    def wait(group):
        for copy in groups[group]:
            copy.wait()

    for which in range(2):
        wait(which)
        values = update(*[ffn_in[index, which] for index in range(5)], rate[3], DECAY_WEIGHT)
        for index, (value, target) in enumerate(zip(values, (ffn_mo, ffn_fo, ffn_so, ffn_ao))):
            ffn_res[index, which] = value
            store(ffn_res.at[index, which], target.at[which])
        ffn_low[which] = values[0].astype(BF16)
        store(ffn_low.at[which], ffn_co.at[which])
    wait(2)
    for which in range(attn_low.shape[0]):
        values = update(*[attn_in[index, which] for index in range(5)], rate[3], DECAY_WEIGHT)
        for index, value in enumerate(values):
            attn_res[index, which] = value
        attn_low[which] = values[0].astype(BF16)
    for index, target in enumerate((attn_mo, attn_fo, attn_so, attn_ao)):
        store(attn_res.at[index], target)
    store(attn_low, attn_co)
    wait(3)
    values = update(*[norm_in[index] for index in range(4)], small[0, pl.ds(0, lines), :], rate[4], 0.0)
    for index, (value, target) in enumerate(zip(values, (norm_mo, norm_fo, norm_so, norm_ao))):
        norm_res[index] = value
        store(norm_res.at[index], target)
    values = update(*[col_in[index] for index in range(5)], rate[4], 0.0)
    for index, (value, target) in enumerate(zip(values, (col_mo, col_fo, col_so, col_ao))):
        col_res[index] = value
        store(col_res.at[index], target)
    loss_out[0] = jnp.sum(small[1, pl.ds(3, 1), pl.ds(0, 1)])
    for copy in stores:
        copy.wait()


def finish(step, rates, grads, loss_rows, attn_state, ffn_state, norm_state, col_state):
    attn_grad, ffn_grad, norm_grad, col_grad, query_grad, passage_grad = grads
    anywhere = pl.BlockSpec(memory_space=pltpu.HBM)
    smem = pl.BlockSpec(memory_space=pltpu.SMEM)
    dma = pltpu.SemaphoreType.DMA
    col_state = [value.reshape(-1, LANES) for value in col_state]
    states = (attn_state, ffn_state, norm_state, col_state)
    shapes = [jax.ShapeDtypeStruct((1,), F32)]
    shapes += [jax.ShapeDtypeStruct(value.shape, F32) for value in (query_grad, passage_grad)]
    shapes += [jax.ShapeDtypeStruct(value.shape, F32) for state in states for value in state]
    shapes += [jax.ShapeDtypeStruct(state[0].shape, BF16) for state in (attn_state, ffn_state)]
    scratch = []
    for state in (attn_state, ffn_state):
        shape = state[0].shape
        scratch += [pltpu.VMEM((5,) + shape, F32), pltpu.VMEM((4,) + shape, F32), pltpu.VMEM(shape, BF16)]
    for state, count in ((norm_state, 4), (col_state, 5)):
        shape = state[0].shape
        scratch += [pltpu.VMEM((count,) + shape, F32), pltpu.VMEM((4,) + shape, F32)]
    outs = pl.pallas_call(
        finish_kernel,
        out_shape=tuple(shapes),
        in_specs=[smem] * 2 + [anywhere] * 23,
        out_specs=(smem,) + (anywhere,) * 20,
        scratch_shapes=scratch + [pltpu.VMEM((2,) + norm_grad.shape, F32), dma((26,)), dma((28,))],
        compiler_params=pltpu.CompilerParams(vmem_limit_bytes=40 * MIB),
        name="finish",
    )(step, rates, query_grad, passage_grad, attn_grad, ffn_grad, norm_grad, col_grad, loss_rows,
      *attn_state, *ffn_state, *norm_state, *col_state)
    outs = list(outs)
    outs[15:19] = [value.reshape(-1) for value in outs[15:19]]
    return outs


def attend_kernel(spans, lens_ref, q_ref, k_ref, v_ref, o_ref):
    for index, (start, slots) in enumerate(spans):
        length = lens_ref[index]
        keys = k_ref[0, pl.ds(start, slots), :]
        values = v_ref[0, pl.ds(start, slots), :]
        lane = first_head(keys.shape)
        scaled = keys * jnp.asarray(HD**-0.5, BF16)
        zero = jnp.zeros_like(scaled)
        head_keys = (jnp.where(lane, scaled, zero), jnp.where(lane, zero, scaled))
        block = min(slots, 256)
        for at in range(0, slots, block):
            queries = q_ref[0, pl.ds(start + at, block), :]
            outs = []
            for head in range(2):
                scores = mm_nt(queries, head_keys[head])
                valid = lax.broadcasted_iota(jnp.int32, scores.shape, 1) < length
                scores = jnp.where(valid, scores, NEG_FILL)
                top = jnp.max(scores, axis=1, keepdims=True)
                weight = jnp.exp(scores - top)
                total = jnp.sum(weight, axis=1, keepdims=True)
                probs = (weight * (1.0 / total)).astype(BF16)
                outs.append(mm(probs, values))
            o_ref[pl.ds(start + at, block), :] = jnp.where(
                first_head(outs[0].shape), outs[0], outs[1]
            ).astype(BF16)


def attend_back_kernel(spans, lens_ref, q_ref, k_ref, v_ref, g_ref, d_ref):
    scale = HD**-0.5
    for index, (start, slots) in enumerate(spans):
        length = lens_ref[index]
        keys = k_ref[0, pl.ds(start, slots), :]
        values = v_ref[0, pl.ds(start, slots), :]
        lane = first_head(keys.shape)
        scaled = keys * jnp.asarray(scale, BF16)
        zero = jnp.zeros_like(scaled)
        head_keys = (jnp.where(lane, scaled, zero), jnp.where(lane, zero, scaled))
        head_values = (jnp.where(lane, values, zero), jnp.where(lane, zero, values))
        block = min(slots, 256)
        grad_k = [None, None]
        grad_v = [None, None]
        for at in range(0, slots, block):
            queries = q_ref[0, pl.ds(start + at, block), :]
            grads = g_ref[pl.ds(start + at, block), :]
            grad_q = []
            for head in range(2):
                scores = mm_nt(head_keys[head], queries)
                valid = lax.broadcasted_iota(jnp.int32, scores.shape, 0) < length
                scores = jnp.where(valid, scores, NEG_FILL)
                top = jnp.max(scores, axis=0, keepdims=True)
                weight = jnp.exp(scores - top)
                total = jnp.sum(weight, axis=0, keepdims=True)
                probs = weight * (1.0 / total)
                grad_probs = mm_nt(head_values[head], grads)
                inner = jnp.sum(probs * grad_probs, axis=0, keepdims=True)
                grad_scores = (probs * (grad_probs - inner)).astype(BF16)
                part_v = mm(probs.astype(BF16), grads)
                part_k = mm(grad_scores, queries)
                grad_v[head] = part_v if at == 0 else grad_v[head] + part_v
                grad_k[head] = part_k if at == 0 else grad_k[head] + part_k
                grad_q.append(mm_tn(grad_scores, keys))
            d_ref[0, pl.ds(start + at, block), :] = (
                jnp.where(first_head(grad_q[0].shape), grad_q[0], grad_q[1]) * scale
            ).astype(BF16)
        d_ref[1, pl.ds(start, slots), :] = (jnp.where(lane, grad_k[0], grad_k[1]) * scale).astype(BF16)
        d_ref[2, pl.ds(start, slots), :] = jnp.where(lane, grad_v[0], grad_v[1]).astype(BF16)


def head_specs(tokens):
    return [pl.BlockSpec((1, tokens, LANES), functools.partial(lambda s, i, lens: (s, 0, i), s)) for s in range(3)]


def attend(proj, lens, spans):
    _, tokens, width = proj.shape
    flops = sum(4 * slots * slots * width for _, slots in spans)
    return pl.pallas_call(
        functools.partial(attend_kernel, spans),
        out_shape=jax.ShapeDtypeStruct((tokens, width), BF16),
        grid_spec=pltpu.PrefetchScalarGridSpec(
            num_scalar_prefetch=1,
            grid=(width // LANES,),
            in_specs=head_specs(tokens),
            out_specs=pl.BlockSpec((tokens, LANES), lambda i, lens: (0, i)),
        ),
        compiler_params=pltpu.CompilerParams(vmem_limit_bytes=40 * MIB),
        cost_estimate=pl.CostEstimate(flops=8 * flops, bytes_accessed=8 * tokens * width, transcendentals=0),
        name="attend",
    )(lens, proj, proj, proj)


def attend_back(proj, grad_out, lens, spans):
    _, tokens, width = proj.shape
    flops = sum(10 * slots * slots * width for _, slots in spans)
    return pl.pallas_call(
        functools.partial(attend_back_kernel, spans),
        out_shape=jax.ShapeDtypeStruct((3, tokens, width), BF16),
        grid_spec=pltpu.PrefetchScalarGridSpec(
            num_scalar_prefetch=1,
            grid=(width // LANES,),
            in_specs=head_specs(tokens) + [pl.BlockSpec((tokens, LANES), lambda i, lens: (0, i))],
            out_specs=pl.BlockSpec((3, tokens, LANES), lambda i, lens: (0, 0, i)),
        ),
        compiler_params=pltpu.CompilerParams(vmem_limit_bytes=40 * MIB),
        cost_estimate=pl.CostEstimate(flops=8 * flops, bytes_accessed=14 * tokens * width, transcendentals=0),
        name="attend_back",
    )(lens, proj, proj, proj, grad_out)


def up_kernel(x_ref, w_ref, b_ref, g_ref, s_ref):
    hidden = mm(x_ref[...], w_ref[0]) + b_ref[...]
    active, slope = gelu_and_slope(hidden)
    g_ref[...] = active.astype(BF16)
    s_ref[...] = slope


def feed_up(low, ffn_half, bias):
    tokens, width = low.shape
    units = ffn_half.shape[2]
    tile = 256
    return pl.pallas_call(
        up_kernel,
        out_shape=(jax.ShapeDtypeStruct((tokens, units), BF16), jax.ShapeDtypeStruct((tokens, units), F32)),
        grid=(units // tile,),
        in_specs=[
            pl.BlockSpec((tokens, width), lambda i: (0, 0)),
            pl.BlockSpec((1, width, tile), lambda i: (0, 0, i)),
            pl.BlockSpec((1, tile), lambda i: (0, i)),
        ],
        out_specs=(pl.BlockSpec((tokens, tile), lambda i: (0, i)), pl.BlockSpec((tokens, tile), lambda i: (0, i))),
        compiler_params=pltpu.CompilerParams(vmem_limit_bytes=40 * MIB),
        cost_estimate=pl.CostEstimate(
            flops=2 * tokens * width * units, bytes_accessed=8 * tokens * units, transcendentals=tokens * units
        ),
        name="feed_up",
    )(low, ffn_half, bias.reshape(1, -1))


def swap_cores(values):
    return lax.ppermute(values, "mp", [(0, 1), (1, 0)])


def scatter_sum(own_parts, other_parts):
    summed = [own + swap_cores(other).astype(F32) for own, other in zip(own_parts, other_parts)]
    return [lax.psum_scatter(value, "dp", scatter_dimension=1, tiled=True) for value in summed]


def adam_update(master, first, second, average, grad, rate, decay_w, rates, step_count):
    first_new = rates[0] * first + (1.0 - rates[0]) * grad
    second_new = rates[1] * second + (1.0 - rates[1]) * grad * grad
    fixed_one = first_new / (1.0 - rates[0] ** step_count)
    fixed_two = second_new / (1.0 - rates[1] ** step_count)
    master_new = master - rate * (fixed_one / (jnp.sqrt(fixed_two) + ADAM_EPS) + decay_w * master)
    average_new = rates[2] * average + (1.0 - rates[2]) * master_new
    return (master_new, first_new, second_new, average_new)


def forward_plain(tokens, lens, attn_low, ffn_low, col_bias, norm_params, spans):
    attn_full = lax.all_gather(attn_low, "dp", axis=1, tiled=True)
    ffn_full = lax.all_gather(ffn_low, "dp", axis=1, tiled=True)
    attn_w = (attn_full, swap_cores(attn_full))
    ffn_w = (ffn_full, swap_cores(ffn_full))
    col = (col_bias, swap_cores(col_bias))
    width = attn_w[0].shape[2]

    projected, mixed = [], []
    branch = None
    for half in range(2):
        bias = jnp.stack([col[half][:width], jnp.zeros((width,), F32), col[half][width : 2 * width]])
        proj = (
            jnp.einsum("td,sde->ste", tokens, attn_w[half][:3], preferred_element_type=F32) + bias[:, None, :]
        ).astype(BF16)
        out = attend(proj, lens, spans)
        part = mm_nt(out, attn_w[half][3])
        branch = part if branch is None else branch + part
        projected.append(proj)
        mixed.append(out)
    z_one = tokens.astype(F32) + branch + norm_params[0]
    unit_one, inverse_one = normalize(z_one)
    first_norm = unit_one * norm_params[1] + norm_params[2]
    first_low = first_norm.astype(BF16)
    active, slope = [], []
    branch_two = None
    for half in range(2):
        act, slo = feed_up(first_low, ffn_w[half], col[half][2 * width :])
        part = mm_nt(act, ffn_w[half][1])
        branch_two = part if branch_two is None else branch_two + part
        active.append(act)
        slope.append(slo)
    z_two = first_norm + branch_two + norm_params[3]
    return attn_w, ffn_w, projected, mixed, unit_one, inverse_one, first_low, active, slope, z_two


def loss_plain(z_two, lens, target_mine, norm_params, spans, pairs):
    query_slots, passage_slots = spans[0][1], spans[1][1]
    model_width = z_two.shape[1]
    core = lax.axis_index("mp")
    unit_two, inverse_two = normalize(z_two)
    places = jnp.arange(query_slots + passage_slots)
    in_query = (places < query_slots) & (places < lens[0])
    in_passage = (places >= query_slots) & (places - query_slots < lens[1])
    share = (
        jnp.stack([in_query, in_passage]).astype(F32) / lens.astype(F32)[:, None]
    )
    mean_unit = jnp.dot(share, unit_two, precision=PRECISE, preferred_element_type=F32)
    pooled = mean_unit * norm_params[4] + norm_params[5]
    shrink = lax.rsqrt(jnp.sum(pooled * pooled, axis=1, keepdims=True) + POOL_EPS)
    embed = pooled * shrink

    payload = jnp.concatenate([embed.reshape(-1), target_mine])
    every = lax.all_gather(payload, ("dp", "mp"), axis=0)
    every_q = every[:, :model_width]
    every_p = every[:, model_width : 2 * model_width]
    target = (jnp.arange(pairs)[None, :].astype(F32) == every[:, 2 * model_width :][:, :1]).astype(F32)
    logits = lax.dot_general(every_q, every_p, (((1,), (1,)), ((), ())), precision=PRECISE) / SOFTMAX_TEMPER
    row_top = jnp.max(logits, axis=1, keepdims=True)
    exp_logits = jnp.exp(logits - row_top)
    row_total = jnp.sum(exp_logits, axis=1, keepdims=True)
    log_total = row_top[:, 0] + jnp.log(row_total[:, 0])
    loss_value = (jnp.sum(log_total - jnp.sum(logits * target, axis=1)) / pairs).reshape(1)
    grad_logits = (exp_logits / row_total - target) / (pairs * SOFTMAX_TEMPER)
    rank = lax.axis_index("dp") * lax.axis_size("mp") + core
    grad_uq = jnp.dot(lax.dynamic_index_in_dim(grad_logits, rank, 0, keepdims=True), every_p, precision=PRECISE)
    grad_up = jnp.dot(
        lax.dynamic_index_in_dim(grad_logits, rank, 1, keepdims=False)[None], every_q, precision=PRECISE
    )
    grad_embed = jnp.concatenate([grad_uq, grad_up], axis=0)

    grad_pooled = shrink * (grad_embed - embed * jnp.sum(grad_embed * embed, axis=1, keepdims=True))
    grad_gain_two = jnp.sum(grad_pooled * mean_unit, axis=0)
    grad_shift_two = jnp.sum(grad_pooled, axis=0)
    grad_unit_two = lax.dot_general(
        share, grad_pooled * norm_params[4], (((0,), (0,)), ((), ())), precision=PRECISE
    )
    grad_ztwo = normalize_back(unit_two, inverse_two, grad_unit_two)
    grad_bias_two = jnp.sum(grad_ztwo, axis=0)
    grad_two_low = grad_ztwo.astype(BF16)
    return grad_ztwo, grad_two_low, loss_value, grad_bias_two, grad_gain_two, grad_shift_two


def backward_plain(tokens, lens, kept, grad_ztwo, grad_two_low, norm_params, second_grads, spans):
    attn_w, ffn_w, projected, mixed, unit_one, inverse_one, first_low, active, slope = kept
    grad_bias_two, grad_gain_two, grad_shift_two = second_grads
    query_slots = spans[0][1]
    core = lax.axis_index("mp")
    cut = ffn_w[0].shape[2] // 2
    width = attn_w[0].shape[2]

    def two_parts(values):
        return values[:, :cut], values[:, cut:]

    def parted_product(left, halves):
        own = [mm_tn(left, part)[None] for part in two_parts(halves[0])]
        other = [mm_tn(left, part).astype(BF16)[None] for part in two_parts(halves[1])]
        return own, other

    down_grad = scatter_sum(*parted_product(grad_two_low, active))
    grad_hidden, grad_first = [], grad_ztwo
    for half in (1, 0):
        grad_hid = (mm(grad_two_low, ffn_w[half][1]) * slope[half]).astype(BF16)
        grad_hidden.insert(0, grad_hid)
        grad_first = grad_first + mm_nt(grad_hid, ffn_w[half][0])
    grad_hidden_bias = [jnp.sum(value.astype(F32), axis=0) for value in grad_hidden]
    up_grad = scatter_sum(*parted_product(first_low, grad_hidden))

    grad_gain_one = jnp.sum(grad_first * unit_one, axis=0)
    grad_shift_one = jnp.sum(grad_first, axis=0)
    grad_zone = normalize_back(unit_one, inverse_one, grad_first * norm_params[1])
    grad_bias_out = jnp.sum(grad_zone, axis=0)
    grad_one_low = grad_zone.astype(BF16)
    grad_tokens = grad_zone
    grad_query_bias, grad_value_bias, attn_parts = [None, None], [None, None], [None, None]
    for half in (1, 0):
        grad_out = mm(grad_one_low, attn_w[half][3]).astype(BF16)
        grad_proj = attend_back(projected[half], grad_out, lens, spans)
        grad_query_bias[half] = jnp.sum(grad_proj[0].astype(F32), axis=0)
        grad_value_bias[half] = jnp.sum(grad_proj[2].astype(F32), axis=0)
        in_grads = jnp.einsum("td,ste->sde", tokens, grad_proj, preferred_element_type=F32)
        out_grad = mm_tn(grad_one_low, mixed[half])
        parts = [in_grads[:2], jnp.stack([in_grads[2], out_grad])]
        attn_parts[half] = parts if half == 0 else [part.astype(BF16) for part in parts]
        for index in range(3):
            grad_tokens = grad_tokens + mm_nt(grad_proj[index], attn_w[half][index])
    attn_grads = scatter_sum(*attn_parts)

    col_parts = [
        jnp.concatenate([grad_query_bias[half], grad_value_bias[half], grad_hidden_bias[half]]) for half in range(2)
    ]
    norm_part = jnp.stack(
        [grad_bias_out, grad_gain_one, grad_shift_one, grad_bias_two, grad_gain_two, grad_shift_two]
    )
    norm_part = norm_part + swap_cores(norm_part)
    col_part = col_parts[0] + swap_cores(col_parts[1])
    small = lax.psum(jnp.concatenate([norm_part.reshape(-1), col_part]), "dp")
    norm_grad = small[: norm_part.size].reshape(norm_part.shape)
    col_grad = small[norm_part.size :]

    attn_grad = jnp.concatenate(attn_grads, axis=0)
    ffn_grad = jnp.stack([jnp.concatenate(parts, axis=-1)[0] for parts in (up_grad, down_grad)])
    grad_twin = swap_cores(grad_tokens)
    first_pair = jnp.where(core == 0, grad_tokens, grad_twin)
    second_pair = jnp.where(core == 0, grad_twin, grad_tokens)
    query_grad = jnp.stack([first_pair[:query_slots], second_pair[:query_slots]])
    passage_grad = jnp.stack([first_pair[query_slots:], second_pair[query_slots:]])
    return attn_grad, ffn_grad, norm_grad, col_grad, query_grad, passage_grad


def per_device(
    query_in,
    passage_in,
    query_len,
    passage_len,
    positive,
    step,
    rates,
    attn_master,
    attn_first,
    attn_second,
    attn_average,
    ffn_master,
    ffn_first,
    ffn_second,
    ffn_average,
    norm_params,
    norm_first,
    norm_second,
    norm_average,
    col_bias,
    col_first,
    col_second,
    col_average,
):
    size = lax.axis_size("dp")
    query_slots = query_in.shape[1]
    spans = ((0, query_slots), (query_slots, passage_in.shape[1]))
    pairs = query_in.shape[0] * size
    attn_state = (attn_master, attn_first, attn_second, attn_average)
    ffn_state = (ffn_master, ffn_first, ffn_second, ffn_average)
    norm_state = (norm_params, norm_first, norm_second, norm_average)
    col_state = (col_bias, col_first, col_second, col_average)
    if size == 16:
        kept = forward(
            query_in, passage_in, query_len, passage_len, positive, attn_master, ffn_master, col_bias, norm_params, spans,
            pairs,
        )
        grads = backward(query_len, passage_len, kept, norm_params, spans)
        return tuple(finish(step, rates, grads, kept[11], attn_state, ffn_state, norm_state, col_state))

    core = lax.axis_index("mp")

    def pick(values, index):
        return lax.dynamic_index_in_dim(values, index, 0, keepdims=False)

    tokens = jnp.concatenate([pick(query_in, core), pick(passage_in, core)], axis=0)
    lens = jnp.stack([pick(query_len, core), pick(passage_len, core)])
    target = jnp.broadcast_to(pick(positive, core).astype(F32), (LANES,))
    outs = forward_plain(tokens, lens, attn_master.astype(BF16), ffn_master.astype(BF16), col_bias, norm_params, spans)
    kept, z_two = outs[:9], outs[9]
    outs = loss_plain(z_two, lens, target, norm_params, spans, pairs)
    grad_ztwo, grad_two_low, loss_value, *second_grads = outs
    attn_grad, ffn_grad, norm_grad, col_grad, query_grad, passage_grad = backward_plain(
        tokens, lens, kept, grad_ztwo, grad_two_low, norm_params, second_grads, spans
    )
    step_count = step[0].astype(F32)
    outs = []
    for state, grad, rate, decay in (
        (attn_state, attn_grad, rates[3], DECAY_WEIGHT),
        (ffn_state, ffn_grad, rates[3], DECAY_WEIGHT),
        (norm_state, norm_grad, rates[4], 0.0),
        (col_state, col_grad, rates[4], 0.0),
    ):
        outs.extend(adam_update(*state, grad, rate, decay, rates, step_count))
    return (loss_value, query_grad, passage_grad, *outs, outs[0].astype(BF16), outs[4].astype(BF16))


def solution(mesh):
    matrix = P(None, "dp", "mp")
    rows = P("dp", None, None)
    placed = (rows, rows, P("dp"), P("dp"), P("dp"), P(), P(), *[matrix] * 8, *[P()] * 4, *[P("mp")] * 4)
    return jax.shard_map(
        per_device,
        mesh=mesh,
        in_specs=placed,
        out_specs=(P(), rows, rows, *[matrix] * 8, *[P()] * 4, *[P("mp")] * 4, matrix, matrix),
        check_vma=False,
    )
```

```python
import functools

import jax
import jax.numpy as jnp
from jax import lax
from jax.experimental import pallas as pl
from jax.experimental.pallas import tpu as pltpu
from jax.sharding import PartitionSpec as P

HD = 64
LANES = 128
NEG_FILL = -1e30
SOFTMAX_TEMPER = 0.02
NORM_EPS = 1e-12
POOL_EPS = 1e-06
DECAY_WEIGHT = 0.01
ADAM_EPS = 1e-08
PRECISE = lax.Precision.HIGHEST
MESH = pl.DeviceIdType.MESH
MIB = 2**20
F32 = jnp.float32
BF16 = jnp.bfloat16

ERFC_STEP = 0.46
ERFC_HALF = (
    0.5 * 0.26113873056821263,
    0.5 * 0.23637801512084577,
    0.5 * 0.3601812301921897,
    -0.5 * 0.18740624158431016,
    0.5 * 0.6751549397754679,
    -0.5 * 0.4305350150859377,
    0.5 * 0.0850883282904581,
)
ROOT_HALF = 0.7071067811865476
DENSITY = 0.3989422804014327


def gelu_and_slope(hidden):
    bell = jnp.exp(hidden * hidden * (-0.5))
    step = 1.0 / (1.0 + (ERFC_STEP * ROOT_HALF) * jnp.abs(hidden))
    tail = ERFC_HALF[6]
    for coefficient in ERFC_HALF[5::-1]:
        tail = tail * step + coefficient
    tail = tail * step * bell
    below = jnp.where(hidden >= 0.0, 1.0 - tail, tail)
    return hidden * below, below + hidden * bell * DENSITY


def mm(left, right):
    return jnp.dot(left, right, preferred_element_type=F32)


def mm_nt(left, right):
    return lax.dot_general(left, right, (((1,), (1,)), ((), ())), preferred_element_type=F32)


def mm_tn(left, right):
    return lax.dot_general(left, right, (((0,), (0,)), ((), ())), preferred_element_type=F32)


def first_head(shape):
    return lax.broadcasted_iota(jnp.int32, shape, 1) < HD


def stack_heads(values):
    place = lax.broadcasted_iota(jnp.int32, values.shape, 1) // HD
    zero = jnp.zeros_like(values)
    return jnp.concatenate(
        [jnp.where(place == head, values, zero) for head in range(values.shape[1] // HD)], axis=0
    )


def unstack_heads(values, count):
    place = lax.broadcasted_iota(jnp.int32, (count, values.shape[1]), 1) // HD
    total = None
    for head in range(values.shape[1] // HD):
        piece = jnp.where(place == head, values[head * count : (head + 1) * count], 0.0)
        total = piece if total is None else total + piece
    return total


def split_pair(values):
    lane = first_head(values.shape)
    zero = jnp.zeros_like(values)
    return jnp.where(lane, values, zero), jnp.where(lane, zero, values)


def probabilities(scores, length):
    valid = lax.broadcasted_iota(jnp.int32, scores.shape, 1) < length
    scores = jnp.where(valid, scores, NEG_FILL)
    weight = jnp.exp(scores - jnp.max(scores, axis=1, keepdims=True))
    return weight * (1.0 / jnp.sum(weight, axis=1, keepdims=True))


def normalize(values):
    center = values - jnp.mean(values, axis=-1, keepdims=True)
    spread = jnp.mean(center * center, axis=-1, keepdims=True)
    inverse = lax.rsqrt(spread + NORM_EPS)
    return center * inverse, inverse


def normalize_back(unit, inverse, grad_unit):
    return inverse * (
        grad_unit
        - jnp.mean(grad_unit, axis=-1, keepdims=True)
        - unit * jnp.mean(grad_unit * unit, axis=-1, keepdims=True)
    )


SCALE = HD**-0.5
SLAB = 16


class Mesh:
    def __init__(self):
        self.me = lax.axis_index("dp")
        self.core = lax.axis_index("mp")
        self.x, self.y, self.z = lax.rem(self.me, 2), lax.rem(self.me // 2, 2), self.me // 4
        self.x_peer = (self.index(self.z, self.y, 1 - self.x), self.core)
        self.y_peer = (self.index(self.z, 1 - self.y, self.x), self.core)
        self.c_peer = (self.me, 1 - self.core)
        self.z_peer = [None] + [(self.index(lax.rem(self.z + k, 4), self.y, self.x), self.core) for k in range(1, 4)]
        self.column = [lax.rem(self.z - k + 4, 4) for k in range(4)]

    def index(self, z, y, x):
        return (z * 2 + y) * 2 + x


def remote(source, target, send, recv, peer):
    return pltpu.make_async_remote_copy(
        src_ref=source, dst_ref=target, send_sem=send, recv_sem=recv, device_id=peer, device_id_type=MESH
    )


def forward_kernel(
    spans, total,
    query_len, passage_len, positive, query_ref, passage_ref, attn_ref, ffn_ref, col_ref, norm_ref,
    weight_out, proj_out, mixed_out, unit_out, inverse_out, low_out, active_out, slope_out, tokens_out,
    grad_out, grad_low_out, small_out,
    weight, proj, mixed, unit, inverse, low, active, slope, tokens, z_two, grad_low, small,
    col, attn_in, ffn_in, unit_two, slab, every,
    z_send, z_recv, x_send, x_recv, y_send, y_recv, d_send, d_recv, c_send, c_recv, b_send, b_recv, here_sem, out_sem,
    e_send, e_recv, p_send, p_recv, pz_send, pz_recv,
):
    at = Mesh()
    me, core = at.me, at.core
    my_rank = me * 2 + core
    rows, width = attn_ref.shape[1:]
    units = ffn_ref.shape[2]
    slots, model = tokens.shape

    def device(step):
        rank = lax.rem(my_rank + step, total)
        return (rank // 2, lax.rem(rank, 2))

    incoming = [
        pltpu.make_async_copy(attn_ref, attn_in, here_sem.at[0]),
        pltpu.make_async_copy(ffn_ref.at[0], ffn_in.at[0], here_sem.at[1]),
        pltpu.make_async_copy(ffn_ref.at[1], ffn_in.at[1], here_sem.at[2]),
        pltpu.make_async_copy(query_ref.at[core], tokens.at[pl.ds(*spans[0]), :], here_sem.at[3]),
        pltpu.make_async_copy(passage_ref.at[core], tokens.at[pl.ds(*spans[1]), :], here_sem.at[4]),
    ]
    for copy in incoming:
        copy.start()
    lens = (query_len[core], passage_len[core])
    barrier = pltpu.get_barrier_semaphore()
    for step in range(1, total):
        pl.semaphore_signal(barrier, inc=1, device_id=device(step), device_id_type=MESH)
    for line in range(col_ref.shape[0]):
        col[0, :, pl.ds(line * LANES, LANES)] = col_ref[pl.ds(line, 1), :]
    pl.semaphore_wait(barrier, total - 1)

    every_lane = pl.ds(0, units)
    cut = units * 2 // 3

    def column_lanes(q):
        return pl.ds(0, units if q < 2 else cut)

    def half_lanes(q, which):
        count = (units if q < 2 else cut) // 2
        return pl.ds(which * count, count)

    layer_lanes = pl.ds(cut, units - cut)

    def layer_half(which):
        count = (units - cut) // 2
        return pl.ds(cut + which * count, count)

    def block(q, index, lanes=None, count=1, far=0):
        lanes = column_lanes(q) if lanes is None else lanes
        return weight.at[far, q, pl.ds(pl.multiple_of(index * rows, rows), count * rows), lanes]

    sends = []
    stores = []

    def push(ref, send, recv, peer, target=None):
        copy = remote(ref, ref if target is None else target, send, recv, peer)
        copy.start()
        sends.append(copy)

    def landed(ref, send, recv, peer):
        remote(ref, ref, send, recv, peer).wait_recv()

    def store(source, target):
        copy = pltpu.make_async_copy(source, target, out_sem.at[len(stores)])
        copy.start()
        stores.append(copy)

    def cast_own(q):
        incoming[q].wait()
        here = pl.ds(pl.multiple_of(me * rows, rows), rows)
        if q == 0:
            for index in range(4):
                weight[0, 0, here, pl.ds(index * width, width)] = attn_in[index].astype(BF16)
        else:
            weight[0, q, here, :] = ffn_in[q - 1].astype(BF16)

    def own_along_column(q):
        for k in range(1, 4):
            push(block(q, me), z_send.at[q, k], z_recv.at[q, k], at.z_peer[k])

    def own_to_sides(q):
        push(block(q, me), x_send.at[q, 0], x_recv.at[q, 0], at.x_peer)
        push(block(q, me), y_send.at[q, 0], y_recv.at[q, 0], at.y_peer)

    def column_to_sides(q):
        for k in range(1, 4):
            ref = block(q, at.index(at.column[k], at.y, at.x))
            landed(ref, z_send.at[q, k], z_recv.at[q, k], at.z_peer[k])
            push(ref, x_send.at[q, k], x_recv.at[q, k], at.x_peer)
            push(ref, y_send.at[q, k], y_recv.at[q, k], at.y_peer)

    def round_corner(q, ks=range(4)):
        for k in ks:
            beside = at.index(at.column[k], at.y, 1 - at.x)
            landed(block(q, beside), x_send.at[q, k], x_recv.at[q, k], at.x_peer)
            push(block(q, beside, half_lanes(q, 0)), d_send.at[q, k, 0], d_recv.at[q, k, 0], at.y_peer)
            beside = at.index(at.column[k], 1 - at.y, at.x)
            landed(block(q, beside), y_send.at[q, k], y_recv.at[q, k], at.y_peer)
            push(block(q, beside, half_lanes(q, 1)), d_send.at[q, k, 1], d_recv.at[q, k, 1], at.x_peer)

    def layer_to_sides():
        ref = block(2, me, layer_lanes)
        push(ref, p_send.at[0], p_recv.at[0], at.x_peer)
        push(ref, p_send.at[1], p_recv.at[1], at.y_peer)

    def layer_round_corner():
        beside = at.index(at.z, at.y, 1 - at.x)
        landed(block(2, beside, layer_lanes), p_send.at[0], p_recv.at[0], at.x_peer)
        push(block(2, beside, layer_half(0)), p_send.at[2], p_recv.at[2], at.y_peer)
        beside = at.index(at.z, 1 - at.y, at.x)
        landed(block(2, beside, layer_lanes), p_send.at[1], p_recv.at[1], at.y_peer)
        push(block(2, beside, layer_half(1)), p_send.at[3], p_recv.at[3], at.x_peer)

    def layer_along_column():
        across = at.index(at.z, 1 - at.y, 1 - at.x)
        landed(block(2, across, layer_half(0)), p_send.at[2], p_recv.at[2], at.y_peer)
        landed(block(2, across, layer_half(1)), p_send.at[3], p_recv.at[3], at.x_peer)
        for k in range(1, 4):
            push(block(2, at.index(at.z, 0, 0), layer_lanes, 4), pz_send.at[k], pz_recv.at[k], at.z_peer[k])

    def to_other_core(q, ks=range(4)):
        for k in ks:
            across = at.index(at.column[k], 1 - at.y, 1 - at.x)
            landed(block(q, across, half_lanes(q, 0)), d_send.at[q, k, 0], d_recv.at[q, k, 0], at.y_peer)
            landed(block(q, across, half_lanes(q, 1)), d_send.at[q, k, 1], d_recv.at[q, k, 1], at.x_peer)
            layer = at.index(at.column[k], 0, 0)
            if q == 2 and k:
                landed(block(2, layer, layer_lanes, 4), pz_send.at[k], pz_recv.at[k], at.z_peer[k])
            push(
                block(q, layer, every_lane, 4), c_send.at[q, k], c_recv.at[q, k], at.c_peer,
                block(q, layer, every_lane, 4, 1),
            )

    def from_other_core(q):
        for k in range(4):
            layer = at.index(at.column[k], 0, 0)
            landed(block(q, layer, every_lane, 4, 1), c_send.at[q, k], c_recv.at[q, k], at.c_peer)

    def project(half):
        bias = jnp.concatenate(
            [
                col[half, :, pl.ds(0, width)],
                jnp.zeros((1, width), F32),
                col[half, :, pl.ds(width, width)],
            ],
            axis=1,
        )
        proj[half] = (mm(tokens[...], weight[half, 0, :, pl.ds(0, 3 * width)]) + bias).astype(BF16)

    def query_heads(half):
        place = pl.ds(*spans[0])
        queries = stack_heads(proj[half, place, pl.ds(0, width)] * jnp.asarray(SCALE, BF16))
        probs = probabilities(mm_nt(queries, proj[half, place, pl.ds(width, width)]), lens[0])
        value = mm(probs.astype(BF16), proj[half, place, pl.ds(2 * width, width)])
        mixed[half, place, :] = unstack_heads(value, spans[0][1]).astype(BF16)

    def passage_heads(half, pair):
        place = pl.ds(*spans[1])
        queries = proj[half, place, pl.ds(pair * LANES, LANES)]
        keys = split_pair(proj[half, place, pl.ds(width + pair * LANES, LANES)] * jnp.asarray(SCALE, BF16))
        values = proj[half, place, pl.ds(2 * width + pair * LANES, LANES)]
        scores = [mm_nt(queries, key) for key in keys]
        outs = [mm(probabilities(score, lens[1]).astype(BF16), values) for score in scores]
        mixed[half, place, pl.ds(pair * LANES, LANES)] = jnp.where(first_head(outs[0].shape), *outs).astype(BF16)

    def first_norm():
        step = 192
        for start in range(0, slots, step):
            place = pl.ds(start, step)
            value = tokens[place, :].astype(F32) + norm_ref[pl.ds(0, 1), :]
            for half in range(2):
                value = value + mm_nt(mixed[half, place, :], weight[half, 0, :, pl.ds(3 * width, width)])
            normed, scale = normalize(value)
            unit[place, :] = normed
            inverse[place, :] = jnp.broadcast_to(scale, (step, LANES))
            value = normed * norm_ref[pl.ds(1, 1), :] + norm_ref[pl.ds(2, 1), :]
            z_two[place, :] = value + norm_ref[pl.ds(3, 1), :]
            low[place, :] = value.astype(BF16)

    tile = 256

    def up(half, part):
        for start in range(part * units // 2, (part + 1) * units // 2, tile):
            lanes = pl.ds(start, tile)
            hidden = mm(low[...], weight[half, 1, :, lanes]) + col[half, :, pl.ds(2 * width + start, tile)]
            value, grad = gelu_and_slope(hidden)
            active[half, :, lanes] = value.astype(BF16)
            slope[half, :, lanes] = grad

    def down(half):
        z_two[...] = z_two[...] + mm_nt(active[half], weight[half, 2])

    cast_own(0)
    own_along_column(0)
    own_to_sides(0)
    push(col.at[0], b_send, b_recv, at.c_peer, col.at[1])
    cast_own(1)
    own_to_sides(1)
    cast_own(2)
    layer_to_sides()
    own_to_sides(2)
    incoming[3].wait()
    incoming[4].wait()
    store(tokens, tokens_out)
    column_to_sides(0)
    layer_round_corner()
    own_along_column(1)
    round_corner(0)
    column_to_sides(1)
    own_along_column(2)
    layer_along_column()
    to_other_core(0)
    project(0)
    query_heads(0)
    passage_heads(0, 0)
    round_corner(1, (0,))
    passage_heads(0, 1)
    round_corner(1, (1,))
    passage_heads(0, 2)
    landed(col.at[1], b_send, b_recv, at.c_peer)
    from_other_core(0)
    project(1)
    for half in range(2):
        store(weight.at[half, 0], weight_out.at[half, 0])
    store(proj, proj_out)
    round_corner(1, (2,))
    query_heads(1)
    round_corner(1, (3,))
    passage_heads(1, 0)
    column_to_sides(2)
    passage_heads(1, 1)
    passage_heads(1, 2)
    store(mixed, mixed_out)
    first_norm()
    store(unit, unit_out)
    store(inverse, inverse_out)
    store(low, low_out)
    to_other_core(1)
    round_corner(2, (0,))
    up(0, 0)
    round_corner(2, (1,))
    up(0, 1)
    store(slope.at[0], slope_out.at[0])
    store(weight.at[0, 1], weight_out.at[0, 1])
    round_corner(2, (2,))
    from_other_core(1)
    up(1, 0)
    round_corner(2, (3,))
    up(1, 1)
    store(slope.at[1], slope_out.at[1])
    store(weight.at[1, 1], weight_out.at[1, 1])
    store(active, active_out)
    to_other_core(2)
    store(weight.at[0, 2], weight_out.at[0, 2])
    down(0)
    from_other_core(2)
    store(weight.at[1, 2], weight_out.at[1, 2])
    down(1)

    pieces = model // LANES
    gain, shift = norm_ref[pl.ds(4, 1), :], norm_ref[pl.ds(5, 1), :]
    embeds, shrinks, means, inverses, valids = [], [], [], [], []
    for index, (start, count) in enumerate(spans):
        normed, scale = normalize(z_two[pl.ds(start, count), :])
        unit_two[pl.ds(start, count), :] = normed
        valid = lax.broadcasted_iota(jnp.int32, (count, 1), 0) < lens[index]
        mean = jnp.sum(jnp.where(valid, normed, 0.0), axis=0, keepdims=True) / lens[index].astype(F32)
        pooled = mean * gain + shift
        shrink = lax.rsqrt(jnp.sum(pooled * pooled, axis=1, keepdims=True) + POOL_EPS)
        embed = pooled * shrink
        for piece in range(pieces):
            slab[pl.ds(index * pieces + piece, 1), :] = embed[:, piece * LANES : (piece + 1) * LANES]
        embeds.append(embed)
        shrinks.append(shrink)
        means.append(mean)
        inverses.append(jnp.where(valid, scale, 0.0))
    slab[pl.ds(2 * pieces, 1), :] = jnp.full((1, LANES), positive[core], jnp.int32).astype(F32)
    copies = []
    for step in range(1, total):
        copy = remote(slab, every.at[my_rank], e_send.at[step], e_recv.at[step], device(step))
        copy.start()
        copies.append(copy)
    sends.extend(copies)
    every[my_rank] = slab[...]
    for copy in copies:
        copy.wait_recv()

    queries = jnp.concatenate([every[:, piece, :] for piece in range(pieces)], axis=1)
    passages = jnp.concatenate([every[:, pieces + piece, :] for piece in range(pieces)], axis=1)
    wanted = every[:, 2 * pieces, :][:, :1]
    logits = lax.dot_general(
        queries, passages, (((1,), (1,)), ((), ())), precision=PRECISE, preferred_element_type=F32
    ) / SOFTMAX_TEMPER
    place = lax.broadcasted_iota(jnp.int32, logits.shape, 1)
    target = (place.astype(F32) == wanted).astype(F32)
    top = jnp.max(logits, axis=1, keepdims=True)
    weights = jnp.exp(logits - top)
    row_total = jnp.sum(weights, axis=1, keepdims=True)
    log_total = top + jnp.log(row_total)
    loss = jnp.sum(log_total - jnp.sum(logits * target, axis=1, keepdims=True), axis=0, keepdims=True) / total
    grad_logits = (weights / row_total - target) / (total * SOFTMAX_TEMPER)
    grad_column = jnp.sum(jnp.where(place == my_rank, grad_logits, 0.0), axis=1, keepdims=True)
    value = jnp.dot(grad_logits, passages, precision=PRECISE, preferred_element_type=F32)
    line = lax.broadcasted_iota(jnp.int32, value.shape, 0)
    grad_embeds = (
        jnp.sum(jnp.where(line == my_rank, value, 0.0), axis=0, keepdims=True),
        jnp.sum(grad_column * queries, axis=0, keepdims=True),
    )

    grad_gain, grad_shift, grad_bias = 0.0, 0.0, 0.0
    for index, (start, count) in enumerate(spans):
        embed, grad_embed = embeds[index], grad_embeds[index]
        grad_pooled = shrinks[index] * (grad_embed - embed * jnp.sum(grad_embed * embed, axis=1, keepdims=True))
        grad_gain = grad_gain + grad_pooled * means[index]
        grad_shift = grad_shift + grad_pooled
        spread = grad_pooled * gain / lens[index].astype(F32)
        centered = spread - jnp.mean(spread, axis=1, keepdims=True)
        normed = unit_two[pl.ds(start, count), :]
        value = inverses[index] * (centered - normed * jnp.mean(spread * normed, axis=1, keepdims=True))
        z_two[pl.ds(start, count), :] = value
        grad_low[pl.ds(start, count), :] = value.astype(BF16)
        grad_bias = grad_bias + jnp.sum(value, axis=0, keepdims=True)
    store(grad_low, grad_low_out)
    store(z_two, grad_out)
    small[pl.ds(0, 1), :] = grad_bias
    small[pl.ds(1, 1), :] = grad_gain
    small[pl.ds(2, 1), :] = grad_shift
    small[pl.ds(3, 1), :] = jnp.broadcast_to(loss, (1, model))
    small[pl.ds(4, 4), :] = jnp.zeros((4, model), F32)
    store(small, small_out)
    for copy in sends:
        copy.wait_send()
    for copy in stores:
        copy.wait()


def forward(query_in, passage_in, query_len, passage_len, positive, attn_master, ffn_master, col_bias, norm_params, spans, total):
    rows, width = attn_master.shape[1:]
    units = ffn_master.shape[2]
    slots, model = spans[1][0] + spans[1][1], query_in.shape[2]
    dma = pltpu.SemaphoreType.DMA
    col = col_bias.reshape(-1, LANES)
    anywhere = pl.BlockSpec(memory_space=pltpu.HBM)
    vmem = pl.BlockSpec(memory_space=pltpu.VMEM)
    smem = pl.BlockSpec(memory_space=pltpu.SMEM)
    results = (
        ((2, 3, model, units), BF16),
        ((2, slots, 3 * width), BF16),
        ((2, slots, width), BF16),
        ((slots, model), F32),
        ((slots, LANES), F32),
        ((slots, model), BF16),
        ((2, slots, units), BF16),
        ((2, slots, units), F32),
        ((slots, model), BF16),
        ((slots, model), F32),
        ((slots, model), BF16),
        ((8, model), F32),
    )
    return pl.pallas_call(
        functools.partial(forward_kernel, spans, total),
        out_shape=tuple(jax.ShapeDtypeStruct(*result) for result in results),
        in_specs=[smem] * 3 + [anywhere] * 4 + [vmem] * 2,
        out_specs=(anywhere,) * len(results),
        scratch_shapes=[pltpu.VMEM(*result) for result in results]
        + [
            pltpu.VMEM((2, 1, col_bias.shape[0]), F32),
            pltpu.VMEM(attn_master.shape, F32),
            pltpu.VMEM(ffn_master.shape, F32),
            pltpu.VMEM((slots, model), F32),
            pltpu.VMEM((SLAB, LANES), F32),
            pltpu.VMEM((total, SLAB, LANES), F32),
        ]
        + [dma((3, 4))] * 6
        + [dma((3, 4, 2))] * 2
        + [dma((3, 4))] * 2
        + [dma(()), dma(()), dma((5,)), dma((20,)), dma((total,)), dma((total,))]
        + [dma((4,))] * 4,
        compiler_params=pltpu.CompilerParams(collective_id=0, has_side_effects=True, vmem_limit_bytes=58 * MIB),
        name="forward",
    )(query_len, passage_len, positive, query_in, passage_in, attn_master, ffn_master, col, norm_params)


def backward_kernel(
    spans,
    query_len, passage_len, weight_ref, proj_ref, mixed_ref, unit_ref, inverse_ref, low_ref, active_ref, slope_ref,
    tokens_ref, grad_ref, grad_low_ref, norm_ref, small_ref,
    attn_out, ffn_out, small_out, col_out, query_out, passage_out,
    weight, proj, mixed, inverse, low, active, slope, tokens, total, down, grad_out, grad_proj,
    temp, far_send, far_recv, kept, one_send, one_recv, two_send, two_recv, z_send, z_recv, result, vector, vec_send,
    vec_recv, col,
    load_sem, slope_sem, c_send, c_recv, s1_send, s1_recv, s2_send, s2_recv, s3_send, s3_recv,
    v_send, v_recv, t_send, t_recv, credit, out_sem, layer_recv,
):
    at = Mesh()
    me, core = at.me, at.core
    slots, model = tokens.shape
    width = grad_out.shape[1]
    rows = model // 16
    lens = (query_len[core], passage_len[core])
    near_peer = (at.index(at.z + 1 - 2 * lax.rem(at.z, 2), at.y, at.x), core)
    over_peer = at.z_peer[2]

    sends = {}
    stores = []
    loads = {}

    def load(name, *pairs):
        copies = []
        for source, target in pairs:
            copy = pltpu.make_async_copy(source, target, load_sem.at[sum(len(v) for v in loads.values()) + len(copies)])
            copy.start()
            copies.append(copy)
        loads[name] = copies

    def ready(name):
        for copy in loads[name]:
            copy.wait()

    def store(source, target):
        copy = pltpu.make_async_copy(source, target, out_sem.at[len(stores)])
        copy.start()
        stores.append(copy)

    def push(name, source, target, send, recv, peer):
        copy = remote(source, target, send, recv, peer)
        copy.start()
        sends[name] = copy

    def landed(target, send, recv, peer):
        remote(target, target, send, recv, peer).wait_recv()

    lanes_of = [pl.ds(t * width, width) for t in range(4)]
    pair_lanes = (pl.ds(0, 2 * width), pl.ds(2 * width, 2 * width))

    def slope_tile(half, t):
        index = half * 4 + t
        return pltpu.make_async_copy(slope_ref.at[half, :, lanes_of[t]], slope.at[t % 2], slope_sem.at[index])

    load("down", (grad_low_ref, down))
    load("active1", (active_ref.at[1], active.at[1]))
    barrier = pltpu.get_barrier_semaphore()
    for peer in [*at.z_peer[1:], at.x_peer, at.y_peer, at.c_peer]:
        pl.semaphore_signal(barrier, inc=1, device_id=peer, device_id_type=MESH)
    load("down1", (weight_ref.at[1, 2], weight.at[0]))
    slope_tile(1, 0).start()
    slope_tile(1, 1).start()
    load("active0", (active_ref.at[0], active.at[0]))

    def far_slot(q):
        return q % 2

    def send_far(q, t, value):
        if q == 2:
            sends[("c", 0, t)].wait_send()
        far_send[far_slot(q), t] = value.astype(BF16)
        push(
            ("c", q, t), far_send.at[far_slot(q), t], far_recv.at[far_slot(q), t], c_send.at[q, t], c_recv.at[q, t],
            at.c_peer,
        )

    def side(t):
        steps = ((at.x, at.x_peer), (at.y, at.y_peer))
        return steps if t % 2 == 0 else steps[::-1]

    def block(index, count=1):
        return pl.ds(pl.multiple_of(index * rows, rows), count * rows)

    def first_step(q, t, lanes):
        landed(far_recv.at[far_slot(q), t], c_send.at[q, t], c_recv.at[q, t], at.c_peer)
        (bit, peer), _ = side(t)
        for layer in range(4):
            for other in range(2):
                if t % 2 == 0:
                    mine, theirs = at.index(layer, other, bit), at.index(layer, other, 1 - bit)
                else:
                    mine, theirs = at.index(layer, bit, other), at.index(layer, 1 - bit, other)
                place = pl.ds((layer * 2 + other) * rows, rows)
                far = far_recv[far_slot(q), t, block(theirs), :].astype(F32)
                one_send[q, t, place, :] = (temp[block(theirs), lanes] + far).astype(BF16)
                far = far_recv[far_slot(q), t, block(mine), :].astype(F32)
                kept[q, t, place, :] = temp[block(mine), lanes] + far
        push(("1", q, t), one_send.at[q, t], one_recv.at[q, t], s1_send.at[q, t], s1_recv.at[q, t], peer)

    def second_step(q, t):
        (_, before), (bit, peer) = side(t)
        landed(one_recv.at[q, t], s1_send.at[q, t], s1_recv.at[q, t], before)
        for layer in range(4):
            theirs = block(layer * 2 + 1 - bit)
            value = kept[q, t, theirs, :] + one_recv[q, t, theirs, :].astype(F32)
            two_send[q, t, pl.ds(layer * rows, rows), :] = value.astype(BF16)
            mine = block(layer * 2 + bit)
            kept[q, t, mine, :] = kept[q, t, mine, :] + one_recv[q, t, mine, :].astype(F32)
        push(("2", q, t), two_send.at[q, t], two_recv.at[q, t], s2_send.at[q, t], s2_recv.at[q, t], peer)

    def third_step(q, t):
        _, (bit, before) = side(t)
        landed(two_recv.at[q, t], s2_send.at[q, t], s2_recv.at[q, t], before)
        for k in range(1, 4):
            layer = lax.rem(at.z + k, 4)
            value = kept[q, t, block(layer * 2 + bit), :] + two_recv[q, t, block(layer), :].astype(F32)
            z_send[q, t, k - 1] = value.astype(BF16)
            push(
                ("3", q, t, k), z_send.at[q, t, k - 1], z_recv.at[q, t, k - 1], s3_send.at[q, t, k], s3_recv.at[q, t, k],
                at.z_peer[k],
            )
        result[q, t] = kept[q, t, block(at.z * 2 + bit), :] + two_recv[q, t, block(at.z), :].astype(F32)

    def last_step(q, t):
        for k in range(1, 4):
            landed(z_recv.at[q, t, k - 1], s3_send.at[q, t, k], s3_recv.at[q, t, k], at.z_peer[k])
        value = result[q, t]
        for k in range(3):
            value = value + z_recv[q, t, k].astype(F32)
        result[q, t] = value
        store_result(q, t)

    def store_result(q, t):
        if q < 2:
            store(result.at[q, t], ffn_out.at[1 - q, :, lanes_of[t]])
        elif t == 3:
            store(result.at[q, t], attn_out.at[3])
        else:
            for index in range(3):
                store(result.at[q, t, :, pl.ds(index * LANES, LANES)], attn_out.at[index, :, pl.ds(t * LANES, LANES)])

    def layer_first_step(q, t, lanes):
        landed(far_recv.at[far_slot(q), t], c_send.at[q, t], c_recv.at[q, t], at.c_peer)
        for k in range(1, 4):
            theirs = block(at.index(lax.rem(at.z + k, 4), 0, 0), 4)
            value = temp[theirs, lanes] + far_recv[far_slot(q), t, theirs, :].astype(F32)
            if k < 3:
                source = one_send.at[q, t, pl.ds((k - 1) * 4 * rows, 4 * rows), :]
            else:
                source = two_send.at[q, t]
            source[...] = value.astype(BF16)
            push(
                ("1", q, t, k), source, layer_recv.at[t, k - 1], s3_send.at[q, t, k],
                s3_recv.at[q, t, k], at.z_peer[k],
            )
        mine = block(at.index(at.z, 0, 0), 4)
        kept[q, t, pl.ds(0, 4 * rows), :] = temp[mine, lanes] + far_recv[far_slot(q), t, mine, :].astype(F32)

    def layer_second_step(q, t):
        for k in range(1, 4):
            landed(layer_recv.at[t, k - 1], s3_send.at[q, t, k], s3_recv.at[q, t, k], at.z_peer[k])
        value = kept[q, t, pl.ds(0, 4 * rows), :]
        for k in range(3):
            value = value + layer_recv[t, k].astype(F32)
        kept[q, t, pl.ds(0, 4 * rows), :] = value
        for line in range(2):
            z_send[q, t, line] = kept[q, t, block(line * 2 + 1 - at.x), :].astype(BF16)
        push(
            ("2", q, t), z_send.at[q, t, pl.ds(0, 2)], z_recv.at[q, t, pl.ds(0, 2)], s1_send.at[q, t], s1_recv.at[q, t],
            at.x_peer,
        )

    def layer_third_step(q, t):
        landed(z_recv.at[q, t, pl.ds(0, 2)], s1_send.at[q, t], s1_recv.at[q, t], at.x_peer)
        theirs = kept[q, t, block((1 - at.y) * 2 + at.x), :] + z_recv[q, t, 1 - at.y].astype(F32)
        z_send[q, t, 2] = theirs.astype(BF16)
        push(
            ("3", q, t), z_send.at[q, t, 2], z_recv.at[q, t, 2], s2_send.at[q, t], s2_recv.at[q, t],
            at.y_peer,
        )
        result[q, t] = kept[q, t, block(at.y * 2 + at.x), :] + z_recv[q, t, at.y].astype(F32)

    def layer_last_step(q, t):
        landed(z_recv.at[q, t, 2], s2_send.at[q, t], s2_recv.at[q, t], at.y_peer)
        result[q, t] = result[q, t] + z_recv[q, t, 2].astype(F32)
        store_result(q, t)

    def far_product(q, left, right):
        for pair in (1, 0) if q == 0 else (0, 1):
            value = mm_tn(left[...], right[:, pair_lanes[pair]])
            send_far(q, 2 * pair, value[:, :width])
            send_far(q, 2 * pair + 1, value[:, width:])

    def own_product(q, left, right, pair):
        temp[...] = mm_tn(left[...], right[:, pair_lanes[pair]])
        step = layer_first_step if (q, pair) == (0, 0) else first_step
        step(q, 2 * pair, lanes_of[0])
        step(q, 2 * pair + 1, lanes_of[1])

    def hidden_grad(half, slot, pair, following):
        for t in (2 * pair, 2 * pair + 1):
            slope_tile(half, t).wait()
        value = mm(down[...], weight[slot, :, pair_lanes[pair]])
        for side_of, t in enumerate((2 * pair, 2 * pair + 1)):
            piece = (value[:, side_of * width : (side_of + 1) * width] * slope[side_of]).astype(BF16)
            active[half, :, lanes_of[t]] = piece
            vec = vector if half == 0 else vec_send.at[0]
            vec[pl.ds(9 + pair, 1), lanes_of[side_of]] = jnp.sum(piece.astype(F32), axis=0, keepdims=True)
        if following is not None:
            for t in (0, 1):
                slope_tile(following[0], 2 * following[1] + t).start()

    def add_back(source, slot, lanes):
        total[...] = total[...] + mm_nt(source, weight[slot, :, lanes])

    def first_norm_back():
        sums = [None, None, None]
        step = 192
        for start in range(0, slots, step):
            place = pl.ds(start, step)
            grad = total[place, :]
            normed = jnp.concatenate([slope[0, place, :], slope[1, place, :]], axis=1)
            back = normalize_back(normed, inverse[place, pl.ds(0, 1)], grad * norm_ref[pl.ds(1, 1), :])
            for index, value in enumerate((back, grad * normed, grad)):
                value = jnp.sum(value, axis=0, keepdims=True)
                sums[index] = value if sums[index] is None else sums[index] + value
            total[place, :] = back
            down[place, :] = back.astype(BF16)
        for index in range(3):
            vector[pl.ds(index, 1), :] = sums[index]
            vec_send[0, pl.ds(index, 1), :] = sums[index]

    def out_grad(slot):
        grad_out[...] = mm(down[...], weight[slot, :, lanes_of[3]]).astype(BF16)

    def query_back(half):
        place = pl.ds(*spans[0])
        queries = stack_heads(proj[half, place, lanes_of[0]])
        grads = stack_heads(grad_out[place, :])
        keys = proj[half, place, lanes_of[1]]
        probs = probabilities(mm_nt(queries * jnp.asarray(SCALE, BF16), keys), lens[0])
        grad_probs = mm_nt(grads, proj[half, place, lanes_of[2]])
        inner = jnp.sum(probs * grad_probs, axis=1, keepdims=True)
        grad_scores = (probs * (grad_probs - inner)).astype(BF16)
        value = unstack_heads(mm(grad_scores, keys), spans[0][1]) * SCALE
        grad_proj[half, place, lanes_of[0]] = value.astype(BF16)
        grad_proj[half, place, lanes_of[1]] = (mm_tn(grad_scores, queries) * SCALE).astype(BF16)
        grad_proj[half, place, lanes_of[2]] = mm_tn(probs.astype(BF16), grads).astype(BF16)

    def passage_back(half, pair):
        place = pl.ds(*spans[1])
        spot = [pl.ds(index * width + pair * LANES, LANES) for index in range(3)]
        queries, keys = proj[half, place, spot[0]], proj[half, place, spot[1]]
        grads = grad_out[place, pl.ds(pair * LANES, LANES)]
        scores = [mm_nt(queries, key) for key in split_pair(keys * jnp.asarray(SCALE, BF16))]
        grad_probs = [mm_nt(grads, value) for value in split_pair(proj[half, place, spot[2]])]
        outs = []
        for head in range(2):
            probs = probabilities(scores[head], lens[1])
            inner = jnp.sum(probs * grad_probs[head], axis=1, keepdims=True)
            grad_scores = (probs * (grad_probs[head] - inner)).astype(BF16)
            outs.append(
                (mm(grad_scores, keys) * SCALE, mm_tn(grad_scores, queries) * SCALE, mm_tn(probs.astype(BF16), grads))
            )
        lane = first_head(queries.shape)
        for index in range(3):
            grad_proj[half, place, spot[index]] = jnp.where(lane, outs[0][index], outs[1][index]).astype(BF16)

    def pair_product(half, pair):
        spot = [pl.ds(index * width + pair * LANES, LANES) for index in range(3)]
        return mm_tn(tokens[...], jnp.concatenate([grad_proj[half, :, lanes] for lanes in spot], axis=1))

    def attn_biases(half):
        vec = vector if half == 0 else vec_send.at[0]
        for index in (0, 1):
            value = grad_proj[half, :, lanes_of[2 * index]].astype(F32)
            vec[pl.ds(8, 1), lanes_of[index]] = jnp.sum(value, axis=0, keepdims=True)

    def vector_step(step, peer):
        if step:
            vec_send[step] = vector[...]
        push(("v", step), vec_send.at[step], vec_recv.at[step], v_send.at[step], v_recv.at[step], peer)

    def vector_sum(step, peer):
        landed(vec_recv.at[step], v_send.at[step], v_recv.at[step], peer)
        vector[...] = vector[...] + vec_recv[step]

    for target in (vector, vec_send.at[0]):
        target[pl.ds(3, 3), :] = small_ref[pl.ds(0, 3), :]
        target[pl.ds(6, 2), :] = jnp.zeros((2, model), F32)
        target[pl.ds(11, 5), :] = jnp.zeros((5, model), F32)

    ready("down")
    ready("active1")
    pl.semaphore_wait(barrier, 6)
    far_product(0, down, active.at[1])
    load("down0", (weight_ref.at[0, 2], weight.at[1]))
    load("low", (low_ref, low))
    load("up1", (weight_ref.at[1, 1], weight.at[2]))
    ready("active0")
    own_product(0, down, active.at[0], 1)
    ready("down1")
    hidden_grad(1, 0, 0, (1, 1))
    own_product(0, down, active.at[0], 0)
    pl.semaphore_signal(credit, inc=1, device_id=at.c_peer, device_id_type=MESH)
    hidden_grad(1, 0, 1, (0, 0))
    load("up0", (weight_ref.at[0, 1], weight.at[0]))
    load("total", (grad_ref, total))
    load("inverse", (inverse_ref, inverse))
    ready("low")
    far_product(1, low, active.at[1])
    ready("down0")
    hidden_grad(0, 1, 0, (0, 1))
    ready("total")
    ready("up1")
    add_back(active[1], 2, pl.ds(0, 4 * width))
    hidden_grad(0, 1, 1, None)
    load("unit", *[(unit_ref.at[:, lanes_of[t]], slope.at[t]) for t in range(2)])
    load("attn1", (weight_ref.at[1, 0], weight.at[1]))
    load("proj", (proj_ref, proj), (mixed_ref, mixed), (tokens_ref, tokens))
    load("attn0", (weight_ref.at[0, 0], weight.at[2]))
    second_step(0, 2)
    own_product(1, low, active.at[0], 0)
    second_step(0, 3)
    own_product(1, low, active.at[0], 1)
    ready("up0")
    add_back(active[0], 0, pl.ds(0, 4 * width))
    ready("inverse")
    ready("unit")
    first_norm_back()
    ready("proj")
    pl.semaphore_wait(credit, 1)
    send_far(2, 3, mm_tn(down[...], mixed[1]))
    ready("attn1")
    out_grad(1)
    query_back(1)
    temp[:, lanes_of[0]] = mm_tn(down[...], mixed[0])
    first_step(2, 3, lanes_of[0])
    second_step(1, 0)
    second_step(1, 1)
    passage_back(1, 0)
    send_far(2, 0, pair_product(1, 0))
    layer_second_step(0, 0)
    third_step(0, 2)
    third_step(0, 3)
    passage_back(1, 1)
    send_far(2, 1, pair_product(1, 1))
    passage_back(1, 2)
    send_far(2, 2, pair_product(1, 2))
    attn_biases(1)
    vector_step(0, at.c_peer)
    second_step(1, 2)
    second_step(1, 3)
    ready("attn0")
    out_grad(2)
    query_back(0)
    layer_second_step(0, 1)
    layer_third_step(0, 0)
    third_step(1, 0)
    third_step(1, 1)
    passage_back(0, 0)
    temp[:, lanes_of[1]] = pair_product(0, 0)
    first_step(2, 0, lanes_of[1])
    last_step(0, 2)
    last_step(0, 3)
    passage_back(0, 1)
    temp[:, lanes_of[0]] = pair_product(0, 1)
    first_step(2, 1, lanes_of[0])
    second_step(2, 3)
    layer_third_step(0, 1)
    passage_back(0, 2)
    temp[:, lanes_of[1]] = pair_product(0, 2)
    first_step(2, 2, lanes_of[1])
    third_step(1, 2)
    third_step(1, 3)
    attn_biases(0)
    vector_sum(0, at.c_peer)
    vector_step(1, at.x_peer)
    add_back(grad_proj[1], 1, pl.ds(0, 3 * width))
    second_step(2, 0)
    add_back(grad_proj[0], 2, pl.ds(0, 3 * width))
    for index, target in ((0, query_out), (1, passage_out)):
        part = total.at[pl.ds(*spans[index]), :]
        store(part, target.at[core])
        push(("t", index), part, target.at[core], t_send.at[index], t_recv.at[index], at.c_peer)
    third_step(2, 3)
    vector_sum(1, at.x_peer)
    vector_step(2, at.y_peer)
    layer_last_step(0, 0)
    layer_last_step(0, 1)
    last_step(1, 0)
    last_step(1, 1)
    second_step(2, 1)
    third_step(2, 0)
    vector_sum(2, at.y_peer)
    vector_step(3, near_peer)
    last_step(1, 2)
    last_step(1, 3)
    second_step(2, 2)
    vector_sum(3, near_peer)
    vector_step(4, over_peer)
    third_step(2, 1)
    last_step(2, 3)
    last_step(2, 0)
    vector_sum(4, over_peer)
    store(vector.at[pl.ds(0, 8), :], small_out)
    for line in range(3):
        for piece in range(model // LANES):
            col[pl.ds(line * (model // LANES) + piece, 1), :] = vector[pl.ds(8 + line, 1), pl.ds(piece * LANES, LANES)]
    store(col, col_out)
    third_step(2, 2)
    last_step(2, 1)
    last_step(2, 2)
    for index, target in ((0, query_out), (1, passage_out)):
        landed(target.at[1 - core], t_send.at[index], t_recv.at[index], at.c_peer)
    for copy in stores:
        copy.wait()
    for name, copy in sends.items():
        if name[:2] != ("c", 0):
            copy.wait_send()


def backward(query_len, passage_len, kept, norm_params, spans):
    weight, proj, mixed, unit, inverse, low, active, slope, tokens, grad_ztwo, grad_low, small = kept
    slots, model = tokens.shape
    width = mixed.shape[2]
    rows = model // 16
    anywhere = pl.BlockSpec(memory_space=pltpu.HBM)
    vmem = pl.BlockSpec(memory_space=pltpu.VMEM)
    smem = pl.BlockSpec(memory_space=pltpu.SMEM)
    dma = pltpu.SemaphoreType.DMA
    lines = 3 * model // LANES
    scratch = [
        pltpu.VMEM((3, model, 4 * width), BF16),
        pltpu.VMEM(proj.shape, BF16),
        pltpu.VMEM(mixed.shape, BF16),
        pltpu.VMEM(inverse.shape, F32),
        pltpu.VMEM(low.shape, BF16),
        pltpu.VMEM(active.shape, BF16),
        pltpu.VMEM((2, slots, width), F32),
        pltpu.VMEM(tokens.shape, BF16),
        pltpu.VMEM((slots, model), F32),
        pltpu.VMEM((slots, model), BF16),
        pltpu.VMEM((slots, width), BF16),
        pltpu.VMEM((2, slots, 3 * width), BF16),
        pltpu.VMEM((model, 2 * width), F32),
        pltpu.VMEM((2, 4, model, width), BF16),
        pltpu.VMEM((2, 4, model, width), BF16),
        pltpu.VMEM((3, 4, 8 * rows, width), F32),
        pltpu.VMEM((3, 4, 8 * rows, width), BF16),
        pltpu.VMEM((3, 4, 8 * rows, width), BF16),
        pltpu.VMEM((3, 4, 4 * rows, width), BF16),
        pltpu.VMEM((3, 4, 4 * rows, width), BF16),
        pltpu.VMEM((3, 4, 3, rows, width), BF16),
        pltpu.VMEM((3, 4, 3, rows, width), BF16),
        pltpu.VMEM((3, 4, rows, width), F32),
        pltpu.VMEM((16, model), F32),
        pltpu.VMEM((5, 16, model), F32),
        pltpu.VMEM((5, 16, model), F32),
        pltpu.VMEM((lines, LANES), F32),
        dma((20,)), dma((8,)),
        dma((3, 4)), dma((3, 4)), dma((3, 4)), dma((3, 4)), dma((3, 4)), dma((3, 4)),
        dma((3, 4, 4)), dma((3, 4, 4)),
        dma((5,)), dma((5,)), dma((2,)), dma((2,)),
        pltpu.SemaphoreType.REGULAR,
        dma((24,)),
        pltpu.VMEM((2, 3, 4 * rows, width), BF16),
    ]
    return pl.pallas_call(
        functools.partial(backward_kernel, spans),
        out_shape=(
            jax.ShapeDtypeStruct((4, rows, width), F32),
            jax.ShapeDtypeStruct((2, rows, 4 * width), F32),
            jax.ShapeDtypeStruct((8, model), F32),
            jax.ShapeDtypeStruct((lines, LANES), F32),
            jax.ShapeDtypeStruct((2, spans[0][1], model), F32),
            jax.ShapeDtypeStruct((2, spans[1][1], model), F32),
        ),
        in_specs=[smem] * 2 + [anywhere] * 11 + [vmem, vmem],
        out_specs=(anywhere,) * 6,
        scratch_shapes=scratch,
        compiler_params=pltpu.CompilerParams(collective_id=2, has_side_effects=True, vmem_limit_bytes=60 * MIB),
        name="backward",
    )(query_len, passage_len, weight, proj, mixed, unit, inverse, low, active, slope, tokens, grad_ztwo, grad_low,
      norm_params, small)


def finish_kernel(
    step_ref, rates_ref, query_ref, passage_ref,
    attn_grad, ffn_grad, norm_grad, col_grad, loss_ref,
    attn_m, attn_f, attn_s, attn_a, ffn_m, ffn_f, ffn_s, ffn_a,
    norm_m, norm_f, norm_s, norm_a, col_m, col_f, col_s, col_a,
    loss_out, query_out, passage_out,
    attn_mo, attn_fo, attn_so, attn_ao, ffn_mo, ffn_fo, ffn_so, ffn_ao,
    norm_mo, norm_fo, norm_so, norm_ao, col_mo, col_fo, col_so, col_ao, attn_co, ffn_co,
    attn_in, attn_res, attn_low, ffn_in, ffn_res, ffn_low, norm_in, norm_res, col_in, col_res, small, query, passage,
    in_sem, out_sem,
):
    loads, stores = [], []

    def load(source, target):
        copy = pltpu.make_async_copy(source, target, in_sem.at[len(loads)])
        copy.start()
        loads.append(copy)
        return copy

    def store(source, target):
        copy = pltpu.make_async_copy(source, target, out_sem.at[len(stores)])
        copy.start()
        stores.append(copy)

    groups = [
        [
            load(source.at[which], ffn_in.at[index, which])
            for index, source in enumerate((ffn_m, ffn_f, ffn_s, ffn_a, ffn_grad))
        ]
        for which in range(2)
    ]
    groups.append(
        [load(source, attn_in.at[index]) for index, source in enumerate((attn_m, attn_f, attn_s, attn_a, attn_grad))]
    )
    lines = norm_in.shape[1]
    groups.append(
        [load(source, norm_in.at[index]) for index, source in enumerate((norm_m, norm_f, norm_s, norm_a))]
        + [load(norm_grad, small.at[0]), load(loss_ref, small.at[1])]
        + [load(source, col_in.at[index]) for index, source in enumerate((col_m, col_f, col_s, col_a, col_grad))]
    )
    half = passage.shape[1] // 2
    parts = [(pair, pl.ds(at * half, half)) for pair in range(2) for at in range(2)]

    count = jnp.full((1, 1), step_ref[0], jnp.int32).astype(F32)
    rate = [jnp.full((1, 1), rates_ref[index], F32) for index in range(5)]
    to_first, to_second = [1.0 / (1.0 - jnp.exp(count * jnp.log(rate[index]))) for index in range(2)]

    def update(master, first, second, average, grad, learn, decay):
        first_new = rate[0] * first + (1.0 - rate[0]) * grad
        second_new = rate[1] * second + (1.0 - rate[1]) * grad * grad
        move = (first_new * to_first) / (jnp.sqrt(second_new * to_second) + ADAM_EPS)
        if decay:
            move = move + decay * master
        master_new = master - learn * move
        average_new = rate[2] * average + (1.0 - rate[2]) * master_new
        return master_new, first_new, second_new, average_new

    def wait(group):
        for copy in groups[group]:
            copy.wait()

    for which in range(2):
        wait(which)
        if which == 0:
            groups.append([load(query_ref, query)])
            for pair, place in parts:
                groups.append([load(passage_ref.at[pair, place, :], passage.at[pair, place, :])])
        values = update(*[ffn_in[index, which] for index in range(5)], rate[3], DECAY_WEIGHT)
        for index, (value, target) in enumerate(zip(values, (ffn_mo, ffn_fo, ffn_so, ffn_ao))):
            ffn_res[index, which] = value
            store(ffn_res.at[index, which], target.at[which])
        ffn_low[which] = values[0].astype(BF16)
        store(ffn_low.at[which], ffn_co.at[which])
    wait(2)
    for which in range(attn_low.shape[0]):
        values = update(*[attn_in[index, which] for index in range(5)], rate[3], DECAY_WEIGHT)
        for index, value in enumerate(values):
            attn_res[index, which] = value
        attn_low[which] = values[0].astype(BF16)
    for index, target in enumerate((attn_mo, attn_fo, attn_so, attn_ao)):
        store(attn_res.at[index], target)
    store(attn_low, attn_co)
    wait(3)
    values = update(*[norm_in[index] for index in range(4)], small[0, pl.ds(0, lines), :], rate[4], 0.0)
    for index, (value, target) in enumerate(zip(values, (norm_mo, norm_fo, norm_so, norm_ao))):
        norm_res[index] = value
        store(norm_res.at[index], target)
    values = update(*[col_in[index] for index in range(5)], rate[4], 0.0)
    for index, (value, target) in enumerate(zip(values, (col_mo, col_fo, col_so, col_ao))):
        col_res[index] = value
        store(col_res.at[index], target)
    wait(4)
    store(query, query_out)
    for index, (pair, place) in enumerate(parts):
        wait(5 + index)
        store(passage.at[pair, place, :], passage_out.at[pair, place, :])
    loss_out[0] = jnp.sum(small[1, pl.ds(3, 1), pl.ds(0, 1)])
    for copy in stores:
        copy.wait()


def finish(step, rates, grads, loss_rows, attn_state, ffn_state, norm_state, col_state):
    attn_grad, ffn_grad, norm_grad, col_grad, query_grad, passage_grad = grads
    anywhere = pl.BlockSpec(memory_space=pltpu.HBM)
    smem = pl.BlockSpec(memory_space=pltpu.SMEM)
    dma = pltpu.SemaphoreType.DMA
    col_state = [value.reshape(-1, LANES) for value in col_state]
    states = (attn_state, ffn_state, norm_state, col_state)
    shapes = [jax.ShapeDtypeStruct((1,), F32)]
    shapes += [jax.ShapeDtypeStruct(value.shape, F32) for value in (query_grad, passage_grad)]
    shapes += [jax.ShapeDtypeStruct(value.shape, F32) for state in states for value in state]
    shapes += [jax.ShapeDtypeStruct(state[0].shape, BF16) for state in (attn_state, ffn_state)]
    scratch = []
    for state in (attn_state, ffn_state):
        shape = state[0].shape
        scratch += [pltpu.VMEM((5,) + shape, F32), pltpu.VMEM((4,) + shape, F32), pltpu.VMEM(shape, BF16)]
    for state, count in ((norm_state, 4), (col_state, 5)):
        shape = state[0].shape
        scratch += [pltpu.VMEM((count,) + shape, F32), pltpu.VMEM((4,) + shape, F32)]
    outs = pl.pallas_call(
        finish_kernel,
        out_shape=tuple(shapes),
        in_specs=[smem] * 2 + [anywhere] * 23,
        out_specs=(smem,) + (anywhere,) * 20,
        scratch_shapes=scratch
        + [pltpu.VMEM((2,) + norm_grad.shape, F32), pltpu.VMEM(query_grad.shape, F32), pltpu.VMEM(passage_grad.shape, F32)]
        + [dma((32,)), dma((32,))],
        compiler_params=pltpu.CompilerParams(vmem_limit_bytes=60 * MIB),
        name="finish",
    )(step, rates, query_grad, passage_grad, attn_grad, ffn_grad, norm_grad, col_grad, loss_rows,
      *attn_state, *ffn_state, *norm_state, *col_state)
    outs = list(outs)
    outs[15:19] = [value.reshape(-1) for value in outs[15:19]]
    return outs


def attend_kernel(spans, lens_ref, q_ref, k_ref, v_ref, o_ref):
    for index, (start, slots) in enumerate(spans):
        length = lens_ref[index]
        keys = k_ref[0, pl.ds(start, slots), :]
        values = v_ref[0, pl.ds(start, slots), :]
        lane = first_head(keys.shape)
        scaled = keys * jnp.asarray(HD**-0.5, BF16)
        zero = jnp.zeros_like(scaled)
        head_keys = (jnp.where(lane, scaled, zero), jnp.where(lane, zero, scaled))
        block = min(slots, 256)
        for at in range(0, slots, block):
            queries = q_ref[0, pl.ds(start + at, block), :]
            outs = []
            for head in range(2):
                scores = mm_nt(queries, head_keys[head])
                valid = lax.broadcasted_iota(jnp.int32, scores.shape, 1) < length
                scores = jnp.where(valid, scores, NEG_FILL)
                top = jnp.max(scores, axis=1, keepdims=True)
                weight = jnp.exp(scores - top)
                total = jnp.sum(weight, axis=1, keepdims=True)
                probs = (weight * (1.0 / total)).astype(BF16)
                outs.append(mm(probs, values))
            o_ref[pl.ds(start + at, block), :] = jnp.where(
                first_head(outs[0].shape), outs[0], outs[1]
            ).astype(BF16)


def attend_back_kernel(spans, lens_ref, q_ref, k_ref, v_ref, g_ref, d_ref):
    scale = HD**-0.5
    for index, (start, slots) in enumerate(spans):
        length = lens_ref[index]
        keys = k_ref[0, pl.ds(start, slots), :]
        values = v_ref[0, pl.ds(start, slots), :]
        lane = first_head(keys.shape)
        scaled = keys * jnp.asarray(scale, BF16)
        zero = jnp.zeros_like(scaled)
        head_keys = (jnp.where(lane, scaled, zero), jnp.where(lane, zero, scaled))
        head_values = (jnp.where(lane, values, zero), jnp.where(lane, zero, values))
        block = min(slots, 256)
        grad_k = [None, None]
        grad_v = [None, None]
        for at in range(0, slots, block):
            queries = q_ref[0, pl.ds(start + at, block), :]
            grads = g_ref[pl.ds(start + at, block), :]
            grad_q = []
            for head in range(2):
                scores = mm_nt(head_keys[head], queries)
                valid = lax.broadcasted_iota(jnp.int32, scores.shape, 0) < length
                scores = jnp.where(valid, scores, NEG_FILL)
                top = jnp.max(scores, axis=0, keepdims=True)
                weight = jnp.exp(scores - top)
                total = jnp.sum(weight, axis=0, keepdims=True)
                probs = weight * (1.0 / total)
                grad_probs = mm_nt(head_values[head], grads)
                inner = jnp.sum(probs * grad_probs, axis=0, keepdims=True)
                grad_scores = (probs * (grad_probs - inner)).astype(BF16)
                part_v = mm(probs.astype(BF16), grads)
                part_k = mm(grad_scores, queries)
                grad_v[head] = part_v if at == 0 else grad_v[head] + part_v
                grad_k[head] = part_k if at == 0 else grad_k[head] + part_k
                grad_q.append(mm_tn(grad_scores, keys))
            d_ref[0, pl.ds(start + at, block), :] = (
                jnp.where(first_head(grad_q[0].shape), grad_q[0], grad_q[1]) * scale
            ).astype(BF16)
        d_ref[1, pl.ds(start, slots), :] = (jnp.where(lane, grad_k[0], grad_k[1]) * scale).astype(BF16)
        d_ref[2, pl.ds(start, slots), :] = jnp.where(lane, grad_v[0], grad_v[1]).astype(BF16)


def head_specs(tokens):
    return [pl.BlockSpec((1, tokens, LANES), functools.partial(lambda s, i, lens: (s, 0, i), s)) for s in range(3)]


def attend(proj, lens, spans):
    _, tokens, width = proj.shape
    flops = sum(4 * slots * slots * width for _, slots in spans)
    return pl.pallas_call(
        functools.partial(attend_kernel, spans),
        out_shape=jax.ShapeDtypeStruct((tokens, width), BF16),
        grid_spec=pltpu.PrefetchScalarGridSpec(
            num_scalar_prefetch=1,
            grid=(width // LANES,),
            in_specs=head_specs(tokens),
            out_specs=pl.BlockSpec((tokens, LANES), lambda i, lens: (0, i)),
        ),
        compiler_params=pltpu.CompilerParams(vmem_limit_bytes=40 * MIB),
        cost_estimate=pl.CostEstimate(flops=8 * flops, bytes_accessed=8 * tokens * width, transcendentals=0),
        name="attend",
    )(lens, proj, proj, proj)


def attend_back(proj, grad_out, lens, spans):
    _, tokens, width = proj.shape
    flops = sum(10 * slots * slots * width for _, slots in spans)
    return pl.pallas_call(
        functools.partial(attend_back_kernel, spans),
        out_shape=jax.ShapeDtypeStruct((3, tokens, width), BF16),
        grid_spec=pltpu.PrefetchScalarGridSpec(
            num_scalar_prefetch=1,
            grid=(width // LANES,),
            in_specs=head_specs(tokens) + [pl.BlockSpec((tokens, LANES), lambda i, lens: (0, i))],
            out_specs=pl.BlockSpec((3, tokens, LANES), lambda i, lens: (0, 0, i)),
        ),
        compiler_params=pltpu.CompilerParams(vmem_limit_bytes=40 * MIB),
        cost_estimate=pl.CostEstimate(flops=8 * flops, bytes_accessed=14 * tokens * width, transcendentals=0),
        name="attend_back",
    )(lens, proj, proj, proj, grad_out)


def up_kernel(x_ref, w_ref, b_ref, g_ref, s_ref):
    hidden = mm(x_ref[...], w_ref[0]) + b_ref[...]
    active, slope = gelu_and_slope(hidden)
    g_ref[...] = active.astype(BF16)
    s_ref[...] = slope


def feed_up(low, ffn_half, bias):
    tokens, width = low.shape
    units = ffn_half.shape[2]
    tile = 256
    return pl.pallas_call(
        up_kernel,
        out_shape=(jax.ShapeDtypeStruct((tokens, units), BF16), jax.ShapeDtypeStruct((tokens, units), F32)),
        grid=(units // tile,),
        in_specs=[
            pl.BlockSpec((tokens, width), lambda i: (0, 0)),
            pl.BlockSpec((1, width, tile), lambda i: (0, 0, i)),
            pl.BlockSpec((1, tile), lambda i: (0, i)),
        ],
        out_specs=(pl.BlockSpec((tokens, tile), lambda i: (0, i)), pl.BlockSpec((tokens, tile), lambda i: (0, i))),
        compiler_params=pltpu.CompilerParams(vmem_limit_bytes=40 * MIB),
        cost_estimate=pl.CostEstimate(
            flops=2 * tokens * width * units, bytes_accessed=8 * tokens * units, transcendentals=tokens * units
        ),
        name="feed_up",
    )(low, ffn_half, bias.reshape(1, -1))


def swap_cores(values):
    return lax.ppermute(values, "mp", [(0, 1), (1, 0)])


def scatter_sum(own_parts, other_parts):
    summed = [own + swap_cores(other).astype(F32) for own, other in zip(own_parts, other_parts)]
    return [lax.psum_scatter(value, "dp", scatter_dimension=1, tiled=True) for value in summed]


def adam_update(master, first, second, average, grad, rate, decay_w, rates, step_count):
    first_new = rates[0] * first + (1.0 - rates[0]) * grad
    second_new = rates[1] * second + (1.0 - rates[1]) * grad * grad
    fixed_one = first_new / (1.0 - rates[0] ** step_count)
    fixed_two = second_new / (1.0 - rates[1] ** step_count)
    master_new = master - rate * (fixed_one / (jnp.sqrt(fixed_two) + ADAM_EPS) + decay_w * master)
    average_new = rates[2] * average + (1.0 - rates[2]) * master_new
    return (master_new, first_new, second_new, average_new)


def forward_plain(tokens, lens, attn_low, ffn_low, col_bias, norm_params, spans):
    attn_full = lax.all_gather(attn_low, "dp", axis=1, tiled=True)
    ffn_full = lax.all_gather(ffn_low, "dp", axis=1, tiled=True)
    attn_w = (attn_full, swap_cores(attn_full))
    ffn_w = (ffn_full, swap_cores(ffn_full))
    col = (col_bias, swap_cores(col_bias))
    width = attn_w[0].shape[2]

    projected, mixed = [], []
    branch = None
    for half in range(2):
        bias = jnp.stack([col[half][:width], jnp.zeros((width,), F32), col[half][width : 2 * width]])
        proj = (
            jnp.einsum("td,sde->ste", tokens, attn_w[half][:3], preferred_element_type=F32) + bias[:, None, :]
        ).astype(BF16)
        out = attend(proj, lens, spans)
        part = mm_nt(out, attn_w[half][3])
        branch = part if branch is None else branch + part
        projected.append(proj)
        mixed.append(out)
    z_one = tokens.astype(F32) + branch + norm_params[0]
    unit_one, inverse_one = normalize(z_one)
    first_norm = unit_one * norm_params[1] + norm_params[2]
    first_low = first_norm.astype(BF16)
    active, slope = [], []
    branch_two = None
    for half in range(2):
        act, slo = feed_up(first_low, ffn_w[half], col[half][2 * width :])
        part = mm_nt(act, ffn_w[half][1])
        branch_two = part if branch_two is None else branch_two + part
        active.append(act)
        slope.append(slo)
    z_two = first_norm + branch_two + norm_params[3]
    return attn_w, ffn_w, projected, mixed, unit_one, inverse_one, first_low, active, slope, z_two


def loss_plain(z_two, lens, target_mine, norm_params, spans, pairs):
    query_slots, passage_slots = spans[0][1], spans[1][1]
    model_width = z_two.shape[1]
    core = lax.axis_index("mp")
    unit_two, inverse_two = normalize(z_two)
    places = jnp.arange(query_slots + passage_slots)
    in_query = (places < query_slots) & (places < lens[0])
    in_passage = (places >= query_slots) & (places - query_slots < lens[1])
    share = (
        jnp.stack([in_query, in_passage]).astype(F32) / lens.astype(F32)[:, None]
    )
    mean_unit = jnp.dot(share, unit_two, precision=PRECISE, preferred_element_type=F32)
    pooled = mean_unit * norm_params[4] + norm_params[5]
    shrink = lax.rsqrt(jnp.sum(pooled * pooled, axis=1, keepdims=True) + POOL_EPS)
    embed = pooled * shrink

    payload = jnp.concatenate([embed.reshape(-1), target_mine])
    every = lax.all_gather(payload, ("dp", "mp"), axis=0)
    every_q = every[:, :model_width]
    every_p = every[:, model_width : 2 * model_width]
    target = (jnp.arange(pairs)[None, :].astype(F32) == every[:, 2 * model_width :][:, :1]).astype(F32)
    logits = lax.dot_general(every_q, every_p, (((1,), (1,)), ((), ())), precision=PRECISE) / SOFTMAX_TEMPER
    row_top = jnp.max(logits, axis=1, keepdims=True)
    exp_logits = jnp.exp(logits - row_top)
    row_total = jnp.sum(exp_logits, axis=1, keepdims=True)
    log_total = row_top[:, 0] + jnp.log(row_total[:, 0])
    loss_value = (jnp.sum(log_total - jnp.sum(logits * target, axis=1)) / pairs).reshape(1)
    grad_logits = (exp_logits / row_total - target) / (pairs * SOFTMAX_TEMPER)
    rank = lax.axis_index("dp") * lax.axis_size("mp") + core
    grad_uq = jnp.dot(lax.dynamic_index_in_dim(grad_logits, rank, 0, keepdims=True), every_p, precision=PRECISE)
    grad_up = jnp.dot(
        lax.dynamic_index_in_dim(grad_logits, rank, 1, keepdims=False)[None], every_q, precision=PRECISE
    )
    grad_embed = jnp.concatenate([grad_uq, grad_up], axis=0)

    grad_pooled = shrink * (grad_embed - embed * jnp.sum(grad_embed * embed, axis=1, keepdims=True))
    grad_gain_two = jnp.sum(grad_pooled * mean_unit, axis=0)
    grad_shift_two = jnp.sum(grad_pooled, axis=0)
    grad_unit_two = lax.dot_general(
        share, grad_pooled * norm_params[4], (((0,), (0,)), ((), ())), precision=PRECISE
    )
    grad_ztwo = normalize_back(unit_two, inverse_two, grad_unit_two)
    grad_bias_two = jnp.sum(grad_ztwo, axis=0)
    grad_two_low = grad_ztwo.astype(BF16)
    return grad_ztwo, grad_two_low, loss_value, grad_bias_two, grad_gain_two, grad_shift_two


def backward_plain(tokens, lens, kept, grad_ztwo, grad_two_low, norm_params, second_grads, spans):
    attn_w, ffn_w, projected, mixed, unit_one, inverse_one, first_low, active, slope = kept
    grad_bias_two, grad_gain_two, grad_shift_two = second_grads
    query_slots = spans[0][1]
    core = lax.axis_index("mp")
    cut = ffn_w[0].shape[2] // 2
    width = attn_w[0].shape[2]

    def two_parts(values):
        return values[:, :cut], values[:, cut:]

    def parted_product(left, halves):
        own = [mm_tn(left, part)[None] for part in two_parts(halves[0])]
        other = [mm_tn(left, part).astype(BF16)[None] for part in two_parts(halves[1])]
        return own, other

    down_grad = scatter_sum(*parted_product(grad_two_low, active))
    grad_hidden, grad_first = [], grad_ztwo
    for half in (1, 0):
        grad_hid = (mm(grad_two_low, ffn_w[half][1]) * slope[half]).astype(BF16)
        grad_hidden.insert(0, grad_hid)
        grad_first = grad_first + mm_nt(grad_hid, ffn_w[half][0])
    grad_hidden_bias = [jnp.sum(value.astype(F32), axis=0) for value in grad_hidden]
    up_grad = scatter_sum(*parted_product(first_low, grad_hidden))

    grad_gain_one = jnp.sum(grad_first * unit_one, axis=0)
    grad_shift_one = jnp.sum(grad_first, axis=0)
    grad_zone = normalize_back(unit_one, inverse_one, grad_first * norm_params[1])
    grad_bias_out = jnp.sum(grad_zone, axis=0)
    grad_one_low = grad_zone.astype(BF16)
    grad_tokens = grad_zone
    grad_query_bias, grad_value_bias, attn_parts = [None, None], [None, None], [None, None]
    for half in (1, 0):
        grad_out = mm(grad_one_low, attn_w[half][3]).astype(BF16)
        grad_proj = attend_back(projected[half], grad_out, lens, spans)
        grad_query_bias[half] = jnp.sum(grad_proj[0].astype(F32), axis=0)
        grad_value_bias[half] = jnp.sum(grad_proj[2].astype(F32), axis=0)
        in_grads = jnp.einsum("td,ste->sde", tokens, grad_proj, preferred_element_type=F32)
        out_grad = mm_tn(grad_one_low, mixed[half])
        parts = [in_grads[:2], jnp.stack([in_grads[2], out_grad])]
        attn_parts[half] = parts if half == 0 else [part.astype(BF16) for part in parts]
        for index in range(3):
            grad_tokens = grad_tokens + mm_nt(grad_proj[index], attn_w[half][index])
    attn_grads = scatter_sum(*attn_parts)

    col_parts = [
        jnp.concatenate([grad_query_bias[half], grad_value_bias[half], grad_hidden_bias[half]]) for half in range(2)
    ]
    norm_part = jnp.stack(
        [grad_bias_out, grad_gain_one, grad_shift_one, grad_bias_two, grad_gain_two, grad_shift_two]
    )
    norm_part = norm_part + swap_cores(norm_part)
    col_part = col_parts[0] + swap_cores(col_parts[1])
    small = lax.psum(jnp.concatenate([norm_part.reshape(-1), col_part]), "dp")
    norm_grad = small[: norm_part.size].reshape(norm_part.shape)
    col_grad = small[norm_part.size :]

    attn_grad = jnp.concatenate(attn_grads, axis=0)
    ffn_grad = jnp.stack([jnp.concatenate(parts, axis=-1)[0] for parts in (up_grad, down_grad)])
    grad_twin = swap_cores(grad_tokens)
    first_pair = jnp.where(core == 0, grad_tokens, grad_twin)
    second_pair = jnp.where(core == 0, grad_twin, grad_tokens)
    query_grad = jnp.stack([first_pair[:query_slots], second_pair[:query_slots]])
    passage_grad = jnp.stack([first_pair[query_slots:], second_pair[query_slots:]])
    return attn_grad, ffn_grad, norm_grad, col_grad, query_grad, passage_grad


def per_device(
    query_in,
    passage_in,
    query_len,
    passage_len,
    positive,
    step,
    rates,
    attn_master,
    attn_first,
    attn_second,
    attn_average,
    ffn_master,
    ffn_first,
    ffn_second,
    ffn_average,
    norm_params,
    norm_first,
    norm_second,
    norm_average,
    col_bias,
    col_first,
    col_second,
    col_average,
):
    size = lax.axis_size("dp")
    query_slots = query_in.shape[1]
    spans = ((0, query_slots), (query_slots, passage_in.shape[1]))
    pairs = query_in.shape[0] * size
    attn_state = (attn_master, attn_first, attn_second, attn_average)
    ffn_state = (ffn_master, ffn_first, ffn_second, ffn_average)
    norm_state = (norm_params, norm_first, norm_second, norm_average)
    col_state = (col_bias, col_first, col_second, col_average)
    if size == 16:
        kept = forward(
            query_in, passage_in, query_len, passage_len, positive, attn_master, ffn_master, col_bias, norm_params, spans,
            pairs,
        )
        grads = backward(query_len, passage_len, kept, norm_params, spans)
        return tuple(finish(step, rates, grads, kept[11], attn_state, ffn_state, norm_state, col_state))

    core = lax.axis_index("mp")

    def pick(values, index):
        return lax.dynamic_index_in_dim(values, index, 0, keepdims=False)

    tokens = jnp.concatenate([pick(query_in, core), pick(passage_in, core)], axis=0)
    lens = jnp.stack([pick(query_len, core), pick(passage_len, core)])
    target = jnp.broadcast_to(pick(positive, core).astype(F32), (LANES,))
    outs = forward_plain(tokens, lens, attn_master.astype(BF16), ffn_master.astype(BF16), col_bias, norm_params, spans)
    kept, z_two = outs[:9], outs[9]
    outs = loss_plain(z_two, lens, target, norm_params, spans, pairs)
    grad_ztwo, grad_two_low, loss_value, *second_grads = outs
    attn_grad, ffn_grad, norm_grad, col_grad, query_grad, passage_grad = backward_plain(
        tokens, lens, kept, grad_ztwo, grad_two_low, norm_params, second_grads, spans
    )
    step_count = step[0].astype(F32)
    outs = []
    for state, grad, rate, decay in (
        (attn_state, attn_grad, rates[3], DECAY_WEIGHT),
        (ffn_state, ffn_grad, rates[3], DECAY_WEIGHT),
        (norm_state, norm_grad, rates[4], 0.0),
        (col_state, col_grad, rates[4], 0.0),
    ):
        outs.extend(adam_update(*state, grad, rate, decay, rates, step_count))
    return (loss_value, query_grad, passage_grad, *outs, outs[0].astype(BF16), outs[4].astype(BF16))


def solution(mesh):
    matrix = P(None, "dp", "mp")
    rows = P("dp", None, None)
    placed = (rows, rows, P("dp"), P("dp"), P("dp"), P(), P(), *[matrix] * 8, *[P()] * 4, *[P("mp")] * 4)
    return jax.shard_map(
        per_device,
        mesh=mesh,
        in_specs=placed,
        out_specs=(P(), rows, rows, *[matrix] * 8, *[P()] * 4, *[P("mp")] * 4, matrix, matrix),
        check_vma=False,
    )
```

```python
import functools

import jax
import jax.numpy as jnp
from jax import lax
from jax.experimental import pallas as pl
from jax.experimental.pallas import tpu as pltpu
from jax.sharding import PartitionSpec as P

HD = 64
LANES = 128
NEG_FILL = -1e30
SOFTMAX_TEMPER = 0.02
NORM_EPS = 1e-12
POOL_EPS = 1e-06
DECAY_WEIGHT = 0.01
ADAM_EPS = 1e-08
PRECISE = lax.Precision.HIGHEST
MESH = pl.DeviceIdType.MESH
MIB = 2**20
F32 = jnp.float32
BF16 = jnp.bfloat16

ERFC_STEP = 0.46
ERFC_HALF = (
    0.5 * 0.26113873056821263,
    0.5 * 0.23637801512084577,
    0.5 * 0.3601812301921897,
    -0.5 * 0.18740624158431016,
    0.5 * 0.6751549397754679,
    -0.5 * 0.4305350150859377,
    0.5 * 0.0850883282904581,
)
ROOT_HALF = 0.7071067811865476
DENSITY = 0.3989422804014327


def gelu_and_slope(hidden):
    bell = jnp.exp(hidden * hidden * (-0.5))
    step = 1.0 / (1.0 + (ERFC_STEP * ROOT_HALF) * jnp.abs(hidden))
    tail = ERFC_HALF[6]
    for coefficient in ERFC_HALF[5::-1]:
        tail = tail * step + coefficient
    tail = tail * step * bell
    below = jnp.where(hidden >= 0.0, 1.0 - tail, tail)
    return hidden * below, below + hidden * bell * DENSITY


def mm(left, right):
    return jnp.dot(left, right, preferred_element_type=F32)


def mm_nt(left, right):
    return lax.dot_general(left, right, (((1,), (1,)), ((), ())), preferred_element_type=F32)


def mm_tn(left, right):
    return lax.dot_general(left, right, (((0,), (0,)), ((), ())), preferred_element_type=F32)


def first_head(shape):
    return lax.broadcasted_iota(jnp.int32, shape, 1) < HD


def stack_heads(values):
    place = lax.broadcasted_iota(jnp.int32, values.shape, 1) // HD
    zero = jnp.zeros_like(values)
    return jnp.concatenate(
        [jnp.where(place == head, values, zero) for head in range(values.shape[1] // HD)], axis=0
    )


def unstack_heads(values, count):
    place = lax.broadcasted_iota(jnp.int32, (count, values.shape[1]), 1) // HD
    total = None
    for head in range(values.shape[1] // HD):
        piece = jnp.where(place == head, values[head * count : (head + 1) * count], 0.0)
        total = piece if total is None else total + piece
    return total


def split_pair(values):
    lane = first_head(values.shape)
    zero = jnp.zeros_like(values)
    return jnp.where(lane, values, zero), jnp.where(lane, zero, values)


def probabilities(scores, length):
    valid = lax.broadcasted_iota(jnp.int32, scores.shape, 1) < length
    scores = jnp.where(valid, scores, NEG_FILL)
    weight = jnp.exp(scores - jnp.max(scores, axis=1, keepdims=True))
    return weight * (1.0 / jnp.sum(weight, axis=1, keepdims=True))


def normalize(values):
    center = values - jnp.mean(values, axis=-1, keepdims=True)
    spread = jnp.mean(center * center, axis=-1, keepdims=True)
    inverse = lax.rsqrt(spread + NORM_EPS)
    return center * inverse, inverse


def normalize_back(unit, inverse, grad_unit):
    return inverse * (
        grad_unit
        - jnp.mean(grad_unit, axis=-1, keepdims=True)
        - unit * jnp.mean(grad_unit * unit, axis=-1, keepdims=True)
    )


SCALE = HD**-0.5
SLAB = 16


class Mesh:
    def __init__(self):
        self.me = lax.axis_index("dp")
        self.core = lax.axis_index("mp")
        self.x, self.y, self.z = lax.rem(self.me, 2), lax.rem(self.me // 2, 2), self.me // 4
        self.x_peer = (self.index(self.z, self.y, 1 - self.x), self.core)
        self.y_peer = (self.index(self.z, 1 - self.y, self.x), self.core)
        self.c_peer = (self.me, 1 - self.core)
        self.z_peer = [None] + [(self.index(lax.rem(self.z + k, 4), self.y, self.x), self.core) for k in range(1, 4)]
        self.column = [lax.rem(self.z - k + 4, 4) for k in range(4)]

    def index(self, z, y, x):
        return (z * 2 + y) * 2 + x


def remote(source, target, send, recv, peer):
    return pltpu.make_async_remote_copy(
        src_ref=source, dst_ref=target, send_sem=send, recv_sem=recv, device_id=peer, device_id_type=MESH
    )


def forward_kernel(
    spans, total,
    query_len, passage_len, positive, query_ref, passage_ref, attn_ref, ffn_ref, col_ref, norm_ref,
    weight_out, proj_out, mixed_out, unit_out, inverse_out, low_out, active_out, slope_out, tokens_out,
    grad_out, grad_low_out, small_out,
    weight, proj, mixed, unit, inverse, low, active, slope, tokens, z_two, grad_low, small,
    col, attn_in, ffn_in, unit_two, slab, every,
    z_send, z_recv, x_send, x_recv, y_send, y_recv, d_send, d_recv, c_send, c_recv, b_send, b_recv, here_sem, out_sem,
    e_send, e_recv, p_send, p_recv, pz_send, pz_recv,
):
    at = Mesh()
    me, core = at.me, at.core
    my_rank = me * 2 + core
    rows, width = attn_ref.shape[1:]
    units = ffn_ref.shape[2]
    slots, model = tokens.shape

    def device(step):
        rank = lax.rem(my_rank + step, total)
        return (rank // 2, lax.rem(rank, 2))

    incoming = [
        pltpu.make_async_copy(attn_ref, attn_in, here_sem.at[0]),
        pltpu.make_async_copy(ffn_ref.at[0], ffn_in.at[0], here_sem.at[1]),
        pltpu.make_async_copy(ffn_ref.at[1], ffn_in.at[1], here_sem.at[2]),
        pltpu.make_async_copy(query_ref.at[core], tokens.at[pl.ds(*spans[0]), :], here_sem.at[3]),
        pltpu.make_async_copy(passage_ref.at[core], tokens.at[pl.ds(*spans[1]), :], here_sem.at[4]),
    ]
    for copy in incoming:
        copy.start()
    lens = (query_len[core], passage_len[core])
    barrier = pltpu.get_barrier_semaphore()
    for step in range(1, total):
        pl.semaphore_signal(barrier, inc=1, device_id=device(step), device_id_type=MESH)
    for line in range(col_ref.shape[0]):
        col[0, :, pl.ds(line * LANES, LANES)] = col_ref[pl.ds(line, 1), :]
    pl.semaphore_wait(barrier, total - 1)

    every_lane = pl.ds(0, units)
    cut = units * 2 // 3

    def column_lanes(q):
        return pl.ds(0, units if q < 2 else cut)

    def half_lanes(q, which):
        count = (units if q < 2 else cut) // 2
        return pl.ds(which * count, count)

    layer_lanes = pl.ds(cut, units - cut)

    def layer_half(which):
        count = (units - cut) // 2
        return pl.ds(cut + which * count, count)

    def block(q, index, lanes=None, count=1, far=0):
        lanes = column_lanes(q) if lanes is None else lanes
        return weight.at[far, q, pl.ds(pl.multiple_of(index * rows, rows), count * rows), lanes]

    sends = []
    stores = []

    def push(ref, send, recv, peer, target=None):
        copy = remote(ref, ref if target is None else target, send, recv, peer)
        copy.start()
        sends.append(copy)

    def landed(ref, send, recv, peer):
        remote(ref, ref, send, recv, peer).wait_recv()

    def store(source, target):
        copy = pltpu.make_async_copy(source, target, out_sem.at[len(stores)])
        copy.start()
        stores.append(copy)

    def cast_own(q):
        incoming[q].wait()
        here = pl.ds(pl.multiple_of(me * rows, rows), rows)
        if q == 0:
            for index in range(4):
                weight[0, 0, here, pl.ds(index * width, width)] = attn_in[index].astype(BF16)
        else:
            weight[0, q, here, :] = ffn_in[q - 1].astype(BF16)

    def own_along_column(q):
        for k in range(1, 4):
            push(block(q, me), z_send.at[q, k], z_recv.at[q, k], at.z_peer[k])

    def own_to_sides(q):
        push(block(q, me), x_send.at[q, 0], x_recv.at[q, 0], at.x_peer)
        push(block(q, me), y_send.at[q, 0], y_recv.at[q, 0], at.y_peer)

    def column_to_sides(q):
        for k in range(1, 4):
            ref = block(q, at.index(at.column[k], at.y, at.x))
            landed(ref, z_send.at[q, k], z_recv.at[q, k], at.z_peer[k])
            push(ref, x_send.at[q, k], x_recv.at[q, k], at.x_peer)
            push(ref, y_send.at[q, k], y_recv.at[q, k], at.y_peer)

    def round_corner(q, ks=range(4)):
        for k in ks:
            beside = at.index(at.column[k], at.y, 1 - at.x)
            landed(block(q, beside), x_send.at[q, k], x_recv.at[q, k], at.x_peer)
            push(block(q, beside, half_lanes(q, 0)), d_send.at[q, k, 0], d_recv.at[q, k, 0], at.y_peer)
            beside = at.index(at.column[k], 1 - at.y, at.x)
            landed(block(q, beside), y_send.at[q, k], y_recv.at[q, k], at.y_peer)
            push(block(q, beside, half_lanes(q, 1)), d_send.at[q, k, 1], d_recv.at[q, k, 1], at.x_peer)

    def layer_to_sides():
        ref = block(2, me, layer_lanes)
        push(ref, p_send.at[0], p_recv.at[0], at.x_peer)
        push(ref, p_send.at[1], p_recv.at[1], at.y_peer)

    def layer_round_corner():
        beside = at.index(at.z, at.y, 1 - at.x)
        landed(block(2, beside, layer_lanes), p_send.at[0], p_recv.at[0], at.x_peer)
        push(block(2, beside, layer_half(0)), p_send.at[2], p_recv.at[2], at.y_peer)
        beside = at.index(at.z, 1 - at.y, at.x)
        landed(block(2, beside, layer_lanes), p_send.at[1], p_recv.at[1], at.y_peer)
        push(block(2, beside, layer_half(1)), p_send.at[3], p_recv.at[3], at.x_peer)

    def layer_along_column():
        across = at.index(at.z, 1 - at.y, 1 - at.x)
        landed(block(2, across, layer_half(0)), p_send.at[2], p_recv.at[2], at.y_peer)
        landed(block(2, across, layer_half(1)), p_send.at[3], p_recv.at[3], at.x_peer)
        for k in range(1, 4):
            push(block(2, at.index(at.z, 0, 0), layer_lanes, 4), pz_send.at[k], pz_recv.at[k], at.z_peer[k])

    def to_other_core(q, ks=range(4)):
        for k in ks:
            across = at.index(at.column[k], 1 - at.y, 1 - at.x)
            landed(block(q, across, half_lanes(q, 0)), d_send.at[q, k, 0], d_recv.at[q, k, 0], at.y_peer)
            landed(block(q, across, half_lanes(q, 1)), d_send.at[q, k, 1], d_recv.at[q, k, 1], at.x_peer)
            layer = at.index(at.column[k], 0, 0)
            if q == 2 and k:
                landed(block(2, layer, layer_lanes, 4), pz_send.at[k], pz_recv.at[k], at.z_peer[k])
            push(
                block(q, layer, every_lane, 4), c_send.at[q, k], c_recv.at[q, k], at.c_peer,
                block(q, layer, every_lane, 4, 1),
            )

    def from_other_core(q):
        for k in range(4):
            layer = at.index(at.column[k], 0, 0)
            landed(block(q, layer, every_lane, 4, 1), c_send.at[q, k], c_recv.at[q, k], at.c_peer)

    def project(half):
        bias = jnp.concatenate(
            [
                col[half, :, pl.ds(0, width)],
                jnp.zeros((1, width), F32),
                col[half, :, pl.ds(width, width)],
            ],
            axis=1,
        )
        proj[half] = (mm(tokens[...], weight[half, 0, :, pl.ds(0, 3 * width)]) + bias).astype(BF16)

    def query_heads(half):
        place = pl.ds(*spans[0])
        queries = stack_heads(proj[half, place, pl.ds(0, width)] * jnp.asarray(SCALE, BF16))
        probs = probabilities(mm_nt(queries, proj[half, place, pl.ds(width, width)]), lens[0])
        value = mm(probs.astype(BF16), proj[half, place, pl.ds(2 * width, width)])
        mixed[half, place, :] = unstack_heads(value, spans[0][1]).astype(BF16)

    def passage_heads(half, pair):
        place = pl.ds(*spans[1])
        queries = proj[half, place, pl.ds(pair * LANES, LANES)]
        keys = split_pair(proj[half, place, pl.ds(width + pair * LANES, LANES)] * jnp.asarray(SCALE, BF16))
        values = proj[half, place, pl.ds(2 * width + pair * LANES, LANES)]
        scores = [mm_nt(queries, key) for key in keys]
        outs = [mm(probabilities(score, lens[1]).astype(BF16), values) for score in scores]
        mixed[half, place, pl.ds(pair * LANES, LANES)] = jnp.where(first_head(outs[0].shape), *outs).astype(BF16)

    def first_norm():
        step = 192
        for start in range(0, slots, step):
            place = pl.ds(start, step)
            value = tokens[place, :].astype(F32) + norm_ref[pl.ds(0, 1), :]
            for half in range(2):
                value = value + mm_nt(mixed[half, place, :], weight[half, 0, :, pl.ds(3 * width, width)])
            normed, scale = normalize(value)
            unit[place, :] = normed
            inverse[place, :] = jnp.broadcast_to(scale, (step, LANES))
            value = normed * norm_ref[pl.ds(1, 1), :] + norm_ref[pl.ds(2, 1), :]
            z_two[place, :] = value + norm_ref[pl.ds(3, 1), :]
            low[place, :] = value.astype(BF16)

    tile = 256

    def up(half, part):
        for start in range(part * units // 2, (part + 1) * units // 2, tile):
            lanes = pl.ds(start, tile)
            hidden = mm(low[...], weight[half, 1, :, lanes]) + col[half, :, pl.ds(2 * width + start, tile)]
            value, grad = gelu_and_slope(hidden)
            active[half, :, lanes] = value.astype(BF16)
            slope[half, :, lanes] = grad

    def down(half):
        z_two[...] = z_two[...] + mm_nt(active[half], weight[half, 2])

    cast_own(0)
    own_along_column(0)
    own_to_sides(0)
    push(col.at[0], b_send, b_recv, at.c_peer, col.at[1])
    cast_own(1)
    own_to_sides(1)
    cast_own(2)
    layer_to_sides()
    own_to_sides(2)
    incoming[3].wait()
    incoming[4].wait()
    store(tokens, tokens_out)
    column_to_sides(0)
    layer_round_corner()
    own_along_column(1)
    round_corner(0)
    column_to_sides(1)
    own_along_column(2)
    layer_along_column()
    to_other_core(0)
    project(0)
    query_heads(0)
    passage_heads(0, 0)
    round_corner(1, (0,))
    passage_heads(0, 1)
    round_corner(1, (1,))
    passage_heads(0, 2)
    landed(col.at[1], b_send, b_recv, at.c_peer)
    from_other_core(0)
    project(1)
    for half in range(2):
        store(weight.at[half, 0], weight_out.at[half, 0])
    store(proj, proj_out)
    round_corner(1, (2,))
    query_heads(1)
    round_corner(1, (3,))
    passage_heads(1, 0)
    column_to_sides(2)
    passage_heads(1, 1)
    passage_heads(1, 2)
    store(mixed, mixed_out)
    first_norm()
    store(unit, unit_out)
    store(inverse, inverse_out)
    store(low, low_out)
    to_other_core(1)
    round_corner(2, (0,))
    up(0, 0)
    round_corner(2, (1,))
    up(0, 1)
    store(slope.at[0], slope_out.at[0])
    store(weight.at[0, 1], weight_out.at[0, 1])
    round_corner(2, (2,))
    from_other_core(1)
    up(1, 0)
    round_corner(2, (3,))
    up(1, 1)
    store(slope.at[1], slope_out.at[1])
    store(weight.at[1, 1], weight_out.at[1, 1])
    store(active, active_out)
    to_other_core(2)
    store(weight.at[0, 2], weight_out.at[0, 2])
    down(0)
    from_other_core(2)
    store(weight.at[1, 2], weight_out.at[1, 2])
    down(1)

    pieces = model // LANES
    gain, shift = norm_ref[pl.ds(4, 1), :], norm_ref[pl.ds(5, 1), :]
    embeds, shrinks, means, inverses, valids = [], [], [], [], []
    for index, (start, count) in enumerate(spans):
        normed, scale = normalize(z_two[pl.ds(start, count), :])
        unit_two[pl.ds(start, count), :] = normed
        valid = lax.broadcasted_iota(jnp.int32, (count, 1), 0) < lens[index]
        mean = jnp.sum(jnp.where(valid, normed, 0.0), axis=0, keepdims=True) / lens[index].astype(F32)
        pooled = mean * gain + shift
        shrink = lax.rsqrt(jnp.sum(pooled * pooled, axis=1, keepdims=True) + POOL_EPS)
        embed = pooled * shrink
        for piece in range(pieces):
            slab[pl.ds(index * pieces + piece, 1), :] = embed[:, piece * LANES : (piece + 1) * LANES]
        embeds.append(embed)
        shrinks.append(shrink)
        means.append(mean)
        inverses.append(jnp.where(valid, scale, 0.0))
    slab[pl.ds(2 * pieces, 1), :] = jnp.full((1, LANES), positive[core], jnp.int32).astype(F32)
    copies = []
    for step in range(1, total):
        copy = remote(slab, every.at[my_rank], e_send.at[step], e_recv.at[step], device(step))
        copy.start()
        copies.append(copy)
    sends.extend(copies)
    every[my_rank] = slab[...]
    for copy in copies:
        copy.wait_recv()

    queries = jnp.concatenate([every[:, piece, :] for piece in range(pieces)], axis=1)
    passages = jnp.concatenate([every[:, pieces + piece, :] for piece in range(pieces)], axis=1)
    wanted = every[:, 2 * pieces, :][:, :1]
    logits = lax.dot_general(
        queries, passages, (((1,), (1,)), ((), ())), precision=PRECISE, preferred_element_type=F32
    ) / SOFTMAX_TEMPER
    place = lax.broadcasted_iota(jnp.int32, logits.shape, 1)
    target = (place.astype(F32) == wanted).astype(F32)
    top = jnp.max(logits, axis=1, keepdims=True)
    weights = jnp.exp(logits - top)
    row_total = jnp.sum(weights, axis=1, keepdims=True)
    log_total = top + jnp.log(row_total)
    loss = jnp.sum(log_total - jnp.sum(logits * target, axis=1, keepdims=True), axis=0, keepdims=True) / total
    grad_logits = (weights / row_total - target) / (total * SOFTMAX_TEMPER)
    grad_column = jnp.sum(jnp.where(place == my_rank, grad_logits, 0.0), axis=1, keepdims=True)
    value = jnp.dot(grad_logits, passages, precision=PRECISE, preferred_element_type=F32)
    line = lax.broadcasted_iota(jnp.int32, value.shape, 0)
    grad_embeds = (
        jnp.sum(jnp.where(line == my_rank, value, 0.0), axis=0, keepdims=True),
        jnp.sum(grad_column * queries, axis=0, keepdims=True),
    )

    grad_gain, grad_shift, grad_bias = 0.0, 0.0, 0.0
    for index, (start, count) in enumerate(spans):
        embed, grad_embed = embeds[index], grad_embeds[index]
        grad_pooled = shrinks[index] * (grad_embed - embed * jnp.sum(grad_embed * embed, axis=1, keepdims=True))
        grad_gain = grad_gain + grad_pooled * means[index]
        grad_shift = grad_shift + grad_pooled
        spread = grad_pooled * gain / lens[index].astype(F32)
        centered = spread - jnp.mean(spread, axis=1, keepdims=True)
        normed = unit_two[pl.ds(start, count), :]
        value = inverses[index] * (centered - normed * jnp.mean(spread * normed, axis=1, keepdims=True))
        z_two[pl.ds(start, count), :] = value
        grad_low[pl.ds(start, count), :] = value.astype(BF16)
        grad_bias = grad_bias + jnp.sum(value, axis=0, keepdims=True)
    store(grad_low, grad_low_out)
    store(z_two, grad_out)
    small[pl.ds(0, 1), :] = grad_bias
    small[pl.ds(1, 1), :] = grad_gain
    small[pl.ds(2, 1), :] = grad_shift
    small[pl.ds(3, 1), :] = jnp.broadcast_to(loss, (1, model))
    small[pl.ds(4, 4), :] = jnp.zeros((4, model), F32)
    store(small, small_out)
    for copy in sends:
        copy.wait_send()
    for copy in stores:
        copy.wait()


def forward(query_in, passage_in, query_len, passage_len, positive, attn_master, ffn_master, col_bias, norm_params, spans, total):
    rows, width = attn_master.shape[1:]
    units = ffn_master.shape[2]
    slots, model = spans[1][0] + spans[1][1], query_in.shape[2]
    dma = pltpu.SemaphoreType.DMA
    col = col_bias.reshape(-1, LANES)
    anywhere = pl.BlockSpec(memory_space=pltpu.HBM)
    vmem = pl.BlockSpec(memory_space=pltpu.VMEM)
    smem = pl.BlockSpec(memory_space=pltpu.SMEM)
    results = (
        ((2, 3, model, units), BF16),
        ((2, slots, 3 * width), BF16),
        ((2, slots, width), BF16),
        ((slots, model), F32),
        ((slots, LANES), F32),
        ((slots, model), BF16),
        ((2, slots, units), BF16),
        ((2, slots, units), F32),
        ((slots, model), BF16),
        ((slots, model), F32),
        ((slots, model), BF16),
        ((8, model), F32),
    )
    return pl.pallas_call(
        functools.partial(forward_kernel, spans, total),
        out_shape=tuple(jax.ShapeDtypeStruct(*result) for result in results),
        in_specs=[smem] * 3 + [anywhere] * 4 + [vmem] * 2,
        out_specs=(anywhere,) * len(results),
        scratch_shapes=[pltpu.VMEM(*result) for result in results]
        + [
            pltpu.VMEM((2, 1, col_bias.shape[0]), F32),
            pltpu.VMEM(attn_master.shape, F32),
            pltpu.VMEM(ffn_master.shape, F32),
            pltpu.VMEM((slots, model), F32),
            pltpu.VMEM((SLAB, LANES), F32),
            pltpu.VMEM((total, SLAB, LANES), F32),
        ]
        + [dma((3, 4))] * 6
        + [dma((3, 4, 2))] * 2
        + [dma((3, 4))] * 2
        + [dma(()), dma(()), dma((5,)), dma((20,)), dma((total,)), dma((total,))]
        + [dma((4,))] * 4,
        compiler_params=pltpu.CompilerParams(collective_id=0, has_side_effects=True, vmem_limit_bytes=58 * MIB),
        name="forward",
    )(query_len, passage_len, positive, query_in, passage_in, attn_master, ffn_master, col, norm_params)


def backward_kernel(
    spans,
    query_len, passage_len, weight_ref, proj_ref, mixed_ref, unit_ref, inverse_ref, low_ref, active_ref, slope_ref,
    tokens_ref, grad_ref, grad_low_ref, norm_ref, small_ref,
    attn_out, ffn_out, small_out, col_out, query_out, passage_out,
    weight, proj, mixed, inverse, low, active, slope, tokens, total, down, grad_out, grad_proj,
    temp, far_send, far_recv, kept, one_send, one_recv, two_send, two_recv, z_send, z_recv, result, vector, vec_send,
    vec_recv, col,
    load_sem, slope_sem, c_send, c_recv, s1_send, s1_recv, s2_send, s2_recv, s3_send, s3_recv,
    v_send, v_recv, t_send, t_recv, credit, out_sem, layer_recv,
):
    at = Mesh()
    me, core = at.me, at.core
    slots, model = tokens.shape
    width = grad_out.shape[2]
    rows = model // 16
    lens = (query_len[core], passage_len[core])
    near_peer = (at.index(at.z + 1 - 2 * lax.rem(at.z, 2), at.y, at.x), core)
    over_peer = at.z_peer[2]

    sends = {}
    stores = []
    loads = {}

    def load(name, *pairs):
        copies = []
        for source, target in pairs:
            copy = pltpu.make_async_copy(source, target, load_sem.at[sum(len(v) for v in loads.values()) + len(copies)])
            copy.start()
            copies.append(copy)
        loads[name] = copies

    def ready(name):
        for copy in loads[name]:
            copy.wait()

    def store(source, target):
        copy = pltpu.make_async_copy(source, target, out_sem.at[len(stores)])
        copy.start()
        stores.append(copy)

    def push(name, source, target, send, recv, peer):
        copy = remote(source, target, send, recv, peer)
        copy.start()
        sends[name] = copy

    def landed(target, send, recv, peer):
        remote(target, target, send, recv, peer).wait_recv()

    lanes_of = [pl.ds(t * width, width) for t in range(4)]
    pair_lanes = (pl.ds(0, 2 * width), pl.ds(2 * width, 2 * width))

    def slope_tile(half, t):
        index = half * 4 + t
        return pltpu.make_async_copy(slope_ref.at[half, :, lanes_of[t]], slope.at[t % 2], slope_sem.at[index])

    load("down", (grad_low_ref, down))
    load("active1", (active_ref.at[1], active.at[1]))
    barrier = pltpu.get_barrier_semaphore()
    for peer in [*at.z_peer[1:], at.x_peer, at.y_peer, at.c_peer]:
        pl.semaphore_signal(barrier, inc=1, device_id=peer, device_id_type=MESH)
    load("down1", (weight_ref.at[1, 2], weight.at[0]))
    slope_tile(1, 0).start()
    slope_tile(1, 1).start()
    load("active0", (active_ref.at[0], active.at[0]))

    def far_slot(q):
        return q % 2

    def send_far(q, t, value):
        if q == 2:
            sends[("c", 0, t)].wait_send()
        far_send[far_slot(q), t] = value.astype(BF16)
        push(
            ("c", q, t), far_send.at[far_slot(q), t], far_recv.at[far_slot(q), t], c_send.at[q, t], c_recv.at[q, t],
            at.c_peer,
        )

    def side(t):
        steps = ((at.x, at.x_peer), (at.y, at.y_peer))
        return steps if t % 2 == 0 else steps[::-1]

    def block(index, count=1):
        return pl.ds(pl.multiple_of(index * rows, rows), count * rows)

    def first_step(q, t, lanes):
        landed(far_recv.at[far_slot(q), t], c_send.at[q, t], c_recv.at[q, t], at.c_peer)
        (bit, peer), _ = side(t)
        for layer in range(4):
            for other in range(2):
                if t % 2 == 0:
                    mine, theirs = at.index(layer, other, bit), at.index(layer, other, 1 - bit)
                else:
                    mine, theirs = at.index(layer, bit, other), at.index(layer, 1 - bit, other)
                place = pl.ds((layer * 2 + other) * rows, rows)
                far = far_recv[far_slot(q), t, block(theirs), :].astype(F32)
                one_send[q, t, place, :] = (temp[block(theirs), lanes] + far).astype(BF16)
                far = far_recv[far_slot(q), t, block(mine), :].astype(F32)
                kept[q, t, place, :] = temp[block(mine), lanes] + far
        push(("1", q, t), one_send.at[q, t], one_recv.at[q, t], s1_send.at[q, t], s1_recv.at[q, t], peer)

    def second_step(q, t):
        (_, before), (bit, peer) = side(t)
        landed(one_recv.at[q, t], s1_send.at[q, t], s1_recv.at[q, t], before)
        for layer in range(4):
            theirs = block(layer * 2 + 1 - bit)
            value = kept[q, t, theirs, :] + one_recv[q, t, theirs, :].astype(F32)
            two_send[q, t, pl.ds(layer * rows, rows), :] = value.astype(BF16)
            mine = block(layer * 2 + bit)
            kept[q, t, mine, :] = kept[q, t, mine, :] + one_recv[q, t, mine, :].astype(F32)
        push(("2", q, t), two_send.at[q, t], two_recv.at[q, t], s2_send.at[q, t], s2_recv.at[q, t], peer)

    def third_step(q, t):
        _, (bit, before) = side(t)
        landed(two_recv.at[q, t], s2_send.at[q, t], s2_recv.at[q, t], before)
        for k in range(1, 4):
            layer = lax.rem(at.z + k, 4)
            value = kept[q, t, block(layer * 2 + bit), :] + two_recv[q, t, block(layer), :].astype(F32)
            z_send[q, t, k - 1] = value.astype(BF16)
            push(
                ("3", q, t, k), z_send.at[q, t, k - 1], z_recv.at[q, t, k - 1], s3_send.at[q, t, k], s3_recv.at[q, t, k],
                at.z_peer[k],
            )
        result[q, t] = kept[q, t, block(at.z * 2 + bit), :] + two_recv[q, t, block(at.z), :].astype(F32)

    def last_step(q, t):
        for k in range(1, 4):
            landed(z_recv.at[q, t, k - 1], s3_send.at[q, t, k], s3_recv.at[q, t, k], at.z_peer[k])
        value = result[q, t]
        for k in range(3):
            value = value + z_recv[q, t, k].astype(F32)
        result[q, t] = value
        store_result(q, t)

    def store_result(q, t):
        if q < 2:
            store(result.at[q, t], ffn_out.at[1 - q, :, lanes_of[t]])
        elif t == 3:
            store(result.at[q, t], attn_out.at[3])
        else:
            for index in range(3):
                store(result.at[q, t, :, pl.ds(index * LANES, LANES)], attn_out.at[index, :, pl.ds(t * LANES, LANES)])

    def layer_first_step(q, t, lanes):
        landed(far_recv.at[far_slot(q), t], c_send.at[q, t], c_recv.at[q, t], at.c_peer)
        for k in range(1, 4):
            theirs = block(at.index(lax.rem(at.z + k, 4), 0, 0), 4)
            value = temp[theirs, lanes] + far_recv[far_slot(q), t, theirs, :].astype(F32)
            if k < 3:
                source = one_send.at[q, t, pl.ds((k - 1) * 4 * rows, 4 * rows), :]
            else:
                source = two_send.at[q, t]
            source[...] = value.astype(BF16)
            push(
                ("1", q, t, k), source, layer_recv.at[t, k - 1], s3_send.at[q, t, k],
                s3_recv.at[q, t, k], at.z_peer[k],
            )
        mine = block(at.index(at.z, 0, 0), 4)
        kept[q, t, pl.ds(0, 4 * rows), :] = temp[mine, lanes] + far_recv[far_slot(q), t, mine, :].astype(F32)

    def layer_second_step(q, t):
        for k in range(1, 4):
            landed(layer_recv.at[t, k - 1], s3_send.at[q, t, k], s3_recv.at[q, t, k], at.z_peer[k])
        value = kept[q, t, pl.ds(0, 4 * rows), :]
        for k in range(3):
            value = value + layer_recv[t, k].astype(F32)
        kept[q, t, pl.ds(0, 4 * rows), :] = value
        for line in range(2):
            z_send[q, t, line] = kept[q, t, block(line * 2 + 1 - at.x), :].astype(BF16)
        push(
            ("2", q, t), z_send.at[q, t, pl.ds(0, 2)], z_recv.at[q, t, pl.ds(0, 2)], s1_send.at[q, t], s1_recv.at[q, t],
            at.x_peer,
        )

    def layer_third_step(q, t):
        landed(z_recv.at[q, t, pl.ds(0, 2)], s1_send.at[q, t], s1_recv.at[q, t], at.x_peer)
        theirs = kept[q, t, block((1 - at.y) * 2 + at.x), :] + z_recv[q, t, 1 - at.y].astype(F32)
        z_send[q, t, 2] = theirs.astype(BF16)
        push(
            ("3", q, t), z_send.at[q, t, 2], z_recv.at[q, t, 2], s2_send.at[q, t], s2_recv.at[q, t],
            at.y_peer,
        )
        result[q, t] = kept[q, t, block(at.y * 2 + at.x), :] + z_recv[q, t, at.y].astype(F32)

    def layer_last_step(q, t):
        landed(z_recv.at[q, t, 2], s2_send.at[q, t], s2_recv.at[q, t], at.y_peer)
        result[q, t] = result[q, t] + z_recv[q, t, 2].astype(F32)
        store_result(q, t)

    def far_product(q, left, right, pair):
        value = mm_tn(left[...], right[:, pair_lanes[pair]])
        send_far(q, 2 * pair, value[:, :width])
        send_far(q, 2 * pair + 1, value[:, width:])

    def own_product(q, left, right, pair):
        temp[...] = mm_tn(left[...], right[:, pair_lanes[pair]])
        step = layer_first_step if (q, pair) == (0, 0) else first_step
        step(q, 2 * pair, lanes_of[0])
        step(q, 2 * pair + 1, lanes_of[1])

    def hidden_grad(half, slot, pair, following):
        for t in (2 * pair, 2 * pair + 1):
            slope_tile(half, t).wait()
        value = mm(down[...], weight[slot, :, pair_lanes[pair]])
        for side_of, t in enumerate((2 * pair, 2 * pair + 1)):
            piece = (value[:, side_of * width : (side_of + 1) * width] * slope[side_of]).astype(BF16)
            active[half, :, lanes_of[t]] = piece
            vec = vector if half == 0 else vec_send.at[0]
            vec[pl.ds(9 + pair, 1), lanes_of[side_of]] = jnp.sum(piece.astype(F32), axis=0, keepdims=True)
        if following is not None:
            for t in (0, 1):
                slope_tile(following[0], 2 * following[1] + t).start()

    def add_back(source, slot, lanes):
        total[...] = total[...] + mm_nt(source, weight[slot, :, lanes])

    def first_norm_back():
        sums = [None, None, None]
        step = 192
        for start in range(0, slots, step):
            place = pl.ds(start, step)
            grad = total[place, :]
            normed = jnp.concatenate([slope[0, place, :], slope[1, place, :]], axis=1)
            back = normalize_back(normed, inverse[place, pl.ds(0, 1)], grad * norm_ref[pl.ds(1, 1), :])
            for index, value in enumerate((back, grad * normed, grad)):
                value = jnp.sum(value, axis=0, keepdims=True)
                sums[index] = value if sums[index] is None else sums[index] + value
            total[place, :] = back
            down[place, :] = back.astype(BF16)
        for index in range(3):
            vector[pl.ds(index, 1), :] = sums[index]
            vec_send[0, pl.ds(index, 1), :] = sums[index]

    def out_grad(half, slot):
        grad_out[half] = mm(down[...], weight[slot, :, lanes_of[3]]).astype(BF16)

    def query_back(half):
        place = pl.ds(*spans[0])
        queries = stack_heads(proj[half, place, lanes_of[0]])
        grads = stack_heads(grad_out[half, place, :])
        keys = proj[half, place, lanes_of[1]]
        probs = probabilities(mm_nt(queries * jnp.asarray(SCALE, BF16), keys), lens[0])
        grad_probs = mm_nt(grads, proj[half, place, lanes_of[2]])
        inner = jnp.sum(probs * grad_probs, axis=1, keepdims=True)
        grad_scores = (probs * (grad_probs - inner)).astype(BF16)
        value = unstack_heads(mm(grad_scores, keys), spans[0][1]) * SCALE
        grad_proj[half, place, lanes_of[0]] = value.astype(BF16)
        grad_proj[half, place, lanes_of[1]] = (mm_tn(grad_scores, queries) * SCALE).astype(BF16)
        grad_proj[half, place, lanes_of[2]] = mm_tn(probs.astype(BF16), grads).astype(BF16)

    def passage_back(half, pair):
        place = pl.ds(*spans[1])
        spot = [pl.ds(index * width + pair * LANES, LANES) for index in range(3)]
        queries, keys = proj[half, place, spot[0]], proj[half, place, spot[1]]
        grads = grad_out[half, place, pl.ds(pair * LANES, LANES)]
        scores = [mm_nt(queries, key) for key in split_pair(keys * jnp.asarray(SCALE, BF16))]
        grad_probs = [mm_nt(grads, value) for value in split_pair(proj[half, place, spot[2]])]
        outs = []
        for head in range(2):
            probs = probabilities(scores[head], lens[1])
            inner = jnp.sum(probs * grad_probs[head], axis=1, keepdims=True)
            grad_scores = (probs * (grad_probs[head] - inner)).astype(BF16)
            outs.append(
                (mm(grad_scores, keys) * SCALE, mm_tn(grad_scores, queries) * SCALE, mm_tn(probs.astype(BF16), grads))
            )
        lane = first_head(queries.shape)
        for index in range(3):
            grad_proj[half, place, spot[index]] = jnp.where(lane, outs[0][index], outs[1][index]).astype(BF16)

    def pair_product(half, pair):
        spot = [pl.ds(index * width + pair * LANES, LANES) for index in range(3)]
        return mm_tn(tokens[...], jnp.concatenate([grad_proj[half, :, lanes] for lanes in spot], axis=1))

    def attn_biases(half):
        vec = vector if half == 0 else vec_send.at[0]
        for index in (0, 1):
            value = grad_proj[half, :, lanes_of[2 * index]].astype(F32)
            vec[pl.ds(8, 1), lanes_of[index]] = jnp.sum(value, axis=0, keepdims=True)

    def vector_step(step, peer):
        if step:
            vec_send[step] = vector[...]
        push(("v", step), vec_send.at[step], vec_recv.at[step], v_send.at[step], v_recv.at[step], peer)

    def vector_sum(step, peer):
        landed(vec_recv.at[step], v_send.at[step], v_recv.at[step], peer)
        vector[...] = vector[...] + vec_recv[step]

    for target in (vector, vec_send.at[0]):
        target[pl.ds(3, 3), :] = small_ref[pl.ds(0, 3), :]
        target[pl.ds(6, 2), :] = jnp.zeros((2, model), F32)
        target[pl.ds(11, 5), :] = jnp.zeros((5, model), F32)

    ready("down")
    ready("active1")
    pl.semaphore_wait(barrier, 6)
    far_product(0, down, active.at[1], 1)
    far_product(0, down, active.at[1], 0)
    load("down0", (weight_ref.at[0, 2], weight.at[1]))
    load("low", (low_ref, low))
    load("up1", (weight_ref.at[1, 1], weight.at[2]))
    ready("active0")
    own_product(0, down, active.at[0], 1)
    ready("down1")
    hidden_grad(1, 0, 0, (0, 0))
    own_product(0, down, active.at[0], 0)
    pl.semaphore_signal(credit, inc=1, device_id=at.c_peer, device_id_type=MESH)
    ready("low")
    far_product(1, low, active.at[1], 0)
    ready("down0")
    hidden_grad(0, 1, 0, (1, 1))
    load("total", (grad_ref, total))
    load("inverse", (inverse_ref, inverse))
    own_product(1, low, active.at[0], 0)
    hidden_grad(1, 0, 1, (0, 1))
    load("up0", (weight_ref.at[0, 1], weight.at[0]))
    far_product(1, low, active.at[1], 1)
    second_step(0, 2)
    second_step(0, 3)
    hidden_grad(0, 1, 1, None)
    load("unit", *[(unit_ref.at[:, lanes_of[t]], slope.at[t]) for t in range(2)])
    load("attn1", (weight_ref.at[1, 0], weight.at[1]))
    load("proj", (proj_ref, proj), (mixed_ref, mixed), (tokens_ref, tokens))
    own_product(1, low, active.at[0], 1)
    ready("total")
    ready("up1")
    add_back(active[1], 2, pl.ds(0, 4 * width))
    load("attn0", (weight_ref.at[0, 0], weight.at[2]))
    ready("up0")
    add_back(active[0], 0, pl.ds(0, 4 * width))
    second_step(1, 0)
    second_step(1, 1)
    ready("inverse")
    ready("unit")
    first_norm_back()
    ready("proj")
    pl.semaphore_wait(credit, 1)
    send_far(2, 3, mm_tn(down[...], mixed[1]))
    ready("attn1")
    out_grad(1, 1)
    query_back(1)
    temp[:, lanes_of[0]] = mm_tn(down[...], mixed[0])
    first_step(2, 3, lanes_of[0])
    third_step(0, 2)
    third_step(0, 3)
    passage_back(1, 0)
    send_far(2, 0, pair_product(1, 0))
    ready("attn0")
    out_grad(0, 2)
    query_back(0)
    layer_second_step(0, 0)
    passage_back(0, 0)
    temp[:, lanes_of[1]] = pair_product(0, 0)
    first_step(2, 0, lanes_of[1])
    second_step(1, 2)
    second_step(1, 3)
    passage_back(1, 1)
    send_far(2, 1, pair_product(1, 1))
    third_step(1, 0)
    third_step(1, 1)
    layer_second_step(0, 1)
    layer_third_step(0, 0)
    passage_back(0, 1)
    temp[:, lanes_of[0]] = pair_product(0, 1)
    first_step(2, 1, lanes_of[0])
    last_step(0, 2)
    last_step(0, 3)
    passage_back(1, 2)
    send_far(2, 2, pair_product(1, 2))
    attn_biases(1)
    vector_step(0, at.c_peer)
    second_step(2, 3)
    layer_third_step(0, 1)
    passage_back(0, 2)
    temp[:, lanes_of[1]] = pair_product(0, 2)
    first_step(2, 2, lanes_of[1])
    second_step(2, 0)
    third_step(1, 2)
    third_step(1, 3)
    attn_biases(0)
    vector_sum(0, at.c_peer)
    vector_step(1, at.x_peer)
    add_back(grad_proj[1], 1, pl.ds(0, 3 * width))
    second_step(2, 1)
    third_step(2, 3)
    add_back(grad_proj[0], 2, pl.ds(0, 3 * width))
    for index, target in ((0, query_out), (1, passage_out)):
        part = total.at[pl.ds(*spans[index]), :]
        store(part, target.at[core])
        push(("t", index), part, target.at[core], t_send.at[index], t_recv.at[index], at.c_peer)
    third_step(2, 0)
    vector_sum(1, at.x_peer)
    vector_step(2, at.y_peer)
    layer_last_step(0, 0)
    layer_last_step(0, 1)
    last_step(1, 0)
    last_step(1, 1)
    vector_sum(2, at.y_peer)
    vector_step(3, near_peer)
    last_step(1, 2)
    last_step(1, 3)
    second_step(2, 2)
    vector_sum(3, near_peer)
    vector_step(4, over_peer)
    third_step(2, 1)
    last_step(2, 3)
    last_step(2, 0)
    vector_sum(4, over_peer)
    store(vector.at[pl.ds(0, 8), :], small_out)
    for line in range(3):
        for piece in range(model // LANES):
            col[pl.ds(line * (model // LANES) + piece, 1), :] = vector[pl.ds(8 + line, 1), pl.ds(piece * LANES, LANES)]
    store(col, col_out)
    third_step(2, 2)
    last_step(2, 1)
    last_step(2, 2)
    for index, target in ((0, query_out), (1, passage_out)):
        landed(target.at[1 - core], t_send.at[index], t_recv.at[index], at.c_peer)
    for copy in stores:
        copy.wait()
    for name, copy in sends.items():
        if name[:2] != ("c", 0):
            copy.wait_send()


def backward(query_len, passage_len, kept, norm_params, spans):
    weight, proj, mixed, unit, inverse, low, active, slope, tokens, grad_ztwo, grad_low, small = kept
    slots, model = tokens.shape
    width = mixed.shape[2]
    rows = model // 16
    anywhere = pl.BlockSpec(memory_space=pltpu.HBM)
    vmem = pl.BlockSpec(memory_space=pltpu.VMEM)
    smem = pl.BlockSpec(memory_space=pltpu.SMEM)
    dma = pltpu.SemaphoreType.DMA
    lines = 3 * model // LANES
    scratch = [
        pltpu.VMEM((3, model, 4 * width), BF16),
        pltpu.VMEM(proj.shape, BF16),
        pltpu.VMEM(mixed.shape, BF16),
        pltpu.VMEM(inverse.shape, F32),
        pltpu.VMEM(low.shape, BF16),
        pltpu.VMEM(active.shape, BF16),
        pltpu.VMEM((2, slots, width), F32),
        pltpu.VMEM(tokens.shape, BF16),
        pltpu.VMEM((slots, model), F32),
        pltpu.VMEM((slots, model), BF16),
        pltpu.VMEM((2, slots, width), BF16),
        pltpu.VMEM((2, slots, 3 * width), BF16),
        pltpu.VMEM((model, 2 * width), F32),
        pltpu.VMEM((2, 4, model, width), BF16),
        pltpu.VMEM((2, 4, model, width), BF16),
        pltpu.VMEM((3, 4, 8 * rows, width), F32),
        pltpu.VMEM((3, 4, 8 * rows, width), BF16),
        pltpu.VMEM((3, 4, 8 * rows, width), BF16),
        pltpu.VMEM((3, 4, 4 * rows, width), BF16),
        pltpu.VMEM((3, 4, 4 * rows, width), BF16),
        pltpu.VMEM((3, 4, 3, rows, width), BF16),
        pltpu.VMEM((3, 4, 3, rows, width), BF16),
        pltpu.VMEM((3, 4, rows, width), F32),
        pltpu.VMEM((16, model), F32),
        pltpu.VMEM((5, 16, model), F32),
        pltpu.VMEM((5, 16, model), F32),
        pltpu.VMEM((lines, LANES), F32),
        dma((20,)), dma((8,)),
        dma((3, 4)), dma((3, 4)), dma((3, 4)), dma((3, 4)), dma((3, 4)), dma((3, 4)),
        dma((3, 4, 4)), dma((3, 4, 4)),
        dma((5,)), dma((5,)), dma((2,)), dma((2,)),
        pltpu.SemaphoreType.REGULAR,
        dma((24,)),
        pltpu.VMEM((2, 3, 4 * rows, width), BF16),
    ]
    return pl.pallas_call(
        functools.partial(backward_kernel, spans),
        out_shape=(
            jax.ShapeDtypeStruct((4, rows, width), F32),
            jax.ShapeDtypeStruct((2, rows, 4 * width), F32),
            jax.ShapeDtypeStruct((8, model), F32),
            jax.ShapeDtypeStruct((lines, LANES), F32),
            jax.ShapeDtypeStruct((2, spans[0][1], model), F32),
            jax.ShapeDtypeStruct((2, spans[1][1], model), F32),
        ),
        in_specs=[smem] * 2 + [anywhere] * 11 + [vmem, vmem],
        out_specs=(anywhere,) * 6,
        scratch_shapes=scratch,
        compiler_params=pltpu.CompilerParams(collective_id=2, has_side_effects=True, vmem_limit_bytes=60 * MIB),
        name="backward",
    )(query_len, passage_len, weight, proj, mixed, unit, inverse, low, active, slope, tokens, grad_ztwo, grad_low,
      norm_params, small)


def finish_kernel(
    step_ref, rates_ref, query_ref, passage_ref,
    attn_grad, ffn_grad, norm_grad, col_grad, loss_ref,
    attn_m, attn_f, attn_s, attn_a, ffn_m, ffn_f, ffn_s, ffn_a,
    norm_m, norm_f, norm_s, norm_a, col_m, col_f, col_s, col_a,
    loss_out, query_out, passage_out,
    attn_mo, attn_fo, attn_so, attn_ao, ffn_mo, ffn_fo, ffn_so, ffn_ao,
    norm_mo, norm_fo, norm_so, norm_ao, col_mo, col_fo, col_so, col_ao, attn_co, ffn_co,
    attn_in, attn_res, attn_low, ffn_in, ffn_res, ffn_low, norm_in, norm_res, col_in, col_res, small, query, passage,
    in_sem, out_sem,
):
    loads, stores = [], []

    def load(source, target):
        copy = pltpu.make_async_copy(source, target, in_sem.at[len(loads)])
        copy.start()
        loads.append(copy)
        return copy

    def store(source, target):
        copy = pltpu.make_async_copy(source, target, out_sem.at[len(stores)])
        copy.start()
        stores.append(copy)

    groups = [
        [
            load(source.at[which], ffn_in.at[index, which])
            for index, source in enumerate((ffn_m, ffn_f, ffn_s, ffn_a, ffn_grad))
        ]
        for which in range(2)
    ]
    groups.append(
        [load(source, attn_in.at[index]) for index, source in enumerate((attn_m, attn_f, attn_s, attn_a, attn_grad))]
    )
    lines = norm_in.shape[1]
    groups.append(
        [load(source, norm_in.at[index]) for index, source in enumerate((norm_m, norm_f, norm_s, norm_a))]
        + [load(norm_grad, small.at[0]), load(loss_ref, small.at[1])]
        + [load(source, col_in.at[index]) for index, source in enumerate((col_m, col_f, col_s, col_a, col_grad))]
    )
    half = passage.shape[1] // 2
    parts = [(pair, pl.ds(at * half, half)) for pair in range(2) for at in range(2)]

    count = jnp.full((1, 1), step_ref[0], jnp.int32).astype(F32)
    rate = [jnp.full((1, 1), rates_ref[index], F32) for index in range(5)]
    to_first, to_second = [1.0 / (1.0 - jnp.exp(count * jnp.log(rate[index]))) for index in range(2)]

    def update(master, first, second, average, grad, learn, decay):
        first_new = rate[0] * first + (1.0 - rate[0]) * grad
        second_new = rate[1] * second + (1.0 - rate[1]) * grad * grad
        move = (first_new * to_first) / (jnp.sqrt(second_new * to_second) + ADAM_EPS)
        if decay:
            move = move + decay * master
        master_new = master - learn * move
        average_new = rate[2] * average + (1.0 - rate[2]) * master_new
        return master_new, first_new, second_new, average_new

    def wait(group):
        for copy in groups[group]:
            copy.wait()

    for which in range(2):
        wait(which)
        if which == 0:
            groups.append([load(query_ref, query)])
            for pair, place in parts:
                groups.append([load(passage_ref.at[pair, place, :], passage.at[pair, place, :])])
        values = update(*[ffn_in[index, which] for index in range(5)], rate[3], DECAY_WEIGHT)
        for index, (value, target) in enumerate(zip(values, (ffn_mo, ffn_fo, ffn_so, ffn_ao))):
            ffn_res[index, which] = value
            store(ffn_res.at[index, which], target.at[which])
        ffn_low[which] = values[0].astype(BF16)
        store(ffn_low.at[which], ffn_co.at[which])
    wait(2)
    for which in range(attn_low.shape[0]):
        values = update(*[attn_in[index, which] for index in range(5)], rate[3], DECAY_WEIGHT)
        for index, value in enumerate(values):
            attn_res[index, which] = value
        attn_low[which] = values[0].astype(BF16)
    for index, target in enumerate((attn_mo, attn_fo, attn_so, attn_ao)):
        store(attn_res.at[index], target)
    store(attn_low, attn_co)
    wait(3)
    values = update(*[norm_in[index] for index in range(4)], small[0, pl.ds(0, lines), :], rate[4], 0.0)
    for index, (value, target) in enumerate(zip(values, (norm_mo, norm_fo, norm_so, norm_ao))):
        norm_res[index] = value
        store(norm_res.at[index], target)
    values = update(*[col_in[index] for index in range(5)], rate[4], 0.0)
    for index, (value, target) in enumerate(zip(values, (col_mo, col_fo, col_so, col_ao))):
        col_res[index] = value
        store(col_res.at[index], target)
    wait(4)
    store(query, query_out)
    for index, (pair, place) in enumerate(parts):
        wait(5 + index)
        store(passage.at[pair, place, :], passage_out.at[pair, place, :])
    loss_out[0] = jnp.sum(small[1, pl.ds(3, 1), pl.ds(0, 1)])
    for copy in stores:
        copy.wait()


def finish(step, rates, grads, loss_rows, attn_state, ffn_state, norm_state, col_state):
    attn_grad, ffn_grad, norm_grad, col_grad, query_grad, passage_grad = grads
    anywhere = pl.BlockSpec(memory_space=pltpu.HBM)
    smem = pl.BlockSpec(memory_space=pltpu.SMEM)
    dma = pltpu.SemaphoreType.DMA
    col_state = [value.reshape(-1, LANES) for value in col_state]
    states = (attn_state, ffn_state, norm_state, col_state)
    shapes = [jax.ShapeDtypeStruct((1,), F32)]
    shapes += [jax.ShapeDtypeStruct(value.shape, F32) for value in (query_grad, passage_grad)]
    shapes += [jax.ShapeDtypeStruct(value.shape, F32) for state in states for value in state]
    shapes += [jax.ShapeDtypeStruct(state[0].shape, BF16) for state in (attn_state, ffn_state)]
    scratch = []
    for state in (attn_state, ffn_state):
        shape = state[0].shape
        scratch += [pltpu.VMEM((5,) + shape, F32), pltpu.VMEM((4,) + shape, F32), pltpu.VMEM(shape, BF16)]
    for state, count in ((norm_state, 4), (col_state, 5)):
        shape = state[0].shape
        scratch += [pltpu.VMEM((count,) + shape, F32), pltpu.VMEM((4,) + shape, F32)]
    outs = pl.pallas_call(
        finish_kernel,
        out_shape=tuple(shapes),
        in_specs=[smem] * 2 + [anywhere] * 23,
        out_specs=(smem,) + (anywhere,) * 20,
        scratch_shapes=scratch
        + [pltpu.VMEM((2,) + norm_grad.shape, F32), pltpu.VMEM(query_grad.shape, F32), pltpu.VMEM(passage_grad.shape, F32)]
        + [dma((32,)), dma((32,))],
        compiler_params=pltpu.CompilerParams(vmem_limit_bytes=60 * MIB),
        name="finish",
    )(step, rates, query_grad, passage_grad, attn_grad, ffn_grad, norm_grad, col_grad, loss_rows,
      *attn_state, *ffn_state, *norm_state, *col_state)
    outs = list(outs)
    outs[15:19] = [value.reshape(-1) for value in outs[15:19]]
    return outs


def attend_kernel(spans, lens_ref, q_ref, k_ref, v_ref, o_ref):
    for index, (start, slots) in enumerate(spans):
        length = lens_ref[index]
        keys = k_ref[0, pl.ds(start, slots), :]
        values = v_ref[0, pl.ds(start, slots), :]
        lane = first_head(keys.shape)
        scaled = keys * jnp.asarray(HD**-0.5, BF16)
        zero = jnp.zeros_like(scaled)
        head_keys = (jnp.where(lane, scaled, zero), jnp.where(lane, zero, scaled))
        block = min(slots, 256)
        for at in range(0, slots, block):
            queries = q_ref[0, pl.ds(start + at, block), :]
            outs = []
            for head in range(2):
                scores = mm_nt(queries, head_keys[head])
                valid = lax.broadcasted_iota(jnp.int32, scores.shape, 1) < length
                scores = jnp.where(valid, scores, NEG_FILL)
                top = jnp.max(scores, axis=1, keepdims=True)
                weight = jnp.exp(scores - top)
                total = jnp.sum(weight, axis=1, keepdims=True)
                probs = (weight * (1.0 / total)).astype(BF16)
                outs.append(mm(probs, values))
            o_ref[pl.ds(start + at, block), :] = jnp.where(
                first_head(outs[0].shape), outs[0], outs[1]
            ).astype(BF16)


def attend_back_kernel(spans, lens_ref, q_ref, k_ref, v_ref, g_ref, d_ref):
    scale = HD**-0.5
    for index, (start, slots) in enumerate(spans):
        length = lens_ref[index]
        keys = k_ref[0, pl.ds(start, slots), :]
        values = v_ref[0, pl.ds(start, slots), :]
        lane = first_head(keys.shape)
        scaled = keys * jnp.asarray(scale, BF16)
        zero = jnp.zeros_like(scaled)
        head_keys = (jnp.where(lane, scaled, zero), jnp.where(lane, zero, scaled))
        head_values = (jnp.where(lane, values, zero), jnp.where(lane, zero, values))
        block = min(slots, 256)
        grad_k = [None, None]
        grad_v = [None, None]
        for at in range(0, slots, block):
            queries = q_ref[0, pl.ds(start + at, block), :]
            grads = g_ref[pl.ds(start + at, block), :]
            grad_q = []
            for head in range(2):
                scores = mm_nt(head_keys[head], queries)
                valid = lax.broadcasted_iota(jnp.int32, scores.shape, 0) < length
                scores = jnp.where(valid, scores, NEG_FILL)
                top = jnp.max(scores, axis=0, keepdims=True)
                weight = jnp.exp(scores - top)
                total = jnp.sum(weight, axis=0, keepdims=True)
                probs = weight * (1.0 / total)
                grad_probs = mm_nt(head_values[head], grads)
                inner = jnp.sum(probs * grad_probs, axis=0, keepdims=True)
                grad_scores = (probs * (grad_probs - inner)).astype(BF16)
                part_v = mm(probs.astype(BF16), grads)
                part_k = mm(grad_scores, queries)
                grad_v[head] = part_v if at == 0 else grad_v[head] + part_v
                grad_k[head] = part_k if at == 0 else grad_k[head] + part_k
                grad_q.append(mm_tn(grad_scores, keys))
            d_ref[0, pl.ds(start + at, block), :] = (
                jnp.where(first_head(grad_q[0].shape), grad_q[0], grad_q[1]) * scale
            ).astype(BF16)
        d_ref[1, pl.ds(start, slots), :] = (jnp.where(lane, grad_k[0], grad_k[1]) * scale).astype(BF16)
        d_ref[2, pl.ds(start, slots), :] = jnp.where(lane, grad_v[0], grad_v[1]).astype(BF16)


def head_specs(tokens):
    return [pl.BlockSpec((1, tokens, LANES), functools.partial(lambda s, i, lens: (s, 0, i), s)) for s in range(3)]


def attend(proj, lens, spans):
    _, tokens, width = proj.shape
    flops = sum(4 * slots * slots * width for _, slots in spans)
    return pl.pallas_call(
        functools.partial(attend_kernel, spans),
        out_shape=jax.ShapeDtypeStruct((tokens, width), BF16),
        grid_spec=pltpu.PrefetchScalarGridSpec(
            num_scalar_prefetch=1,
            grid=(width // LANES,),
            in_specs=head_specs(tokens),
            out_specs=pl.BlockSpec((tokens, LANES), lambda i, lens: (0, i)),
        ),
        compiler_params=pltpu.CompilerParams(vmem_limit_bytes=40 * MIB),
        cost_estimate=pl.CostEstimate(flops=8 * flops, bytes_accessed=8 * tokens * width, transcendentals=0),
        name="attend",
    )(lens, proj, proj, proj)


def attend_back(proj, grad_out, lens, spans):
    _, tokens, width = proj.shape
    flops = sum(10 * slots * slots * width for _, slots in spans)
    return pl.pallas_call(
        functools.partial(attend_back_kernel, spans),
        out_shape=jax.ShapeDtypeStruct((3, tokens, width), BF16),
        grid_spec=pltpu.PrefetchScalarGridSpec(
            num_scalar_prefetch=1,
            grid=(width // LANES,),
            in_specs=head_specs(tokens) + [pl.BlockSpec((tokens, LANES), lambda i, lens: (0, i))],
            out_specs=pl.BlockSpec((3, tokens, LANES), lambda i, lens: (0, 0, i)),
        ),
        compiler_params=pltpu.CompilerParams(vmem_limit_bytes=40 * MIB),
        cost_estimate=pl.CostEstimate(flops=8 * flops, bytes_accessed=14 * tokens * width, transcendentals=0),
        name="attend_back",
    )(lens, proj, proj, proj, grad_out)


def up_kernel(x_ref, w_ref, b_ref, g_ref, s_ref):
    hidden = mm(x_ref[...], w_ref[0]) + b_ref[...]
    active, slope = gelu_and_slope(hidden)
    g_ref[...] = active.astype(BF16)
    s_ref[...] = slope


def feed_up(low, ffn_half, bias):
    tokens, width = low.shape
    units = ffn_half.shape[2]
    tile = 256
    return pl.pallas_call(
        up_kernel,
        out_shape=(jax.ShapeDtypeStruct((tokens, units), BF16), jax.ShapeDtypeStruct((tokens, units), F32)),
        grid=(units // tile,),
        in_specs=[
            pl.BlockSpec((tokens, width), lambda i: (0, 0)),
            pl.BlockSpec((1, width, tile), lambda i: (0, 0, i)),
            pl.BlockSpec((1, tile), lambda i: (0, i)),
        ],
        out_specs=(pl.BlockSpec((tokens, tile), lambda i: (0, i)), pl.BlockSpec((tokens, tile), lambda i: (0, i))),
        compiler_params=pltpu.CompilerParams(vmem_limit_bytes=40 * MIB),
        cost_estimate=pl.CostEstimate(
            flops=2 * tokens * width * units, bytes_accessed=8 * tokens * units, transcendentals=tokens * units
        ),
        name="feed_up",
    )(low, ffn_half, bias.reshape(1, -1))


def swap_cores(values):
    return lax.ppermute(values, "mp", [(0, 1), (1, 0)])


def scatter_sum(own_parts, other_parts):
    summed = [own + swap_cores(other).astype(F32) for own, other in zip(own_parts, other_parts)]
    return [lax.psum_scatter(value, "dp", scatter_dimension=1, tiled=True) for value in summed]


def adam_update(master, first, second, average, grad, rate, decay_w, rates, step_count):
    first_new = rates[0] * first + (1.0 - rates[0]) * grad
    second_new = rates[1] * second + (1.0 - rates[1]) * grad * grad
    fixed_one = first_new / (1.0 - rates[0] ** step_count)
    fixed_two = second_new / (1.0 - rates[1] ** step_count)
    master_new = master - rate * (fixed_one / (jnp.sqrt(fixed_two) + ADAM_EPS) + decay_w * master)
    average_new = rates[2] * average + (1.0 - rates[2]) * master_new
    return (master_new, first_new, second_new, average_new)


def forward_plain(tokens, lens, attn_low, ffn_low, col_bias, norm_params, spans):
    attn_full = lax.all_gather(attn_low, "dp", axis=1, tiled=True)
    ffn_full = lax.all_gather(ffn_low, "dp", axis=1, tiled=True)
    attn_w = (attn_full, swap_cores(attn_full))
    ffn_w = (ffn_full, swap_cores(ffn_full))
    col = (col_bias, swap_cores(col_bias))
    width = attn_w[0].shape[2]

    projected, mixed = [], []
    branch = None
    for half in range(2):
        bias = jnp.stack([col[half][:width], jnp.zeros((width,), F32), col[half][width : 2 * width]])
        proj = (
            jnp.einsum("td,sde->ste", tokens, attn_w[half][:3], preferred_element_type=F32) + bias[:, None, :]
        ).astype(BF16)
        out = attend(proj, lens, spans)
        part = mm_nt(out, attn_w[half][3])
        branch = part if branch is None else branch + part
        projected.append(proj)
        mixed.append(out)
    z_one = tokens.astype(F32) + branch + norm_params[0]
    unit_one, inverse_one = normalize(z_one)
    first_norm = unit_one * norm_params[1] + norm_params[2]
    first_low = first_norm.astype(BF16)
    active, slope = [], []
    branch_two = None
    for half in range(2):
        act, slo = feed_up(first_low, ffn_w[half], col[half][2 * width :])
        part = mm_nt(act, ffn_w[half][1])
        branch_two = part if branch_two is None else branch_two + part
        active.append(act)
        slope.append(slo)
    z_two = first_norm + branch_two + norm_params[3]
    return attn_w, ffn_w, projected, mixed, unit_one, inverse_one, first_low, active, slope, z_two


def loss_plain(z_two, lens, target_mine, norm_params, spans, pairs):
    query_slots, passage_slots = spans[0][1], spans[1][1]
    model_width = z_two.shape[1]
    core = lax.axis_index("mp")
    unit_two, inverse_two = normalize(z_two)
    places = jnp.arange(query_slots + passage_slots)
    in_query = (places < query_slots) & (places < lens[0])
    in_passage = (places >= query_slots) & (places - query_slots < lens[1])
    share = (
        jnp.stack([in_query, in_passage]).astype(F32) / lens.astype(F32)[:, None]
    )
    mean_unit = jnp.dot(share, unit_two, precision=PRECISE, preferred_element_type=F32)
    pooled = mean_unit * norm_params[4] + norm_params[5]
    shrink = lax.rsqrt(jnp.sum(pooled * pooled, axis=1, keepdims=True) + POOL_EPS)
    embed = pooled * shrink

    payload = jnp.concatenate([embed.reshape(-1), target_mine])
    every = lax.all_gather(payload, ("dp", "mp"), axis=0)
    every_q = every[:, :model_width]
    every_p = every[:, model_width : 2 * model_width]
    target = (jnp.arange(pairs)[None, :].astype(F32) == every[:, 2 * model_width :][:, :1]).astype(F32)
    logits = lax.dot_general(every_q, every_p, (((1,), (1,)), ((), ())), precision=PRECISE) / SOFTMAX_TEMPER
    row_top = jnp.max(logits, axis=1, keepdims=True)
    exp_logits = jnp.exp(logits - row_top)
    row_total = jnp.sum(exp_logits, axis=1, keepdims=True)
    log_total = row_top[:, 0] + jnp.log(row_total[:, 0])
    loss_value = (jnp.sum(log_total - jnp.sum(logits * target, axis=1)) / pairs).reshape(1)
    grad_logits = (exp_logits / row_total - target) / (pairs * SOFTMAX_TEMPER)
    rank = lax.axis_index("dp") * lax.axis_size("mp") + core
    grad_uq = jnp.dot(lax.dynamic_index_in_dim(grad_logits, rank, 0, keepdims=True), every_p, precision=PRECISE)
    grad_up = jnp.dot(
        lax.dynamic_index_in_dim(grad_logits, rank, 1, keepdims=False)[None], every_q, precision=PRECISE
    )
    grad_embed = jnp.concatenate([grad_uq, grad_up], axis=0)

    grad_pooled = shrink * (grad_embed - embed * jnp.sum(grad_embed * embed, axis=1, keepdims=True))
    grad_gain_two = jnp.sum(grad_pooled * mean_unit, axis=0)
    grad_shift_two = jnp.sum(grad_pooled, axis=0)
    grad_unit_two = lax.dot_general(
        share, grad_pooled * norm_params[4], (((0,), (0,)), ((), ())), precision=PRECISE
    )
    grad_ztwo = normalize_back(unit_two, inverse_two, grad_unit_two)
    grad_bias_two = jnp.sum(grad_ztwo, axis=0)
    grad_two_low = grad_ztwo.astype(BF16)
    return grad_ztwo, grad_two_low, loss_value, grad_bias_two, grad_gain_two, grad_shift_two


def backward_plain(tokens, lens, kept, grad_ztwo, grad_two_low, norm_params, second_grads, spans):
    attn_w, ffn_w, projected, mixed, unit_one, inverse_one, first_low, active, slope = kept
    grad_bias_two, grad_gain_two, grad_shift_two = second_grads
    query_slots = spans[0][1]
    core = lax.axis_index("mp")
    cut = ffn_w[0].shape[2] // 2
    width = attn_w[0].shape[2]

    def two_parts(values):
        return values[:, :cut], values[:, cut:]

    def parted_product(left, halves):
        own = [mm_tn(left, part)[None] for part in two_parts(halves[0])]
        other = [mm_tn(left, part).astype(BF16)[None] for part in two_parts(halves[1])]
        return own, other

    down_grad = scatter_sum(*parted_product(grad_two_low, active))
    grad_hidden, grad_first = [], grad_ztwo
    for half in (1, 0):
        grad_hid = (mm(grad_two_low, ffn_w[half][1]) * slope[half]).astype(BF16)
        grad_hidden.insert(0, grad_hid)
        grad_first = grad_first + mm_nt(grad_hid, ffn_w[half][0])
    grad_hidden_bias = [jnp.sum(value.astype(F32), axis=0) for value in grad_hidden]
    up_grad = scatter_sum(*parted_product(first_low, grad_hidden))

    grad_gain_one = jnp.sum(grad_first * unit_one, axis=0)
    grad_shift_one = jnp.sum(grad_first, axis=0)
    grad_zone = normalize_back(unit_one, inverse_one, grad_first * norm_params[1])
    grad_bias_out = jnp.sum(grad_zone, axis=0)
    grad_one_low = grad_zone.astype(BF16)
    grad_tokens = grad_zone
    grad_query_bias, grad_value_bias, attn_parts = [None, None], [None, None], [None, None]
    for half in (1, 0):
        grad_out = mm(grad_one_low, attn_w[half][3]).astype(BF16)
        grad_proj = attend_back(projected[half], grad_out, lens, spans)
        grad_query_bias[half] = jnp.sum(grad_proj[0].astype(F32), axis=0)
        grad_value_bias[half] = jnp.sum(grad_proj[2].astype(F32), axis=0)
        in_grads = jnp.einsum("td,ste->sde", tokens, grad_proj, preferred_element_type=F32)
        out_grad = mm_tn(grad_one_low, mixed[half])
        parts = [in_grads[:2], jnp.stack([in_grads[2], out_grad])]
        attn_parts[half] = parts if half == 0 else [part.astype(BF16) for part in parts]
        for index in range(3):
            grad_tokens = grad_tokens + mm_nt(grad_proj[index], attn_w[half][index])
    attn_grads = scatter_sum(*attn_parts)

    col_parts = [
        jnp.concatenate([grad_query_bias[half], grad_value_bias[half], grad_hidden_bias[half]]) for half in range(2)
    ]
    norm_part = jnp.stack(
        [grad_bias_out, grad_gain_one, grad_shift_one, grad_bias_two, grad_gain_two, grad_shift_two]
    )
    norm_part = norm_part + swap_cores(norm_part)
    col_part = col_parts[0] + swap_cores(col_parts[1])
    small = lax.psum(jnp.concatenate([norm_part.reshape(-1), col_part]), "dp")
    norm_grad = small[: norm_part.size].reshape(norm_part.shape)
    col_grad = small[norm_part.size :]

    attn_grad = jnp.concatenate(attn_grads, axis=0)
    ffn_grad = jnp.stack([jnp.concatenate(parts, axis=-1)[0] for parts in (up_grad, down_grad)])
    grad_twin = swap_cores(grad_tokens)
    first_pair = jnp.where(core == 0, grad_tokens, grad_twin)
    second_pair = jnp.where(core == 0, grad_twin, grad_tokens)
    query_grad = jnp.stack([first_pair[:query_slots], second_pair[:query_slots]])
    passage_grad = jnp.stack([first_pair[query_slots:], second_pair[query_slots:]])
    return attn_grad, ffn_grad, norm_grad, col_grad, query_grad, passage_grad


def per_device(
    query_in,
    passage_in,
    query_len,
    passage_len,
    positive,
    step,
    rates,
    attn_master,
    attn_first,
    attn_second,
    attn_average,
    ffn_master,
    ffn_first,
    ffn_second,
    ffn_average,
    norm_params,
    norm_first,
    norm_second,
    norm_average,
    col_bias,
    col_first,
    col_second,
    col_average,
):
    size = lax.axis_size("dp")
    query_slots = query_in.shape[1]
    spans = ((0, query_slots), (query_slots, passage_in.shape[1]))
    pairs = query_in.shape[0] * size
    attn_state = (attn_master, attn_first, attn_second, attn_average)
    ffn_state = (ffn_master, ffn_first, ffn_second, ffn_average)
    norm_state = (norm_params, norm_first, norm_second, norm_average)
    col_state = (col_bias, col_first, col_second, col_average)
    if size == 16:
        kept = forward(
            query_in, passage_in, query_len, passage_len, positive, attn_master, ffn_master, col_bias, norm_params, spans,
            pairs,
        )
        grads = backward(query_len, passage_len, kept, norm_params, spans)
        return tuple(finish(step, rates, grads, kept[11], attn_state, ffn_state, norm_state, col_state))

    core = lax.axis_index("mp")

    def pick(values, index):
        return lax.dynamic_index_in_dim(values, index, 0, keepdims=False)

    tokens = jnp.concatenate([pick(query_in, core), pick(passage_in, core)], axis=0)
    lens = jnp.stack([pick(query_len, core), pick(passage_len, core)])
    target = jnp.broadcast_to(pick(positive, core).astype(F32), (LANES,))
    outs = forward_plain(tokens, lens, attn_master.astype(BF16), ffn_master.astype(BF16), col_bias, norm_params, spans)
    kept, z_two = outs[:9], outs[9]
    outs = loss_plain(z_two, lens, target, norm_params, spans, pairs)
    grad_ztwo, grad_two_low, loss_value, *second_grads = outs
    attn_grad, ffn_grad, norm_grad, col_grad, query_grad, passage_grad = backward_plain(
        tokens, lens, kept, grad_ztwo, grad_two_low, norm_params, second_grads, spans
    )
    step_count = step[0].astype(F32)
    outs = []
    for state, grad, rate, decay in (
        (attn_state, attn_grad, rates[3], DECAY_WEIGHT),
        (ffn_state, ffn_grad, rates[3], DECAY_WEIGHT),
        (norm_state, norm_grad, rates[4], 0.0),
        (col_state, col_grad, rates[4], 0.0),
    ):
        outs.extend(adam_update(*state, grad, rate, decay, rates, step_count))
    return (loss_value, query_grad, passage_grad, *outs, outs[0].astype(BF16), outs[4].astype(BF16))


def solution(mesh):
    matrix = P(None, "dp", "mp")
    rows = P("dp", None, None)
    placed = (rows, rows, P("dp"), P("dp"), P("dp"), P(), P(), *[matrix] * 8, *[P()] * 4, *[P("mp")] * 4)
    return jax.shard_map(
        per_device,
        mesh=mesh,
        in_specs=placed,
        out_specs=(P(), rows, rows, *[matrix] * 8, *[P()] * 4, *[P("mp")] * 4, matrix, matrix),
        check_vma=False,
    )
```

```python
import functools

import jax
import jax.numpy as jnp
from jax import lax
from jax.experimental import pallas as pl
from jax.experimental.pallas import tpu as pltpu
from jax.sharding import PartitionSpec as P

HD = 64
LANES = 128
NEG_FILL = -1e30
SOFTMAX_TEMPER = 0.02
NORM_EPS = 1e-12
POOL_EPS = 1e-06
DECAY_WEIGHT = 0.01
ADAM_EPS = 1e-08
PRECISE = lax.Precision.HIGHEST
MESH = pl.DeviceIdType.MESH
MIB = 2**20
F32 = jnp.float32
BF16 = jnp.bfloat16

ERFC_STEP = 0.46
ERFC_HALF = (
    0.5 * 0.26113873056821263,
    0.5 * 0.23637801512084577,
    0.5 * 0.3601812301921897,
    -0.5 * 0.18740624158431016,
    0.5 * 0.6751549397754679,
    -0.5 * 0.4305350150859377,
    0.5 * 0.0850883282904581,
)
ROOT_HALF = 0.7071067811865476
DENSITY = 0.3989422804014327


def gelu_and_slope(hidden):
    bell = jnp.exp(hidden * hidden * (-0.5))
    step = 1.0 / (1.0 + (ERFC_STEP * ROOT_HALF) * jnp.abs(hidden))
    tail = ERFC_HALF[6]
    for coefficient in ERFC_HALF[5::-1]:
        tail = tail * step + coefficient
    tail = tail * step * bell
    below = jnp.where(hidden >= 0.0, 1.0 - tail, tail)
    return hidden * below, below + hidden * bell * DENSITY


def mm(left, right):
    return jnp.dot(left, right, preferred_element_type=F32)


def mm_nt(left, right):
    return lax.dot_general(left, right, (((1,), (1,)), ((), ())), preferred_element_type=F32)


def mm_tn(left, right):
    return lax.dot_general(left, right, (((0,), (0,)), ((), ())), preferred_element_type=F32)


def first_head(shape):
    return lax.broadcasted_iota(jnp.int32, shape, 1) < HD


def stack_heads(values):
    place = lax.broadcasted_iota(jnp.int32, values.shape, 1) // HD
    zero = jnp.zeros_like(values)
    return jnp.concatenate(
        [jnp.where(place == head, values, zero) for head in range(values.shape[1] // HD)], axis=0
    )


def unstack_heads(values, count):
    place = lax.broadcasted_iota(jnp.int32, (count, values.shape[1]), 1) // HD
    total = None
    for head in range(values.shape[1] // HD):
        piece = jnp.where(place == head, values[head * count : (head + 1) * count], 0.0)
        total = piece if total is None else total + piece
    return total


def split_pair(values):
    lane = first_head(values.shape)
    zero = jnp.zeros_like(values)
    return jnp.where(lane, values, zero), jnp.where(lane, zero, values)


def probabilities(scores, length):
    valid = lax.broadcasted_iota(jnp.int32, scores.shape, 1) < length
    scores = jnp.where(valid, scores, NEG_FILL)
    weight = jnp.exp(scores - jnp.max(scores, axis=1, keepdims=True))
    return weight * (1.0 / jnp.sum(weight, axis=1, keepdims=True))


def normalize(values):
    center = values - jnp.mean(values, axis=-1, keepdims=True)
    spread = jnp.mean(center * center, axis=-1, keepdims=True)
    inverse = lax.rsqrt(spread + NORM_EPS)
    return center * inverse, inverse


def normalize_back(unit, inverse, grad_unit):
    return inverse * (
        grad_unit
        - jnp.mean(grad_unit, axis=-1, keepdims=True)
        - unit * jnp.mean(grad_unit * unit, axis=-1, keepdims=True)
    )


SCALE = HD**-0.5
SLAB = 16


class Mesh:
    def __init__(self):
        self.me = lax.axis_index("dp")
        self.core = lax.axis_index("mp")
        self.x, self.y, self.z = lax.rem(self.me, 2), lax.rem(self.me // 2, 2), self.me // 4
        self.x_peer = (self.index(self.z, self.y, 1 - self.x), self.core)
        self.y_peer = (self.index(self.z, 1 - self.y, self.x), self.core)
        self.c_peer = (self.me, 1 - self.core)
        self.z_peer = [None] + [(self.index(lax.rem(self.z + k, 4), self.y, self.x), self.core) for k in range(1, 4)]
        self.column = [lax.rem(self.z - k + 4, 4) for k in range(4)]

    def index(self, z, y, x):
        return (z * 2 + y) * 2 + x


def remote(source, target, send, recv, peer):
    return pltpu.make_async_remote_copy(
        src_ref=source, dst_ref=target, send_sem=send, recv_sem=recv, device_id=peer, device_id_type=MESH
    )


def forward_kernel(
    spans, total,
    query_len, passage_len, positive, query_ref, passage_ref, attn_ref, ffn_ref, col_ref, norm_ref,
    weight_out, proj_out, mixed_out, unit_out, inverse_out, low_out, active_out, slope_out, tokens_out,
    grad_out, grad_low_out, small_out,
    weight, proj, mixed, unit, inverse, low, active, slope, tokens, z_two, grad_low, small,
    col, attn_in, ffn_in, unit_two, slab, every,
    z_send, z_recv, x_send, x_recv, y_send, y_recv, d_send, d_recv, c_send, c_recv, b_send, b_recv, here_sem, out_sem,
    e_send, e_recv, p_send, p_recv, pz_send, pz_recv,
):
    at = Mesh()
    me, core = at.me, at.core
    my_rank = me * 2 + core
    rows, width = attn_ref.shape[1:]
    units = ffn_ref.shape[2]
    slots, model = tokens.shape

    def device(step):
        rank = lax.rem(my_rank + step, total)
        return (rank // 2, lax.rem(rank, 2))

    incoming = [
        pltpu.make_async_copy(attn_ref, attn_in, here_sem.at[0]),
        pltpu.make_async_copy(ffn_ref.at[0], ffn_in.at[0], here_sem.at[1]),
        pltpu.make_async_copy(ffn_ref.at[1], ffn_in.at[1], here_sem.at[2]),
        pltpu.make_async_copy(query_ref.at[core], tokens.at[pl.ds(*spans[0]), :], here_sem.at[3]),
        pltpu.make_async_copy(passage_ref.at[core], tokens.at[pl.ds(*spans[1]), :], here_sem.at[4]),
    ]
    for copy in incoming:
        copy.start()
    lens = (query_len[core], passage_len[core])
    barrier = pltpu.get_barrier_semaphore()
    for step in range(1, total):
        pl.semaphore_signal(barrier, inc=1, device_id=device(step), device_id_type=MESH)
    for line in range(col_ref.shape[0]):
        col[0, :, pl.ds(line * LANES, LANES)] = col_ref[pl.ds(line, 1), :]
    pl.semaphore_wait(barrier, total - 1)

    every_lane = pl.ds(0, units)
    cut = units * 2 // 3

    def column_lanes(q):
        return pl.ds(0, units if q < 2 else cut)

    def half_lanes(q, which):
        count = (units if q < 2 else cut) // 2
        return pl.ds(which * count, count)

    layer_lanes = pl.ds(cut, units - cut)

    def layer_half(which):
        count = (units - cut) // 2
        return pl.ds(cut + which * count, count)

    def block(q, index, lanes=None, count=1, far=0):
        lanes = column_lanes(q) if lanes is None else lanes
        return weight.at[far, q, pl.ds(pl.multiple_of(index * rows, rows), count * rows), lanes]

    sends = []
    stores = []

    def push(ref, send, recv, peer, target=None):
        copy = remote(ref, ref if target is None else target, send, recv, peer)
        copy.start()
        sends.append(copy)

    def landed(ref, send, recv, peer):
        remote(ref, ref, send, recv, peer).wait_recv()

    def store(source, target):
        copy = pltpu.make_async_copy(source, target, out_sem.at[len(stores)])
        copy.start()
        stores.append(copy)

    def cast_own(q):
        incoming[q].wait()
        here = pl.ds(pl.multiple_of(me * rows, rows), rows)
        if q == 0:
            for index in range(4):
                weight[0, 0, here, pl.ds(index * width, width)] = attn_in[index].astype(BF16)
        else:
            weight[0, q, here, :] = ffn_in[q - 1].astype(BF16)

    def own_along_column(q):
        for k in range(1, 4):
            push(block(q, me), z_send.at[q, k], z_recv.at[q, k], at.z_peer[k])

    def own_to_sides(q):
        push(block(q, me), x_send.at[q, 0], x_recv.at[q, 0], at.x_peer)
        push(block(q, me), y_send.at[q, 0], y_recv.at[q, 0], at.y_peer)

    def column_to_sides(q):
        for k in range(1, 4):
            ref = block(q, at.index(at.column[k], at.y, at.x))
            landed(ref, z_send.at[q, k], z_recv.at[q, k], at.z_peer[k])
            push(ref, x_send.at[q, k], x_recv.at[q, k], at.x_peer)
            push(ref, y_send.at[q, k], y_recv.at[q, k], at.y_peer)

    def round_corner(q, ks=range(4)):
        for k in ks:
            beside = at.index(at.column[k], at.y, 1 - at.x)
            landed(block(q, beside), x_send.at[q, k], x_recv.at[q, k], at.x_peer)
            push(block(q, beside, half_lanes(q, 0)), d_send.at[q, k, 0], d_recv.at[q, k, 0], at.y_peer)
            beside = at.index(at.column[k], 1 - at.y, at.x)
            landed(block(q, beside), y_send.at[q, k], y_recv.at[q, k], at.y_peer)
            push(block(q, beside, half_lanes(q, 1)), d_send.at[q, k, 1], d_recv.at[q, k, 1], at.x_peer)

    def layer_to_sides():
        ref = block(2, me, layer_lanes)
        push(ref, p_send.at[0], p_recv.at[0], at.x_peer)
        push(ref, p_send.at[1], p_recv.at[1], at.y_peer)

    def layer_round_corner():
        beside = at.index(at.z, at.y, 1 - at.x)
        landed(block(2, beside, layer_lanes), p_send.at[0], p_recv.at[0], at.x_peer)
        push(block(2, beside, layer_half(0)), p_send.at[2], p_recv.at[2], at.y_peer)
        beside = at.index(at.z, 1 - at.y, at.x)
        landed(block(2, beside, layer_lanes), p_send.at[1], p_recv.at[1], at.y_peer)
        push(block(2, beside, layer_half(1)), p_send.at[3], p_recv.at[3], at.x_peer)

    def layer_along_column():
        across = at.index(at.z, 1 - at.y, 1 - at.x)
        landed(block(2, across, layer_half(0)), p_send.at[2], p_recv.at[2], at.y_peer)
        landed(block(2, across, layer_half(1)), p_send.at[3], p_recv.at[3], at.x_peer)
        for k in range(1, 4):
            push(block(2, at.index(at.z, 0, 0), layer_lanes, 4), pz_send.at[k], pz_recv.at[k], at.z_peer[k])

    def to_other_core(q, ks=range(4)):
        for k in ks:
            across = at.index(at.column[k], 1 - at.y, 1 - at.x)
            landed(block(q, across, half_lanes(q, 0)), d_send.at[q, k, 0], d_recv.at[q, k, 0], at.y_peer)
            landed(block(q, across, half_lanes(q, 1)), d_send.at[q, k, 1], d_recv.at[q, k, 1], at.x_peer)
            layer = at.index(at.column[k], 0, 0)
            if q == 2 and k:
                landed(block(2, layer, layer_lanes, 4), pz_send.at[k], pz_recv.at[k], at.z_peer[k])
            push(
                block(q, layer, every_lane, 4), c_send.at[q, k], c_recv.at[q, k], at.c_peer,
                block(q, layer, every_lane, 4, 1),
            )

    def from_other_core(q):
        for k in range(4):
            layer = at.index(at.column[k], 0, 0)
            landed(block(q, layer, every_lane, 4, 1), c_send.at[q, k], c_recv.at[q, k], at.c_peer)

    def project(half):
        bias = jnp.concatenate(
            [
                col[half, :, pl.ds(0, width)],
                jnp.zeros((1, width), F32),
                col[half, :, pl.ds(width, width)],
            ],
            axis=1,
        )
        proj[half] = (mm(tokens[...], weight[half, 0, :, pl.ds(0, 3 * width)]) + bias).astype(BF16)

    def query_heads(half):
        place = pl.ds(*spans[0])
        queries = stack_heads(proj[half, place, pl.ds(0, width)] * jnp.asarray(SCALE, BF16))
        probs = probabilities(mm_nt(queries, proj[half, place, pl.ds(width, width)]), lens[0])
        value = mm(probs.astype(BF16), proj[half, place, pl.ds(2 * width, width)])
        mixed[half, place, :] = unstack_heads(value, spans[0][1]).astype(BF16)

    def passage_heads(half, pair):
        place = pl.ds(*spans[1])
        queries = proj[half, place, pl.ds(pair * LANES, LANES)]
        keys = split_pair(proj[half, place, pl.ds(width + pair * LANES, LANES)] * jnp.asarray(SCALE, BF16))
        values = proj[half, place, pl.ds(2 * width + pair * LANES, LANES)]
        scores = [mm_nt(queries, key) for key in keys]
        outs = [mm(probabilities(score, lens[1]).astype(BF16), values) for score in scores]
        mixed[half, place, pl.ds(pair * LANES, LANES)] = jnp.where(first_head(outs[0].shape), *outs).astype(BF16)

    def first_norm():
        step = 192
        for start in range(0, slots, step):
            place = pl.ds(start, step)
            value = tokens[place, :].astype(F32) + norm_ref[pl.ds(0, 1), :]
            for half in range(2):
                value = value + mm_nt(mixed[half, place, :], weight[half, 0, :, pl.ds(3 * width, width)])
            normed, scale = normalize(value)
            unit[place, :] = normed
            inverse[place, :] = jnp.broadcast_to(scale, (step, LANES))
            value = normed * norm_ref[pl.ds(1, 1), :] + norm_ref[pl.ds(2, 1), :]
            z_two[place, :] = value + norm_ref[pl.ds(3, 1), :]
            low[place, :] = value.astype(BF16)

    tile = 256

    def up(half, part):
        for start in range(part * units // 2, (part + 1) * units // 2, tile):
            lanes = pl.ds(start, tile)
            hidden = mm(low[...], weight[half, 1, :, lanes]) + col[half, :, pl.ds(2 * width + start, tile)]
            value, grad = gelu_and_slope(hidden)
            active[half, :, lanes] = value.astype(BF16)
            slope[half, :, lanes] = grad

    def down(half):
        z_two[...] = z_two[...] + mm_nt(active[half], weight[half, 2])

    cast_own(0)
    own_along_column(0)
    own_to_sides(0)
    push(col.at[0], b_send, b_recv, at.c_peer, col.at[1])
    cast_own(1)
    own_to_sides(1)
    cast_own(2)
    layer_to_sides()
    own_to_sides(2)
    incoming[3].wait()
    incoming[4].wait()
    store(tokens, tokens_out)
    column_to_sides(0)
    layer_round_corner()
    own_along_column(1)
    round_corner(0)
    column_to_sides(1)
    own_along_column(2)
    layer_along_column()
    to_other_core(0)
    project(0)
    query_heads(0)
    passage_heads(0, 0)
    round_corner(1, (0,))
    passage_heads(0, 1)
    round_corner(1, (1,))
    passage_heads(0, 2)
    landed(col.at[1], b_send, b_recv, at.c_peer)
    from_other_core(0)
    project(1)
    for half in range(2):
        store(weight.at[half, 0], weight_out.at[half, 0])
    store(proj, proj_out)
    round_corner(1, (2,))
    query_heads(1)
    round_corner(1, (3,))
    passage_heads(1, 0)
    column_to_sides(2)
    passage_heads(1, 1)
    passage_heads(1, 2)
    store(mixed, mixed_out)
    first_norm()
    store(unit, unit_out)
    store(inverse, inverse_out)
    store(low, low_out)
    to_other_core(1)
    round_corner(2, (0,))
    up(0, 0)
    round_corner(2, (1,))
    up(0, 1)
    store(slope.at[0], slope_out.at[0])
    store(weight.at[0, 1], weight_out.at[0, 1])
    round_corner(2, (2,))
    from_other_core(1)
    up(1, 0)
    round_corner(2, (3,))
    up(1, 1)
    store(slope.at[1], slope_out.at[1])
    store(weight.at[1, 1], weight_out.at[1, 1])
    store(active, active_out)
    to_other_core(2)
    store(weight.at[0, 2], weight_out.at[0, 2])
    down(0)
    from_other_core(2)
    store(weight.at[1, 2], weight_out.at[1, 2])
    down(1)

    pieces = model // LANES
    gain, shift = norm_ref[pl.ds(4, 1), :], norm_ref[pl.ds(5, 1), :]
    embeds, shrinks, means, inverses, valids = [], [], [], [], []
    for index, (start, count) in enumerate(spans):
        normed, scale = normalize(z_two[pl.ds(start, count), :])
        unit_two[pl.ds(start, count), :] = normed
        valid = lax.broadcasted_iota(jnp.int32, (count, 1), 0) < lens[index]
        mean = jnp.sum(jnp.where(valid, normed, 0.0), axis=0, keepdims=True) / lens[index].astype(F32)
        pooled = mean * gain + shift
        shrink = lax.rsqrt(jnp.sum(pooled * pooled, axis=1, keepdims=True) + POOL_EPS)
        embed = pooled * shrink
        for piece in range(pieces):
            slab[pl.ds(index * pieces + piece, 1), :] = embed[:, piece * LANES : (piece + 1) * LANES]
        embeds.append(embed)
        shrinks.append(shrink)
        means.append(mean)
        inverses.append(jnp.where(valid, scale, 0.0))
    slab[pl.ds(2 * pieces, 1), :] = jnp.full((1, LANES), positive[core], jnp.int32).astype(F32)
    copies = []
    for step in range(1, total):
        copy = remote(slab, every.at[my_rank], e_send.at[step], e_recv.at[step], device(step))
        copy.start()
        copies.append(copy)
    sends.extend(copies)
    every[my_rank] = slab[...]
    for copy in copies:
        copy.wait_recv()

    queries = jnp.concatenate([every[:, piece, :] for piece in range(pieces)], axis=1)
    passages = jnp.concatenate([every[:, pieces + piece, :] for piece in range(pieces)], axis=1)
    wanted = every[:, 2 * pieces, :][:, :1]
    logits = lax.dot_general(
        queries, passages, (((1,), (1,)), ((), ())), precision=PRECISE, preferred_element_type=F32
    ) / SOFTMAX_TEMPER
    place = lax.broadcasted_iota(jnp.int32, logits.shape, 1)
    target = (place.astype(F32) == wanted).astype(F32)
    top = jnp.max(logits, axis=1, keepdims=True)
    weights = jnp.exp(logits - top)
    row_total = jnp.sum(weights, axis=1, keepdims=True)
    log_total = top + jnp.log(row_total)
    loss = jnp.sum(log_total - jnp.sum(logits * target, axis=1, keepdims=True), axis=0, keepdims=True) / total
    grad_logits = (weights / row_total - target) / (total * SOFTMAX_TEMPER)
    grad_column = jnp.sum(jnp.where(place == my_rank, grad_logits, 0.0), axis=1, keepdims=True)
    value = jnp.dot(grad_logits, passages, precision=PRECISE, preferred_element_type=F32)
    line = lax.broadcasted_iota(jnp.int32, value.shape, 0)
    grad_embeds = (
        jnp.sum(jnp.where(line == my_rank, value, 0.0), axis=0, keepdims=True),
        jnp.sum(grad_column * queries, axis=0, keepdims=True),
    )

    grad_gain, grad_shift, grad_bias = 0.0, 0.0, 0.0
    for index, (start, count) in enumerate(spans):
        embed, grad_embed = embeds[index], grad_embeds[index]
        grad_pooled = shrinks[index] * (grad_embed - embed * jnp.sum(grad_embed * embed, axis=1, keepdims=True))
        grad_gain = grad_gain + grad_pooled * means[index]
        grad_shift = grad_shift + grad_pooled
        spread = grad_pooled * gain / lens[index].astype(F32)
        centered = spread - jnp.mean(spread, axis=1, keepdims=True)
        normed = unit_two[pl.ds(start, count), :]
        value = inverses[index] * (centered - normed * jnp.mean(spread * normed, axis=1, keepdims=True))
        z_two[pl.ds(start, count), :] = value
        grad_low[pl.ds(start, count), :] = value.astype(BF16)
        grad_bias = grad_bias + jnp.sum(value, axis=0, keepdims=True)
    store(grad_low, grad_low_out)
    store(z_two, grad_out)
    small[pl.ds(0, 1), :] = grad_bias
    small[pl.ds(1, 1), :] = grad_gain
    small[pl.ds(2, 1), :] = grad_shift
    small[pl.ds(3, 1), :] = jnp.broadcast_to(loss, (1, model))
    small[pl.ds(4, 4), :] = jnp.zeros((4, model), F32)
    store(small, small_out)
    for copy in sends:
        copy.wait_send()
    for copy in stores:
        copy.wait()


def forward(query_in, passage_in, query_len, passage_len, positive, attn_master, ffn_master, col_bias, norm_params, spans, total):
    rows, width = attn_master.shape[1:]
    units = ffn_master.shape[2]
    slots, model = spans[1][0] + spans[1][1], query_in.shape[2]
    dma = pltpu.SemaphoreType.DMA
    col = col_bias.reshape(-1, LANES)
    anywhere = pl.BlockSpec(memory_space=pltpu.HBM)
    vmem = pl.BlockSpec(memory_space=pltpu.VMEM)
    smem = pl.BlockSpec(memory_space=pltpu.SMEM)
    results = (
        ((2, 3, model, units), BF16),
        ((2, slots, 3 * width), BF16),
        ((2, slots, width), BF16),
        ((slots, model), F32),
        ((slots, LANES), F32),
        ((slots, model), BF16),
        ((2, slots, units), BF16),
        ((2, slots, units), F32),
        ((slots, model), BF16),
        ((slots, model), F32),
        ((slots, model), BF16),
        ((8, model), F32),
    )
    return pl.pallas_call(
        functools.partial(forward_kernel, spans, total),
        out_shape=tuple(jax.ShapeDtypeStruct(*result) for result in results),
        in_specs=[smem] * 3 + [anywhere] * 4 + [vmem] * 2,
        out_specs=(anywhere,) * len(results),
        scratch_shapes=[pltpu.VMEM(*result) for result in results]
        + [
            pltpu.VMEM((2, 1, col_bias.shape[0]), F32),
            pltpu.VMEM(attn_master.shape, F32),
            pltpu.VMEM(ffn_master.shape, F32),
            pltpu.VMEM((slots, model), F32),
            pltpu.VMEM((SLAB, LANES), F32),
            pltpu.VMEM((total, SLAB, LANES), F32),
        ]
        + [dma((3, 4))] * 6
        + [dma((3, 4, 2))] * 2
        + [dma((3, 4))] * 2
        + [dma(()), dma(()), dma((5,)), dma((20,)), dma((total,)), dma((total,))]
        + [dma((4,))] * 4,
        compiler_params=pltpu.CompilerParams(collective_id=0, has_side_effects=True, vmem_limit_bytes=58 * MIB),
        name="forward",
    )(query_len, passage_len, positive, query_in, passage_in, attn_master, ffn_master, col, norm_params)


def backward_kernel(
    spans,
    query_len, passage_len, weight_ref, proj_ref, mixed_ref, unit_ref, inverse_ref, low_ref, active_ref, slope_ref,
    tokens_ref, grad_ref, grad_low_ref, norm_ref, small_ref,
    attn_out, ffn_out, small_out, col_out, query_out, passage_out,
    weight, proj, mixed, inverse, low, active, slope, tokens, total, down, grad_out, grad_proj,
    temp, far_send, far_recv, kept, one_send, one_recv, two_send, two_recv, z_send, z_recv, result, vector, vec_send,
    vec_recv, col,
    load_sem, slope_sem, c_send, c_recv, s1_send, s1_recv, s2_send, s2_recv, s3_send, s3_recv,
    v_send, v_recv, t_send, t_recv, credit, out_sem, layer_recv,
):
    at = Mesh()
    me, core = at.me, at.core
    slots, model = tokens.shape
    width = grad_out.shape[2]
    rows = model // 16
    lens = (query_len[core], passage_len[core])
    near_peer = (at.index(at.z + 1 - 2 * lax.rem(at.z, 2), at.y, at.x), core)
    over_peer = at.z_peer[2]

    sends = {}
    stores = []
    loads = {}

    def load(name, *pairs):
        copies = []
        for source, target in pairs:
            copy = pltpu.make_async_copy(source, target, load_sem.at[sum(len(v) for v in loads.values()) + len(copies)])
            copy.start()
            copies.append(copy)
        loads[name] = copies

    def ready(name):
        for copy in loads[name]:
            copy.wait()

    def store(source, target):
        copy = pltpu.make_async_copy(source, target, out_sem.at[len(stores)])
        copy.start()
        stores.append(copy)

    def push(name, source, target, send, recv, peer):
        copy = remote(source, target, send, recv, peer)
        copy.start()
        sends[name] = copy

    def landed(target, send, recv, peer):
        remote(target, target, send, recv, peer).wait_recv()

    lanes_of = [pl.ds(t * width, width) for t in range(4)]
    pair_lanes = (pl.ds(0, 2 * width), pl.ds(2 * width, 2 * width))

    def slope_tile(half, t):
        index = half * 4 + t
        return pltpu.make_async_copy(slope_ref.at[half, :, lanes_of[t]], slope.at[t % 2], slope_sem.at[index])

    load("down", (grad_low_ref, down))
    load("active1", (active_ref.at[1], active.at[1]))
    barrier = pltpu.get_barrier_semaphore()
    for peer in [*at.z_peer[1:], at.x_peer, at.y_peer, at.c_peer]:
        pl.semaphore_signal(barrier, inc=1, device_id=peer, device_id_type=MESH)
    load("down1", (weight_ref.at[1, 2], weight.at[0]))
    slope_tile(1, 0).start()
    slope_tile(1, 1).start()
    load("active0", (active_ref.at[0], active.at[0]))

    def far_slot(q):
        return q % 2

    def send_far(q, t, value):
        if q == 2:
            sends[("c", 0, t)].wait_send()
        far_send[far_slot(q), t] = value.astype(BF16)
        push(
            ("c", q, t), far_send.at[far_slot(q), t], far_recv.at[far_slot(q), t], c_send.at[q, t], c_recv.at[q, t],
            at.c_peer,
        )

    def side(t):
        steps = ((at.x, at.x_peer), (at.y, at.y_peer))
        return steps if t % 2 == 0 else steps[::-1]

    def block(index, count=1):
        return pl.ds(pl.multiple_of(index * rows, rows), count * rows)

    def first_step(q, t, lanes):
        landed(far_recv.at[far_slot(q), t], c_send.at[q, t], c_recv.at[q, t], at.c_peer)
        (bit, peer), _ = side(t)
        for layer in range(4):
            for other in range(2):
                if t % 2 == 0:
                    mine, theirs = at.index(layer, other, bit), at.index(layer, other, 1 - bit)
                else:
                    mine, theirs = at.index(layer, bit, other), at.index(layer, 1 - bit, other)
                place = pl.ds((layer * 2 + other) * rows, rows)
                far = far_recv[far_slot(q), t, block(theirs), :].astype(F32)
                one_send[q, t, place, :] = (temp[block(theirs), lanes] + far).astype(BF16)
                far = far_recv[far_slot(q), t, block(mine), :].astype(F32)
                kept[q, t, place, :] = temp[block(mine), lanes] + far
        push(("1", q, t), one_send.at[q, t], one_recv.at[q, t], s1_send.at[q, t], s1_recv.at[q, t], peer)

    def second_step(q, t):
        (_, before), (bit, peer) = side(t)
        landed(one_recv.at[q, t], s1_send.at[q, t], s1_recv.at[q, t], before)
        for layer in range(4):
            theirs = block(layer * 2 + 1 - bit)
            value = kept[q, t, theirs, :] + one_recv[q, t, theirs, :].astype(F32)
            two_send[q, t, pl.ds(layer * rows, rows), :] = value.astype(BF16)
            mine = block(layer * 2 + bit)
            kept[q, t, mine, :] = kept[q, t, mine, :] + one_recv[q, t, mine, :].astype(F32)
        push(("2", q, t), two_send.at[q, t], two_recv.at[q, t], s2_send.at[q, t], s2_recv.at[q, t], peer)

    def third_step(q, t):
        _, (bit, before) = side(t)
        landed(two_recv.at[q, t], s2_send.at[q, t], s2_recv.at[q, t], before)
        for k in range(1, 4):
            layer = lax.rem(at.z + k, 4)
            value = kept[q, t, block(layer * 2 + bit), :] + two_recv[q, t, block(layer), :].astype(F32)
            z_send[q, t, k - 1] = value.astype(BF16)
            push(
                ("3", q, t, k), z_send.at[q, t, k - 1], z_recv.at[q, t, k - 1], s3_send.at[q, t, k], s3_recv.at[q, t, k],
                at.z_peer[k],
            )
        result[q, t] = kept[q, t, block(at.z * 2 + bit), :] + two_recv[q, t, block(at.z), :].astype(F32)

    def last_step(q, t):
        for k in range(1, 4):
            landed(z_recv.at[q, t, k - 1], s3_send.at[q, t, k], s3_recv.at[q, t, k], at.z_peer[k])
        value = result[q, t]
        for k in range(3):
            value = value + z_recv[q, t, k].astype(F32)
        result[q, t] = value
        store_result(q, t)

    def store_result(q, t):
        if q < 2:
            store(result.at[q, t], ffn_out.at[1 - q, :, lanes_of[t]])
        elif t == 3:
            store(result.at[q, t], attn_out.at[3])
        else:
            for index in range(3):
                store(result.at[q, t, :, pl.ds(index * LANES, LANES)], attn_out.at[index, :, pl.ds(t * LANES, LANES)])

    def layer_first_step(q, t, lanes):
        landed(far_recv.at[far_slot(q), t], c_send.at[q, t], c_recv.at[q, t], at.c_peer)
        for k in range(1, 4):
            theirs = block(at.index(lax.rem(at.z + k, 4), 0, 0), 4)
            value = temp[theirs, lanes] + far_recv[far_slot(q), t, theirs, :].astype(F32)
            if k < 3:
                source = one_send.at[q, t, pl.ds((k - 1) * 4 * rows, 4 * rows), :]
            else:
                source = two_send.at[q, t]
            source[...] = value.astype(BF16)
            push(
                ("1", q, t, k), source, layer_recv.at[t, k - 1], s3_send.at[q, t, k],
                s3_recv.at[q, t, k], at.z_peer[k],
            )
        mine = block(at.index(at.z, 0, 0), 4)
        kept[q, t, pl.ds(0, 4 * rows), :] = temp[mine, lanes] + far_recv[far_slot(q), t, mine, :].astype(F32)

    def layer_second_step(q, t):
        for k in range(1, 4):
            landed(layer_recv.at[t, k - 1], s3_send.at[q, t, k], s3_recv.at[q, t, k], at.z_peer[k])
        value = kept[q, t, pl.ds(0, 4 * rows), :]
        for k in range(3):
            value = value + layer_recv[t, k].astype(F32)
        kept[q, t, pl.ds(0, 4 * rows), :] = value
        for line in range(2):
            z_send[q, t, line] = kept[q, t, block(line * 2 + 1 - at.x), :].astype(BF16)
        push(
            ("2", q, t), z_send.at[q, t, pl.ds(0, 2)], z_recv.at[q, t, pl.ds(0, 2)], s1_send.at[q, t], s1_recv.at[q, t],
            at.x_peer,
        )

    def layer_third_step(q, t):
        landed(z_recv.at[q, t, pl.ds(0, 2)], s1_send.at[q, t], s1_recv.at[q, t], at.x_peer)
        theirs = kept[q, t, block((1 - at.y) * 2 + at.x), :] + z_recv[q, t, 1 - at.y].astype(F32)
        z_send[q, t, 2] = theirs.astype(BF16)
        push(
            ("3", q, t), z_send.at[q, t, 2], z_recv.at[q, t, 2], s2_send.at[q, t], s2_recv.at[q, t],
            at.y_peer,
        )
        result[q, t] = kept[q, t, block(at.y * 2 + at.x), :] + z_recv[q, t, at.y].astype(F32)

    def layer_last_step(q, t):
        landed(z_recv.at[q, t, 2], s2_send.at[q, t], s2_recv.at[q, t], at.y_peer)
        result[q, t] = result[q, t] + z_recv[q, t, 2].astype(F32)
        store_result(q, t)

    def far_product(q, left, right, pair):
        value = mm_tn(left[...], right[:, pair_lanes[pair]])
        send_far(q, 2 * pair, value[:, :width])
        send_far(q, 2 * pair + 1, value[:, width:])

    def own_product(q, left, right, pair):
        temp[...] = mm_tn(left[...], right[:, pair_lanes[pair]])
        step = layer_first_step if (q, pair) == (0, 0) else first_step
        step(q, 2 * pair, lanes_of[0])
        step(q, 2 * pair + 1, lanes_of[1])

    def hidden_grad(half, slot, pair, following):
        for t in (2 * pair, 2 * pair + 1):
            slope_tile(half, t).wait()
        value = mm(down[...], weight[slot, :, pair_lanes[pair]])
        for side_of, t in enumerate((2 * pair, 2 * pair + 1)):
            piece = (value[:, side_of * width : (side_of + 1) * width] * slope[side_of]).astype(BF16)
            active[half, :, lanes_of[t]] = piece
            vec = vector if half == 0 else vec_send.at[0]
            vec[pl.ds(9 + pair, 1), lanes_of[side_of]] = jnp.sum(piece.astype(F32), axis=0, keepdims=True)
        if following is not None:
            for t in (0, 1):
                slope_tile(following[0], 2 * following[1] + t).start()

    def add_back(source, slot, lanes):
        total[...] = total[...] + mm_nt(source, weight[slot, :, lanes])

    def first_norm_back():
        sums = [None, None, None]
        step = 192
        for start in range(0, slots, step):
            place = pl.ds(start, step)
            grad = total[place, :]
            normed = jnp.concatenate([slope[0, place, :], slope[1, place, :]], axis=1)
            back = normalize_back(normed, inverse[place, pl.ds(0, 1)], grad * norm_ref[pl.ds(1, 1), :])
            for index, value in enumerate((back, grad * normed, grad)):
                value = jnp.sum(value, axis=0, keepdims=True)
                sums[index] = value if sums[index] is None else sums[index] + value
            total[place, :] = back
            down[place, :] = back.astype(BF16)
        for index in range(3):
            vector[pl.ds(index, 1), :] = sums[index]
            vec_send[0, pl.ds(index, 1), :] = sums[index]

    def out_grad(half, slot):
        grad_out[half] = mm(down[...], weight[slot, :, lanes_of[3]]).astype(BF16)

    def query_back(half):
        place = pl.ds(*spans[0])
        queries = stack_heads(proj[half, place, lanes_of[0]])
        grads = stack_heads(grad_out[half, place, :])
        keys = proj[half, place, lanes_of[1]]
        probs = probabilities(mm_nt(queries * jnp.asarray(SCALE, BF16), keys), lens[0])
        grad_probs = mm_nt(grads, proj[half, place, lanes_of[2]])
        inner = jnp.sum(probs * grad_probs, axis=1, keepdims=True)
        grad_scores = (probs * (grad_probs - inner)).astype(BF16)
        value = unstack_heads(mm(grad_scores, keys), spans[0][1]) * SCALE
        grad_proj[half, place, lanes_of[0]] = value.astype(BF16)
        grad_proj[half, place, lanes_of[1]] = (mm_tn(grad_scores, queries) * SCALE).astype(BF16)
        grad_proj[half, place, lanes_of[2]] = mm_tn(probs.astype(BF16), grads).astype(BF16)

    def passage_back(half, pair):
        place = pl.ds(*spans[1])
        spot = [pl.ds(index * width + pair * LANES, LANES) for index in range(3)]
        queries, keys = proj[half, place, spot[0]], proj[half, place, spot[1]]
        grads = grad_out[half, place, pl.ds(pair * LANES, LANES)]
        scores = [mm_nt(queries, key) for key in split_pair(keys * jnp.asarray(SCALE, BF16))]
        grad_probs = [mm_nt(grads, value) for value in split_pair(proj[half, place, spot[2]])]
        outs = []
        for head in range(2):
            probs = probabilities(scores[head], lens[1])
            inner = jnp.sum(probs * grad_probs[head], axis=1, keepdims=True)
            grad_scores = (probs * (grad_probs[head] - inner)).astype(BF16)
            outs.append(
                (mm(grad_scores, keys) * SCALE, mm_tn(grad_scores, queries) * SCALE, mm_tn(probs.astype(BF16), grads))
            )
        lane = first_head(queries.shape)
        for index in range(3):
            grad_proj[half, place, spot[index]] = jnp.where(lane, outs[0][index], outs[1][index]).astype(BF16)

    def pair_product(half, pair):
        spot = [pl.ds(index * width + pair * LANES, LANES) for index in range(3)]
        return mm_tn(tokens[...], jnp.concatenate([grad_proj[half, :, lanes] for lanes in spot], axis=1))

    def attn_biases(half):
        vec = vector if half == 0 else vec_send.at[0]
        for index in (0, 1):
            value = grad_proj[half, :, lanes_of[2 * index]].astype(F32)
            vec[pl.ds(8, 1), lanes_of[index]] = jnp.sum(value, axis=0, keepdims=True)

    def vector_step(step, peer):
        if step:
            vec_send[step] = vector[...]
        push(("v", step), vec_send.at[step], vec_recv.at[step], v_send.at[step], v_recv.at[step], peer)

    def vector_sum(step, peer):
        landed(vec_recv.at[step], v_send.at[step], v_recv.at[step], peer)
        vector[...] = vector[...] + vec_recv[step]

    for target in (vector, vec_send.at[0]):
        target[pl.ds(3, 3), :] = small_ref[pl.ds(0, 3), :]
        target[pl.ds(6, 2), :] = jnp.zeros((2, model), F32)
        target[pl.ds(11, 5), :] = jnp.zeros((5, model), F32)

    ready("down")
    ready("active1")
    pl.semaphore_wait(barrier, 6)
    far_product(0, down, active.at[1], 1)
    far_product(0, down, active.at[1], 0)
    load("down0", (weight_ref.at[0, 2], weight.at[1]))
    load("low", (low_ref, low))
    load("up1", (weight_ref.at[1, 1], weight.at[2]))
    ready("active0")
    own_product(0, down, active.at[0], 1)
    ready("down1")
    hidden_grad(1, 0, 0, (0, 0))
    own_product(0, down, active.at[0], 0)
    pl.semaphore_signal(credit, inc=1, device_id=at.c_peer, device_id_type=MESH)
    ready("low")
    far_product(1, low, active.at[1], 0)
    ready("down0")
    hidden_grad(0, 1, 0, (1, 1))
    load("total", (grad_ref, total))
    load("inverse", (inverse_ref, inverse))
    own_product(1, low, active.at[0], 0)
    hidden_grad(1, 0, 1, (0, 1))
    load("up0", (weight_ref.at[0, 1], weight.at[0]))
    far_product(1, low, active.at[1], 1)
    second_step(0, 2)
    second_step(0, 3)
    hidden_grad(0, 1, 1, None)
    load("unit", *[(unit_ref.at[:, lanes_of[t]], slope.at[t]) for t in range(2)])
    load("attn1", (weight_ref.at[1, 0], weight.at[1]))
    load("proj", (proj_ref, proj), (mixed_ref, mixed), (tokens_ref, tokens))
    own_product(1, low, active.at[0], 1)
    ready("total")
    ready("up1")
    add_back(active[1], 2, pl.ds(0, 4 * width))
    load("attn0", (weight_ref.at[0, 0], weight.at[2]))
    ready("up0")
    add_back(active[0], 0, pl.ds(0, 4 * width))
    second_step(1, 0)
    second_step(1, 1)
    ready("inverse")
    ready("unit")
    first_norm_back()
    ready("proj")
    pl.semaphore_wait(credit, 1)
    send_far(2, 3, mm_tn(down[...], mixed[1]))
    ready("attn1")
    out_grad(1, 1)
    query_back(1)
    temp[:, lanes_of[0]] = mm_tn(down[...], mixed[0])
    first_step(2, 3, lanes_of[0])
    third_step(0, 2)
    third_step(0, 3)
    passage_back(1, 0)
    send_far(2, 0, pair_product(1, 0))
    ready("attn0")
    out_grad(0, 2)
    query_back(0)
    layer_second_step(0, 0)
    passage_back(0, 0)
    temp[:, lanes_of[1]] = pair_product(0, 0)
    first_step(2, 0, lanes_of[1])
    second_step(1, 2)
    second_step(1, 3)
    passage_back(1, 1)
    send_far(2, 1, pair_product(1, 1))
    third_step(1, 0)
    third_step(1, 1)
    layer_second_step(0, 1)
    layer_third_step(0, 0)
    passage_back(0, 1)
    temp[:, lanes_of[0]] = pair_product(0, 1)
    first_step(2, 1, lanes_of[0])
    last_step(0, 2)
    last_step(0, 3)
    passage_back(1, 2)
    send_far(2, 2, pair_product(1, 2))
    attn_biases(1)
    vector_step(0, at.c_peer)
    second_step(2, 3)
    layer_third_step(0, 1)
    passage_back(0, 2)
    temp[:, lanes_of[1]] = pair_product(0, 2)
    first_step(2, 2, lanes_of[1])
    second_step(2, 0)
    third_step(1, 2)
    third_step(1, 3)
    attn_biases(0)
    vector_sum(0, at.c_peer)
    vector_step(1, at.x_peer)
    add_back(grad_proj[1], 1, pl.ds(0, 3 * width))
    second_step(2, 1)
    third_step(2, 3)
    add_back(grad_proj[0], 2, pl.ds(0, 3 * width))
    for index, target in ((0, query_out), (1, passage_out)):
        part = total.at[pl.ds(*spans[index]), :]
        store(part, target.at[core])
        push(("t", index), part, target.at[core], t_send.at[index], t_recv.at[index], at.c_peer)
    third_step(2, 0)
    vector_sum(1, at.x_peer)
    vector_step(2, at.y_peer)
    layer_last_step(0, 0)
    layer_last_step(0, 1)
    last_step(1, 0)
    last_step(1, 1)
    last_step(1, 2)
    last_step(1, 3)
    third_step(2, 1)
    second_step(2, 2)
    vector_sum(2, at.y_peer)
    vector_step(3, near_peer)
    last_step(2, 3)
    last_step(2, 0)
    third_step(2, 2)
    vector_sum(3, near_peer)
    vector_step(4, over_peer)
    last_step(2, 1)
    last_step(2, 2)
    vector_sum(4, over_peer)
    store(vector.at[pl.ds(0, 8), :], small_out)
    for line in range(3):
        for piece in range(model // LANES):
            col[pl.ds(line * (model // LANES) + piece, 1), :] = vector[pl.ds(8 + line, 1), pl.ds(piece * LANES, LANES)]
    store(col, col_out)
    for index, target in ((0, query_out), (1, passage_out)):
        landed(target.at[1 - core], t_send.at[index], t_recv.at[index], at.c_peer)
    for copy in stores:
        copy.wait()
    for name, copy in sends.items():
        if name[:2] != ("c", 0):
            copy.wait_send()


def backward(query_len, passage_len, kept, norm_params, spans):
    weight, proj, mixed, unit, inverse, low, active, slope, tokens, grad_ztwo, grad_low, small = kept
    slots, model = tokens.shape
    width = mixed.shape[2]
    rows = model // 16
    anywhere = pl.BlockSpec(memory_space=pltpu.HBM)
    vmem = pl.BlockSpec(memory_space=pltpu.VMEM)
    smem = pl.BlockSpec(memory_space=pltpu.SMEM)
    dma = pltpu.SemaphoreType.DMA
    lines = 3 * model // LANES
    scratch = [
        pltpu.VMEM((3, model, 4 * width), BF16),
        pltpu.VMEM(proj.shape, BF16),
        pltpu.VMEM(mixed.shape, BF16),
        pltpu.VMEM(inverse.shape, F32),
        pltpu.VMEM(low.shape, BF16),
        pltpu.VMEM(active.shape, BF16),
        pltpu.VMEM((2, slots, width), F32),
        pltpu.VMEM(tokens.shape, BF16),
        pltpu.VMEM((slots, model), F32),
        pltpu.VMEM((slots, model), BF16),
        pltpu.VMEM((2, slots, width), BF16),
        pltpu.VMEM((2, slots, 3 * width), BF16),
        pltpu.VMEM((model, 2 * width), F32),
        pltpu.VMEM((2, 4, model, width), BF16),
        pltpu.VMEM((2, 4, model, width), BF16),
        pltpu.VMEM((3, 4, 8 * rows, width), F32),
        pltpu.VMEM((3, 4, 8 * rows, width), BF16),
        pltpu.VMEM((3, 4, 8 * rows, width), BF16),
        pltpu.VMEM((3, 4, 4 * rows, width), BF16),
        pltpu.VMEM((3, 4, 4 * rows, width), BF16),
        pltpu.VMEM((3, 4, 3, rows, width), BF16),
        pltpu.VMEM((3, 4, 3, rows, width), BF16),
        pltpu.VMEM((3, 4, rows, width), F32),
        pltpu.VMEM((16, model), F32),
        pltpu.VMEM((5, 16, model), F32),
        pltpu.VMEM((5, 16, model), F32),
        pltpu.VMEM((lines, LANES), F32),
        dma((20,)), dma((8,)),
        dma((3, 4)), dma((3, 4)), dma((3, 4)), dma((3, 4)), dma((3, 4)), dma((3, 4)),
        dma((3, 4, 4)), dma((3, 4, 4)),
        dma((5,)), dma((5,)), dma((2,)), dma((2,)),
        pltpu.SemaphoreType.REGULAR,
        dma((24,)),
        pltpu.VMEM((2, 3, 4 * rows, width), BF16),
    ]
    return pl.pallas_call(
        functools.partial(backward_kernel, spans),
        out_shape=(
            jax.ShapeDtypeStruct((4, rows, width), F32),
            jax.ShapeDtypeStruct((2, rows, 4 * width), F32),
            jax.ShapeDtypeStruct((8, model), F32),
            jax.ShapeDtypeStruct((lines, LANES), F32),
            jax.ShapeDtypeStruct((2, spans[0][1], model), F32),
            jax.ShapeDtypeStruct((2, spans[1][1], model), F32),
        ),
        in_specs=[smem] * 2 + [anywhere] * 11 + [vmem, vmem],
        out_specs=(anywhere,) * 6,
        scratch_shapes=scratch,
        compiler_params=pltpu.CompilerParams(collective_id=2, has_side_effects=True, vmem_limit_bytes=60 * MIB),
        name="backward",
    )(query_len, passage_len, weight, proj, mixed, unit, inverse, low, active, slope, tokens, grad_ztwo, grad_low,
      norm_params, small)


def finish_kernel(
    step_ref, rates_ref, query_ref, passage_ref,
    attn_grad, ffn_grad, norm_grad, col_grad, loss_ref,
    attn_m, attn_f, attn_s, attn_a, ffn_m, ffn_f, ffn_s, ffn_a,
    norm_m, norm_f, norm_s, norm_a, col_m, col_f, col_s, col_a,
    loss_out, query_out, passage_out,
    attn_mo, attn_fo, attn_so, attn_ao, ffn_mo, ffn_fo, ffn_so, ffn_ao,
    norm_mo, norm_fo, norm_so, norm_ao, col_mo, col_fo, col_so, col_ao, attn_co, ffn_co,
    attn_in, attn_res, attn_low, ffn_in, ffn_res, ffn_low, norm_in, norm_res, col_in, col_res, small, query, passage,
    in_sem, out_sem,
):
    loads, stores = [], []

    def load(source, target):
        copy = pltpu.make_async_copy(source, target, in_sem.at[len(loads)])
        copy.start()
        loads.append(copy)
        return copy

    def store(source, target):
        copy = pltpu.make_async_copy(source, target, out_sem.at[len(stores)])
        copy.start()
        stores.append(copy)

    groups = [
        [
            load(source.at[which], ffn_in.at[index, which])
            for index, source in enumerate((ffn_m, ffn_f, ffn_s, ffn_a, ffn_grad))
        ]
        for which in range(2)
    ]
    groups.append(
        [load(source, attn_in.at[index]) for index, source in enumerate((attn_m, attn_f, attn_s, attn_a, attn_grad))]
    )
    lines = norm_in.shape[1]
    groups.append(
        [load(source, norm_in.at[index]) for index, source in enumerate((norm_m, norm_f, norm_s, norm_a))]
        + [load(norm_grad, small.at[0]), load(loss_ref, small.at[1])]
        + [load(source, col_in.at[index]) for index, source in enumerate((col_m, col_f, col_s, col_a, col_grad))]
    )
    half = passage.shape[1] // 2
    parts = [(pair, pl.ds(at * half, half)) for pair in range(2) for at in range(2)]

    count = jnp.full((1, 1), step_ref[0], jnp.int32).astype(F32)
    rate = [jnp.full((1, 1), rates_ref[index], F32) for index in range(5)]
    to_first, to_second = [1.0 / (1.0 - jnp.exp(count * jnp.log(rate[index]))) for index in range(2)]

    def update(master, first, second, average, grad, learn, decay):
        first_new = rate[0] * first + (1.0 - rate[0]) * grad
        second_new = rate[1] * second + (1.0 - rate[1]) * grad * grad
        move = (first_new * to_first) / (jnp.sqrt(second_new * to_second) + ADAM_EPS)
        if decay:
            move = move + decay * master
        master_new = master - learn * move
        average_new = rate[2] * average + (1.0 - rate[2]) * master_new
        return master_new, first_new, second_new, average_new

    def wait(group):
        for copy in groups[group]:
            copy.wait()

    for which in range(2):
        wait(which)
        if which == 0:
            groups.append([load(query_ref, query)])
            for pair, place in parts:
                groups.append([load(passage_ref.at[pair, place, :], passage.at[pair, place, :])])
        values = update(*[ffn_in[index, which] for index in range(5)], rate[3], DECAY_WEIGHT)
        for index, (value, target) in enumerate(zip(values, (ffn_mo, ffn_fo, ffn_so, ffn_ao))):
            ffn_res[index, which] = value
            store(ffn_res.at[index, which], target.at[which])
        ffn_low[which] = values[0].astype(BF16)
        store(ffn_low.at[which], ffn_co.at[which])
    wait(2)
    for which in range(attn_low.shape[0]):
        values = update(*[attn_in[index, which] for index in range(5)], rate[3], DECAY_WEIGHT)
        for index, value in enumerate(values):
            attn_res[index, which] = value
        attn_low[which] = values[0].astype(BF16)
    for index, target in enumerate((attn_mo, attn_fo, attn_so, attn_ao)):
        store(attn_res.at[index], target)
    store(attn_low, attn_co)
    wait(3)
    values = update(*[norm_in[index] for index in range(4)], small[0, pl.ds(0, lines), :], rate[4], 0.0)
    for index, (value, target) in enumerate(zip(values, (norm_mo, norm_fo, norm_so, norm_ao))):
        norm_res[index] = value
        store(norm_res.at[index], target)
    values = update(*[col_in[index] for index in range(5)], rate[4], 0.0)
    for index, (value, target) in enumerate(zip(values, (col_mo, col_fo, col_so, col_ao))):
        col_res[index] = value
        store(col_res.at[index], target)
    wait(4)
    store(query, query_out)
    for index, (pair, place) in enumerate(parts):
        wait(5 + index)
        store(passage.at[pair, place, :], passage_out.at[pair, place, :])
    loss_out[0] = jnp.sum(small[1, pl.ds(3, 1), pl.ds(0, 1)])
    for copy in stores:
        copy.wait()


def finish(step, rates, grads, loss_rows, attn_state, ffn_state, norm_state, col_state):
    attn_grad, ffn_grad, norm_grad, col_grad, query_grad, passage_grad = grads
    anywhere = pl.BlockSpec(memory_space=pltpu.HBM)
    smem = pl.BlockSpec(memory_space=pltpu.SMEM)
    dma = pltpu.SemaphoreType.DMA
    col_state = [value.reshape(-1, LANES) for value in col_state]
    states = (attn_state, ffn_state, norm_state, col_state)
    shapes = [jax.ShapeDtypeStruct((1,), F32)]
    shapes += [jax.ShapeDtypeStruct(value.shape, F32) for value in (query_grad, passage_grad)]
    shapes += [jax.ShapeDtypeStruct(value.shape, F32) for state in states for value in state]
    shapes += [jax.ShapeDtypeStruct(state[0].shape, BF16) for state in (attn_state, ffn_state)]
    scratch = []
    for state in (attn_state, ffn_state):
        shape = state[0].shape
        scratch += [pltpu.VMEM((5,) + shape, F32), pltpu.VMEM((4,) + shape, F32), pltpu.VMEM(shape, BF16)]
    for state, count in ((norm_state, 4), (col_state, 5)):
        shape = state[0].shape
        scratch += [pltpu.VMEM((count,) + shape, F32), pltpu.VMEM((4,) + shape, F32)]
    outs = pl.pallas_call(
        finish_kernel,
        out_shape=tuple(shapes),
        in_specs=[smem] * 2 + [anywhere] * 23,
        out_specs=(smem,) + (anywhere,) * 20,
        scratch_shapes=scratch
        + [pltpu.VMEM((2,) + norm_grad.shape, F32), pltpu.VMEM(query_grad.shape, F32), pltpu.VMEM(passage_grad.shape, F32)]
        + [dma((32,)), dma((32,))],
        compiler_params=pltpu.CompilerParams(vmem_limit_bytes=60 * MIB),
        name="finish",
    )(step, rates, query_grad, passage_grad, attn_grad, ffn_grad, norm_grad, col_grad, loss_rows,
      *attn_state, *ffn_state, *norm_state, *col_state)
    outs = list(outs)
    outs[15:19] = [value.reshape(-1) for value in outs[15:19]]
    return outs


def attend_kernel(spans, lens_ref, q_ref, k_ref, v_ref, o_ref):
    for index, (start, slots) in enumerate(spans):
        length = lens_ref[index]
        keys = k_ref[0, pl.ds(start, slots), :]
        values = v_ref[0, pl.ds(start, slots), :]
        lane = first_head(keys.shape)
        scaled = keys * jnp.asarray(HD**-0.5, BF16)
        zero = jnp.zeros_like(scaled)
        head_keys = (jnp.where(lane, scaled, zero), jnp.where(lane, zero, scaled))
        block = min(slots, 256)
        for at in range(0, slots, block):
            queries = q_ref[0, pl.ds(start + at, block), :]
            outs = []
            for head in range(2):
                scores = mm_nt(queries, head_keys[head])
                valid = lax.broadcasted_iota(jnp.int32, scores.shape, 1) < length
                scores = jnp.where(valid, scores, NEG_FILL)
                top = jnp.max(scores, axis=1, keepdims=True)
                weight = jnp.exp(scores - top)
                total = jnp.sum(weight, axis=1, keepdims=True)
                probs = (weight * (1.0 / total)).astype(BF16)
                outs.append(mm(probs, values))
            o_ref[pl.ds(start + at, block), :] = jnp.where(
                first_head(outs[0].shape), outs[0], outs[1]
            ).astype(BF16)


def attend_back_kernel(spans, lens_ref, q_ref, k_ref, v_ref, g_ref, d_ref):
    scale = HD**-0.5
    for index, (start, slots) in enumerate(spans):
        length = lens_ref[index]
        keys = k_ref[0, pl.ds(start, slots), :]
        values = v_ref[0, pl.ds(start, slots), :]
        lane = first_head(keys.shape)
        scaled = keys * jnp.asarray(scale, BF16)
        zero = jnp.zeros_like(scaled)
        head_keys = (jnp.where(lane, scaled, zero), jnp.where(lane, zero, scaled))
        head_values = (jnp.where(lane, values, zero), jnp.where(lane, zero, values))
        block = min(slots, 256)
        grad_k = [None, None]
        grad_v = [None, None]
        for at in range(0, slots, block):
            queries = q_ref[0, pl.ds(start + at, block), :]
            grads = g_ref[pl.ds(start + at, block), :]
            grad_q = []
            for head in range(2):
                scores = mm_nt(head_keys[head], queries)
                valid = lax.broadcasted_iota(jnp.int32, scores.shape, 0) < length
                scores = jnp.where(valid, scores, NEG_FILL)
                top = jnp.max(scores, axis=0, keepdims=True)
                weight = jnp.exp(scores - top)
                total = jnp.sum(weight, axis=0, keepdims=True)
                probs = weight * (1.0 / total)
                grad_probs = mm_nt(head_values[head], grads)
                inner = jnp.sum(probs * grad_probs, axis=0, keepdims=True)
                grad_scores = (probs * (grad_probs - inner)).astype(BF16)
                part_v = mm(probs.astype(BF16), grads)
                part_k = mm(grad_scores, queries)
                grad_v[head] = part_v if at == 0 else grad_v[head] + part_v
                grad_k[head] = part_k if at == 0 else grad_k[head] + part_k
                grad_q.append(mm_tn(grad_scores, keys))
            d_ref[0, pl.ds(start + at, block), :] = (
                jnp.where(first_head(grad_q[0].shape), grad_q[0], grad_q[1]) * scale
            ).astype(BF16)
        d_ref[1, pl.ds(start, slots), :] = (jnp.where(lane, grad_k[0], grad_k[1]) * scale).astype(BF16)
        d_ref[2, pl.ds(start, slots), :] = jnp.where(lane, grad_v[0], grad_v[1]).astype(BF16)


def head_specs(tokens):
    return [pl.BlockSpec((1, tokens, LANES), functools.partial(lambda s, i, lens: (s, 0, i), s)) for s in range(3)]


def attend(proj, lens, spans):
    _, tokens, width = proj.shape
    flops = sum(4 * slots * slots * width for _, slots in spans)
    return pl.pallas_call(
        functools.partial(attend_kernel, spans),
        out_shape=jax.ShapeDtypeStruct((tokens, width), BF16),
        grid_spec=pltpu.PrefetchScalarGridSpec(
            num_scalar_prefetch=1,
            grid=(width // LANES,),
            in_specs=head_specs(tokens),
            out_specs=pl.BlockSpec((tokens, LANES), lambda i, lens: (0, i)),
        ),
        compiler_params=pltpu.CompilerParams(vmem_limit_bytes=40 * MIB),
        cost_estimate=pl.CostEstimate(flops=8 * flops, bytes_accessed=8 * tokens * width, transcendentals=0),
        name="attend",
    )(lens, proj, proj, proj)


def attend_back(proj, grad_out, lens, spans):
    _, tokens, width = proj.shape
    flops = sum(10 * slots * slots * width for _, slots in spans)
    return pl.pallas_call(
        functools.partial(attend_back_kernel, spans),
        out_shape=jax.ShapeDtypeStruct((3, tokens, width), BF16),
        grid_spec=pltpu.PrefetchScalarGridSpec(
            num_scalar_prefetch=1,
            grid=(width // LANES,),
            in_specs=head_specs(tokens) + [pl.BlockSpec((tokens, LANES), lambda i, lens: (0, i))],
            out_specs=pl.BlockSpec((3, tokens, LANES), lambda i, lens: (0, 0, i)),
        ),
        compiler_params=pltpu.CompilerParams(vmem_limit_bytes=40 * MIB),
        cost_estimate=pl.CostEstimate(flops=8 * flops, bytes_accessed=14 * tokens * width, transcendentals=0),
        name="attend_back",
    )(lens, proj, proj, proj, grad_out)


def up_kernel(x_ref, w_ref, b_ref, g_ref, s_ref):
    hidden = mm(x_ref[...], w_ref[0]) + b_ref[...]
    active, slope = gelu_and_slope(hidden)
    g_ref[...] = active.astype(BF16)
    s_ref[...] = slope


def feed_up(low, ffn_half, bias):
    tokens, width = low.shape
    units = ffn_half.shape[2]
    tile = 256
    return pl.pallas_call(
        up_kernel,
        out_shape=(jax.ShapeDtypeStruct((tokens, units), BF16), jax.ShapeDtypeStruct((tokens, units), F32)),
        grid=(units // tile,),
        in_specs=[
            pl.BlockSpec((tokens, width), lambda i: (0, 0)),
            pl.BlockSpec((1, width, tile), lambda i: (0, 0, i)),
            pl.BlockSpec((1, tile), lambda i: (0, i)),
        ],
        out_specs=(pl.BlockSpec((tokens, tile), lambda i: (0, i)), pl.BlockSpec((tokens, tile), lambda i: (0, i))),
        compiler_params=pltpu.CompilerParams(vmem_limit_bytes=40 * MIB),
        cost_estimate=pl.CostEstimate(
            flops=2 * tokens * width * units, bytes_accessed=8 * tokens * units, transcendentals=tokens * units
        ),
        name="feed_up",
    )(low, ffn_half, bias.reshape(1, -1))


def swap_cores(values):
    return lax.ppermute(values, "mp", [(0, 1), (1, 0)])


def scatter_sum(own_parts, other_parts):
    summed = [own + swap_cores(other).astype(F32) for own, other in zip(own_parts, other_parts)]
    return [lax.psum_scatter(value, "dp", scatter_dimension=1, tiled=True) for value in summed]


def adam_update(master, first, second, average, grad, rate, decay_w, rates, step_count):
    first_new = rates[0] * first + (1.0 - rates[0]) * grad
    second_new = rates[1] * second + (1.0 - rates[1]) * grad * grad
    fixed_one = first_new / (1.0 - rates[0] ** step_count)
    fixed_two = second_new / (1.0 - rates[1] ** step_count)
    master_new = master - rate * (fixed_one / (jnp.sqrt(fixed_two) + ADAM_EPS) + decay_w * master)
    average_new = rates[2] * average + (1.0 - rates[2]) * master_new
    return (master_new, first_new, second_new, average_new)


def forward_plain(tokens, lens, attn_low, ffn_low, col_bias, norm_params, spans):
    attn_full = lax.all_gather(attn_low, "dp", axis=1, tiled=True)
    ffn_full = lax.all_gather(ffn_low, "dp", axis=1, tiled=True)
    attn_w = (attn_full, swap_cores(attn_full))
    ffn_w = (ffn_full, swap_cores(ffn_full))
    col = (col_bias, swap_cores(col_bias))
    width = attn_w[0].shape[2]

    projected, mixed = [], []
    branch = None
    for half in range(2):
        bias = jnp.stack([col[half][:width], jnp.zeros((width,), F32), col[half][width : 2 * width]])
        proj = (
            jnp.einsum("td,sde->ste", tokens, attn_w[half][:3], preferred_element_type=F32) + bias[:, None, :]
        ).astype(BF16)
        out = attend(proj, lens, spans)
        part = mm_nt(out, attn_w[half][3])
        branch = part if branch is None else branch + part
        projected.append(proj)
        mixed.append(out)
    z_one = tokens.astype(F32) + branch + norm_params[0]
    unit_one, inverse_one = normalize(z_one)
    first_norm = unit_one * norm_params[1] + norm_params[2]
    first_low = first_norm.astype(BF16)
    active, slope = [], []
    branch_two = None
    for half in range(2):
        act, slo = feed_up(first_low, ffn_w[half], col[half][2 * width :])
        part = mm_nt(act, ffn_w[half][1])
        branch_two = part if branch_two is None else branch_two + part
        active.append(act)
        slope.append(slo)
    z_two = first_norm + branch_two + norm_params[3]
    return attn_w, ffn_w, projected, mixed, unit_one, inverse_one, first_low, active, slope, z_two


def loss_plain(z_two, lens, target_mine, norm_params, spans, pairs):
    query_slots, passage_slots = spans[0][1], spans[1][1]
    model_width = z_two.shape[1]
    core = lax.axis_index("mp")
    unit_two, inverse_two = normalize(z_two)
    places = jnp.arange(query_slots + passage_slots)
    in_query = (places < query_slots) & (places < lens[0])
    in_passage = (places >= query_slots) & (places - query_slots < lens[1])
    share = (
        jnp.stack([in_query, in_passage]).astype(F32) / lens.astype(F32)[:, None]
    )
    mean_unit = jnp.dot(share, unit_two, precision=PRECISE, preferred_element_type=F32)
    pooled = mean_unit * norm_params[4] + norm_params[5]
    shrink = lax.rsqrt(jnp.sum(pooled * pooled, axis=1, keepdims=True) + POOL_EPS)
    embed = pooled * shrink

    payload = jnp.concatenate([embed.reshape(-1), target_mine])
    every = lax.all_gather(payload, ("dp", "mp"), axis=0)
    every_q = every[:, :model_width]
    every_p = every[:, model_width : 2 * model_width]
    target = (jnp.arange(pairs)[None, :].astype(F32) == every[:, 2 * model_width :][:, :1]).astype(F32)
    logits = lax.dot_general(every_q, every_p, (((1,), (1,)), ((), ())), precision=PRECISE) / SOFTMAX_TEMPER
    row_top = jnp.max(logits, axis=1, keepdims=True)
    exp_logits = jnp.exp(logits - row_top)
    row_total = jnp.sum(exp_logits, axis=1, keepdims=True)
    log_total = row_top[:, 0] + jnp.log(row_total[:, 0])
    loss_value = (jnp.sum(log_total - jnp.sum(logits * target, axis=1)) / pairs).reshape(1)
    grad_logits = (exp_logits / row_total - target) / (pairs * SOFTMAX_TEMPER)
    rank = lax.axis_index("dp") * lax.axis_size("mp") + core
    grad_uq = jnp.dot(lax.dynamic_index_in_dim(grad_logits, rank, 0, keepdims=True), every_p, precision=PRECISE)
    grad_up = jnp.dot(
        lax.dynamic_index_in_dim(grad_logits, rank, 1, keepdims=False)[None], every_q, precision=PRECISE
    )
    grad_embed = jnp.concatenate([grad_uq, grad_up], axis=0)

    grad_pooled = shrink * (grad_embed - embed * jnp.sum(grad_embed * embed, axis=1, keepdims=True))
    grad_gain_two = jnp.sum(grad_pooled * mean_unit, axis=0)
    grad_shift_two = jnp.sum(grad_pooled, axis=0)
    grad_unit_two = lax.dot_general(
        share, grad_pooled * norm_params[4], (((0,), (0,)), ((), ())), precision=PRECISE
    )
    grad_ztwo = normalize_back(unit_two, inverse_two, grad_unit_two)
    grad_bias_two = jnp.sum(grad_ztwo, axis=0)
    grad_two_low = grad_ztwo.astype(BF16)
    return grad_ztwo, grad_two_low, loss_value, grad_bias_two, grad_gain_two, grad_shift_two


def backward_plain(tokens, lens, kept, grad_ztwo, grad_two_low, norm_params, second_grads, spans):
    attn_w, ffn_w, projected, mixed, unit_one, inverse_one, first_low, active, slope = kept
    grad_bias_two, grad_gain_two, grad_shift_two = second_grads
    query_slots = spans[0][1]
    core = lax.axis_index("mp")
    cut = ffn_w[0].shape[2] // 2
    width = attn_w[0].shape[2]

    def two_parts(values):
        return values[:, :cut], values[:, cut:]

    def parted_product(left, halves):
        own = [mm_tn(left, part)[None] for part in two_parts(halves[0])]
        other = [mm_tn(left, part).astype(BF16)[None] for part in two_parts(halves[1])]
        return own, other

    down_grad = scatter_sum(*parted_product(grad_two_low, active))
    grad_hidden, grad_first = [], grad_ztwo
    for half in (1, 0):
        grad_hid = (mm(grad_two_low, ffn_w[half][1]) * slope[half]).astype(BF16)
        grad_hidden.insert(0, grad_hid)
        grad_first = grad_first + mm_nt(grad_hid, ffn_w[half][0])
    grad_hidden_bias = [jnp.sum(value.astype(F32), axis=0) for value in grad_hidden]
    up_grad = scatter_sum(*parted_product(first_low, grad_hidden))

    grad_gain_one = jnp.sum(grad_first * unit_one, axis=0)
    grad_shift_one = jnp.sum(grad_first, axis=0)
    grad_zone = normalize_back(unit_one, inverse_one, grad_first * norm_params[1])
    grad_bias_out = jnp.sum(grad_zone, axis=0)
    grad_one_low = grad_zone.astype(BF16)
    grad_tokens = grad_zone
    grad_query_bias, grad_value_bias, attn_parts = [None, None], [None, None], [None, None]
    for half in (1, 0):
        grad_out = mm(grad_one_low, attn_w[half][3]).astype(BF16)
        grad_proj = attend_back(projected[half], grad_out, lens, spans)
        grad_query_bias[half] = jnp.sum(grad_proj[0].astype(F32), axis=0)
        grad_value_bias[half] = jnp.sum(grad_proj[2].astype(F32), axis=0)
        in_grads = jnp.einsum("td,ste->sde", tokens, grad_proj, preferred_element_type=F32)
        out_grad = mm_tn(grad_one_low, mixed[half])
        parts = [in_grads[:2], jnp.stack([in_grads[2], out_grad])]
        attn_parts[half] = parts if half == 0 else [part.astype(BF16) for part in parts]
        for index in range(3):
            grad_tokens = grad_tokens + mm_nt(grad_proj[index], attn_w[half][index])
    attn_grads = scatter_sum(*attn_parts)

    col_parts = [
        jnp.concatenate([grad_query_bias[half], grad_value_bias[half], grad_hidden_bias[half]]) for half in range(2)
    ]
    norm_part = jnp.stack(
        [grad_bias_out, grad_gain_one, grad_shift_one, grad_bias_two, grad_gain_two, grad_shift_two]
    )
    norm_part = norm_part + swap_cores(norm_part)
    col_part = col_parts[0] + swap_cores(col_parts[1])
    small = lax.psum(jnp.concatenate([norm_part.reshape(-1), col_part]), "dp")
    norm_grad = small[: norm_part.size].reshape(norm_part.shape)
    col_grad = small[norm_part.size :]

    attn_grad = jnp.concatenate(attn_grads, axis=0)
    ffn_grad = jnp.stack([jnp.concatenate(parts, axis=-1)[0] for parts in (up_grad, down_grad)])
    grad_twin = swap_cores(grad_tokens)
    first_pair = jnp.where(core == 0, grad_tokens, grad_twin)
    second_pair = jnp.where(core == 0, grad_twin, grad_tokens)
    query_grad = jnp.stack([first_pair[:query_slots], second_pair[:query_slots]])
    passage_grad = jnp.stack([first_pair[query_slots:], second_pair[query_slots:]])
    return attn_grad, ffn_grad, norm_grad, col_grad, query_grad, passage_grad


def per_device(
    query_in,
    passage_in,
    query_len,
    passage_len,
    positive,
    step,
    rates,
    attn_master,
    attn_first,
    attn_second,
    attn_average,
    ffn_master,
    ffn_first,
    ffn_second,
    ffn_average,
    norm_params,
    norm_first,
    norm_second,
    norm_average,
    col_bias,
    col_first,
    col_second,
    col_average,
):
    size = lax.axis_size("dp")
    query_slots = query_in.shape[1]
    spans = ((0, query_slots), (query_slots, passage_in.shape[1]))
    pairs = query_in.shape[0] * size
    attn_state = (attn_master, attn_first, attn_second, attn_average)
    ffn_state = (ffn_master, ffn_first, ffn_second, ffn_average)
    norm_state = (norm_params, norm_first, norm_second, norm_average)
    col_state = (col_bias, col_first, col_second, col_average)
    if size == 16:
        kept = forward(
            query_in, passage_in, query_len, passage_len, positive, attn_master, ffn_master, col_bias, norm_params, spans,
            pairs,
        )
        grads = backward(query_len, passage_len, kept, norm_params, spans)
        return tuple(finish(step, rates, grads, kept[11], attn_state, ffn_state, norm_state, col_state))

    core = lax.axis_index("mp")

    def pick(values, index):
        return lax.dynamic_index_in_dim(values, index, 0, keepdims=False)

    tokens = jnp.concatenate([pick(query_in, core), pick(passage_in, core)], axis=0)
    lens = jnp.stack([pick(query_len, core), pick(passage_len, core)])
    target = jnp.broadcast_to(pick(positive, core).astype(F32), (LANES,))
    outs = forward_plain(tokens, lens, attn_master.astype(BF16), ffn_master.astype(BF16), col_bias, norm_params, spans)
    kept, z_two = outs[:9], outs[9]
    outs = loss_plain(z_two, lens, target, norm_params, spans, pairs)
    grad_ztwo, grad_two_low, loss_value, *second_grads = outs
    attn_grad, ffn_grad, norm_grad, col_grad, query_grad, passage_grad = backward_plain(
        tokens, lens, kept, grad_ztwo, grad_two_low, norm_params, second_grads, spans
    )
    step_count = step[0].astype(F32)
    outs = []
    for state, grad, rate, decay in (
        (attn_state, attn_grad, rates[3], DECAY_WEIGHT),
        (ffn_state, ffn_grad, rates[3], DECAY_WEIGHT),
        (norm_state, norm_grad, rates[4], 0.0),
        (col_state, col_grad, rates[4], 0.0),
    ):
        outs.extend(adam_update(*state, grad, rate, decay, rates, step_count))
    return (loss_value, query_grad, passage_grad, *outs, outs[0].astype(BF16), outs[4].astype(BF16))


def solution(mesh):
    matrix = P(None, "dp", "mp")
    rows = P("dp", None, None)
    placed = (rows, rows, P("dp"), P("dp"), P("dp"), P(), P(), *[matrix] * 8, *[P()] * 4, *[P("mp")] * 4)
    return jax.shard_map(
        per_device,
        mesh=mesh,
        in_specs=placed,
        out_specs=(P(), rows, rows, *[matrix] * 8, *[P()] * 4, *[P("mp")] * 4, matrix, matrix),
        check_vma=False,
    )
```

```python
import functools

import jax
import jax.numpy as jnp
from jax import lax
from jax.experimental import pallas as pl
from jax.experimental.pallas import tpu as pltpu
from jax.sharding import PartitionSpec as P

HD = 64
LANES = 128
NEG_FILL = -1e30
SOFTMAX_TEMPER = 0.02
NORM_EPS = 1e-12
POOL_EPS = 1e-06
DECAY_WEIGHT = 0.01
ADAM_EPS = 1e-08
PRECISE = lax.Precision.HIGHEST
MESH = pl.DeviceIdType.MESH
MIB = 2**20
F32 = jnp.float32
BF16 = jnp.bfloat16

ERFC_STEP = 0.46
ERFC_HALF = (
    0.5 * 0.26113873056821263,
    0.5 * 0.23637801512084577,
    0.5 * 0.3601812301921897,
    -0.5 * 0.18740624158431016,
    0.5 * 0.6751549397754679,
    -0.5 * 0.4305350150859377,
    0.5 * 0.0850883282904581,
)
ROOT_HALF = 0.7071067811865476
DENSITY = 0.3989422804014327


def gelu_and_slope(hidden):
    bell = jnp.exp(hidden * hidden * (-0.5))
    step = 1.0 / (1.0 + (ERFC_STEP * ROOT_HALF) * jnp.abs(hidden))
    tail = ERFC_HALF[6]
    for coefficient in ERFC_HALF[5::-1]:
        tail = tail * step + coefficient
    tail = tail * step * bell
    below = jnp.where(hidden >= 0.0, 1.0 - tail, tail)
    return hidden * below, below + hidden * bell * DENSITY


def mm(left, right):
    return jnp.dot(left, right, preferred_element_type=F32)


def mm_nt(left, right):
    return lax.dot_general(left, right, (((1,), (1,)), ((), ())), preferred_element_type=F32)


def mm_tn(left, right):
    return lax.dot_general(left, right, (((0,), (0,)), ((), ())), preferred_element_type=F32)


def first_head(shape):
    return lax.broadcasted_iota(jnp.int32, shape, 1) < HD


def stack_heads(values):
    place = lax.broadcasted_iota(jnp.int32, values.shape, 1) // HD
    zero = jnp.zeros_like(values)
    return jnp.concatenate(
        [jnp.where(place == head, values, zero) for head in range(values.shape[1] // HD)], axis=0
    )


def unstack_heads(values, count):
    place = lax.broadcasted_iota(jnp.int32, (count, values.shape[1]), 1) // HD
    total = None
    for head in range(values.shape[1] // HD):
        piece = jnp.where(place == head, values[head * count : (head + 1) * count], 0.0)
        total = piece if total is None else total + piece
    return total


def split_pair(values):
    lane = first_head(values.shape)
    zero = jnp.zeros_like(values)
    return jnp.where(lane, values, zero), jnp.where(lane, zero, values)


def probabilities(scores, length):
    valid = lax.broadcasted_iota(jnp.int32, scores.shape, 1) < length
    scores = jnp.where(valid, scores, NEG_FILL)
    weight = jnp.exp(scores - jnp.max(scores, axis=1, keepdims=True))
    return weight * (1.0 / jnp.sum(weight, axis=1, keepdims=True))


def normalize(values):
    center = values - jnp.mean(values, axis=-1, keepdims=True)
    spread = jnp.mean(center * center, axis=-1, keepdims=True)
    inverse = lax.rsqrt(spread + NORM_EPS)
    return center * inverse, inverse


def normalize_back(unit, inverse, grad_unit):
    return inverse * (
        grad_unit
        - jnp.mean(grad_unit, axis=-1, keepdims=True)
        - unit * jnp.mean(grad_unit * unit, axis=-1, keepdims=True)
    )


SCALE = HD**-0.5
SLAB = 16


class Mesh:
    def __init__(self):
        self.me = lax.axis_index("dp")
        self.core = lax.axis_index("mp")
        self.x, self.y, self.z = lax.rem(self.me, 2), lax.rem(self.me // 2, 2), self.me // 4
        self.x_peer = (self.index(self.z, self.y, 1 - self.x), self.core)
        self.y_peer = (self.index(self.z, 1 - self.y, self.x), self.core)
        self.c_peer = (self.me, 1 - self.core)
        self.z_peer = [None] + [(self.index(lax.rem(self.z + k, 4), self.y, self.x), self.core) for k in range(1, 4)]
        self.column = [lax.rem(self.z - k + 4, 4) for k in range(4)]

    def index(self, z, y, x):
        return (z * 2 + y) * 2 + x


def remote(source, target, send, recv, peer):
    return pltpu.make_async_remote_copy(
        src_ref=source, dst_ref=target, send_sem=send, recv_sem=recv, device_id=peer, device_id_type=MESH
    )


def forward_kernel(
    spans, total,
    query_len, passage_len, positive, query_ref, passage_ref, attn_ref, ffn_ref, col_ref, norm_ref,
    weight_out, proj_out, mixed_out, unit_out, inverse_out, low_out, active_out, slope_out, tokens_out,
    grad_out, grad_low_out, small_out,
    weight, proj, mixed, unit, inverse, low, active, slope, tokens, z_two, grad_low, small,
    col, attn_in, ffn_in, unit_two, slab, every,
    z_send, z_recv, x_send, x_recv, y_send, y_recv, d_send, d_recv, c_send, c_recv, b_send, b_recv, here_sem, out_sem,
    e_send, e_recv, p_send, p_recv, pz_send, pz_recv,
):
    at = Mesh()
    me, core = at.me, at.core
    my_rank = me * 2 + core
    rows, width = attn_ref.shape[1:]
    units = ffn_ref.shape[2]
    slots, model = tokens.shape

    def device(step):
        rank = lax.rem(my_rank + step, total)
        return (rank // 2, lax.rem(rank, 2))

    incoming = [
        pltpu.make_async_copy(attn_ref, attn_in, here_sem.at[0]),
        pltpu.make_async_copy(ffn_ref.at[0], ffn_in.at[0], here_sem.at[1]),
        pltpu.make_async_copy(ffn_ref.at[1], ffn_in.at[1], here_sem.at[2]),
        pltpu.make_async_copy(query_ref.at[core], tokens.at[pl.ds(*spans[0]), :], here_sem.at[3]),
        pltpu.make_async_copy(passage_ref.at[core], tokens.at[pl.ds(*spans[1]), :], here_sem.at[4]),
    ]
    for copy in incoming:
        copy.start()
    lens = (query_len[core], passage_len[core])
    barrier = pltpu.get_barrier_semaphore()
    for step in range(1, total):
        pl.semaphore_signal(barrier, inc=1, device_id=device(step), device_id_type=MESH)
    for line in range(col_ref.shape[0]):
        col[0, :, pl.ds(line * LANES, LANES)] = col_ref[pl.ds(line, 1), :]
    pl.semaphore_wait(barrier, total - 1)

    every_lane = pl.ds(0, units)
    cut = units * 2 // 3

    def column_lanes(q):
        return pl.ds(0, units if q < 2 else cut)

    def half_lanes(q, which):
        count = (units if q < 2 else cut) // 2
        return pl.ds(which * count, count)

    layer_lanes = pl.ds(cut, units - cut)

    def layer_half(which):
        count = (units - cut) // 2
        return pl.ds(cut + which * count, count)

    def block(q, index, lanes=None, count=1, far=0):
        lanes = column_lanes(q) if lanes is None else lanes
        return weight.at[far, q, pl.ds(pl.multiple_of(index * rows, rows), count * rows), lanes]

    sends = []
    stores = []

    def push(ref, send, recv, peer, target=None):
        copy = remote(ref, ref if target is None else target, send, recv, peer)
        copy.start()
        sends.append(copy)

    def landed(ref, send, recv, peer):
        remote(ref, ref, send, recv, peer).wait_recv()

    def store(source, target):
        copy = pltpu.make_async_copy(source, target, out_sem.at[len(stores)])
        copy.start()
        stores.append(copy)

    def cast_own(q):
        incoming[q].wait()
        here = pl.ds(pl.multiple_of(me * rows, rows), rows)
        if q == 0:
            for index in range(4):
                weight[0, 0, here, pl.ds(index * width, width)] = attn_in[index].astype(BF16)
        else:
            weight[0, q, here, :] = ffn_in[q - 1].astype(BF16)

    def own_along_column(q):
        for k in range(1, 4):
            push(block(q, me), z_send.at[q, k], z_recv.at[q, k], at.z_peer[k])

    def own_to_sides(q):
        push(block(q, me), x_send.at[q, 0], x_recv.at[q, 0], at.x_peer)
        push(block(q, me), y_send.at[q, 0], y_recv.at[q, 0], at.y_peer)

    def column_to_sides(q):
        for k in range(1, 4):
            ref = block(q, at.index(at.column[k], at.y, at.x))
            landed(ref, z_send.at[q, k], z_recv.at[q, k], at.z_peer[k])
            push(ref, x_send.at[q, k], x_recv.at[q, k], at.x_peer)
            push(ref, y_send.at[q, k], y_recv.at[q, k], at.y_peer)

    def round_corner(q, ks=range(4)):
        for k in ks:
            beside = at.index(at.column[k], at.y, 1 - at.x)
            landed(block(q, beside), x_send.at[q, k], x_recv.at[q, k], at.x_peer)
            push(block(q, beside, half_lanes(q, 0)), d_send.at[q, k, 0], d_recv.at[q, k, 0], at.y_peer)
            beside = at.index(at.column[k], 1 - at.y, at.x)
            landed(block(q, beside), y_send.at[q, k], y_recv.at[q, k], at.y_peer)
            push(block(q, beside, half_lanes(q, 1)), d_send.at[q, k, 1], d_recv.at[q, k, 1], at.x_peer)

    def layer_to_sides():
        ref = block(2, me, layer_lanes)
        push(ref, p_send.at[0], p_recv.at[0], at.x_peer)
        push(ref, p_send.at[1], p_recv.at[1], at.y_peer)

    def layer_round_corner():
        beside = at.index(at.z, at.y, 1 - at.x)
        landed(block(2, beside, layer_lanes), p_send.at[0], p_recv.at[0], at.x_peer)
        push(block(2, beside, layer_half(0)), p_send.at[2], p_recv.at[2], at.y_peer)
        beside = at.index(at.z, 1 - at.y, at.x)
        landed(block(2, beside, layer_lanes), p_send.at[1], p_recv.at[1], at.y_peer)
        push(block(2, beside, layer_half(1)), p_send.at[3], p_recv.at[3], at.x_peer)

    def layer_along_column():
        across = at.index(at.z, 1 - at.y, 1 - at.x)
        landed(block(2, across, layer_half(0)), p_send.at[2], p_recv.at[2], at.y_peer)
        landed(block(2, across, layer_half(1)), p_send.at[3], p_recv.at[3], at.x_peer)
        for k in range(1, 4):
            push(block(2, at.index(at.z, 0, 0), layer_lanes, 4), pz_send.at[k], pz_recv.at[k], at.z_peer[k])

    def to_other_core(q, ks=range(4)):
        for k in ks:
            across = at.index(at.column[k], 1 - at.y, 1 - at.x)
            landed(block(q, across, half_lanes(q, 0)), d_send.at[q, k, 0], d_recv.at[q, k, 0], at.y_peer)
            landed(block(q, across, half_lanes(q, 1)), d_send.at[q, k, 1], d_recv.at[q, k, 1], at.x_peer)
            layer = at.index(at.column[k], 0, 0)
            if q == 2 and k:
                landed(block(2, layer, layer_lanes, 4), pz_send.at[k], pz_recv.at[k], at.z_peer[k])
            push(
                block(q, layer, every_lane, 4), c_send.at[q, k], c_recv.at[q, k], at.c_peer,
                block(q, layer, every_lane, 4, 1),
            )

    def from_other_core(q):
        for k in range(4):
            layer = at.index(at.column[k], 0, 0)
            landed(block(q, layer, every_lane, 4, 1), c_send.at[q, k], c_recv.at[q, k], at.c_peer)

    def project(half):
        bias = jnp.concatenate(
            [
                col[half, :, pl.ds(0, width)],
                jnp.zeros((1, width), F32),
                col[half, :, pl.ds(width, width)],
            ],
            axis=1,
        )
        proj[half] = (mm(tokens[...], weight[half, 0, :, pl.ds(0, 3 * width)]) + bias).astype(BF16)

    def query_heads(half):
        place = pl.ds(*spans[0])
        queries = stack_heads(proj[half, place, pl.ds(0, width)] * jnp.asarray(SCALE, BF16))
        probs = probabilities(mm_nt(queries, proj[half, place, pl.ds(width, width)]), lens[0])
        value = mm(probs.astype(BF16), proj[half, place, pl.ds(2 * width, width)])
        mixed[half, place, :] = unstack_heads(value, spans[0][1]).astype(BF16)

    def passage_heads(half, pair):
        place = pl.ds(*spans[1])
        queries = proj[half, place, pl.ds(pair * LANES, LANES)]
        keys = split_pair(proj[half, place, pl.ds(width + pair * LANES, LANES)] * jnp.asarray(SCALE, BF16))
        values = proj[half, place, pl.ds(2 * width + pair * LANES, LANES)]
        scores = [mm_nt(queries, key) for key in keys]
        outs = [mm(probabilities(score, lens[1]).astype(BF16), values) for score in scores]
        mixed[half, place, pl.ds(pair * LANES, LANES)] = jnp.where(first_head(outs[0].shape), *outs).astype(BF16)

    def first_norm():
        step = 192
        for start in range(0, slots, step):
            place = pl.ds(start, step)
            value = tokens[place, :].astype(F32) + norm_ref[pl.ds(0, 1), :]
            for half in range(2):
                value = value + mm_nt(mixed[half, place, :], weight[half, 0, :, pl.ds(3 * width, width)])
            normed, scale = normalize(value)
            unit[place, :] = normed
            inverse[place, :] = jnp.broadcast_to(scale, (step, LANES))
            value = normed * norm_ref[pl.ds(1, 1), :] + norm_ref[pl.ds(2, 1), :]
            z_two[place, :] = value + norm_ref[pl.ds(3, 1), :]
            low[place, :] = value.astype(BF16)

    tile = 256

    def up(half, part):
        for start in range(part * units // 2, (part + 1) * units // 2, tile):
            lanes = pl.ds(start, tile)
            hidden = mm(low[...], weight[half, 1, :, lanes]) + col[half, :, pl.ds(2 * width + start, tile)]
            value, grad = gelu_and_slope(hidden)
            active[half, :, lanes] = value.astype(BF16)
            slope[half, :, lanes] = grad

    def down(half):
        z_two[...] = z_two[...] + mm_nt(active[half], weight[half, 2])

    cast_own(0)
    own_along_column(0)
    own_to_sides(0)
    push(col.at[0], b_send, b_recv, at.c_peer, col.at[1])
    cast_own(1)
    own_to_sides(1)
    cast_own(2)
    layer_to_sides()
    own_to_sides(2)
    incoming[3].wait()
    incoming[4].wait()
    store(tokens, tokens_out)
    column_to_sides(0)
    layer_round_corner()
    own_along_column(1)
    round_corner(0)
    column_to_sides(1)
    own_along_column(2)
    layer_along_column()
    to_other_core(0)
    project(0)
    query_heads(0)
    passage_heads(0, 0)
    round_corner(1, (0,))
    passage_heads(0, 1)
    round_corner(1, (1,))
    passage_heads(0, 2)
    landed(col.at[1], b_send, b_recv, at.c_peer)
    from_other_core(0)
    project(1)
    for half in range(2):
        store(weight.at[half, 0], weight_out.at[half, 0])
    store(proj, proj_out)
    round_corner(1, (2,))
    query_heads(1)
    round_corner(1, (3,))
    passage_heads(1, 0)
    column_to_sides(2)
    passage_heads(1, 1)
    passage_heads(1, 2)
    store(mixed, mixed_out)
    first_norm()
    store(unit, unit_out)
    store(inverse, inverse_out)
    store(low, low_out)
    to_other_core(1)
    round_corner(2, (0,))
    up(0, 0)
    round_corner(2, (1,))
    up(0, 1)
    store(slope.at[0], slope_out.at[0])
    store(weight.at[0, 1], weight_out.at[0, 1])
    round_corner(2, (2,))
    from_other_core(1)
    up(1, 0)
    round_corner(2, (3,))
    up(1, 1)
    store(slope.at[1], slope_out.at[1])
    store(weight.at[1, 1], weight_out.at[1, 1])
    store(active, active_out)
    to_other_core(2)
    store(weight.at[0, 2], weight_out.at[0, 2])
    down(0)
    from_other_core(2)
    store(weight.at[1, 2], weight_out.at[1, 2])
    down(1)

    pieces = model // LANES
    gain, shift = norm_ref[pl.ds(4, 1), :], norm_ref[pl.ds(5, 1), :]
    embeds, shrinks, means, inverses, valids = [], [], [], [], []
    for index, (start, count) in enumerate(spans):
        normed, scale = normalize(z_two[pl.ds(start, count), :])
        unit_two[pl.ds(start, count), :] = normed
        valid = lax.broadcasted_iota(jnp.int32, (count, 1), 0) < lens[index]
        mean = jnp.sum(jnp.where(valid, normed, 0.0), axis=0, keepdims=True) / lens[index].astype(F32)
        pooled = mean * gain + shift
        shrink = lax.rsqrt(jnp.sum(pooled * pooled, axis=1, keepdims=True) + POOL_EPS)
        embed = pooled * shrink
        for piece in range(pieces):
            slab[pl.ds(index * pieces + piece, 1), :] = embed[:, piece * LANES : (piece + 1) * LANES]
        embeds.append(embed)
        shrinks.append(shrink)
        means.append(mean)
        inverses.append(jnp.where(valid, scale, 0.0))
    slab[pl.ds(2 * pieces, 1), :] = jnp.full((1, LANES), positive[core], jnp.int32).astype(F32)
    copies = []
    for step in range(1, total):
        copy = remote(slab, every.at[my_rank], e_send.at[step], e_recv.at[step], device(step))
        copy.start()
        copies.append(copy)
    sends.extend(copies)
    every[my_rank] = slab[...]
    for copy in copies:
        copy.wait_recv()

    queries = jnp.concatenate([every[:, piece, :] for piece in range(pieces)], axis=1)
    passages = jnp.concatenate([every[:, pieces + piece, :] for piece in range(pieces)], axis=1)
    wanted = every[:, 2 * pieces, :][:, :1]
    logits = lax.dot_general(
        queries, passages, (((1,), (1,)), ((), ())), precision=PRECISE, preferred_element_type=F32
    ) / SOFTMAX_TEMPER
    place = lax.broadcasted_iota(jnp.int32, logits.shape, 1)
    target = (place.astype(F32) == wanted).astype(F32)
    top = jnp.max(logits, axis=1, keepdims=True)
    weights = jnp.exp(logits - top)
    row_total = jnp.sum(weights, axis=1, keepdims=True)
    log_total = top + jnp.log(row_total)
    loss = jnp.sum(log_total - jnp.sum(logits * target, axis=1, keepdims=True), axis=0, keepdims=True) / total
    grad_logits = (weights / row_total - target) / (total * SOFTMAX_TEMPER)
    grad_column = jnp.sum(jnp.where(place == my_rank, grad_logits, 0.0), axis=1, keepdims=True)
    value = jnp.dot(grad_logits, passages, precision=PRECISE, preferred_element_type=F32)
    line = lax.broadcasted_iota(jnp.int32, value.shape, 0)
    grad_embeds = (
        jnp.sum(jnp.where(line == my_rank, value, 0.0), axis=0, keepdims=True),
        jnp.sum(grad_column * queries, axis=0, keepdims=True),
    )

    grad_gain, grad_shift, grad_bias = 0.0, 0.0, 0.0
    for index, (start, count) in enumerate(spans):
        embed, grad_embed = embeds[index], grad_embeds[index]
        grad_pooled = shrinks[index] * (grad_embed - embed * jnp.sum(grad_embed * embed, axis=1, keepdims=True))
        grad_gain = grad_gain + grad_pooled * means[index]
        grad_shift = grad_shift + grad_pooled
        spread = grad_pooled * gain / lens[index].astype(F32)
        centered = spread - jnp.mean(spread, axis=1, keepdims=True)
        normed = unit_two[pl.ds(start, count), :]
        value = inverses[index] * (centered - normed * jnp.mean(spread * normed, axis=1, keepdims=True))
        z_two[pl.ds(start, count), :] = value
        grad_low[pl.ds(start, count), :] = value.astype(BF16)
        grad_bias = grad_bias + jnp.sum(value, axis=0, keepdims=True)
    store(grad_low, grad_low_out)
    store(z_two, grad_out)
    small[pl.ds(0, 1), :] = grad_bias
    small[pl.ds(1, 1), :] = grad_gain
    small[pl.ds(2, 1), :] = grad_shift
    small[pl.ds(3, 1), :] = jnp.broadcast_to(loss, (1, model))
    small[pl.ds(4, 4), :] = jnp.zeros((4, model), F32)
    store(small, small_out)
    for copy in sends:
        copy.wait_send()
    for copy in stores:
        copy.wait()


def forward(query_in, passage_in, query_len, passage_len, positive, attn_master, ffn_master, col_bias, norm_params, spans, total):
    rows, width = attn_master.shape[1:]
    units = ffn_master.shape[2]
    slots, model = spans[1][0] + spans[1][1], query_in.shape[2]
    dma = pltpu.SemaphoreType.DMA
    col = col_bias.reshape(-1, LANES)
    anywhere = pl.BlockSpec(memory_space=pltpu.HBM)
    vmem = pl.BlockSpec(memory_space=pltpu.VMEM)
    smem = pl.BlockSpec(memory_space=pltpu.SMEM)
    results = (
        ((2, 3, model, units), BF16),
        ((2, slots, 3 * width), BF16),
        ((2, slots, width), BF16),
        ((slots, model), F32),
        ((slots, LANES), F32),
        ((slots, model), BF16),
        ((2, slots, units), BF16),
        ((2, slots, units), F32),
        ((slots, model), BF16),
        ((slots, model), F32),
        ((slots, model), BF16),
        ((8, model), F32),
    )
    return pl.pallas_call(
        functools.partial(forward_kernel, spans, total),
        out_shape=tuple(jax.ShapeDtypeStruct(*result) for result in results),
        in_specs=[smem] * 3 + [anywhere] * 4 + [vmem] * 2,
        out_specs=(anywhere,) * len(results),
        scratch_shapes=[pltpu.VMEM(*result) for result in results]
        + [
            pltpu.VMEM((2, 1, col_bias.shape[0]), F32),
            pltpu.VMEM(attn_master.shape, F32),
            pltpu.VMEM(ffn_master.shape, F32),
            pltpu.VMEM((slots, model), F32),
            pltpu.VMEM((SLAB, LANES), F32),
            pltpu.VMEM((total, SLAB, LANES), F32),
        ]
        + [dma((3, 4))] * 6
        + [dma((3, 4, 2))] * 2
        + [dma((3, 4))] * 2
        + [dma(()), dma(()), dma((5,)), dma((20,)), dma((total,)), dma((total,))]
        + [dma((4,))] * 4,
        compiler_params=pltpu.CompilerParams(collective_id=0, has_side_effects=True, vmem_limit_bytes=58 * MIB),
        name="forward",
    )(query_len, passage_len, positive, query_in, passage_in, attn_master, ffn_master, col, norm_params)


def backward_kernel(
    spans,
    query_len, passage_len, weight_ref, proj_ref, mixed_ref, unit_ref, inverse_ref, low_ref, active_ref, slope_ref,
    tokens_ref, grad_ref, grad_low_ref, norm_ref, small_ref,
    attn_out, ffn_out, small_out, col_out, query_out, passage_out,
    weight, proj, mixed, inverse, low, active, slope, tokens, total, down, grad_out, grad_proj,
    temp, far_send, far_recv, kept, one_send, one_recv, two_send, two_recv, z_send, z_recv, result, vector, vec_send,
    vec_recv, col,
    load_sem, slope_sem, c_send, c_recv, s1_send, s1_recv, s2_send, s2_recv, s3_send, s3_recv,
    v_send, v_recv, t_send, t_recv, credit, out_sem, layer_recv,
):
    at = Mesh()
    me, core = at.me, at.core
    slots, model = tokens.shape
    width = grad_out.shape[2]
    rows = model // 16
    lens = (query_len[core], passage_len[core])
    near_peer = (at.index(at.z + 1 - 2 * lax.rem(at.z, 2), at.y, at.x), core)
    over_peer = at.z_peer[2]

    sends = {}
    stores = []
    loads = {}

    def load(name, *pairs):
        copies = []
        for source, target in pairs:
            copy = pltpu.make_async_copy(source, target, load_sem.at[sum(len(v) for v in loads.values()) + len(copies)])
            copy.start()
            copies.append(copy)
        loads[name] = copies

    def ready(name):
        for copy in loads[name]:
            copy.wait()

    def store(source, target):
        copy = pltpu.make_async_copy(source, target, out_sem.at[len(stores)])
        copy.start()
        stores.append(copy)

    def push(name, source, target, send, recv, peer):
        copy = remote(source, target, send, recv, peer)
        copy.start()
        sends[name] = copy

    def landed(target, send, recv, peer):
        remote(target, target, send, recv, peer).wait_recv()

    lanes_of = [pl.ds(t * width, width) for t in range(4)]
    pair_lanes = (pl.ds(0, 2 * width), pl.ds(2 * width, 2 * width))

    def slope_tile(half, t):
        index = half * 4 + t
        return pltpu.make_async_copy(slope_ref.at[half, :, lanes_of[t]], slope.at[t % 2], slope_sem.at[index])

    load("down", (grad_low_ref, down))
    load("active1", (active_ref.at[1], active.at[1]))
    barrier = pltpu.get_barrier_semaphore()
    for peer in [*at.z_peer[1:], at.x_peer, at.y_peer, at.c_peer]:
        pl.semaphore_signal(barrier, inc=1, device_id=peer, device_id_type=MESH)
    load("down1", (weight_ref.at[1, 2], weight.at[0]))
    slope_tile(1, 0).start()
    slope_tile(1, 1).start()
    load("active0", (active_ref.at[0], active.at[0]))

    def far_slot(q):
        return q % 2

    def send_far(q, t, value):
        if q == 2:
            sends[("c", 0, t)].wait_send()
        far_send[far_slot(q), t] = value.astype(BF16)
        push(
            ("c", q, t), far_send.at[far_slot(q), t], far_recv.at[far_slot(q), t], c_send.at[q, t], c_recv.at[q, t],
            at.c_peer,
        )

    def side(t):
        steps = ((at.x, at.x_peer), (at.y, at.y_peer))
        return steps if t % 2 == 0 else steps[::-1]

    def block(index, count=1):
        return pl.ds(pl.multiple_of(index * rows, rows), count * rows)

    def first_step(q, t, lanes):
        landed(far_recv.at[far_slot(q), t], c_send.at[q, t], c_recv.at[q, t], at.c_peer)
        (bit, peer), _ = side(t)
        for layer in range(4):
            for other in range(2):
                if t % 2 == 0:
                    mine, theirs = at.index(layer, other, bit), at.index(layer, other, 1 - bit)
                else:
                    mine, theirs = at.index(layer, bit, other), at.index(layer, 1 - bit, other)
                place = pl.ds((layer * 2 + other) * rows, rows)
                far = far_recv[far_slot(q), t, block(theirs), :].astype(F32)
                one_send[q, t, place, :] = (temp[block(theirs), lanes] + far).astype(BF16)
                far = far_recv[far_slot(q), t, block(mine), :].astype(F32)
                kept[q, t, place, :] = temp[block(mine), lanes] + far
        push(("1", q, t), one_send.at[q, t], one_recv.at[q, t], s1_send.at[q, t], s1_recv.at[q, t], peer)

    def second_step(q, t):
        (_, before), (bit, peer) = side(t)
        landed(one_recv.at[q, t], s1_send.at[q, t], s1_recv.at[q, t], before)
        for layer in range(4):
            theirs = block(layer * 2 + 1 - bit)
            value = kept[q, t, theirs, :] + one_recv[q, t, theirs, :].astype(F32)
            two_send[q, t, pl.ds(layer * rows, rows), :] = value.astype(BF16)
            mine = block(layer * 2 + bit)
            kept[q, t, mine, :] = kept[q, t, mine, :] + one_recv[q, t, mine, :].astype(F32)
        push(("2", q, t), two_send.at[q, t], two_recv.at[q, t], s2_send.at[q, t], s2_recv.at[q, t], peer)

    def third_step(q, t):
        _, (bit, before) = side(t)
        landed(two_recv.at[q, t], s2_send.at[q, t], s2_recv.at[q, t], before)
        for k in range(1, 4):
            layer = lax.rem(at.z + k, 4)
            value = kept[q, t, block(layer * 2 + bit), :] + two_recv[q, t, block(layer), :].astype(F32)
            z_send[q, t, k - 1] = value.astype(BF16)
            push(
                ("3", q, t, k), z_send.at[q, t, k - 1], z_recv.at[q, t, k - 1], s3_send.at[q, t, k], s3_recv.at[q, t, k],
                at.z_peer[k],
            )
        result[q, t] = kept[q, t, block(at.z * 2 + bit), :] + two_recv[q, t, block(at.z), :].astype(F32)

    def last_step(q, t):
        for k in range(1, 4):
            landed(z_recv.at[q, t, k - 1], s3_send.at[q, t, k], s3_recv.at[q, t, k], at.z_peer[k])
        value = result[q, t]
        for k in range(3):
            value = value + z_recv[q, t, k].astype(F32)
        result[q, t] = value
        store_result(q, t)

    def store_result(q, t):
        if q < 2:
            store(result.at[q, t], ffn_out.at[1 - q, :, lanes_of[t]])
        elif t == 3:
            store(result.at[q, t], attn_out.at[3])
        else:
            for index in range(3):
                store(result.at[q, t, :, pl.ds(index * LANES, LANES)], attn_out.at[index, :, pl.ds(t * LANES, LANES)])

    def layer_first_step(q, t, lanes):
        landed(far_recv.at[far_slot(q), t], c_send.at[q, t], c_recv.at[q, t], at.c_peer)
        for k in range(1, 4):
            theirs = block(at.index(lax.rem(at.z + k, 4), 0, 0), 4)
            value = temp[theirs, lanes] + far_recv[far_slot(q), t, theirs, :].astype(F32)
            if k < 3:
                source = one_send.at[q, t, pl.ds((k - 1) * 4 * rows, 4 * rows), :]
            else:
                source = two_send.at[q, t]
            source[...] = value.astype(BF16)
            push(
                ("1", q, t, k), source, layer_recv.at[t, k - 1], s3_send.at[q, t, k],
                s3_recv.at[q, t, k], at.z_peer[k],
            )
        mine = block(at.index(at.z, 0, 0), 4)
        kept[q, t, pl.ds(0, 4 * rows), :] = temp[mine, lanes] + far_recv[far_slot(q), t, mine, :].astype(F32)

    def layer_second_step(q, t):
        for k in range(1, 4):
            landed(layer_recv.at[t, k - 1], s3_send.at[q, t, k], s3_recv.at[q, t, k], at.z_peer[k])
        value = kept[q, t, pl.ds(0, 4 * rows), :]
        for k in range(3):
            value = value + layer_recv[t, k].astype(F32)
        kept[q, t, pl.ds(0, 4 * rows), :] = value
        for line in range(2):
            z_send[q, t, line] = kept[q, t, block(line * 2 + 1 - at.x), :].astype(BF16)
        push(
            ("2", q, t), z_send.at[q, t, pl.ds(0, 2)], z_recv.at[q, t, pl.ds(0, 2)], s1_send.at[q, t], s1_recv.at[q, t],
            at.x_peer,
        )

    def layer_third_step(q, t):
        landed(z_recv.at[q, t, pl.ds(0, 2)], s1_send.at[q, t], s1_recv.at[q, t], at.x_peer)
        theirs = kept[q, t, block((1 - at.y) * 2 + at.x), :] + z_recv[q, t, 1 - at.y].astype(F32)
        z_send[q, t, 2] = theirs.astype(BF16)
        push(
            ("3", q, t), z_send.at[q, t, 2], z_recv.at[q, t, 2], s2_send.at[q, t], s2_recv.at[q, t],
            at.y_peer,
        )
        result[q, t] = kept[q, t, block(at.y * 2 + at.x), :] + z_recv[q, t, at.y].astype(F32)

    def layer_last_step(q, t):
        landed(z_recv.at[q, t, 2], s2_send.at[q, t], s2_recv.at[q, t], at.y_peer)
        result[q, t] = result[q, t] + z_recv[q, t, 2].astype(F32)
        store_result(q, t)

    def far_product(q, left, right, pair):
        value = mm_tn(left[...], right[:, pair_lanes[pair]])
        send_far(q, 2 * pair, value[:, :width])
        send_far(q, 2 * pair + 1, value[:, width:])

    def own_product(q, left, right, pair):
        temp[...] = mm_tn(left[...], right[:, pair_lanes[pair]])
        step = layer_first_step if (q, pair) == (0, 0) else first_step
        step(q, 2 * pair, lanes_of[0])
        step(q, 2 * pair + 1, lanes_of[1])

    def hidden_grad(half, slot, pair, following):
        for t in (2 * pair, 2 * pair + 1):
            slope_tile(half, t).wait()
        value = mm(down[...], weight[slot, :, pair_lanes[pair]])
        for side_of, t in enumerate((2 * pair, 2 * pair + 1)):
            piece = (value[:, side_of * width : (side_of + 1) * width] * slope[side_of]).astype(BF16)
            active[half, :, lanes_of[t]] = piece
            vec = vector if half == 0 else vec_send.at[0]
            vec[pl.ds(9 + pair, 1), lanes_of[side_of]] = jnp.sum(piece.astype(F32), axis=0, keepdims=True)
        if following is not None:
            for t in (0, 1):
                slope_tile(following[0], 2 * following[1] + t).start()

    def add_back(source, slot, lanes):
        total[...] = total[...] + mm_nt(source, weight[slot, :, lanes])

    def first_norm_back():
        sums = [None, None, None]
        step = 192
        for start in range(0, slots, step):
            place = pl.ds(start, step)
            grad = total[place, :]
            normed = jnp.concatenate([slope[0, place, :], slope[1, place, :]], axis=1)
            back = normalize_back(normed, inverse[place, pl.ds(0, 1)], grad * norm_ref[pl.ds(1, 1), :])
            for index, value in enumerate((back, grad * normed, grad)):
                value = jnp.sum(value, axis=0, keepdims=True)
                sums[index] = value if sums[index] is None else sums[index] + value
            total[place, :] = back
            down[place, :] = back.astype(BF16)
        for index in range(3):
            vector[pl.ds(index, 1), :] = sums[index]
            vec_send[0, pl.ds(index, 1), :] = sums[index]

    def out_grad(half, slot):
        grad_out[half] = mm(down[...], weight[slot, :, lanes_of[3]]).astype(BF16)

    def query_back(half):
        place = pl.ds(*spans[0])
        queries = stack_heads(proj[half, place, lanes_of[0]])
        grads = stack_heads(grad_out[half, place, :])
        keys = proj[half, place, lanes_of[1]]
        probs = probabilities(mm_nt(queries * jnp.asarray(SCALE, BF16), keys), lens[0])
        grad_probs = mm_nt(grads, proj[half, place, lanes_of[2]])
        inner = jnp.sum(probs * grad_probs, axis=1, keepdims=True)
        grad_scores = (probs * (grad_probs - inner)).astype(BF16)
        value = unstack_heads(mm(grad_scores, keys), spans[0][1]) * SCALE
        grad_proj[half, place, lanes_of[0]] = value.astype(BF16)
        grad_proj[half, place, lanes_of[1]] = (mm_tn(grad_scores, queries) * SCALE).astype(BF16)
        grad_proj[half, place, lanes_of[2]] = mm_tn(probs.astype(BF16), grads).astype(BF16)

    def passage_back(half, pair):
        place = pl.ds(*spans[1])
        spot = [pl.ds(index * width + pair * LANES, LANES) for index in range(3)]
        queries, keys = proj[half, place, spot[0]], proj[half, place, spot[1]]
        grads = grad_out[half, place, pl.ds(pair * LANES, LANES)]
        scores = [mm_nt(queries, key) for key in split_pair(keys * jnp.asarray(SCALE, BF16))]
        grad_probs = [mm_nt(grads, value) for value in split_pair(proj[half, place, spot[2]])]
        outs = []
        for head in range(2):
            probs = probabilities(scores[head], lens[1])
            inner = jnp.sum(probs * grad_probs[head], axis=1, keepdims=True)
            grad_scores = (probs * (grad_probs[head] - inner)).astype(BF16)
            outs.append(
                (mm(grad_scores, keys) * SCALE, mm_tn(grad_scores, queries) * SCALE, mm_tn(probs.astype(BF16), grads))
            )
        lane = first_head(queries.shape)
        for index in range(3):
            grad_proj[half, place, spot[index]] = jnp.where(lane, outs[0][index], outs[1][index]).astype(BF16)

    def pair_product(half, pair):
        spot = [pl.ds(index * width + pair * LANES, LANES) for index in range(3)]
        return mm_tn(tokens[...], jnp.concatenate([grad_proj[half, :, lanes] for lanes in spot], axis=1))

    def attn_biases(half):
        vec = vector if half == 0 else vec_send.at[0]
        for index in (0, 1):
            value = grad_proj[half, :, lanes_of[2 * index]].astype(F32)
            vec[pl.ds(8, 1), lanes_of[index]] = jnp.sum(value, axis=0, keepdims=True)

    def vector_step(step, peer):
        if step:
            vec_send[step] = vector[...]
        push(("v", step), vec_send.at[step], vec_recv.at[step], v_send.at[step], v_recv.at[step], peer)

    def vector_sum(step, peer):
        landed(vec_recv.at[step], v_send.at[step], v_recv.at[step], peer)
        vector[...] = vector[...] + vec_recv[step]

    for target in (vector, vec_send.at[0]):
        target[pl.ds(3, 3), :] = small_ref[pl.ds(0, 3), :]
        target[pl.ds(6, 2), :] = jnp.zeros((2, model), F32)
        target[pl.ds(11, 5), :] = jnp.zeros((5, model), F32)

    ready("down")
    ready("active1")
    pl.semaphore_wait(barrier, 6)
    far_product(0, down, active.at[1], 1)
    far_product(0, down, active.at[1], 0)
    load("down0", (weight_ref.at[0, 2], weight.at[1]))
    load("low", (low_ref, low))
    load("up1", (weight_ref.at[1, 1], weight.at[2]))
    ready("active0")
    own_product(0, down, active.at[0], 1)
    ready("down1")
    hidden_grad(1, 0, 0, (0, 0))
    own_product(0, down, active.at[0], 0)
    pl.semaphore_signal(credit, inc=1, device_id=at.c_peer, device_id_type=MESH)
    ready("low")
    far_product(1, low, active.at[1], 0)
    ready("down0")
    hidden_grad(0, 1, 0, (1, 1))
    load("total", (grad_ref, total))
    load("inverse", (inverse_ref, inverse))
    own_product(1, low, active.at[0], 0)
    hidden_grad(1, 0, 1, (0, 1))
    load("up0", (weight_ref.at[0, 1], weight.at[0]))
    far_product(1, low, active.at[1], 1)
    second_step(0, 2)
    second_step(0, 3)
    hidden_grad(0, 1, 1, None)
    load("unit", *[(unit_ref.at[:, lanes_of[t]], slope.at[t]) for t in range(2)])
    load("attn1", (weight_ref.at[1, 0], weight.at[1]))
    load("proj", (proj_ref, proj), (mixed_ref, mixed), (tokens_ref, tokens))
    own_product(1, low, active.at[0], 1)
    ready("total")
    ready("up1")
    add_back(active[1], 2, pl.ds(0, 4 * width))
    load("attn0", (weight_ref.at[0, 0], weight.at[2]))
    ready("up0")
    add_back(active[0], 0, pl.ds(0, 4 * width))
    second_step(1, 0)
    second_step(1, 1)
    ready("inverse")
    ready("unit")
    first_norm_back()
    ready("proj")
    pl.semaphore_wait(credit, 1)
    send_far(2, 3, mm_tn(down[...], mixed[1]))
    ready("attn1")
    out_grad(1, 1)
    query_back(1)
    temp[:, lanes_of[0]] = mm_tn(down[...], mixed[0])
    first_step(2, 3, lanes_of[0])
    third_step(0, 2)
    third_step(0, 3)
    passage_back(1, 0)
    send_far(2, 0, pair_product(1, 0))
    ready("attn0")
    out_grad(0, 2)
    query_back(0)
    layer_second_step(0, 0)
    passage_back(0, 0)
    temp[:, lanes_of[1]] = pair_product(0, 0)
    first_step(2, 0, lanes_of[1])
    second_step(1, 2)
    second_step(1, 3)
    passage_back(1, 1)
    send_far(2, 1, pair_product(1, 1))
    third_step(1, 0)
    third_step(1, 1)
    layer_second_step(0, 1)
    layer_third_step(0, 0)
    passage_back(0, 1)
    temp[:, lanes_of[0]] = pair_product(0, 1)
    first_step(2, 1, lanes_of[0])
    last_step(0, 2)
    last_step(0, 3)
    passage_back(1, 2)
    send_far(2, 2, pair_product(1, 2))
    attn_biases(1)
    vector_step(0, at.c_peer)
    second_step(2, 3)
    layer_third_step(0, 1)
    passage_back(0, 2)
    temp[:, lanes_of[1]] = pair_product(0, 2)
    first_step(2, 2, lanes_of[1])
    second_step(2, 0)
    third_step(1, 2)
    third_step(1, 3)
    attn_biases(0)
    vector_sum(0, at.c_peer)
    vector_step(1, at.x_peer)
    add_back(grad_proj[1], 1, pl.ds(0, 3 * width))
    second_step(2, 1)
    third_step(2, 3)
    add_back(grad_proj[0], 2, pl.ds(0, 3 * width))
    for index, target in ((0, query_out), (1, passage_out)):
        part = total.at[pl.ds(*spans[index]), :]
        store(part, target.at[core])
        push(("t", index), part, target.at[core], t_send.at[index], t_recv.at[index], at.c_peer)
    third_step(2, 0)
    vector_sum(1, at.x_peer)
    vector_step(2, at.y_peer)
    layer_last_step(0, 0)
    layer_last_step(0, 1)
    last_step(1, 0)
    last_step(1, 1)
    last_step(1, 2)
    last_step(1, 3)
    third_step(2, 1)
    second_step(2, 2)
    vector_sum(2, at.y_peer)
    vector_step(3, near_peer)
    last_step(2, 3)
    last_step(2, 0)
    third_step(2, 2)
    vector_sum(3, near_peer)
    vector_step(4, over_peer)
    last_step(2, 1)
    last_step(2, 2)
    vector_sum(4, over_peer)
    store(vector.at[pl.ds(0, 8), :], small_out)
    for line in range(3):
        for piece in range(model // LANES):
            col[pl.ds(line * (model // LANES) + piece, 1), :] = vector[pl.ds(8 + line, 1), pl.ds(piece * LANES, LANES)]
    store(col, col_out)
    for index, target in ((0, query_out), (1, passage_out)):
        landed(target.at[1 - core], t_send.at[index], t_recv.at[index], at.c_peer)
    for copy in stores:
        copy.wait()
    for name, copy in sends.items():
        if name[:2] != ("c", 0):
            copy.wait_send()


def backward(query_len, passage_len, kept, norm_params, spans):
    weight, proj, mixed, unit, inverse, low, active, slope, tokens, grad_ztwo, grad_low, small = kept
    slots, model = tokens.shape
    width = mixed.shape[2]
    rows = model // 16
    anywhere = pl.BlockSpec(memory_space=pltpu.HBM)
    vmem = pl.BlockSpec(memory_space=pltpu.VMEM)
    smem = pl.BlockSpec(memory_space=pltpu.SMEM)
    dma = pltpu.SemaphoreType.DMA
    lines = 3 * model // LANES
    scratch = [
        pltpu.VMEM((3, model, 4 * width), BF16),
        pltpu.VMEM(proj.shape, BF16),
        pltpu.VMEM(mixed.shape, BF16),
        pltpu.VMEM(inverse.shape, F32),
        pltpu.VMEM(low.shape, BF16),
        pltpu.VMEM(active.shape, BF16),
        pltpu.VMEM((2, slots, width), F32),
        pltpu.VMEM(tokens.shape, BF16),
        pltpu.VMEM((slots, model), F32),
        pltpu.VMEM((slots, model), BF16),
        pltpu.VMEM((2, slots, width), BF16),
        pltpu.VMEM((2, slots, 3 * width), BF16),
        pltpu.VMEM((model, 2 * width), F32),
        pltpu.VMEM((2, 4, model, width), BF16),
        pltpu.VMEM((2, 4, model, width), BF16),
        pltpu.VMEM((3, 4, 8 * rows, width), F32),
        pltpu.VMEM((3, 4, 8 * rows, width), BF16),
        pltpu.VMEM((3, 4, 8 * rows, width), BF16),
        pltpu.VMEM((3, 4, 4 * rows, width), BF16),
        pltpu.VMEM((3, 4, 4 * rows, width), BF16),
        pltpu.VMEM((3, 4, 3, rows, width), BF16),
        pltpu.VMEM((3, 4, 3, rows, width), BF16),
        pltpu.VMEM((3, 4, rows, width), F32),
        pltpu.VMEM((16, model), F32),
        pltpu.VMEM((5, 16, model), F32),
        pltpu.VMEM((5, 16, model), F32),
        pltpu.VMEM((lines, LANES), F32),
        dma((20,)), dma((8,)),
        dma((3, 4)), dma((3, 4)), dma((3, 4)), dma((3, 4)), dma((3, 4)), dma((3, 4)),
        dma((3, 4, 4)), dma((3, 4, 4)),
        dma((5,)), dma((5,)), dma((2,)), dma((2,)),
        pltpu.SemaphoreType.REGULAR,
        dma((24,)),
        pltpu.VMEM((2, 3, 4 * rows, width), BF16),
    ]
    return pl.pallas_call(
        functools.partial(backward_kernel, spans),
        out_shape=(
            jax.ShapeDtypeStruct((4, rows, width), F32),
            jax.ShapeDtypeStruct((2, rows, 4 * width), F32),
            jax.ShapeDtypeStruct((8, model), F32),
            jax.ShapeDtypeStruct((lines, LANES), F32),
            jax.ShapeDtypeStruct((2, spans[0][1], model), F32),
            jax.ShapeDtypeStruct((2, spans[1][1], model), F32),
        ),
        in_specs=[smem] * 2 + [anywhere] * 11 + [vmem, vmem],
        out_specs=(anywhere,) * 6,
        scratch_shapes=scratch,
        compiler_params=pltpu.CompilerParams(collective_id=2, has_side_effects=True, vmem_limit_bytes=60 * MIB),
        name="backward",
    )(query_len, passage_len, weight, proj, mixed, unit, inverse, low, active, slope, tokens, grad_ztwo, grad_low,
      norm_params, small)


def finish_kernel(
    step_ref, rates_ref, query_ref, passage_ref,
    attn_grad, ffn_grad, norm_grad, col_grad, loss_ref,
    attn_m, attn_f, attn_s, attn_a, ffn_m, ffn_f, ffn_s, ffn_a,
    norm_m, norm_f, norm_s, norm_a, col_m, col_f, col_s, col_a,
    loss_out, query_out, passage_out,
    attn_mo, attn_fo, attn_so, attn_ao, ffn_mo, ffn_fo, ffn_so, ffn_ao,
    norm_mo, norm_fo, norm_so, norm_ao, col_mo, col_fo, col_so, col_ao, attn_co, ffn_co,
    attn_in, attn_res, attn_low, ffn_in, ffn_res, ffn_low, norm_in, norm_res, col_in, col_res, small, query, passage,
    in_sem, out_sem,
):
    loads, stores = [], []

    def load(source, target):
        copy = pltpu.make_async_copy(source, target, in_sem.at[len(loads)])
        copy.start()
        loads.append(copy)
        return copy

    def store(source, target):
        copy = pltpu.make_async_copy(source, target, out_sem.at[len(stores)])
        copy.start()
        stores.append(copy)

    groups = [
        [
            load(source.at[which], ffn_in.at[index, which])
            for index, source in enumerate((ffn_m, ffn_f, ffn_s, ffn_a, ffn_grad))
        ]
        for which in range(2)
    ]
    groups.append(
        [load(source, attn_in.at[index]) for index, source in enumerate((attn_m, attn_f, attn_s, attn_a, attn_grad))]
    )
    lines = norm_in.shape[1]
    groups.append(
        [load(source, norm_in.at[index]) for index, source in enumerate((norm_m, norm_f, norm_s, norm_a))]
        + [load(norm_grad, small.at[0]), load(loss_ref, small.at[1])]
        + [load(source, col_in.at[index]) for index, source in enumerate((col_m, col_f, col_s, col_a, col_grad))]
    )
    half = passage.shape[1] // 2
    parts = [(pair, pl.ds(at * half, half)) for pair in range(2) for at in range(2)]

    count = jnp.full((1, 1), step_ref[0], jnp.int32).astype(F32)
    rate = [jnp.full((1, 1), rates_ref[index], F32) for index in range(5)]
    to_first, to_second = [1.0 / (1.0 - jnp.exp(count * jnp.log(rate[index]))) for index in range(2)]

    def update(master, first, second, average, grad, learn, decay):
        first_new = rate[0] * first + (1.0 - rate[0]) * grad
        second_new = rate[1] * second + (1.0 - rate[1]) * grad * grad
        move = (first_new * to_first) / (jnp.sqrt(second_new * to_second) + ADAM_EPS)
        if decay:
            move = move + decay * master
        master_new = master - learn * move
        average_new = rate[2] * average + (1.0 - rate[2]) * master_new
        return master_new, first_new, second_new, average_new

    def wait(group):
        for copy in groups[group]:
            copy.wait()

    for which in range(2):
        wait(which)
        if which == 0:
            groups.append([load(query_ref, query)])
            for pair, place in parts:
                groups.append([load(passage_ref.at[pair, place, :], passage.at[pair, place, :])])
        values = update(*[ffn_in[index, which] for index in range(5)], rate[3], DECAY_WEIGHT)
        for index, (value, target) in enumerate(zip(values, (ffn_mo, ffn_fo, ffn_so, ffn_ao))):
            ffn_res[index, which] = value
            store(ffn_res.at[index, which], target.at[which])
        ffn_low[which] = values[0].astype(BF16)
        store(ffn_low.at[which], ffn_co.at[which])
    wait(4)
    store(query, query_out)
    for index, (pair, place) in enumerate(parts):
        wait(5 + index)
        store(passage.at[pair, place, :], passage_out.at[pair, place, :])
    wait(2)
    for which in range(attn_low.shape[0]):
        values = update(*[attn_in[index, which] for index in range(5)], rate[3], DECAY_WEIGHT)
        for index, value in enumerate(values):
            attn_res[index, which] = value
        attn_low[which] = values[0].astype(BF16)
    for index, target in enumerate((attn_mo, attn_fo, attn_so, attn_ao)):
        store(attn_res.at[index], target)
    store(attn_low, attn_co)
    wait(3)
    values = update(*[norm_in[index] for index in range(4)], small[0, pl.ds(0, lines), :], rate[4], 0.0)
    for index, (value, target) in enumerate(zip(values, (norm_mo, norm_fo, norm_so, norm_ao))):
        norm_res[index] = value
        store(norm_res.at[index], target)
    values = update(*[col_in[index] for index in range(5)], rate[4], 0.0)
    for index, (value, target) in enumerate(zip(values, (col_mo, col_fo, col_so, col_ao))):
        col_res[index] = value
        store(col_res.at[index], target)
    loss_out[0] = jnp.sum(small[1, pl.ds(3, 1), pl.ds(0, 1)])
    for copy in stores:
        copy.wait()


def finish(step, rates, grads, loss_rows, attn_state, ffn_state, norm_state, col_state):
    attn_grad, ffn_grad, norm_grad, col_grad, query_grad, passage_grad = grads
    anywhere = pl.BlockSpec(memory_space=pltpu.HBM)
    smem = pl.BlockSpec(memory_space=pltpu.SMEM)
    dma = pltpu.SemaphoreType.DMA
    col_state = [value.reshape(-1, LANES) for value in col_state]
    states = (attn_state, ffn_state, norm_state, col_state)
    shapes = [jax.ShapeDtypeStruct((1,), F32)]
    shapes += [jax.ShapeDtypeStruct(value.shape, F32) for value in (query_grad, passage_grad)]
    shapes += [jax.ShapeDtypeStruct(value.shape, F32) for state in states for value in state]
    shapes += [jax.ShapeDtypeStruct(state[0].shape, BF16) for state in (attn_state, ffn_state)]
    scratch = []
    for state in (attn_state, ffn_state):
        shape = state[0].shape
        scratch += [pltpu.VMEM((5,) + shape, F32), pltpu.VMEM((4,) + shape, F32), pltpu.VMEM(shape, BF16)]
    for state, count in ((norm_state, 4), (col_state, 5)):
        shape = state[0].shape
        scratch += [pltpu.VMEM((count,) + shape, F32), pltpu.VMEM((4,) + shape, F32)]
    outs = pl.pallas_call(
        finish_kernel,
        out_shape=tuple(shapes),
        in_specs=[smem] * 2 + [anywhere] * 23,
        out_specs=(smem,) + (anywhere,) * 20,
        scratch_shapes=scratch
        + [pltpu.VMEM((2,) + norm_grad.shape, F32), pltpu.VMEM(query_grad.shape, F32), pltpu.VMEM(passage_grad.shape, F32)]
        + [dma((32,)), dma((32,))],
        compiler_params=pltpu.CompilerParams(vmem_limit_bytes=60 * MIB),
        name="finish",
    )(step, rates, query_grad, passage_grad, attn_grad, ffn_grad, norm_grad, col_grad, loss_rows,
      *attn_state, *ffn_state, *norm_state, *col_state)
    outs = list(outs)
    outs[15:19] = [value.reshape(-1) for value in outs[15:19]]
    return outs


def attend_kernel(spans, lens_ref, q_ref, k_ref, v_ref, o_ref):
    for index, (start, slots) in enumerate(spans):
        length = lens_ref[index]
        keys = k_ref[0, pl.ds(start, slots), :]
        values = v_ref[0, pl.ds(start, slots), :]
        lane = first_head(keys.shape)
        scaled = keys * jnp.asarray(HD**-0.5, BF16)
        zero = jnp.zeros_like(scaled)
        head_keys = (jnp.where(lane, scaled, zero), jnp.where(lane, zero, scaled))
        block = min(slots, 256)
        for at in range(0, slots, block):
            queries = q_ref[0, pl.ds(start + at, block), :]
            outs = []
            for head in range(2):
                scores = mm_nt(queries, head_keys[head])
                valid = lax.broadcasted_iota(jnp.int32, scores.shape, 1) < length
                scores = jnp.where(valid, scores, NEG_FILL)
                top = jnp.max(scores, axis=1, keepdims=True)
                weight = jnp.exp(scores - top)
                total = jnp.sum(weight, axis=1, keepdims=True)
                probs = (weight * (1.0 / total)).astype(BF16)
                outs.append(mm(probs, values))
            o_ref[pl.ds(start + at, block), :] = jnp.where(
                first_head(outs[0].shape), outs[0], outs[1]
            ).astype(BF16)


def attend_back_kernel(spans, lens_ref, q_ref, k_ref, v_ref, g_ref, d_ref):
    scale = HD**-0.5
    for index, (start, slots) in enumerate(spans):
        length = lens_ref[index]
        keys = k_ref[0, pl.ds(start, slots), :]
        values = v_ref[0, pl.ds(start, slots), :]
        lane = first_head(keys.shape)
        scaled = keys * jnp.asarray(scale, BF16)
        zero = jnp.zeros_like(scaled)
        head_keys = (jnp.where(lane, scaled, zero), jnp.where(lane, zero, scaled))
        head_values = (jnp.where(lane, values, zero), jnp.where(lane, zero, values))
        block = min(slots, 256)
        grad_k = [None, None]
        grad_v = [None, None]
        for at in range(0, slots, block):
            queries = q_ref[0, pl.ds(start + at, block), :]
            grads = g_ref[pl.ds(start + at, block), :]
            grad_q = []
            for head in range(2):
                scores = mm_nt(head_keys[head], queries)
                valid = lax.broadcasted_iota(jnp.int32, scores.shape, 0) < length
                scores = jnp.where(valid, scores, NEG_FILL)
                top = jnp.max(scores, axis=0, keepdims=True)
                weight = jnp.exp(scores - top)
                total = jnp.sum(weight, axis=0, keepdims=True)
                probs = weight * (1.0 / total)
                grad_probs = mm_nt(head_values[head], grads)
                inner = jnp.sum(probs * grad_probs, axis=0, keepdims=True)
                grad_scores = (probs * (grad_probs - inner)).astype(BF16)
                part_v = mm(probs.astype(BF16), grads)
                part_k = mm(grad_scores, queries)
                grad_v[head] = part_v if at == 0 else grad_v[head] + part_v
                grad_k[head] = part_k if at == 0 else grad_k[head] + part_k
                grad_q.append(mm_tn(grad_scores, keys))
            d_ref[0, pl.ds(start + at, block), :] = (
                jnp.where(first_head(grad_q[0].shape), grad_q[0], grad_q[1]) * scale
            ).astype(BF16)
        d_ref[1, pl.ds(start, slots), :] = (jnp.where(lane, grad_k[0], grad_k[1]) * scale).astype(BF16)
        d_ref[2, pl.ds(start, slots), :] = jnp.where(lane, grad_v[0], grad_v[1]).astype(BF16)


def head_specs(tokens):
    return [pl.BlockSpec((1, tokens, LANES), functools.partial(lambda s, i, lens: (s, 0, i), s)) for s in range(3)]


def attend(proj, lens, spans):
    _, tokens, width = proj.shape
    flops = sum(4 * slots * slots * width for _, slots in spans)
    return pl.pallas_call(
        functools.partial(attend_kernel, spans),
        out_shape=jax.ShapeDtypeStruct((tokens, width), BF16),
        grid_spec=pltpu.PrefetchScalarGridSpec(
            num_scalar_prefetch=1,
            grid=(width // LANES,),
            in_specs=head_specs(tokens),
            out_specs=pl.BlockSpec((tokens, LANES), lambda i, lens: (0, i)),
        ),
        compiler_params=pltpu.CompilerParams(vmem_limit_bytes=40 * MIB),
        cost_estimate=pl.CostEstimate(flops=8 * flops, bytes_accessed=8 * tokens * width, transcendentals=0),
        name="attend",
    )(lens, proj, proj, proj)


def attend_back(proj, grad_out, lens, spans):
    _, tokens, width = proj.shape
    flops = sum(10 * slots * slots * width for _, slots in spans)
    return pl.pallas_call(
        functools.partial(attend_back_kernel, spans),
        out_shape=jax.ShapeDtypeStruct((3, tokens, width), BF16),
        grid_spec=pltpu.PrefetchScalarGridSpec(
            num_scalar_prefetch=1,
            grid=(width // LANES,),
            in_specs=head_specs(tokens) + [pl.BlockSpec((tokens, LANES), lambda i, lens: (0, i))],
            out_specs=pl.BlockSpec((3, tokens, LANES), lambda i, lens: (0, 0, i)),
        ),
        compiler_params=pltpu.CompilerParams(vmem_limit_bytes=40 * MIB),
        cost_estimate=pl.CostEstimate(flops=8 * flops, bytes_accessed=14 * tokens * width, transcendentals=0),
        name="attend_back",
    )(lens, proj, proj, proj, grad_out)


def up_kernel(x_ref, w_ref, b_ref, g_ref, s_ref):
    hidden = mm(x_ref[...], w_ref[0]) + b_ref[...]
    active, slope = gelu_and_slope(hidden)
    g_ref[...] = active.astype(BF16)
    s_ref[...] = slope


def feed_up(low, ffn_half, bias):
    tokens, width = low.shape
    units = ffn_half.shape[2]
    tile = 256
    return pl.pallas_call(
        up_kernel,
        out_shape=(jax.ShapeDtypeStruct((tokens, units), BF16), jax.ShapeDtypeStruct((tokens, units), F32)),
        grid=(units // tile,),
        in_specs=[
            pl.BlockSpec((tokens, width), lambda i: (0, 0)),
            pl.BlockSpec((1, width, tile), lambda i: (0, 0, i)),
            pl.BlockSpec((1, tile), lambda i: (0, i)),
        ],
        out_specs=(pl.BlockSpec((tokens, tile), lambda i: (0, i)), pl.BlockSpec((tokens, tile), lambda i: (0, i))),
        compiler_params=pltpu.CompilerParams(vmem_limit_bytes=40 * MIB),
        cost_estimate=pl.CostEstimate(
            flops=2 * tokens * width * units, bytes_accessed=8 * tokens * units, transcendentals=tokens * units
        ),
        name="feed_up",
    )(low, ffn_half, bias.reshape(1, -1))


def swap_cores(values):
    return lax.ppermute(values, "mp", [(0, 1), (1, 0)])


def scatter_sum(own_parts, other_parts):
    summed = [own + swap_cores(other).astype(F32) for own, other in zip(own_parts, other_parts)]
    return [lax.psum_scatter(value, "dp", scatter_dimension=1, tiled=True) for value in summed]


def adam_update(master, first, second, average, grad, rate, decay_w, rates, step_count):
    first_new = rates[0] * first + (1.0 - rates[0]) * grad
    second_new = rates[1] * second + (1.0 - rates[1]) * grad * grad
    fixed_one = first_new / (1.0 - rates[0] ** step_count)
    fixed_two = second_new / (1.0 - rates[1] ** step_count)
    master_new = master - rate * (fixed_one / (jnp.sqrt(fixed_two) + ADAM_EPS) + decay_w * master)
    average_new = rates[2] * average + (1.0 - rates[2]) * master_new
    return (master_new, first_new, second_new, average_new)


def forward_plain(tokens, lens, attn_low, ffn_low, col_bias, norm_params, spans):
    attn_full = lax.all_gather(attn_low, "dp", axis=1, tiled=True)
    ffn_full = lax.all_gather(ffn_low, "dp", axis=1, tiled=True)
    attn_w = (attn_full, swap_cores(attn_full))
    ffn_w = (ffn_full, swap_cores(ffn_full))
    col = (col_bias, swap_cores(col_bias))
    width = attn_w[0].shape[2]

    projected, mixed = [], []
    branch = None
    for half in range(2):
        bias = jnp.stack([col[half][:width], jnp.zeros((width,), F32), col[half][width : 2 * width]])
        proj = (
            jnp.einsum("td,sde->ste", tokens, attn_w[half][:3], preferred_element_type=F32) + bias[:, None, :]
        ).astype(BF16)
        out = attend(proj, lens, spans)
        part = mm_nt(out, attn_w[half][3])
        branch = part if branch is None else branch + part
        projected.append(proj)
        mixed.append(out)
    z_one = tokens.astype(F32) + branch + norm_params[0]
    unit_one, inverse_one = normalize(z_one)
    first_norm = unit_one * norm_params[1] + norm_params[2]
    first_low = first_norm.astype(BF16)
    active, slope = [], []
    branch_two = None
    for half in range(2):
        act, slo = feed_up(first_low, ffn_w[half], col[half][2 * width :])
        part = mm_nt(act, ffn_w[half][1])
        branch_two = part if branch_two is None else branch_two + part
        active.append(act)
        slope.append(slo)
    z_two = first_norm + branch_two + norm_params[3]
    return attn_w, ffn_w, projected, mixed, unit_one, inverse_one, first_low, active, slope, z_two


def loss_plain(z_two, lens, target_mine, norm_params, spans, pairs):
    query_slots, passage_slots = spans[0][1], spans[1][1]
    model_width = z_two.shape[1]
    core = lax.axis_index("mp")
    unit_two, inverse_two = normalize(z_two)
    places = jnp.arange(query_slots + passage_slots)
    in_query = (places < query_slots) & (places < lens[0])
    in_passage = (places >= query_slots) & (places - query_slots < lens[1])
    share = (
        jnp.stack([in_query, in_passage]).astype(F32) / lens.astype(F32)[:, None]
    )
    mean_unit = jnp.dot(share, unit_two, precision=PRECISE, preferred_element_type=F32)
    pooled = mean_unit * norm_params[4] + norm_params[5]
    shrink = lax.rsqrt(jnp.sum(pooled * pooled, axis=1, keepdims=True) + POOL_EPS)
    embed = pooled * shrink

    payload = jnp.concatenate([embed.reshape(-1), target_mine])
    every = lax.all_gather(payload, ("dp", "mp"), axis=0)
    every_q = every[:, :model_width]
    every_p = every[:, model_width : 2 * model_width]
    target = (jnp.arange(pairs)[None, :].astype(F32) == every[:, 2 * model_width :][:, :1]).astype(F32)
    logits = lax.dot_general(every_q, every_p, (((1,), (1,)), ((), ())), precision=PRECISE) / SOFTMAX_TEMPER
    row_top = jnp.max(logits, axis=1, keepdims=True)
    exp_logits = jnp.exp(logits - row_top)
    row_total = jnp.sum(exp_logits, axis=1, keepdims=True)
    log_total = row_top[:, 0] + jnp.log(row_total[:, 0])
    loss_value = (jnp.sum(log_total - jnp.sum(logits * target, axis=1)) / pairs).reshape(1)
    grad_logits = (exp_logits / row_total - target) / (pairs * SOFTMAX_TEMPER)
    rank = lax.axis_index("dp") * lax.axis_size("mp") + core
    grad_uq = jnp.dot(lax.dynamic_index_in_dim(grad_logits, rank, 0, keepdims=True), every_p, precision=PRECISE)
    grad_up = jnp.dot(
        lax.dynamic_index_in_dim(grad_logits, rank, 1, keepdims=False)[None], every_q, precision=PRECISE
    )
    grad_embed = jnp.concatenate([grad_uq, grad_up], axis=0)

    grad_pooled = shrink * (grad_embed - embed * jnp.sum(grad_embed * embed, axis=1, keepdims=True))
    grad_gain_two = jnp.sum(grad_pooled * mean_unit, axis=0)
    grad_shift_two = jnp.sum(grad_pooled, axis=0)
    grad_unit_two = lax.dot_general(
        share, grad_pooled * norm_params[4], (((0,), (0,)), ((), ())), precision=PRECISE
    )
    grad_ztwo = normalize_back(unit_two, inverse_two, grad_unit_two)
    grad_bias_two = jnp.sum(grad_ztwo, axis=0)
    grad_two_low = grad_ztwo.astype(BF16)
    return grad_ztwo, grad_two_low, loss_value, grad_bias_two, grad_gain_two, grad_shift_two


def backward_plain(tokens, lens, kept, grad_ztwo, grad_two_low, norm_params, second_grads, spans):
    attn_w, ffn_w, projected, mixed, unit_one, inverse_one, first_low, active, slope = kept
    grad_bias_two, grad_gain_two, grad_shift_two = second_grads
    query_slots = spans[0][1]
    core = lax.axis_index("mp")
    cut = ffn_w[0].shape[2] // 2
    width = attn_w[0].shape[2]

    def two_parts(values):
        return values[:, :cut], values[:, cut:]

    def parted_product(left, halves):
        own = [mm_tn(left, part)[None] for part in two_parts(halves[0])]
        other = [mm_tn(left, part).astype(BF16)[None] for part in two_parts(halves[1])]
        return own, other

    down_grad = scatter_sum(*parted_product(grad_two_low, active))
    grad_hidden, grad_first = [], grad_ztwo
    for half in (1, 0):
        grad_hid = (mm(grad_two_low, ffn_w[half][1]) * slope[half]).astype(BF16)
        grad_hidden.insert(0, grad_hid)
        grad_first = grad_first + mm_nt(grad_hid, ffn_w[half][0])
    grad_hidden_bias = [jnp.sum(value.astype(F32), axis=0) for value in grad_hidden]
    up_grad = scatter_sum(*parted_product(first_low, grad_hidden))

    grad_gain_one = jnp.sum(grad_first * unit_one, axis=0)
    grad_shift_one = jnp.sum(grad_first, axis=0)
    grad_zone = normalize_back(unit_one, inverse_one, grad_first * norm_params[1])
    grad_bias_out = jnp.sum(grad_zone, axis=0)
    grad_one_low = grad_zone.astype(BF16)
    grad_tokens = grad_zone
    grad_query_bias, grad_value_bias, attn_parts = [None, None], [None, None], [None, None]
    for half in (1, 0):
        grad_out = mm(grad_one_low, attn_w[half][3]).astype(BF16)
        grad_proj = attend_back(projected[half], grad_out, lens, spans)
        grad_query_bias[half] = jnp.sum(grad_proj[0].astype(F32), axis=0)
        grad_value_bias[half] = jnp.sum(grad_proj[2].astype(F32), axis=0)
        in_grads = jnp.einsum("td,ste->sde", tokens, grad_proj, preferred_element_type=F32)
        out_grad = mm_tn(grad_one_low, mixed[half])
        parts = [in_grads[:2], jnp.stack([in_grads[2], out_grad])]
        attn_parts[half] = parts if half == 0 else [part.astype(BF16) for part in parts]
        for index in range(3):
            grad_tokens = grad_tokens + mm_nt(grad_proj[index], attn_w[half][index])
    attn_grads = scatter_sum(*attn_parts)

    col_parts = [
        jnp.concatenate([grad_query_bias[half], grad_value_bias[half], grad_hidden_bias[half]]) for half in range(2)
    ]
    norm_part = jnp.stack(
        [grad_bias_out, grad_gain_one, grad_shift_one, grad_bias_two, grad_gain_two, grad_shift_two]
    )
    norm_part = norm_part + swap_cores(norm_part)
    col_part = col_parts[0] + swap_cores(col_parts[1])
    small = lax.psum(jnp.concatenate([norm_part.reshape(-1), col_part]), "dp")
    norm_grad = small[: norm_part.size].reshape(norm_part.shape)
    col_grad = small[norm_part.size :]

    attn_grad = jnp.concatenate(attn_grads, axis=0)
    ffn_grad = jnp.stack([jnp.concatenate(parts, axis=-1)[0] for parts in (up_grad, down_grad)])
    grad_twin = swap_cores(grad_tokens)
    first_pair = jnp.where(core == 0, grad_tokens, grad_twin)
    second_pair = jnp.where(core == 0, grad_twin, grad_tokens)
    query_grad = jnp.stack([first_pair[:query_slots], second_pair[:query_slots]])
    passage_grad = jnp.stack([first_pair[query_slots:], second_pair[query_slots:]])
    return attn_grad, ffn_grad, norm_grad, col_grad, query_grad, passage_grad


def per_device(
    query_in,
    passage_in,
    query_len,
    passage_len,
    positive,
    step,
    rates,
    attn_master,
    attn_first,
    attn_second,
    attn_average,
    ffn_master,
    ffn_first,
    ffn_second,
    ffn_average,
    norm_params,
    norm_first,
    norm_second,
    norm_average,
    col_bias,
    col_first,
    col_second,
    col_average,
):
    size = lax.axis_size("dp")
    query_slots = query_in.shape[1]
    spans = ((0, query_slots), (query_slots, passage_in.shape[1]))
    pairs = query_in.shape[0] * size
    attn_state = (attn_master, attn_first, attn_second, attn_average)
    ffn_state = (ffn_master, ffn_first, ffn_second, ffn_average)
    norm_state = (norm_params, norm_first, norm_second, norm_average)
    col_state = (col_bias, col_first, col_second, col_average)
    if size == 16:
        kept = forward(
            query_in, passage_in, query_len, passage_len, positive, attn_master, ffn_master, col_bias, norm_params, spans,
            pairs,
        )
        grads = backward(query_len, passage_len, kept, norm_params, spans)
        return tuple(finish(step, rates, grads, kept[11], attn_state, ffn_state, norm_state, col_state))

    core = lax.axis_index("mp")

    def pick(values, index):
        return lax.dynamic_index_in_dim(values, index, 0, keepdims=False)

    tokens = jnp.concatenate([pick(query_in, core), pick(passage_in, core)], axis=0)
    lens = jnp.stack([pick(query_len, core), pick(passage_len, core)])
    target = jnp.broadcast_to(pick(positive, core).astype(F32), (LANES,))
    outs = forward_plain(tokens, lens, attn_master.astype(BF16), ffn_master.astype(BF16), col_bias, norm_params, spans)
    kept, z_two = outs[:9], outs[9]
    outs = loss_plain(z_two, lens, target, norm_params, spans, pairs)
    grad_ztwo, grad_two_low, loss_value, *second_grads = outs
    attn_grad, ffn_grad, norm_grad, col_grad, query_grad, passage_grad = backward_plain(
        tokens, lens, kept, grad_ztwo, grad_two_low, norm_params, second_grads, spans
    )
    step_count = step[0].astype(F32)
    outs = []
    for state, grad, rate, decay in (
        (attn_state, attn_grad, rates[3], DECAY_WEIGHT),
        (ffn_state, ffn_grad, rates[3], DECAY_WEIGHT),
        (norm_state, norm_grad, rates[4], 0.0),
        (col_state, col_grad, rates[4], 0.0),
    ):
        outs.extend(adam_update(*state, grad, rate, decay, rates, step_count))
    return (loss_value, query_grad, passage_grad, *outs, outs[0].astype(BF16), outs[4].astype(BF16))


def solution(mesh):
    matrix = P(None, "dp", "mp")
    rows = P("dp", None, None)
    placed = (rows, rows, P("dp"), P("dp"), P("dp"), P(), P(), *[matrix] * 8, *[P()] * 4, *[P("mp")] * 4)
    return jax.shard_map(
        per_device,
        mesh=mesh,
        in_specs=placed,
        out_specs=(P(), rows, rows, *[matrix] * 8, *[P()] * 4, *[P("mp")] * 4, matrix, matrix),
        check_vma=False,
    )
```
